32 devices in a mesh: ctx: 8 (over y, x, core), fsdp: 4 (over z).
Axes of the slice: x: 2, y: 2, z: 4, core: 2. Of those that a mesh axis runs over, the one named last changes fastest.
Arguments:
- states: bfloat16 [4, 3072, 768], P('fsdp', 'ctx'), may hold values from -6 to 6
- lengths: int32 [4], replicated, may hold values from 768 to 3072, as said below
- query_weight: bfloat16 [768, 768], P('fsdp'), may hold values from -0.3125 to 0.3125
- query_bias: bfloat16 [768], P('fsdp'), may hold values from -3 to 3
- key_weight: bfloat16 [768, 768], P('fsdp'), may hold values from -0.3125 to 0.3125
- value_weight: bfloat16 [768, 768], P('fsdp'), may hold values from -0.21875 to 0.21875
- value_bias: bfloat16 [768], P('fsdp'), may hold values from -3 to 3
- output_weight: bfloat16 [768, 768], P('fsdp'), may hold values from -1.25 to 1.25
- output_bias: bfloat16 [768], P('fsdp'), may hold values from -3 to 3
- first_gain: bfloat16 [768], P('fsdp'), may hold values from 0.25 to 1.75
- first_shift: bfloat16 [768], P('fsdp'), may hold values from -3 to 3
- inner_weight: bfloat16 [768, 3072], P('fsdp'), may hold values from -0.21875 to 0.21875
- inner_bias: bfloat16 [3072], P('fsdp'), may hold values from -3 to 3
- outer_weight: bfloat16 [3072, 768], P('fsdp'), may hold values from -0.109375 to 0.109375
- outer_bias: bfloat16 [768], P('fsdp'), may hold values from -3 to 3
- second_gain: bfloat16 [768], P('fsdp'), may hold values from 0.25 to 1.75
- second_shift: bfloat16 [768], P('fsdp'), may hold values from -3 to 3
- cotangent: bfloat16 [4, 3072, 768], P('fsdp', 'ctx'), may hold values from -6 to 6
Outputs:
- layer_output: bfloat16 [4, 3072, 768], P('fsdp', 'ctx')
- input_grad: bfloat16 [4, 3072, 768], P('fsdp', 'ctx')
- query_weight_grad: float32 [768, 768], P('fsdp')
- query_bias_grad: float32 [768], P('fsdp')
- key_weight_grad: float32 [768, 768], P('fsdp')
- value_weight_grad: float32 [768, 768], P('fsdp')
- value_bias_grad: float32 [768], P('fsdp')
- output_weight_grad: float32 [768, 768], P('fsdp')
- output_bias_grad: float32 [768], P('fsdp')
- first_gain_grad: float32 [768], P('fsdp')
- first_shift_grad: float32 [768], P('fsdp')
- inner_weight_grad: float32 [768, 3072], P('fsdp')
- inner_bias_grad: float32 [3072], P('fsdp')
- outer_weight_grad: float32 [3072, 768], P('fsdp')
- outer_bias_grad: float32 [768], P('fsdp')
- second_gain_grad: float32 [768], P('fsdp')
- second_shift_grad: float32 [768], P('fsdp')
The draws below stay inside these ranges and needn't reach their ends.
Inputs may be any that keep to these rules, and one draw needn't show every extreme that they name: lengths[s] is the number of leading slots of sequence s that hold tokens; one sequence is full and one holds exactly 768.
All inputs are finite; a program needn't handle non-finite values.
Results may differ from the reference program's by a relative error of at most 0.025.
Values may be sent and summed in bfloat16 or wider, within the bound.
A program may use at most 128 MiB of HBM per device.

```python
import math
import jax
import jax.numpy as jnp
from jax import lax

D = 768
H = 12
HD = 64
FF = 3072
SEQ_LEN = 3072
SEQS = 4


def draw_lengths(key, part):
    first_key = jax.random.fold_in(key, 11)
    second_key = jax.random.fold_in(key, 23)
    drawn = jax.random.randint(first_key, (SEQS,), SEQ_LEN // 4, SEQ_LEN + 1, dtype=jnp.int32)
    order = jax.random.permutation(second_key, SEQS)
    drawn = drawn.at[order[0]].set(SEQ_LEN)
    drawn = drawn.at[order[1]].set(SEQ_LEN // 4)
    return drawn.astype(jnp.int32)


def steps_of(own_key, shape, shards, least, high):
    def one(dim, parts):
        heights = jax.random.uniform(jax.random.fold_in(jax.random.fold_in(own_key, 6), dim), (parts,), jnp.float32, least / len(shards), high / len(shards))
        return jnp.repeat(jnp.exp(heights), shape[dim] // parts).reshape((-1,) + (1,) * (len(shape) - dim - 1))

    loudness = one(*shards[0])
    for cut in shards[1:]:
        loudness = loudness * one(*cut)
    return loudness


def bell_draw(rng, extent, scale, most, shards=(), kind=jnp.bfloat16):
    result = scale * jax.random.normal(rng, extent, jnp.float32)
    if shards:
        result = result * steps_of(rng, extent, shards, -0.22, 0.18)
    return jnp.clip(result, -most, most).astype(kind)


def setup_inputs(seed: int = 0) -> dict:
    splits = jax.random.split(jax.random.key(seed), 19)
    return {
        "states": bell_draw(splits[0], (SEQS, SEQ_LEN, D), 1.0, 6.0, ((0, 4), (1, 8))),
        "lengths": draw_lengths(jax.random.fold_in(splits[18], 71), 0),
        "query_weight": bell_draw(splits[2], (D, D), (D // 2) ** -0.5, 0.3125, ((0, 4),)),
        "query_bias": bell_draw(splits[3], (D,), 0.5, 3.0, ((0, 4),)),
        "key_weight": bell_draw(splits[4], (D, D), (D // 2) ** -0.5, 0.3125, ((0, 4),)),
        "value_weight": bell_draw(splits[5], (D, D), D ** -0.5, 0.21875, ((0, 4),)),
        "value_bias": bell_draw(splits[6], (D,), 0.5, 3.0, ((0, 4),)),
        "output_weight": bell_draw(splits[7], (D, D), (max(1, 96 * D // SEQ_LEN)) ** -0.5, 1.25, ((0, 4),)),
        "output_bias": bell_draw(splits[8], (D,), 0.5, 3.0, ((0, 4),)),
        "first_gain": jnp.clip(1.0 + 0.15 * jax.random.normal(splits[9], (D,), jnp.float32), 0.25, 1.75).astype(jnp.bfloat16),
        "first_shift": bell_draw(splits[10], (D,), 0.5, 3.0, ((0, 4),)),
        "inner_weight": bell_draw(splits[11], (D, FF), D ** -0.5, 0.21875, ((0, 4),)),
        "inner_bias": bell_draw(splits[12], (FF,), 0.5, 3.0, ((0, 4),)),
        "outer_weight": bell_draw(splits[13], (FF, D), FF ** -0.5, 0.109375, ((0, 4),)),
        "outer_bias": bell_draw(splits[14], (D,), 0.5, 3.0, ((0, 4),)),
        "second_gain": jnp.clip(1.0 + 0.15 * jax.random.normal(splits[15], (D,), jnp.float32), 0.25, 1.75).astype(jnp.bfloat16),
        "second_shift": bell_draw(splits[16], (D,), 0.5, 3.0, ((0, 4),)),
        "cotangent": bell_draw(splits[17], (SEQS, SEQ_LEN, D), 1.0, 6.0, ((0, 4), (1, 8))),
    }


@jax.custom_vjp
def low(v):
    return lax.optimization_barrier(v.astype(jnp.bfloat16)).astype(jnp.float32)

@jax.custom_vjp
def low_back(v):
    return v

def low_keep(v):
    return (low(v), None)

def low_pass(kept, grad):
    return (grad,)

def back_keep(v):
    return (v, None)

def back_low(kept, grad):
    return (low(grad),)
low.defvjp(low_keep, low_pass)
low_back.defvjp(back_keep, back_low)

def product(left, right):
    return jnp.dot(left, right, precision=lax.Precision.HIGHEST)

def normalize(hidden, gain, shift):
    centred = hidden - lax.optimization_barrier(jnp.mean(hidden, axis=-1, keepdims=True))
    scale = lax.rsqrt(lax.optimization_barrier(jnp.mean(centred * centred, axis=-1, keepdims=True)) + 1e-05)
    return centred * scale * gain + shift

def attention(queries, key_rows, values, keep):
    block = math.gcd(512, SEQ_LEN)
    query_heads = queries.reshape(SEQ_LEN // block, block, H, HD)
    key_heads = key_rows.reshape(SEQ_LEN, H, HD)
    value_heads = values.reshape(SEQ_LEN, H, HD)

    def one_block(query_block):
        scores = jnp.einsum('qhd,khd->hqk', query_block, key_heads, precision=lax.Precision.HIGHEST)
        scores = low_back(scores)
        scores = jnp.where(keep[None, None, :], scores, -1e+30)
        log_total = jax.nn.logsumexp(scores, axis=-1, keepdims=True)
        probs = low(jnp.exp(scores - log_total))
        return jnp.einsum('hqk,khd->qhd', probs, value_heads, precision=lax.Precision.HIGHEST)
    blocks = lax.map(jax.checkpoint(one_block), query_heads)
    return blocks.reshape(SEQ_LEN, D)

def sequence_forward(params, states, length):
    query_weight, query_bias, key_weight, value_weight, value_bias, output_weight, output_bias, first_gain, first_shift, inner_weight, inner_bias, outer_weight, outer_bias, second_gain, second_shift = params
    keep = jnp.arange(SEQ_LEN, dtype=jnp.int32) < length
    queries = low_back(low((product(states, query_weight) + query_bias) * 0.125))
    key_rows = low_back(low(product(states, key_weight)))
    values = low_back(low(product(states, value_weight) + value_bias))
    mixed = low_back(low(attention(queries, key_rows, values, keep)))
    attended = low_back(product(mixed, output_weight)) + output_bias
    first = normalize(states + attended, first_gain, first_shift)
    inner = low_back(product(low(first), inner_weight)) + inner_bias
    activated = low(jax.nn.gelu(inner, approximate=False))
    outer = low_back(product(activated, outer_weight)) + outer_bias
    second = normalize(first + outer, second_gain, second_shift)
    return jnp.where(keep[:, None], second, 0.0)

def reference(states, lengths, query_weight, query_bias, key_weight, value_weight, value_bias, output_weight, output_bias, first_gain, first_shift, inner_weight, inner_bias, outer_weight, outer_bias, second_gain, second_shift, cotangent):
    params = (query_weight.astype(jnp.float32), query_bias.astype(jnp.float32), key_weight.astype(jnp.float32), value_weight.astype(jnp.float32), value_bias.astype(jnp.float32), output_weight.astype(jnp.float32), output_bias.astype(jnp.float32), first_gain.astype(jnp.float32), first_shift.astype(jnp.float32), inner_weight.astype(jnp.float32), inner_bias.astype(jnp.float32), outer_weight.astype(jnp.float32), outer_bias.astype(jnp.float32), second_gain.astype(jnp.float32), second_shift.astype(jnp.float32))
    inputs = states.astype(jnp.float32)
    upstream = cotangent.astype(jnp.float32)

    def forward(params, inputs):

        def one_sequence(carried, member):
            sequence_states, length = member
            return (carried, jax.checkpoint(sequence_forward)(params, sequence_states, length))
        unused, outputs = lax.scan(one_sequence, jnp.zeros((), jnp.float32), (inputs, lengths))
        return outputs
    outputs, pullback = jax.vjp(forward, params, inputs)
    param_grads, input_grad = pullback(upstream)
    return (outputs.astype(jnp.bfloat16), input_grad.astype(jnp.bfloat16), param_grads[0].astype(jnp.float32), param_grads[1].astype(jnp.float32), param_grads[2].astype(jnp.float32), param_grads[3].astype(jnp.float32), param_grads[4].astype(jnp.float32), param_grads[5].astype(jnp.float32), param_grads[6].astype(jnp.float32), param_grads[7].astype(jnp.float32), param_grads[8].astype(jnp.float32), param_grads[9].astype(jnp.float32), param_grads[10].astype(jnp.float32), param_grads[11].astype(jnp.float32), param_grads[12].astype(jnp.float32), param_grads[13].astype(jnp.float32), param_grads[14].astype(jnp.float32))
```

```python
import functools

import jax
import jax.numpy as jnp
from jax import lax
from jax.experimental import pallas as pl
from jax.experimental.pallas import tpu as pltpu
from jax.sharding import PartitionSpec as P

D = 768
H = 12
HD = 64


epsilon = 1e-05


def passed_along(value, axis, steps):
    count = lax.axis_size(axis)
    pairs = [(source, (source + steps) % count) for source in range(count)]
    return lax.ppermute(value, axis, pairs)


def normalize(hidden):
    centred = hidden - jnp.mean(hidden, axis=1, keepdims=True)
    scale = lax.rsqrt(jnp.mean(centred * centred, axis=1, keepdims=True) + epsilon)
    return (centred * scale, scale)


def norm_back(upstream, normed, scale, gain):
    gain_grad = jnp.sum(upstream * normed, axis=0)
    shift_grad = jnp.sum(upstream, axis=0)
    scaled = upstream * gain
    hidden_grad = scale * (
        scaled
        - jnp.mean(scaled, axis=1, keepdims=True)
        - normed * jnp.mean(scaled * normed, axis=1, keepdims=True)
    )
    return (hidden_grad, gain_grad, shift_grad)


def gelu_slope(inner):
    return (
        0.5 * (1.0 + lax.erf(inner * 0.7071067811865476))
        + inner * jnp.exp(-0.5 * inner * inner) * 0.3989422804014327
    )


bf16 = jnp.bfloat16
f32 = jnp.float32
D = 768
H = 12
HD = 64
FF = 3072
ROWS = 384
CTX = 8
GROUP = 4
LOCAL = 3
SLOTS = 3072
QUERIES = 1536
TILE = 768
CHUNK = 512
WIDE = 640
MESH = pl.DeviceIdType.MESH


def multiple(value, step):
    return pl.multiple_of(value * step, step)


class Place:
    def __init__(self):
        self.c = lax.axis_index("ctx")
        self.z = lax.axis_index("fsdp")
        c = self.c
        self.core = c % 2
        self.p = c // 2
        self.x = self.p % 2
        self.y = c // 4
        self.p_x = self.p + 1 - 2 * self.x
        self.p_y = self.p + 2 - 4 * self.y
        self.p_d = self.p_y + 1 - 2 * self.x
        self.to_core = (c + 1 - 2 * self.core, self.z)
        self.to_x = (2 * self.p_x + self.core, self.z)
        self.to_y = (2 * self.p_y + self.core, self.z)
        self.to_d = (2 * self.p_d + self.core, self.z)

    def to_z(self, step):
        return (self.c, (self.z + step) % GROUP)

    def from_z(self, step):
        return (self.z + GROUP - step) % GROUP


class Net:
    def __init__(self, sends, receives):
        self.sends = sends
        self.receives = receives
        self.index = {}
        self.open = []

    def of(self, name):
        return self.index.setdefault(name, len(self.index))

    def copy(self, name, src, dst, device):
        i = self.of(name)
        return pltpu.make_async_remote_copy(
            src_ref=src,
            dst_ref=dst,
            send_sem=self.sends.at[i],
            recv_sem=self.receives.at[i],
            device_id=device,
            device_id_type=MESH,
        )

    def start(self, name, src, dst, device):
        self.launch(name, lambda: (src, dst, device))

    def launch(self, name, make):
        self.copy(name, *make()).start()
        self.open.append((name, make))

    def landed(self, name, dst, device):
        self.copy(name, dst, dst, device).wait_recv()

    def drain(self):
        for name, make in self.open:
            self.copy(name, *make()).wait_send()
        self.open = []


def greet(place, with_z=True):
    barrier = pltpu.get_barrier_semaphore()
    partners = [place.to_core, place.to_x, place.to_y, place.to_d]
    if with_z:
        partners += [place.to_z(step) for step in range(1, GROUP)]
    for partner in partners:
        pl.semaphore_signal(barrier, inc=1, device_id=partner, device_id_type=MESH)
    pl.semaphore_wait(barrier, len(partners))


def dot(a, b):
    return jnp.dot(a, b, preferred_element_type=f32)


def dot_nt(a, b):
    return lax.dot_general(a, b, (((1,), (1,)), ((), ())), preferred_element_type=f32)


def forward_kernel(
    length,
    x_in,
    wqkv_in,
    vec_in,
    inner_in,
    outer_in,
    wo_in,
    xall_out,
    wqkv_out,
    vec_out,
    inner_out,
    outer_out,
    wo_out,
    mixed_out,
    qt_out,
    ka_out,
    va_out,
    kt_out,
    ot_out,
    lse_out,
    xall,
    wqkv,
    vec,
    qt,
    ka,
    va,
    kt,
    vt,
    ot,
    lse,
    mix,
    acc,
    top,
    sends,
    receives,
    locals_,
):
    at = Place()
    net = Net(sends, receives)
    c, z, core, p = at.c, at.z, at.core, at.p
    part = c
    own = []

    def local(src, dst):
        copy = pltpu.make_async_copy(src, dst, locals_.at[len(own)])
        own.append(copy)
        copy.start()
        return copy

    def inner_at(ref, chip, side):
        return ref.at[:, pl.ds(multiple(2 * chip + side, 384), 384)]

    def outer_at(ref, chip, side):
        return ref.at[2 * chip + side]

    def wo_at(ref, chip, side):
        return ref.at[chip, :, pl.ds(multiple(side, 384), 384)]

    weights = {
        "wo": (wo_in, wo_out, wo_at),
        "outer": (outer_in, outer_out, outer_at),
        "inner": (inner_in, inner_out, inner_at),
    }

    greet(at)

    low, high = pl.ds(0, 192), pl.ds(192, 192)
    net.start("sx0", x_in.at[low], xall.at[c, low], at.to_x)
    net.start("sy1", x_in.at[high], xall.at[c, high], at.to_y)
    net.start("sx1", x_in.at[high], xall.at[c, high], at.to_x)
    net.start("sy0", x_in.at[low], xall.at[c, low], at.to_y)
    net.start("sc", x_in, xall.at[c], at.to_core)
    for step in range(1, GROUP):
        net.start(f"vec{step}", vec_in, vec.at[z], at.to_z(step))
    for step in range(1, GROUP):
        net.start(f"wq{step}", wqkv_in.at[core], wqkv.at[z, core], at.to_z(step))
    for name, (src, dst, region) in weights.items():
        for step in range(1, GROUP):
            net.start(
                f"{name}z{step}", region(src, p, core), region(dst.at[z], p, core), at.to_z(step)
            )
    first = [local(x_in, xall.at[c]), local(vec_in, vec.at[z]), local(wqkv_in, wqkv.at[z])]
    local(inner_in, inner_out.at[z])
    local(outer_in, outer_out.at[z])
    local(wo_in, wo_out.at[z])

    row64 = lax.broadcasted_iota(jnp.int32, (64, QUERIES), 0)
    for h in range(LOCAL):
        qt[h, 64:128, :] = jnp.where(row64 == 0, 1.0, 0.0).astype(bf16)
        row16 = lax.broadcasted_iota(jnp.int32, (16, SLOTS), 0)
        vt[h, 64:80, :] = jnp.where(row16 == 0, 1.0, 0.0).astype(bf16)

    for step in range(1, GROUP):
        net.landed(f"wq{step}", wqkv.at[at.from_z(step), core], at.to_z(step))
        source = at.from_z(step)
        net.start(f"wqc{step}", wqkv.at[source, core], wqkv.at[source, core], at.to_core)
    cx, cy, cd = at.to_x[0], at.to_y[0], at.to_d[0]
    net.landed("sx0", xall.at[cx, low], at.to_x)
    net.start("rx0", xall.at[cx, low], xall.at[cx, low], at.to_y)
    net.landed("sy1", xall.at[cy, high], at.to_y)
    net.start("ry1", xall.at[cy, high], xall.at[cy, high], at.to_x)
    net.landed("sx1", xall.at[cx, high], at.to_x)
    net.start("cx", xall.at[cx], xall.at[cx], at.to_core)
    net.landed("sy0", xall.at[cy, low], at.to_y)
    net.start("cy", xall.at[cy], xall.at[cy], at.to_core)
    for copy in first:
        copy.wait()
    for step in range(1, GROUP):
        net.landed(f"vec{step}", vec.at[at.from_z(step)], at.to_z(step))
        source = at.from_z(step)
        net.landed(f"wqc{step}", wqkv.at[source, 1 - core], at.to_core)

    bias = vec[p][0:1, 0:WIDE].astype(f32)
    lane = lax.broadcasted_iota(jnp.int32, (ROWS, 128), 1)
    row = lax.broadcasted_iota(jnp.int32, (ROWS, 128), 0)
    count = length[0]

    def project(block, column):
        rows = xall[block]
        keep = block * ROWS + row < count
        mark = jnp.where(keep, 0.0, -1e30)
        at_rows = pl.ds(multiple(block, ROWS), ROWS)
        width = 384 if column is None else WIDE
        full = wqkv[...].reshape(D, WIDE)
        y = dot(rows, full[:, 0:width]) + bias[:, 0:width]
        for h in range(LOCAL):
            g = y[:, 128 * h : 128 * h + 128]
            ka[h, at_rows, :] = jnp.where(
                lane < 64, g, jnp.where(lane == 64, mark, jnp.where(lane < 68, 1.0, 0.0))
            ).astype(bf16)
            va[h, at_rows, :] = jnp.where(
                lane < 64, pltpu.roll(g, 64, 1), jnp.where(lane < 67, 1.0, 0.0)
            ).astype(bf16)
            turned = g.T.astype(bf16)
            kt[h, :, at_rows] = turned[0:64]
            vt[h, 0:64, at_rows] = turned[64:128]
        if column is not None:
            q = (y[:, 384:WIDE] * 0.125).T.astype(bf16)
            for h in range(LOCAL):
                qt[h, 0:64, 384 * column : 384 * column + 384] = q[64 * h : 64 * h + 64]

    project(c, 3)
    net.landed("sc", xall.at[at.to_core[0]], at.to_core)
    project(at.to_core[0], None)
    project(cx, 1)
    project(cy, 2)
    net.landed("cx", xall.at[cx + 1 - 2 * core], at.to_core)
    project(cx + 1 - 2 * core, None)
    net.landed("cy", xall.at[cy + 1 - 2 * core], at.to_core)
    project(cy + 1 - 2 * core, None)
    net.landed("rx0", xall.at[cd, low], at.to_y)
    net.landed("ry1", xall.at[cd, high], at.to_x)
    net.start("cd", xall.at[cd], xall.at[cd], at.to_core)
    project(cd, 0)
    net.landed("cd", xall.at[cd + 1 - 2 * core], at.to_core)
    project(cd + 1 - 2 * core, None)

    local(xall, xall_out)
    local(wqkv, wqkv_out)
    local(vec, vec_out)
    local(qt, qt_out)
    local(ka, ka_out)
    local(va, va_out)
    local(kt, kt_out)

    def part_of(name, step, chip, side):
        _, dst, region = weights[name]
        return region(dst.at[at.from_z(step)], chip, side)

    def hand(label, name, step, chip, device):
        def make():
            ref = part_of(name, step, chip, core)
            return ref, ref, device

        net.launch(label, make)

    def plane_out(name):
        for step in range(1, GROUP):
            net.landed(f"{name}z{step}", part_of(name, step, p, core), at.to_z(step))
            hand(f"{name}x{step}", name, step, p, at.to_x)
            hand(f"{name}y{step}", name, step, p, at.to_y)
            hand(f"{name}c{step}", name, step, p, at.to_core)

    def plane_relay(name, via_x):
        for step in range(1, GROUP):
            net.landed(f"{name}x{step}", part_of(name, step, at.p_x, core), at.to_x)
            net.landed(f"{name}y{step}", part_of(name, step, at.p_y, core), at.to_y)
            if via_x:
                hand(f"{name}r{step}", name, step, at.p_y, at.to_x)
            else:
                hand(f"{name}r{step}", name, step, at.p_x, at.to_y)
            hand(f"{name}cx{step}", name, step, at.p_x, at.to_core)
            hand(f"{name}cy{step}", name, step, at.p_y, at.to_core)

    def plane_last(name, via_x):
        for step in range(1, GROUP):
            far = part_of(name, step, at.p_d, core)
            net.landed(f"{name}r{step}", far, at.to_x if via_x else at.to_y)
            hand(f"{name}cd{step}", name, step, at.p_d, at.to_core)

    def plane_in(name):
        for step in range(1, GROUP):
            for tag, chip in (("c", p), ("cx", at.p_x), ("cy", at.p_y), ("cd", at.p_d)):
                net.landed(f"{name}{tag}{step}", part_of(name, step, chip, 1 - core), at.to_core)

    plane_out("wo")

    def attend(h, tile):
        cols = pl.ds(TILE * tile, TILE)
        queries = qt[h, :, cols]
        for j in range(SLOTS // CHUNK):
            rows = pl.ds(CHUNK * j, CHUNK)
            scores = dot(ka[h, rows, :], queries)
            peak = jnp.max(scores, axis=0, keepdims=True)
            if j == 0:
                newest = peak
            else:
                newest = jnp.maximum(top[0:1, :], peak)
                factor = jnp.exp(top[0:1, :] - newest)
            probs = jnp.exp(scores - newest).astype(bf16)
            update = dot(vt[h, :, rows], probs)
            if j == 0:
                acc[...] = update
            else:
                acc[...] = acc[...] * factor + update
            top[0:1, :] = newest
        total = acc[64:65, :]
        value = acc[0:64, :] / total
        ot[h, :, cols] = value
        lse[h, 0:1, cols] = top[0:1, :] + jnp.log(total)
        low_value = value.astype(bf16)
        at_head = pl.ds(multiple(h, 64), 64)
        mix[2 * tile, at_head, :] = low_value[:, 0:384]
        mix[2 * tile + 1, at_head, :] = low_value[:, 384:768]

    plan = {
        (0, 1): [lambda: plane_relay("wo", True), lambda: plane_out("outer")],
        (0, 2): [lambda: plane_last("wo", True)],
        (1, 0): [lambda: plane_relay("outer", False), lambda: plane_out("inner")],
        (1, 2): [lambda: plane_last("outer", False)],
    }

    def take(steps):
        for step in steps:
            step()

    for tile in range(QUERIES // TILE):

        def head(h, carried, tile=tile):
            for (which, when), steps in plan.items():
                if which == tile:
                    pl.when(h == when)(functools.partial(take, steps))
            attend(h, tile)
            return carried

        lax.fori_loop(0, LOCAL, head, 0)
        if tile == 0:
            net.start("md", mix.at[0], mixed_out.at[p], at.to_d)
            net.start("mx", mix.at[1], mixed_out.at[p], at.to_x)
        else:
            net.start("my", mix.at[2], mixed_out.at[p], at.to_y)
            local(mix.at[3], mixed_out.at[p])
    local(ot, ot_out)
    local(lse, lse_out)
    plane_relay("inner", True)
    plane_last("inner", True)
    for name in weights:
        plane_in(name)
    net.landed("md", mixed_out.at[at.p_d], at.to_d)
    net.landed("mx", mixed_out.at[at.p_x], at.to_x)
    net.landed("my", mixed_out.at[at.p_y], at.to_y)
    for copy in own[3:]:
        copy.wait()
    net.drain()


FORWARD_COPIES = 112


def forward_call(length, x, wqkv, vec, inner, outer, wo):
    any_ = pl.BlockSpec(memory_space=pl.ANY)
    shape = jax.ShapeDtypeStruct
    return pl.pallas_call(
        forward_kernel,
        name="forward_attention",
        out_shape=(
            shape((CTX, ROWS, D), bf16),
            shape((GROUP, 2, 96, WIDE), bf16),
            shape((GROUP, 16, D), bf16),
            shape((GROUP, 192, FF), bf16),
            shape((GROUP, CTX, 96, D), bf16),
            shape((GROUP, GROUP, 48, D), bf16),
            shape((GROUP, 192, ROWS), bf16),
            shape((LOCAL, 128, QUERIES), bf16),
            shape((LOCAL, SLOTS, 128), bf16),
            shape((LOCAL, SLOTS, 128), bf16),
            shape((LOCAL, 64, SLOTS), bf16),
            shape((LOCAL, 64, QUERIES), f32),
            shape((LOCAL, 8, QUERIES), f32),
        ),
        in_specs=[pl.BlockSpec(memory_space=pltpu.SMEM)] + [any_] * 6,
        out_specs=[any_] * 13,
        scratch_shapes=[
            pltpu.VMEM((CTX, ROWS, D), bf16),
            pltpu.VMEM((GROUP, 2, 96, WIDE), bf16),
            pltpu.VMEM((GROUP, 16, D), bf16),
            pltpu.VMEM((LOCAL, 128, QUERIES), bf16),
            pltpu.VMEM((LOCAL, SLOTS, 128), bf16),
            pltpu.VMEM((LOCAL, SLOTS, 128), bf16),
            pltpu.VMEM((LOCAL, 64, SLOTS), bf16),
            pltpu.VMEM((LOCAL, 80, SLOTS), bf16),
            pltpu.VMEM((LOCAL, 64, QUERIES), f32),
            pltpu.VMEM((LOCAL, 8, QUERIES), f32),
            pltpu.VMEM((GROUP, 192, ROWS), bf16),
            pltpu.VMEM((80, TILE), f32),
            pltpu.VMEM((8, TILE), f32),
            pltpu.SemaphoreType.DMA((FORWARD_COPIES,)),
            pltpu.SemaphoreType.DMA((FORWARD_COPIES,)),
            pltpu.SemaphoreType.DMA((24,)),
        ],
        compiler_params=pltpu.CompilerParams(
            collective_id=0, has_side_effects=True, vmem_limit_bytes=60 << 20
        ),
    )(length, x, wqkv, vec, inner, outer, wo)


def split_weights(place_p, query_weight, key_weight, value_weight, query_bias, value_bias):
    def columns(weight):
        return lax.dynamic_slice_in_dim(weight, place_p * 192, 192, axis=1)

    rows = query_weight.shape[0]
    pair = jnp.concatenate(
        [columns(key_weight).reshape(rows, 3, 64), columns(value_weight).reshape(rows, 3, 64)],
        axis=2,
    ).reshape(rows, 384)
    fill = jnp.zeros((rows, 64), bf16)
    return jnp.concatenate([pair, columns(query_weight), fill], axis=1).reshape(2, 96, WIDE)


def pack_vectors(query_bias, value_bias, vectors, inner_bias):
    nothing = jnp.zeros((3, 64), bf16)
    first = jnp.concatenate(
        [
            jnp.concatenate([nothing, value_bias.reshape(3, 64)], axis=1).reshape(384),
            query_bias,
            jnp.zeros((192,), bf16),
        ]
    )
    rest = [jnp.pad(v, (0, 576)) for v in vectors]
    table = jnp.stack([first, inner_bias] + rest)
    return jnp.pad(table, ((0, 16 - table.shape[0]), (0, 0)))


def keep_state(carried):
    return carried


def per_device(
    states,
    lengths,
    query_weight,
    query_bias,
    key_weight,
    value_weight,
    value_bias,
    output_weight,
    output_bias,
    first_gain,
    first_shift,
    inner_weight,
    inner_bias,
    outer_weight,
    outer_bias,
    second_gain,
    second_shift,
    cotangent,
):
    row_count = states.shape[1]
    cycle_size = lax.axis_size("ctx")
    cycle_place = lax.axis_index("ctx")
    sequence = lax.axis_index("fsdp")
    length = lengths[sequence]
    offsets = jnp.arange(row_count, dtype=jnp.int32)
    row_keep = cycle_place * row_count + offsets < length
    inputs = states[0]
    input_float = inputs.astype(jnp.float32)
    attention_set = (
        lax.all_gather(query_weight, "fsdp", axis=0, tiled=True),
        lax.all_gather(key_weight, "fsdp", axis=0, tiled=True),
        lax.all_gather(value_weight, "fsdp", axis=0, tiled=True),
        lax.all_gather(output_weight, "fsdp", axis=0, tiled=True),
        lax.all_gather(query_bias, "fsdp", axis=0, tiled=True),
        lax.all_gather(value_bias, "fsdp", axis=0, tiled=True),
        lax.all_gather(output_bias, "fsdp", axis=0, tiled=True),
        lax.all_gather(first_gain, "fsdp", axis=0, tiled=True),
        lax.all_gather(first_shift, "fsdp", axis=0, tiled=True),
    )
    query_full = attention_set[0]
    key_full = attention_set[1]
    value_full = attention_set[2]
    output_full = attention_set[3]
    query_add = attention_set[4].astype(jnp.float32)
    value_add = attention_set[5].astype(jnp.float32)
    output_add = attention_set[6].astype(jnp.float32)
    gain_one = attention_set[7].astype(jnp.float32)
    shift_one = attention_set[8].astype(jnp.float32)
    queries = (
        (jnp.dot(inputs, query_full, preferred_element_type=jnp.float32) + query_add) * 0.125
    ).astype(jnp.bfloat16)
    key_rows = jnp.dot(inputs, key_full, preferred_element_type=jnp.float32).astype(jnp.bfloat16)
    values = (jnp.dot(inputs, value_full, preferred_element_type=jnp.float32) + value_add).astype(
        jnp.bfloat16
    )
    query_heads = queries.reshape(row_count, H, HD)

    def forward_block(key_block, value_block, key_start, running_state):

        def forward_compute(carried):
            running, exp_total, accum = carried
            key_keep = key_start + offsets < length
            scores = jnp.einsum(
                "qhd,khd->hqk",
                query_heads,
                key_block.reshape(row_count, H, HD),
                preferred_element_type=jnp.float32,
            )
            scores = jnp.where(key_keep[None, None, :], scores, -1e30)
            newest = jnp.maximum(running, jnp.max(scores, axis=2))
            factor = jnp.exp(running - newest)
            weights = jnp.exp(scores - newest[:, :, None])
            exp_total = exp_total * factor + jnp.sum(weights, axis=2)
            update = jnp.einsum(
                "hqk,khd->qhd",
                weights.astype(jnp.bfloat16),
                value_block.reshape(row_count, H, HD),
                preferred_element_type=jnp.float32,
            )
            accum = accum * factor.T[:, :, None] + update
            return (newest, exp_total, accum)

        return lax.cond(key_start < length, forward_compute, keep_state, running_state)

    start_state = (
        jnp.full((H, row_count), -1e30, jnp.float32),
        jnp.zeros((H, row_count), jnp.float32),
        jnp.zeros((row_count, H, HD), jnp.float32),
    )

    def cycle_turn(turn_index, carried):
        key_block, value_block, running_state = carried
        owner_index = (cycle_place - turn_index) % cycle_size
        running_state = forward_block(
            key_block, value_block, owner_index * row_count, running_state
        )
        key_block, value_block = passed_along((key_block, value_block), "ctx", 1)
        return (key_block, value_block, running_state)

    key_block, value_block, running_state = lax.fori_loop(
        0, cycle_size - 1, cycle_turn, (key_rows, values, start_state)
    )
    last_owner = (cycle_place + 1) % cycle_size
    running, exp_total, accum = forward_block(
        key_block, value_block, last_owner * row_count, running_state
    )
    log_total = running + jnp.log(exp_total)
    attention_value = (accum / exp_total.T[:, :, None]).reshape(row_count, D)
    mixed = attention_value.astype(jnp.bfloat16)
    if row_count == ROWS and cycle_size == CTX:
        w = split_weights(cycle_place // 2, query_weight, key_weight, value_weight, query_bias, value_bias)
        v = pack_vectors(query_bias, value_bias, [output_bias, first_gain, first_shift, outer_bias, second_gain, second_shift], inner_bias)
        outs = forward_call(length[None], inputs, w, v, inner_weight, outer_weight.reshape(8, 96, 768), output_weight.reshape(4, 48, 768))
        mixed = outs[6].reshape(D, ROWS).T
    attended = jnp.dot(mixed, output_full, preferred_element_type=jnp.float32) + output_add
    first_normed, first_scale = normalize(input_float + attended)
    first = first_normed * gain_one + shift_one
    first_low = first.astype(jnp.bfloat16)
    feed_set = (
        lax.all_gather(inner_weight, "fsdp", axis=0, tiled=True),
        lax.all_gather(outer_weight, "fsdp", axis=0, tiled=True),
        lax.all_gather(inner_bias, "fsdp", axis=0, tiled=True),
        lax.all_gather(outer_bias, "fsdp", axis=0, tiled=True),
        lax.all_gather(second_gain, "fsdp", axis=0, tiled=True),
        lax.all_gather(second_shift, "fsdp", axis=0, tiled=True),
    )
    inner_full = feed_set[0]
    outer_full = feed_set[1]
    inner_add = feed_set[2].astype(jnp.float32)
    outer_add = feed_set[3].astype(jnp.float32)
    gain_two = feed_set[4].astype(jnp.float32)
    shift_two = feed_set[5].astype(jnp.float32)
    inner = jnp.dot(first_low, inner_full, preferred_element_type=jnp.float32) + inner_add
    activated = jax.nn.gelu(inner, approximate=False).astype(jnp.bfloat16)
    outer = jnp.dot(activated, outer_full, preferred_element_type=jnp.float32) + outer_add
    second_normed, second_scale = normalize(first + outer)
    second = second_normed * gain_two + shift_two
    layer_output = jnp.where(row_keep[:, None], second, 0.0).astype(jnp.bfloat16)[None]
    query_full = attention_set[0]
    key_full = attention_set[1]
    value_full = attention_set[2]
    output_full = attention_set[3]
    gain_one = attention_set[7].astype(jnp.float32)
    inner_full = feed_set[0]
    outer_full = feed_set[1]
    gain_two = feed_set[4].astype(jnp.float32)
    upstream = jnp.where(row_keep[:, None], cotangent[0].astype(jnp.float32), 0.0)
    second_grad, second_gain_grad, second_shift_grad = norm_back(
        upstream, second_normed, second_scale, gain_two
    )
    outer_low = second_grad.astype(jnp.bfloat16)
    outer_bias_grad = jnp.sum(second_grad, axis=0)
    outer_weight_grad = jnp.dot(activated.T, outer_low, preferred_element_type=jnp.float32)
    inner_grad = jnp.dot(outer_low, outer_full.T, preferred_element_type=jnp.float32) * gelu_slope(
        inner
    )
    inner_low = inner_grad.astype(jnp.bfloat16)
    inner_bias_grad = jnp.sum(inner_grad, axis=0)
    inner_weight_grad = jnp.dot(first_low.T, inner_low, preferred_element_type=jnp.float32)
    first_grad = second_grad + jnp.dot(inner_low, inner_full.T, preferred_element_type=jnp.float32)
    hidden_grad, first_gain_grad, first_shift_grad = norm_back(
        first_grad, first_normed, first_scale, gain_one
    )
    attended_low = hidden_grad.astype(jnp.bfloat16)
    output_bias_grad = jnp.sum(hidden_grad, axis=0)
    output_weight_grad = jnp.dot(mixed.T, attended_low, preferred_element_type=jnp.float32)
    mixed_grad = jnp.dot(attended_low, output_full.T, preferred_element_type=jnp.float32).astype(
        jnp.bfloat16
    )
    delta = jnp.sum(
        (mixed_grad.astype(jnp.float32) * attention_value).reshape(row_count, H, HD), axis=2
    ).T

    def back_block(
        query_block,
        upstream_block,
        log_block,
        delta_block,
        key_block,
        value_block,
        key_start,
        grads,
    ):

        def back_compute(carried):
            query_grad, key_grad, value_grad = carried
            key_keep = key_start + offsets < length
            query_three = query_block.reshape(row_count, H, HD)
            upstream_three = upstream_block.reshape(row_count, H, HD)
            key_three = key_block.reshape(row_count, H, HD)
            value_three = value_block.reshape(row_count, H, HD)
            scores = jnp.einsum(
                "qhd,khd->hqk", query_three, key_three, preferred_element_type=jnp.float32
            )
            weights = jnp.where(
                key_keep[None, None, :], jnp.exp(scores - log_block[:, :, None]), 0.0
            )
            weight_grad = jnp.einsum(
                "qhd,khd->hqk", upstream_three, value_three, preferred_element_type=jnp.float32
            )
            score_grad = (weights * (weight_grad - delta_block[:, :, None])).astype(jnp.bfloat16)
            query_grad = query_grad + jnp.einsum(
                "hqk,khd->qhd", score_grad, key_three, preferred_element_type=jnp.float32
            ).reshape(row_count, D)
            key_grad = key_grad + jnp.einsum(
                "hqk,qhd->khd", score_grad, query_three, preferred_element_type=jnp.float32
            ).reshape(row_count, D)
            value_grad = value_grad + jnp.einsum(
                "hqk,qhd->khd",
                weights.astype(jnp.bfloat16),
                upstream_three,
                preferred_element_type=jnp.float32,
            ).reshape(row_count, D)
            return (query_grad, key_grad, value_grad)

        return lax.cond(key_start < length, back_compute, keep_state, grads)

    zero_grad = jnp.zeros((row_count, D), jnp.float32)

    def key_turn(turn_index, carried):
        key_block, value_block, query_grad, key_grad, value_grad = carried
        owner_index = (cycle_place - turn_index) % cycle_size
        query_grad, key_grad, value_grad = back_block(
            queries,
            mixed_grad,
            log_total,
            delta,
            key_block,
            value_block,
            owner_index * row_count,
            (query_grad, key_grad, value_grad),
        )
        key_block, value_block = passed_along((key_block, value_block), "ctx", 1)
        key_grad, value_grad = (
            passed_along(key_grad.astype(jnp.bfloat16), "ctx", 1).astype(key_grad.dtype),
            passed_along(value_grad.astype(jnp.bfloat16), "ctx", 1).astype(value_grad.dtype),
        )
        return (key_block, value_block, query_grad, key_grad, value_grad)

    key_block, value_block, query_grad, key_grad, value_grad = lax.fori_loop(
        0, cycle_size - 1, key_turn, (key_rows, values, zero_grad, zero_grad, zero_grad)
    )
    query_grad, key_grad, value_grad = back_block(
        queries,
        mixed_grad,
        log_total,
        delta,
        key_block,
        value_block,
        last_owner * row_count,
        (query_grad, key_grad, value_grad),
    )
    key_grad, value_grad = (
        passed_along(key_grad.astype(jnp.bfloat16), "ctx", 1).astype(key_grad.dtype),
        passed_along(value_grad.astype(jnp.bfloat16), "ctx", 1).astype(value_grad.dtype),
    )
    query_low = query_grad.astype(jnp.bfloat16) * 0.125
    key_low = key_grad.astype(jnp.bfloat16)
    value_low = value_grad.astype(jnp.bfloat16)
    query_weight_grad = jnp.dot(inputs.T, query_low, preferred_element_type=jnp.float32)
    query_bias_grad = jnp.sum(query_low.astype(jnp.float32), axis=0)
    key_weight_grad = jnp.dot(inputs.T, key_low, preferred_element_type=jnp.float32)
    value_weight_grad = jnp.dot(inputs.T, value_low, preferred_element_type=jnp.float32)
    value_bias_grad = jnp.sum(value_low.astype(jnp.float32), axis=0)
    input_grad = (
        hidden_grad
        + jnp.dot(query_low, query_full.T, preferred_element_type=jnp.float32)
        + jnp.dot(key_low, key_full.T, preferred_element_type=jnp.float32)
        + jnp.dot(value_low, value_full.T, preferred_element_type=jnp.float32)
    ).astype(jnp.bfloat16)[None]
    local_grads = (
        query_weight_grad,
        query_bias_grad,
        key_weight_grad,
        value_weight_grad,
        value_bias_grad,
        output_weight_grad,
        output_bias_grad,
        first_gain_grad,
        first_shift_grad,
        inner_weight_grad,
        inner_bias_grad,
        outer_weight_grad,
        outer_bias_grad,
        second_gain_grad,
        second_shift_grad,
    )
    shards = (
        lax.psum_scatter(
            local_grads[0].astype(jnp.bfloat16), "fsdp", scatter_dimension=0, tiled=True
        ).astype(jnp.float32),
        lax.psum_scatter(
            local_grads[1].astype(jnp.bfloat16), "fsdp", scatter_dimension=0, tiled=True
        ).astype(jnp.float32),
        lax.psum_scatter(
            local_grads[2].astype(jnp.bfloat16), "fsdp", scatter_dimension=0, tiled=True
        ).astype(jnp.float32),
        lax.psum_scatter(
            local_grads[3].astype(jnp.bfloat16), "fsdp", scatter_dimension=0, tiled=True
        ).astype(jnp.float32),
        lax.psum_scatter(
            local_grads[4].astype(jnp.bfloat16), "fsdp", scatter_dimension=0, tiled=True
        ).astype(jnp.float32),
        lax.psum_scatter(
            local_grads[5].astype(jnp.bfloat16), "fsdp", scatter_dimension=0, tiled=True
        ).astype(jnp.float32),
        lax.psum_scatter(
            local_grads[6].astype(jnp.bfloat16), "fsdp", scatter_dimension=0, tiled=True
        ).astype(jnp.float32),
        lax.psum_scatter(
            local_grads[7].astype(jnp.bfloat16), "fsdp", scatter_dimension=0, tiled=True
        ).astype(jnp.float32),
        lax.psum_scatter(
            local_grads[8].astype(jnp.bfloat16), "fsdp", scatter_dimension=0, tiled=True
        ).astype(jnp.float32),
        lax.psum_scatter(
            local_grads[9].astype(jnp.bfloat16), "fsdp", scatter_dimension=0, tiled=True
        ).astype(jnp.float32),
        lax.psum_scatter(
            local_grads[10].astype(jnp.bfloat16), "fsdp", scatter_dimension=0, tiled=True
        ).astype(jnp.float32),
        lax.psum_scatter(
            local_grads[11].astype(jnp.bfloat16), "fsdp", scatter_dimension=0, tiled=True
        ).astype(jnp.float32),
        lax.psum_scatter(
            local_grads[12].astype(jnp.bfloat16), "fsdp", scatter_dimension=0, tiled=True
        ).astype(jnp.float32),
        lax.psum_scatter(
            local_grads[13].astype(jnp.bfloat16), "fsdp", scatter_dimension=0, tiled=True
        ).astype(jnp.float32),
        lax.psum_scatter(
            local_grads[14].astype(jnp.bfloat16), "fsdp", scatter_dimension=0, tiled=True
        ).astype(jnp.float32),
    )
    totals = (
        lax.psum(shards[0].astype(jnp.bfloat16), "ctx").astype(jnp.float32),
        lax.psum(shards[1].astype(jnp.bfloat16), "ctx").astype(jnp.float32),
        lax.psum(shards[2].astype(jnp.bfloat16), "ctx").astype(jnp.float32),
        lax.psum(shards[3].astype(jnp.bfloat16), "ctx").astype(jnp.float32),
        lax.psum(shards[4].astype(jnp.bfloat16), "ctx").astype(jnp.float32),
        lax.psum(shards[5].astype(jnp.bfloat16), "ctx").astype(jnp.float32),
        lax.psum(shards[6].astype(jnp.bfloat16), "ctx").astype(jnp.float32),
        lax.psum(shards[7].astype(jnp.bfloat16), "ctx").astype(jnp.float32),
        lax.psum(shards[8].astype(jnp.bfloat16), "ctx").astype(jnp.float32),
        lax.psum(shards[9].astype(jnp.bfloat16), "ctx").astype(jnp.float32),
        lax.psum(shards[10].astype(jnp.bfloat16), "ctx").astype(jnp.float32),
        lax.psum(shards[11].astype(jnp.bfloat16), "ctx").astype(jnp.float32),
        lax.psum(shards[12].astype(jnp.bfloat16), "ctx").astype(jnp.float32),
        lax.psum(shards[13].astype(jnp.bfloat16), "ctx").astype(jnp.float32),
        lax.psum(shards[14].astype(jnp.bfloat16), "ctx").astype(jnp.float32),
    )
    return (
        layer_output,
        input_grad,
        totals[0],
        totals[1],
        totals[2],
        totals[3],
        totals[4],
        totals[5],
        totals[6],
        totals[7],
        totals[8],
        totals[9],
        totals[10],
        totals[11],
        totals[12],
        totals[13],
        totals[14],
    )


def solution(mesh):
    return jax.shard_map(
        per_device,
        mesh=mesh,
        in_specs=(
            P("fsdp", "ctx", None),
            P(),
            P("fsdp", None),
            P("fsdp"),
            P("fsdp", None),
            P("fsdp", None),
            P("fsdp"),
            P("fsdp", None),
            P("fsdp"),
            P("fsdp"),
            P("fsdp"),
            P("fsdp", None),
            P("fsdp"),
            P("fsdp", None),
            P("fsdp"),
            P("fsdp"),
            P("fsdp"),
            P("fsdp", "ctx", None),
        ),
        out_specs=(
            P("fsdp", "ctx", None),
            P("fsdp", "ctx", None),
            P("fsdp", None),
            P("fsdp"),
            P("fsdp", None),
            P("fsdp", None),
            P("fsdp"),
            P("fsdp", None),
            P("fsdp"),
            P("fsdp"),
            P("fsdp"),
            P("fsdp", None),
            P("fsdp"),
            P("fsdp", None),
            P("fsdp"),
            P("fsdp"),
            P("fsdp"),
        ),
        check_vma=False,
    )
```

```python
import functools

import jax
import jax.numpy as jnp
from jax import lax
from jax.experimental import pallas as pl
from jax.experimental.pallas import tpu as pltpu
from jax.sharding import PartitionSpec as P

D = 768
H = 12
HD = 64


epsilon = 1e-05


def passed_along(value, axis, steps):
    count = lax.axis_size(axis)
    pairs = [(source, (source + steps) % count) for source in range(count)]
    return lax.ppermute(value, axis, pairs)


def normalize(hidden):
    centred = hidden - jnp.mean(hidden, axis=1, keepdims=True)
    scale = lax.rsqrt(jnp.mean(centred * centred, axis=1, keepdims=True) + epsilon)
    return (centred * scale, scale)


def norm_back(upstream, normed, scale, gain):
    gain_grad = jnp.sum(upstream * normed, axis=0)
    shift_grad = jnp.sum(upstream, axis=0)
    scaled = upstream * gain
    hidden_grad = scale * (
        scaled
        - jnp.mean(scaled, axis=1, keepdims=True)
        - normed * jnp.mean(scaled * normed, axis=1, keepdims=True)
    )
    return (hidden_grad, gain_grad, shift_grad)


def gelu_slope(inner):
    return (
        0.5 * (1.0 + lax.erf(inner * 0.7071067811865476))
        + inner * jnp.exp(-0.5 * inner * inner) * 0.3989422804014327
    )


bf16 = jnp.bfloat16
f32 = jnp.float32
FF = 3072
ROWS = 384
CTX = 8
GROUP = 4
LOCAL = 3
SLOTS = 3072
QUERIES = 1536
TILE = 768
CHUNK = 512
WIDE = 640
MESH = pl.DeviceIdType.MESH


def multiple(value, step):
    return pl.multiple_of(value * step, step)


class Place:
    def __init__(self):
        self.c = lax.axis_index("ctx")
        self.z = lax.axis_index("fsdp")
        c = self.c
        self.core = c % 2
        self.p = c // 2
        self.x = self.p % 2
        self.y = c // 4
        self.p_x = self.p + 1 - 2 * self.x
        self.p_y = self.p + 2 - 4 * self.y
        self.p_d = self.p_y + 1 - 2 * self.x
        self.to_core = (c + 1 - 2 * self.core, self.z)
        self.to_x = (2 * self.p_x + self.core, self.z)
        self.to_y = (2 * self.p_y + self.core, self.z)
        self.to_d = (2 * self.p_d + self.core, self.z)

    def to_z(self, step):
        return (self.c, (self.z + step) % GROUP)

    def from_z(self, step):
        return (self.z + GROUP - step) % GROUP


class Net:
    def __init__(self, sends, receives):
        self.sends = sends
        self.receives = receives
        self.index = {}
        self.open = []

    def of(self, name):
        return self.index.setdefault(name, len(self.index))

    def copy(self, name, src, dst, device):
        i = self.of(name)
        return pltpu.make_async_remote_copy(
            src_ref=src,
            dst_ref=dst,
            send_sem=self.sends.at[i],
            recv_sem=self.receives.at[i],
            device_id=device,
            device_id_type=MESH,
        )

    def start(self, name, src, dst, device):
        self.launch(name, lambda: (src, dst, device))

    def launch(self, name, make):
        self.copy(name, *make()).start()
        self.open.append((name, make))

    def landed(self, name, dst, device):
        self.copy(name, dst, dst, device).wait_recv()

    def drain(self):
        for name, make in self.open:
            self.copy(name, *make()).wait_send()
        self.open = []


def greet(place, with_z=True):
    barrier = pltpu.get_barrier_semaphore()
    partners = [place.to_core, place.to_x, place.to_y, place.to_d]
    if with_z:
        partners += [place.to_z(step) for step in range(1, GROUP)]
    for partner in partners:
        pl.semaphore_signal(barrier, inc=1, device_id=partner, device_id_type=MESH)
    pl.semaphore_wait(barrier, len(partners))


def dot(a, b):
    return jnp.dot(a, b, preferred_element_type=f32)


def dot_nt(a, b):
    return lax.dot_general(a, b, (((1,), (1,)), ((), ())), preferred_element_type=f32)


def dot_tn(a, b):
    return lax.dot_general(a, b, (((0,), (0,)), ((), ())), preferred_element_type=f32)


def forward_kernel(
    length,
    x_in,
    wqkv_in,
    vec_in,
    inner_in,
    outer_in,
    wo_in,
    xall_out,
    wqkv_out,
    vec_out,
    inner_out,
    outer_out,
    wo_out,
    mixed_out,
    qt_out,
    ka_out,
    va_out,
    kt_out,
    ot_out,
    lse_out,
    xall,
    wqkv,
    vec,
    qt,
    ka,
    va,
    kt,
    vt,
    ot,
    lse,
    mix,
    acc,
    top,
    sends,
    receives,
    locals_,
):
    at = Place()
    net = Net(sends, receives)
    c, z, core, p = at.c, at.z, at.core, at.p
    part = c
    own = []

    def local(src, dst):
        copy = pltpu.make_async_copy(src, dst, locals_.at[len(own)])
        own.append(copy)
        copy.start()
        return copy

    def inner_at(ref, chip, side):
        return ref.at[:, pl.ds(multiple(2 * chip + side, 384), 384)]

    def outer_at(ref, chip, side):
        return ref.at[2 * chip + side]

    def wo_at(ref, chip, side):
        return ref.at[chip, :, pl.ds(multiple(side, 384), 384)]

    weights = {
        "wo": (wo_in, wo_out, wo_at),
        "outer": (outer_in, outer_out, outer_at),
        "inner": (inner_in, inner_out, inner_at),
    }

    greet(at)

    low, high = pl.ds(0, 192), pl.ds(192, 192)
    net.start("sx0", x_in.at[low], xall.at[c, low], at.to_x)
    net.start("sy1", x_in.at[high], xall.at[c, high], at.to_y)
    net.start("sx1", x_in.at[high], xall.at[c, high], at.to_x)
    net.start("sy0", x_in.at[low], xall.at[c, low], at.to_y)
    net.start("sc", x_in, xall.at[c], at.to_core)
    for step in range(1, GROUP):
        net.start(f"vec{step}", vec_in, vec.at[z], at.to_z(step))
    for step in range(1, GROUP):
        net.start(f"wq{step}", wqkv_in.at[core], wqkv.at[z, core], at.to_z(step))
    for name, (src, dst, region) in weights.items():
        for step in range(1, GROUP):
            net.start(
                f"{name}z{step}", region(src, p, core), region(dst.at[z], p, core), at.to_z(step)
            )
    first = [local(x_in, xall.at[c]), local(vec_in, vec.at[z]), local(wqkv_in, wqkv.at[z])]
    local(inner_in, inner_out.at[z])
    local(outer_in, outer_out.at[z])
    local(wo_in, wo_out.at[z])

    row64 = lax.broadcasted_iota(jnp.int32, (64, QUERIES), 0)
    for h in range(LOCAL):
        qt[h, 64:128, :] = jnp.where(row64 == 0, 1.0, 0.0).astype(bf16)
        row16 = lax.broadcasted_iota(jnp.int32, (16, SLOTS), 0)
        vt[h, 64:80, :] = jnp.where(row16 == 0, 1.0, 0.0).astype(bf16)

    for step in range(1, GROUP):
        net.landed(f"wq{step}", wqkv.at[at.from_z(step), core], at.to_z(step))
        source = at.from_z(step)
        net.start(f"wqc{step}", wqkv.at[source, core], wqkv.at[source, core], at.to_core)
    cx, cy, cd = at.to_x[0], at.to_y[0], at.to_d[0]
    net.landed("sx0", xall.at[cx, low], at.to_x)
    net.start("rx0", xall.at[cx, low], xall.at[cx, low], at.to_y)
    net.landed("sy1", xall.at[cy, high], at.to_y)
    net.start("ry1", xall.at[cy, high], xall.at[cy, high], at.to_x)
    net.landed("sx1", xall.at[cx, high], at.to_x)
    net.start("cx", xall.at[cx], xall.at[cx], at.to_core)
    net.landed("sy0", xall.at[cy, low], at.to_y)
    net.start("cy", xall.at[cy], xall.at[cy], at.to_core)
    for copy in first:
        copy.wait()
    for step in range(1, GROUP):
        net.landed(f"vec{step}", vec.at[at.from_z(step)], at.to_z(step))
        source = at.from_z(step)
        net.landed(f"wqc{step}", wqkv.at[source, 1 - core], at.to_core)

    bias = vec[p][0:1, 0:WIDE].astype(f32)
    lane = lax.broadcasted_iota(jnp.int32, (ROWS, 128), 1)
    row = lax.broadcasted_iota(jnp.int32, (ROWS, 128), 0)
    count = length[0]

    def project(block, column):
        rows = xall[block]
        keep = block * ROWS + row < count
        mark = jnp.where(keep, 0.0, -1e30)
        at_rows = pl.ds(multiple(block, ROWS), ROWS)
        width = 384 if column is None else WIDE
        full = wqkv[...].reshape(D, WIDE)
        y = dot(rows, full[:, 0:width]) + bias[:, 0:width]
        for h in range(LOCAL):
            g = y[:, 128 * h : 128 * h + 128]
            ka[h, at_rows, :] = jnp.where(
                lane < 64, g, jnp.where(lane == 64, mark, jnp.where(lane < 68, 1.0, 0.0))
            ).astype(bf16)
            va[h, at_rows, :] = jnp.where(
                lane < 64, pltpu.roll(g, 64, 1), jnp.where(lane < 67, 1.0, 0.0)
            ).astype(bf16)
            turned = g.T.astype(bf16)
            kt[h, :, at_rows] = turned[0:64]
            vt[h, 0:64, at_rows] = turned[64:128]
        if column is not None:
            q = (y[:, 384:WIDE] * 0.125).T.astype(bf16)
            for h in range(LOCAL):
                qt[h, 0:64, 384 * column : 384 * column + 384] = q[64 * h : 64 * h + 64]

    project(c, 3)
    net.landed("sc", xall.at[at.to_core[0]], at.to_core)
    project(at.to_core[0], None)
    project(cx, 1)
    project(cy, 2)
    net.landed("cx", xall.at[cx + 1 - 2 * core], at.to_core)
    project(cx + 1 - 2 * core, None)
    net.landed("cy", xall.at[cy + 1 - 2 * core], at.to_core)
    project(cy + 1 - 2 * core, None)
    net.landed("rx0", xall.at[cd, low], at.to_y)
    net.landed("ry1", xall.at[cd, high], at.to_x)
    net.start("cd", xall.at[cd], xall.at[cd], at.to_core)
    project(cd, 0)
    net.landed("cd", xall.at[cd + 1 - 2 * core], at.to_core)
    project(cd + 1 - 2 * core, None)

    local(xall, xall_out)
    local(wqkv, wqkv_out)
    local(vec, vec_out)
    local(qt, qt_out)
    local(ka, ka_out)
    local(va, va_out)
    local(kt, kt_out)

    def part_of(name, step, chip, side):
        _, dst, region = weights[name]
        return region(dst.at[at.from_z(step)], chip, side)

    def hand(label, name, step, chip, device):
        def make():
            ref = part_of(name, step, chip, core)
            return ref, ref, device

        net.launch(label, make)

    def plane_out(name):
        for step in range(1, GROUP):
            net.landed(f"{name}z{step}", part_of(name, step, p, core), at.to_z(step))
            hand(f"{name}x{step}", name, step, p, at.to_x)
            hand(f"{name}y{step}", name, step, p, at.to_y)
            hand(f"{name}c{step}", name, step, p, at.to_core)

    def plane_relay(name, via_x):
        for step in range(1, GROUP):
            net.landed(f"{name}x{step}", part_of(name, step, at.p_x, core), at.to_x)
            net.landed(f"{name}y{step}", part_of(name, step, at.p_y, core), at.to_y)
            if via_x:
                hand(f"{name}r{step}", name, step, at.p_y, at.to_x)
            else:
                hand(f"{name}r{step}", name, step, at.p_x, at.to_y)
            hand(f"{name}cx{step}", name, step, at.p_x, at.to_core)
            hand(f"{name}cy{step}", name, step, at.p_y, at.to_core)

    def plane_last(name, via_x):
        for step in range(1, GROUP):
            far = part_of(name, step, at.p_d, core)
            net.landed(f"{name}r{step}", far, at.to_x if via_x else at.to_y)
            hand(f"{name}cd{step}", name, step, at.p_d, at.to_core)

    def plane_in(name):
        for step in range(1, GROUP):
            for tag, chip in (("c", p), ("cx", at.p_x), ("cy", at.p_y), ("cd", at.p_d)):
                net.landed(f"{name}{tag}{step}", part_of(name, step, chip, 1 - core), at.to_core)

    plane_out("wo")

    def attend(h, tile):
        cols = pl.ds(TILE * tile, TILE)
        queries = qt[h, :, cols]
        for j in range(SLOTS // CHUNK):
            rows = pl.ds(CHUNK * j, CHUNK)
            scores = dot(ka[h, rows, :], queries)
            peak = jnp.max(scores, axis=0, keepdims=True)
            if j == 0:
                newest = peak
            else:
                newest = jnp.maximum(top[0:1, :], peak)
                factor = jnp.exp(top[0:1, :] - newest)
            probs = jnp.exp(scores - newest).astype(bf16)
            update = dot(vt[h, :, rows], probs)
            if j == 0:
                acc[...] = update
            else:
                acc[...] = acc[...] * factor + update
            top[0:1, :] = newest
        total = acc[64:65, :]
        value = acc[0:64, :] / total
        ot[h, :, cols] = value
        lse[h, 0:1, cols] = top[0:1, :] + jnp.log(total)
        low_value = value.astype(bf16)
        at_head = pl.ds(multiple(h, 64), 64)
        mix[2 * tile, at_head, :] = low_value[:, 0:384]
        mix[2 * tile + 1, at_head, :] = low_value[:, 384:768]

    plan = {
        (0, 1): [lambda: plane_relay("wo", True), lambda: plane_out("outer")],
        (0, 2): [lambda: plane_last("wo", True)],
        (1, 0): [lambda: plane_relay("outer", False), lambda: plane_out("inner")],
        (1, 2): [lambda: plane_last("outer", False)],
    }

    def take(steps):
        for step in steps:
            step()

    for tile in range(QUERIES // TILE):

        def head(h, carried, tile=tile):
            for (which, when), steps in plan.items():
                if which == tile:
                    pl.when(h == when)(functools.partial(take, steps))
            attend(h, tile)
            return carried

        lax.fori_loop(0, LOCAL, head, 0)
        if tile == 0:
            net.start("md", mix.at[0], mixed_out.at[p], at.to_d)
            net.start("mx", mix.at[1], mixed_out.at[p], at.to_x)
        else:
            net.start("my", mix.at[2], mixed_out.at[p], at.to_y)
            local(mix.at[3], mixed_out.at[p])
    local(ot, ot_out)
    local(lse, lse_out)
    plane_relay("inner", True)
    plane_last("inner", True)
    for name in weights:
        plane_in(name)
    net.landed("md", mixed_out.at[at.p_d], at.to_d)
    net.landed("mx", mixed_out.at[at.p_x], at.to_x)
    net.landed("my", mixed_out.at[at.p_y], at.to_y)
    for copy in own[3:]:
        copy.wait()
    net.drain()


FORWARD_COPIES = 112


def forward_call(length, x, wqkv, vec, inner, outer, wo):
    any_ = pl.BlockSpec(memory_space=pl.ANY)
    shape = jax.ShapeDtypeStruct
    return pl.pallas_call(
        forward_kernel,
        name="forward_attention",
        out_shape=(
            shape((CTX, ROWS, D), bf16),
            shape((GROUP, 2, 96, WIDE), bf16),
            shape((GROUP, 16, D), bf16),
            shape((GROUP, 192, FF), bf16),
            shape((GROUP, CTX, 96, D), bf16),
            shape((GROUP, GROUP, 48, D), bf16),
            shape((GROUP, 192, ROWS), bf16),
            shape((LOCAL, 128, QUERIES), bf16),
            shape((LOCAL, SLOTS, 128), bf16),
            shape((LOCAL, SLOTS, 128), bf16),
            shape((LOCAL, 64, SLOTS), bf16),
            shape((LOCAL, 64, QUERIES), f32),
            shape((LOCAL, 8, QUERIES), f32),
        ),
        in_specs=[pl.BlockSpec(memory_space=pltpu.SMEM)] + [any_] * 6,
        out_specs=[any_] * 13,
        scratch_shapes=[
            pltpu.VMEM((CTX, ROWS, D), bf16),
            pltpu.VMEM((GROUP, 2, 96, WIDE), bf16),
            pltpu.VMEM((GROUP, 16, D), bf16),
            pltpu.VMEM((LOCAL, 128, QUERIES), bf16),
            pltpu.VMEM((LOCAL, SLOTS, 128), bf16),
            pltpu.VMEM((LOCAL, SLOTS, 128), bf16),
            pltpu.VMEM((LOCAL, 64, SLOTS), bf16),
            pltpu.VMEM((LOCAL, 80, SLOTS), bf16),
            pltpu.VMEM((LOCAL, 64, QUERIES), f32),
            pltpu.VMEM((LOCAL, 8, QUERIES), f32),
            pltpu.VMEM((GROUP, 192, ROWS), bf16),
            pltpu.VMEM((80, TILE), f32),
            pltpu.VMEM((8, TILE), f32),
            pltpu.SemaphoreType.DMA((FORWARD_COPIES,)),
            pltpu.SemaphoreType.DMA((FORWARD_COPIES,)),
            pltpu.SemaphoreType.DMA((24,)),
        ],
        compiler_params=pltpu.CompilerParams(
            collective_id=0, has_side_effects=True, vmem_limit_bytes=60 << 20
        ),
    )(length, x, wqkv, vec, inner, outer, wo)


def split_weights(place_p, query_weight, key_weight, value_weight):
    def columns(weight):
        return lax.dynamic_slice_in_dim(weight, place_p * 192, 192, axis=1)

    rows = query_weight.shape[0]
    pair = jnp.concatenate(
        [columns(key_weight).reshape(rows, 3, 64), columns(value_weight).reshape(rows, 3, 64)],
        axis=2,
    ).reshape(rows, 384)
    fill = jnp.zeros((rows, 64), bf16)
    return jnp.concatenate([pair, columns(query_weight), fill], axis=1).reshape(2, 96, WIDE)


def pack_vectors(query_bias, value_bias, inner_bias, vectors):
    nothing = jnp.zeros((3, 64), bf16)
    first = jnp.concatenate(
        [
            jnp.concatenate([nothing, value_bias.reshape(3, 64)], axis=1).reshape(384),
            query_bias,
            jnp.zeros((192,), bf16),
        ]
    )
    rest = [jnp.pad(v, (0, 576)) for v in vectors]
    table = jnp.stack([first, inner_bias] + rest)
    return jnp.pad(table, ((0, 16 - table.shape[0]), (0, 0)))


SPAN = 256


def parts_of(value):
    high = value.astype(bf16).astype(f32)
    rest = value - high
    middle = rest.astype(bf16).astype(f32)
    return high, middle, rest - middle


def added(a, b):
    return (a.astype(f32) + b.astype(f32)).astype(bf16)


def backward_kernel(
    mg_in,
    ot_in,
    lse_in,
    qt_in,
    ka_in,
    va_in,
    kt_in,
    gi_in,
    go_in,
    gw_in,
    xall_in,
    wqkv_in,
    hg_in,
    small_in,
    dx_out,
    gqkv_out,
    gi_out,
    go_out,
    gw_out,
    small_out,
    mg,
    ot,
    lse,
    qa,
    qz,
    ka,
    va,
    kt,
    da,
    dz,
    kv,
    rkv,
    dq,
    so,
    si,
    ro,
    ri,
    ao,
    ai,
    bo,
    bi,
    zo,
    zi,
    xs,
    wqkv,
    dqkv,
    sdx,
    rdx,
    hg,
    dw,
    dwl,
    rdw,
    rzw,
    small,
    rsz,
    rsc,
    rsp,
    ssum,
    sends,
    receives,
    locals_,
):
    at = Place()
    net = Net(sends, receives)
    c, z, core, p = at.c, at.z, at.core, at.p
    other = 1 - core
    chips = [at.p_d, at.p_x, at.p_y, p]
    devices = [at.to_d, at.to_x, at.to_y]
    slots = []

    def local(src, dst):
        copy = pltpu.make_async_copy(src, dst, locals_.at[len(slots)])
        slots.append(copy)
        copy.start()
        return copy

    greet(at)
    for r in range(3):
        net.start(f"mg{r}", mg_in.at[chips[r]], mg.at[r], devices[r])
    own_mg = local(mg_in.at[p], mg.at[3])
    loads = [
        local(ot_in, ot),
        local(lse_in, lse),
        local(qt_in, qa),
        local(ka_in, ka),
        local(va_in, va),
        local(kt_in, kt),
    ]

    def o_at(chip, side):
        return go_in.at[:, 2 * chip + side]

    def i_at(chip, side):
        return gi_in.at[:, :, pl.ds(multiple(2 * chip + side, 384), 384)]

    def w_at(chip, side):
        return gw_in.at[:, chip, :, pl.ds(multiple(side, 384), 384)]

    halves = []
    for r in range(4):
        net.start(f"go{r}", o_at(chips[r], other), ro.at[r], at.to_core)
        net.start(f"gi{r}", i_at(chips[r], other), ri.at[r, :, 0:192], at.to_core)
        net.start(f"gw{r}", w_at(chips[r], other), ri.at[r, :, 192:240], at.to_core)
        halves.append(local(o_at(chips[r], core), so.at[r]))
        halves.append(local(i_at(chips[r], core), si.at[r, :, 0:192]))
        halves.append(local(w_at(chips[r], core), si.at[r, :, 192:240]))
    later = [local(wqkv_in, wqkv), local(hg_in, hg), local(small_in, small)]
    for r in range(4):
        later.append(local(xall_in.at[2 * chips[r] + core], xs.at[r]))

    for copy in loads:
        copy.wait()
    row16 = lax.broadcasted_iota(jnp.int32, (16, QUERIES), 0)
    row128 = lax.broadcasted_iota(jnp.int32, (128, QUERIES), 0)
    for h in range(LOCAL):
        high, middle, rest = parts_of(-lse[h, 0:1, :])
        qz[h] = jnp.where(row128 < 64, qa[h].astype(f32), 0.0).astype(bf16)
        qa[h, 64:80, :] = jnp.where(
            row16 == 0,
            1.0,
            jnp.where(
                row16 == 1, high, jnp.where(row16 == 2, middle, jnp.where(row16 == 3, rest, 0.0))
            ),
        ).astype(bf16)
        kv[h] = jnp.zeros((SLOTS, 128), f32)
        dz[h, 0:64, :] = jnp.zeros((64, QUERIES), bf16)
        da[h, 80:128, :] = jnp.zeros((48, QUERIES), bf16)
    for r in range(3):
        net.landed(f"mg{r}", mg.at[r], devices[r])
    own_mg.wait()
    row16 = lax.broadcasted_iota(jnp.int32, (16, ROWS), 0)
    for r in range(4):
        cols = pl.ds(ROWS * r, ROWS)
        for h in range(LOCAL):
            grad = mg[r, 64 * h : 64 * h + 64, :]
            delta = jnp.sum(grad.astype(f32) * ot[h, :, cols], axis=0, keepdims=True)
            high, middle, rest = parts_of(-delta)
            da[h, 0:64, cols] = grad
            dz[h, 64:128, cols] = grad
            da[h, 64:80, cols] = jnp.where(
                row16 == 0,
                high,
                jnp.where(row16 == 1, middle, jnp.where(row16 == 2, rest, 0.0)),
            ).astype(bf16)

    def add_core():
        for copy in halves:
            copy.wait()
        for r in range(4):
            net.landed(f"go{r}", ro.at[r], at.to_core)
            net.landed(f"gi{r}", ri.at[r, :, 0:192], at.to_core)
            net.landed(f"gw{r}", ri.at[r, :, 192:240], at.to_core)

        def one(t, carried):
            for r in range(4):
                so[r, t] = added(so[r, t], ro[r, t])
                si[r, t] = added(si[r, t], ri[r, t])
            return carried

        lax.fori_loop(0, GROUP, one, 0)
        net.launch("ox", lambda: (so.at[1], ao.at[0], at.to_x))
        net.launch("oxd", lambda: (so.at[0], ao.at[1], at.to_x))
        net.launch("iy", lambda: (si.at[2], ai.at[0], at.to_y))
        net.launch("iyd", lambda: (si.at[0], ai.at[1], at.to_y))

    def add_first():
        net.landed("ox", ao.at[0], at.to_x)
        net.landed("oxd", ao.at[1], at.to_x)
        net.landed("iy", ai.at[0], at.to_y)
        net.landed("iyd", ai.at[1], at.to_y)

        def one(t, carried):
            so[3, t] = added(so[3, t], ao[0, t])
            so[2, t] = added(so[2, t], ao[1, t])
            si[3, t] = added(si[3, t], ai[0, t])
            si[1, t] = added(si[1, t], ai[1, t])
            return carried

        lax.fori_loop(0, GROUP, one, 0)
        net.launch("oy", lambda: (so.at[2], bo, at.to_y))
        net.launch("ix", lambda: (si.at[1], bi, at.to_x))

    def add_second():
        net.landed("oy", bo, at.to_y)
        net.landed("ix", bi, at.to_x)

        def one(t, carried):
            so[3, t] = added(so[3, t], bo[t])
            si[3, t] = added(si[3, t], bi[t])
            return carried

        lax.fori_loop(0, GROUP, one, 0)
        for step in range(1, GROUP):
            net.launch(
                f"oz{step}",
                lambda step=step: (so.at[3, at.to_z(step)[1]], zo.at[step - 1], at.to_z(step)),
            )
            net.launch(
                f"iz{step}",
                lambda step=step: (si.at[3, at.to_z(step)[1]], zi.at[step - 1], at.to_z(step)),
            )

    def add_last():
        for step in range(1, GROUP):
            net.landed(f"oz{step}", zo.at[step - 1], at.to_z(step))
            net.landed(f"iz{step}", zi.at[step - 1], at.to_z(step))
        total_o = so[3, z].astype(f32)
        total_i = si[3, z].astype(f32)
        for step in range(GROUP - 1):
            total_o = total_o + zo[step].astype(f32)
            total_i = total_i + zi[step].astype(f32)
        so[3, z] = total_o.astype(bf16)
        si[3, z] = total_i.astype(bf16)

    def swap_kv(h):
        for r in range(4):
            net.launch(
                f"kv{h}{r}",
                lambda r=r: (
                    kv.at[h, pl.ds(multiple(2 * chips[r] + other, ROWS), ROWS)],
                    rkv.at[h, r],
                    at.to_core,
                ),
            )

    def attend(h, tile):
        cols = pl.ds(multiple(tile, TILE), TILE)
        queries = qa[h, :, cols]
        upstream = da[h, :, cols]
        queries_only = qz[h, :, cols]
        upstream_only = dz[h, :, cols]
        for j in range(SLOTS // SPAN):
            rows = pl.ds(SPAN * j, SPAN)
            probs = jnp.exp(dot(ka[h, rows, :], queries))
            grads = (probs * dot(va[h, rows, :], upstream)).astype(bf16)
            kv[h, rows, :] += dot_nt(grads, queries_only) + dot_nt(
                probs.astype(bf16), upstream_only
            )
            update = dot(kt[h, :, rows], grads)
            if j == 0:
                dq[h, :, cols] = update
            else:
                dq[h, :, cols] += update

    plan = {
        1: [add_core],
        2: [lambda: swap_kv(0)],
        4: [lambda: swap_kv(1), add_first],
    }

    def take(steps):
        for step in steps:
            step()

    def unit(u, carried):
        for when, steps in plan.items():
            pl.when(u == when)(functools.partial(take, steps))
        attend(u // 2, u % 2)
        return carried

    lax.fori_loop(0, 2 * LOCAL, unit, 0)
    swap_kv(2)
    add_second()

    for copy in later:
        copy.wait()
    weights = wqkv[...].reshape(D, WIDE)
    for h in range(LOCAL):
        for r in range(4):
            net.landed(f"kv{h}{r}", rkv.at[h, r], at.to_core)
    sums = jnp.zeros((1, WIDE), f32)
    for r in range(4):
        cols = pl.ds(ROWS * r, ROWS)
        rows = pl.ds(multiple(2 * chips[r] + core, ROWS), ROWS)
        for h in range(LOCAL):
            dqkv[r, :, 128 * h : 128 * h + 128] = (kv[h, rows, :] + rkv[h, r]).astype(bf16)
        turned = jnp.concatenate(
            [dq[h, :, cols] for h in range(LOCAL)] + [jnp.zeros((64, ROWS), f32)], axis=0
        )
        dqkv[r, :, 384:WIDE] = (turned.T * 0.125).astype(bf16)
        block = dqkv[r]
        sums = sums + jnp.sum(block.astype(f32), axis=0, keepdims=True)
        update = dot_nt(block, weights)
        if r < 3:
            sdx[r] = update.astype(bf16)
            net.start(f"dx{r}", sdx.at[r], rdx.at[r], devices[r])
        else:
            hg[...] += update
    small[p, 0:1, 0:WIDE] += sums
    for step in range(1, GROUP):
        net.start(f"sz{step}", small.at[at.to_z(step)[1]], rsz.at[step - 1], at.to_z(step))

    total = None
    for r in range(4):
        term = lax.dot_general(
            xs[r], dqkv[r], (((0,), (0,)), ((), ())), preferred_element_type=f32
        )
        total = term if total is None else total + term
    dw[...] = total.reshape(GROUP, 2, 96, WIDE)
    dwl[...] = dw[:, other].astype(bf16)
    net.start("dwc", dwl, rdw, at.to_core)

    for step in range(1, GROUP):
        net.landed(f"sz{step}", rsz.at[step - 1], at.to_z(step))
    small[z] = small[z] + rsz[0] + rsz[1] + rsz[2]
    net.start("sc", small.at[z], rsc, at.to_core)
    net.landed("dwc", rdw, at.to_core)
    for t in range(GROUP):
        rdw[t] = added(dw[t, core], rdw[t])
    for step in range(1, GROUP):
        net.start(f"dwz{step}", rdw.at[at.to_z(step)[1]], rzw.at[step - 1], at.to_z(step))
    net.landed("sc", rsc, at.to_core)
    rsc[...] = small[z] + rsc[...]
    for r in range(3):
        net.start(f"sp{r}", rsc, rsp.at[r], devices[r])

    def go_at(chip, side):
        return go_out.at[2 * chip + side]

    def gi_at(chip, side):
        return gi_out.at[:, pl.ds(multiple(2 * chip + side, 384), 384)]

    def gw_at(chip, side):
        return gw_out.at[chip, :, pl.ds(multiple(side, 384), 384)]

    add_last()
    mine = {"o": so.at[3, z], "i": si.at[3, z, 0:192], "w": si.at[3, z, 192:240]}
    place_of = {"o": go_at, "i": gi_at, "w": gw_at}
    for name in ("o", "i", "w"):
        net.start(f"f{name}x", mine[name], place_of[name](p, core), at.to_x)
    for name in ("i", "w", "o"):
        net.start(f"f{name}y", mine[name], place_of[name](p, core), at.to_y)
    for name in ("o", "i", "w"):
        net.start(f"f{name}c", mine[name], place_of[name](p, core), at.to_core)
        local(mine[name], place_of[name](p, core))

    for step in range(1, GROUP):
        net.landed(f"dwz{step}", rzw.at[step - 1], at.to_z(step))
    finished = rdw[z].astype(f32)
    for step in range(GROUP - 1):
        finished = finished + rzw[step].astype(f32)
    rdw[z] = finished.astype(bf16)
    for r in range(3):
        net.start(f"fq{r}", rdw.at[z], gqkv_out.at[p, core], devices[r])
    net.start("fqc", rdw.at[z], gqkv_out.at[p, core], at.to_core)
    local(rdw.at[z], gqkv_out.at[p, core])

    for r in range(3):
        net.landed(f"sp{r}", rsp.at[r], devices[r])
    ssum[...] = rsc[...] + rsp[0] + rsp[1] + rsp[2]
    local(ssum, small_out)

    for name in ("o", "i", "w"):
        place = place_of[name]
        a, b = place(at.p_x, core), place(at.p_y, core)
        net.landed(f"f{name}x", a, at.to_x)
        net.landed(f"f{name}y", b, at.to_y)
        if name == "o":
            net.start(f"f{name}r", a, a, at.to_y)
        else:
            net.start(f"f{name}r", b, b, at.to_x)
        net.start(f"f{name}cx", a, a, at.to_core)
        net.start(f"f{name}cy", b, b, at.to_core)
    for r in range(3):
        ref = gqkv_out.at[chips[r], core]
        net.landed(f"fq{r}", ref, devices[r])
        net.start(f"fqc{r}", ref, ref, at.to_core)

    result = hg[...]
    for r in range(3):
        net.landed(f"dx{r}", rdx.at[r], devices[r])
        result = result + rdx[r].astype(f32)
    sdx[3] = result.astype(bf16)
    local(sdx.at[3], dx_out)

    for name in ("o", "i", "w"):
        far = place_of[name](at.p_d, core)
        net.landed(f"f{name}r", far, at.to_y if name == "o" else at.to_x)
        net.start(f"f{name}cd", far, far, at.to_core)
    for name in ("o", "i", "w"):
        place = place_of[name]
        for tag, chip in (("c", p), ("cx", at.p_x), ("cy", at.p_y), ("cd", at.p_d)):
            net.landed(f"f{name}{tag}", place(chip, other), at.to_core)
    net.landed("fqc", gqkv_out.at[p, other], at.to_core)
    for r in range(3):
        net.landed(f"fqc{r}", gqkv_out.at[chips[r], other], at.to_core)
    done = len(loads) + 1 + len(halves) + len(later)
    for copy in slots[done:]:
        copy.wait()
    net.drain()


BACKWARD_COPIES = 96


def backward_call(*operands):
    any_ = pl.BlockSpec(memory_space=pl.ANY)
    shape = jax.ShapeDtypeStruct
    vmem = pltpu.VMEM
    return pl.pallas_call(
        backward_kernel,
        name="backward_attention",
        out_shape=(
            shape((ROWS, D), bf16),
            shape((GROUP, 2, 96, WIDE), bf16),
            shape((192, FF), bf16),
            shape((CTX, 96, D), bf16),
            shape((GROUP, 48, D), bf16),
            shape((8, D), f32),
        ),
        in_specs=[any_] * 14,
        out_specs=[any_] * 6,
        scratch_shapes=[
            vmem((4, 192, ROWS), bf16),
            vmem((LOCAL, 64, QUERIES), f32),
            vmem((LOCAL, 8, QUERIES), f32),
            vmem((LOCAL, 128, QUERIES), bf16),
            vmem((LOCAL, 128, QUERIES), bf16),
            vmem((LOCAL, SLOTS, 128), bf16),
            vmem((LOCAL, SLOTS, 128), bf16),
            vmem((LOCAL, 64, SLOTS), bf16),
            vmem((LOCAL, 128, QUERIES), bf16),
            vmem((LOCAL, 128, QUERIES), bf16),
            vmem((LOCAL, SLOTS, 128), f32),
            vmem((LOCAL, 4, ROWS, 128), f32),
            vmem((LOCAL, 64, QUERIES), f32),
            vmem((4, GROUP, 96, D), bf16),
            vmem((4, GROUP, 240, 384), bf16),
            vmem((4, GROUP, 96, D), bf16),
            vmem((4, GROUP, 240, 384), bf16),
            vmem((2, GROUP, 96, D), bf16),
            vmem((2, GROUP, 240, 384), bf16),
            vmem((GROUP, 96, D), bf16),
            vmem((GROUP, 240, 384), bf16),
            vmem((3, 96, D), bf16),
            vmem((3, 240, 384), bf16),
            vmem((4, ROWS, D), bf16),
            vmem((GROUP, 2, 96, WIDE), bf16),
            vmem((4, ROWS, WIDE), bf16),
            vmem((4, ROWS, D), bf16),
            vmem((3, ROWS, D), bf16),
            vmem((ROWS, D), f32),
            vmem((GROUP, 2, 96, WIDE), f32),
            vmem((GROUP, 96, WIDE), bf16),
            vmem((GROUP, 96, WIDE), bf16),
            vmem((3, 96, WIDE), bf16),
            vmem((GROUP, 8, D), f32),
            vmem((3, 8, D), f32),
            vmem((8, D), f32),
            vmem((3, 8, D), f32),
            vmem((8, D), f32),
            pltpu.SemaphoreType.DMA((BACKWARD_COPIES,)),
            pltpu.SemaphoreType.DMA((BACKWARD_COPIES,)),
            pltpu.SemaphoreType.DMA((48,)),
        ],
        compiler_params=pltpu.CompilerParams(
            collective_id=1, has_side_effects=True, vmem_limit_bytes=63 << 20
        ),
    )(*operands)


def small_plane(
    states,
    lengths,
    query_weight,
    query_bias,
    key_weight,
    value_weight,
    value_bias,
    output_weight,
    output_bias,
    first_gain,
    first_shift,
    inner_weight,
    inner_bias,
    outer_weight,
    outer_bias,
    second_gain,
    second_shift,
    cotangent,
):
    cycle_place = lax.axis_index("ctx")
    length = lengths[lax.axis_index("fsdp")]
    inputs = states[0]
    offsets = jnp.arange(ROWS, dtype=jnp.int32)
    row_keep = cycle_place * ROWS + offsets < length
    wqkv = split_weights(cycle_place // 2, query_weight, key_weight, value_weight)
    vectors = pack_vectors(
        query_bias,
        value_bias,
        inner_bias,
        [output_bias, first_gain, first_shift, outer_bias, second_gain, second_shift],
    )
    xall, wall, vall, inner_all, outer_all, wo_all, mixed_t, qt, ka, va, kt, ot, lse = forward_call(
        length[None],
        inputs,
        wqkv,
        vectors,
        inner_weight,
        outer_weight.reshape(CTX, 96, D),
        output_weight.reshape(GROUP, 48, D),
    )
    mixed_t = mixed_t.reshape(D, ROWS)
    inner_full = inner_all.reshape(D, FF)
    outer_full = outer_all.reshape(FF, D)
    output_full = wo_all.reshape(D, D)
    wide = vall.astype(jnp.float32)
    inner_add = wide[:, 1].reshape(FF)
    output_add, gain_one, shift_one, outer_add, gain_two, shift_two = [
        wide[:, 2 + i, :192].reshape(D) for i in range(6)
    ]
    attended = dot_tn(mixed_t, output_full) + output_add
    first_normed, first_scale = normalize(inputs.astype(jnp.float32) + attended)
    first = first_normed * gain_one + shift_one
    first_low = first.astype(jnp.bfloat16)
    inner = dot(first_low, inner_full) + inner_add
    activated = jax.nn.gelu(inner, approximate=False).astype(jnp.bfloat16)
    outer = dot(activated, outer_full) + outer_add
    second_normed, second_scale = normalize(first + outer)
    second = second_normed * gain_two + shift_two
    layer_output = jnp.where(row_keep[:, None], second, 0.0).astype(jnp.bfloat16)[None]
    upstream = jnp.where(row_keep[:, None], cotangent[0].astype(jnp.float32), 0.0)
    second_grad, second_gain_grad, second_shift_grad = norm_back(
        upstream, second_normed, second_scale, gain_two
    )
    outer_low = second_grad.astype(jnp.bfloat16)
    outer_bias_grad = jnp.sum(second_grad, axis=0)
    outer_weight_grad = dot_tn(activated, outer_low).astype(jnp.bfloat16)
    inner_grad = dot_nt(outer_low, outer_full) * gelu_slope(inner)
    inner_low = inner_grad.astype(jnp.bfloat16)
    inner_bias_grad = jnp.sum(inner_grad, axis=0)
    inner_weight_grad = dot_tn(first_low, inner_low).astype(jnp.bfloat16)
    first_grad = second_grad + dot_nt(inner_low, inner_full)
    hidden_grad, first_gain_grad, first_shift_grad = norm_back(
        first_grad, first_normed, first_scale, gain_one
    )
    attended_low = hidden_grad.astype(jnp.bfloat16)
    output_bias_grad = jnp.sum(hidden_grad, axis=0)
    output_weight_grad = dot(mixed_t, attended_low).astype(jnp.bfloat16)
    mixed_grad_t = dot_nt(output_full, attended_low).astype(jnp.bfloat16)
    narrow = [
        output_bias_grad,
        first_gain_grad,
        first_shift_grad,
        outer_bias_grad,
        second_gain_grad,
        second_shift_grad,
    ]
    small = jnp.stack(
        [jnp.zeros((GROUP, D), jnp.float32), inner_bias_grad.reshape(GROUP, D)]
        + [jnp.pad(v.reshape(GROUP, 192), ((0, 0), (0, 576))) for v in narrow],
        axis=1,
    )
    dx, gqkv, gi, go, gw, sums = backward_call(
        mixed_grad_t.reshape(GROUP, 192, ROWS),
        ot,
        lse,
        qt,
        ka,
        va,
        kt,
        inner_weight_grad.reshape(GROUP, 192, FF),
        outer_weight_grad.reshape(GROUP, CTX, 96, D),
        output_weight_grad.reshape(GROUP, GROUP, 48, D),
        xall,
        wall,
        hidden_grad,
        small,
    )
    gqkv = gqkv.reshape(GROUP, 192, WIDE)
    pairs = gqkv[:, :, :384].reshape(GROUP, 192, LOCAL, 2, 64).transpose(3, 1, 0, 2, 4)
    pairs = pairs.reshape(2, 192, D).astype(jnp.float32)
    query_grad = gqkv[:, :, 384:576].transpose(1, 0, 2).reshape(192, D).astype(jnp.float32)
    value_bias_grad = sums[0, :384].reshape(LOCAL, 2, 64)[:, 1].reshape(192)
    return (
        layer_output,
        dx[None],
        query_grad,
        sums[0, 384:576],
        pairs[0],
        pairs[1],
        value_bias_grad,
        gw.reshape(192, D).astype(jnp.float32),
        sums[2, :192],
        sums[3, :192],
        sums[4, :192],
        gi.astype(jnp.float32),
        sums[1],
        go.reshape(D, D).astype(jnp.float32),
        sums[5, :192],
        sums[6, :192],
        sums[7, :192],
    )


def keep_state(carried):
    return carried


def per_device(
    states,
    lengths,
    query_weight,
    query_bias,
    key_weight,
    value_weight,
    value_bias,
    output_weight,
    output_bias,
    first_gain,
    first_shift,
    inner_weight,
    inner_bias,
    outer_weight,
    outer_bias,
    second_gain,
    second_shift,
    cotangent,
):
    row_count = states.shape[1]
    cycle_size = lax.axis_size("ctx")
    cycle_place = lax.axis_index("ctx")
    sequence = lax.axis_index("fsdp")
    length = lengths[sequence]
    offsets = jnp.arange(row_count, dtype=jnp.int32)
    row_keep = cycle_place * row_count + offsets < length
    inputs = states[0]
    input_float = inputs.astype(jnp.float32)
    attention_set = (
        lax.all_gather(query_weight, "fsdp", axis=0, tiled=True),
        lax.all_gather(key_weight, "fsdp", axis=0, tiled=True),
        lax.all_gather(value_weight, "fsdp", axis=0, tiled=True),
        lax.all_gather(output_weight, "fsdp", axis=0, tiled=True),
        lax.all_gather(query_bias, "fsdp", axis=0, tiled=True),
        lax.all_gather(value_bias, "fsdp", axis=0, tiled=True),
        lax.all_gather(output_bias, "fsdp", axis=0, tiled=True),
        lax.all_gather(first_gain, "fsdp", axis=0, tiled=True),
        lax.all_gather(first_shift, "fsdp", axis=0, tiled=True),
    )
    query_full = attention_set[0]
    key_full = attention_set[1]
    value_full = attention_set[2]
    output_full = attention_set[3]
    query_add = attention_set[4].astype(jnp.float32)
    value_add = attention_set[5].astype(jnp.float32)
    output_add = attention_set[6].astype(jnp.float32)
    gain_one = attention_set[7].astype(jnp.float32)
    shift_one = attention_set[8].astype(jnp.float32)
    queries = (
        (jnp.dot(inputs, query_full, preferred_element_type=jnp.float32) + query_add) * 0.125
    ).astype(jnp.bfloat16)
    key_rows = jnp.dot(inputs, key_full, preferred_element_type=jnp.float32).astype(jnp.bfloat16)
    values = (jnp.dot(inputs, value_full, preferred_element_type=jnp.float32) + value_add).astype(
        jnp.bfloat16
    )
    query_heads = queries.reshape(row_count, H, HD)

    def forward_block(key_block, value_block, key_start, running_state):

        def forward_compute(carried):
            running, exp_total, accum = carried
            key_keep = key_start + offsets < length
            scores = jnp.einsum(
                "qhd,khd->hqk",
                query_heads,
                key_block.reshape(row_count, H, HD),
                preferred_element_type=jnp.float32,
            )
            scores = jnp.where(key_keep[None, None, :], scores, -1e30)
            newest = jnp.maximum(running, jnp.max(scores, axis=2))
            factor = jnp.exp(running - newest)
            weights = jnp.exp(scores - newest[:, :, None])
            exp_total = exp_total * factor + jnp.sum(weights, axis=2)
            update = jnp.einsum(
                "hqk,khd->qhd",
                weights.astype(jnp.bfloat16),
                value_block.reshape(row_count, H, HD),
                preferred_element_type=jnp.float32,
            )
            accum = accum * factor.T[:, :, None] + update
            return (newest, exp_total, accum)

        return lax.cond(key_start < length, forward_compute, keep_state, running_state)

    start_state = (
        jnp.full((H, row_count), -1e30, jnp.float32),
        jnp.zeros((H, row_count), jnp.float32),
        jnp.zeros((row_count, H, HD), jnp.float32),
    )

    def cycle_turn(turn_index, carried):
        key_block, value_block, running_state = carried
        owner_index = (cycle_place - turn_index) % cycle_size
        running_state = forward_block(
            key_block, value_block, owner_index * row_count, running_state
        )
        key_block, value_block = passed_along((key_block, value_block), "ctx", 1)
        return (key_block, value_block, running_state)

    key_block, value_block, running_state = lax.fori_loop(
        0, cycle_size - 1, cycle_turn, (key_rows, values, start_state)
    )
    last_owner = (cycle_place + 1) % cycle_size
    running, exp_total, accum = forward_block(
        key_block, value_block, last_owner * row_count, running_state
    )
    log_total = running + jnp.log(exp_total)
    attention_value = (accum / exp_total.T[:, :, None]).reshape(row_count, D)
    mixed = attention_value.astype(jnp.bfloat16)
    attended = jnp.dot(mixed, output_full, preferred_element_type=jnp.float32) + output_add
    first_normed, first_scale = normalize(input_float + attended)
    first = first_normed * gain_one + shift_one
    first_low = first.astype(jnp.bfloat16)
    feed_set = (
        lax.all_gather(inner_weight, "fsdp", axis=0, tiled=True),
        lax.all_gather(outer_weight, "fsdp", axis=0, tiled=True),
        lax.all_gather(inner_bias, "fsdp", axis=0, tiled=True),
        lax.all_gather(outer_bias, "fsdp", axis=0, tiled=True),
        lax.all_gather(second_gain, "fsdp", axis=0, tiled=True),
        lax.all_gather(second_shift, "fsdp", axis=0, tiled=True),
    )
    inner_full = feed_set[0]
    outer_full = feed_set[1]
    inner_add = feed_set[2].astype(jnp.float32)
    outer_add = feed_set[3].astype(jnp.float32)
    gain_two = feed_set[4].astype(jnp.float32)
    shift_two = feed_set[5].astype(jnp.float32)
    inner = jnp.dot(first_low, inner_full, preferred_element_type=jnp.float32) + inner_add
    activated = jax.nn.gelu(inner, approximate=False).astype(jnp.bfloat16)
    outer = jnp.dot(activated, outer_full, preferred_element_type=jnp.float32) + outer_add
    second_normed, second_scale = normalize(first + outer)
    second = second_normed * gain_two + shift_two
    layer_output = jnp.where(row_keep[:, None], second, 0.0).astype(jnp.bfloat16)[None]
    query_full = attention_set[0]
    key_full = attention_set[1]
    value_full = attention_set[2]
    output_full = attention_set[3]
    gain_one = attention_set[7].astype(jnp.float32)
    inner_full = feed_set[0]
    outer_full = feed_set[1]
    gain_two = feed_set[4].astype(jnp.float32)
    upstream = jnp.where(row_keep[:, None], cotangent[0].astype(jnp.float32), 0.0)
    second_grad, second_gain_grad, second_shift_grad = norm_back(
        upstream, second_normed, second_scale, gain_two
    )
    outer_low = second_grad.astype(jnp.bfloat16)
    outer_bias_grad = jnp.sum(second_grad, axis=0)
    outer_weight_grad = jnp.dot(activated.T, outer_low, preferred_element_type=jnp.float32)
    inner_grad = jnp.dot(outer_low, outer_full.T, preferred_element_type=jnp.float32) * gelu_slope(
        inner
    )
    inner_low = inner_grad.astype(jnp.bfloat16)
    inner_bias_grad = jnp.sum(inner_grad, axis=0)
    inner_weight_grad = jnp.dot(first_low.T, inner_low, preferred_element_type=jnp.float32)
    first_grad = second_grad + jnp.dot(inner_low, inner_full.T, preferred_element_type=jnp.float32)
    hidden_grad, first_gain_grad, first_shift_grad = norm_back(
        first_grad, first_normed, first_scale, gain_one
    )
    attended_low = hidden_grad.astype(jnp.bfloat16)
    output_bias_grad = jnp.sum(hidden_grad, axis=0)
    output_weight_grad = jnp.dot(mixed.T, attended_low, preferred_element_type=jnp.float32)
    mixed_grad = jnp.dot(attended_low, output_full.T, preferred_element_type=jnp.float32).astype(
        jnp.bfloat16
    )
    delta = jnp.sum(
        (mixed_grad.astype(jnp.float32) * attention_value).reshape(row_count, H, HD), axis=2
    ).T

    def back_block(
        query_block,
        upstream_block,
        log_block,
        delta_block,
        key_block,
        value_block,
        key_start,
        grads,
    ):

        def back_compute(carried):
            query_grad, key_grad, value_grad = carried
            key_keep = key_start + offsets < length
            query_three = query_block.reshape(row_count, H, HD)
            upstream_three = upstream_block.reshape(row_count, H, HD)
            key_three = key_block.reshape(row_count, H, HD)
            value_three = value_block.reshape(row_count, H, HD)
            scores = jnp.einsum(
                "qhd,khd->hqk", query_three, key_three, preferred_element_type=jnp.float32
            )
            weights = jnp.where(
                key_keep[None, None, :], jnp.exp(scores - log_block[:, :, None]), 0.0
            )
            weight_grad = jnp.einsum(
                "qhd,khd->hqk", upstream_three, value_three, preferred_element_type=jnp.float32
            )
            score_grad = (weights * (weight_grad - delta_block[:, :, None])).astype(jnp.bfloat16)
            query_grad = query_grad + jnp.einsum(
                "hqk,khd->qhd", score_grad, key_three, preferred_element_type=jnp.float32
            ).reshape(row_count, D)
            key_grad = key_grad + jnp.einsum(
                "hqk,qhd->khd", score_grad, query_three, preferred_element_type=jnp.float32
            ).reshape(row_count, D)
            value_grad = value_grad + jnp.einsum(
                "hqk,qhd->khd",
                weights.astype(jnp.bfloat16),
                upstream_three,
                preferred_element_type=jnp.float32,
            ).reshape(row_count, D)
            return (query_grad, key_grad, value_grad)

        return lax.cond(key_start < length, back_compute, keep_state, grads)

    zero_grad = jnp.zeros((row_count, D), jnp.float32)

    def key_turn(turn_index, carried):
        key_block, value_block, query_grad, key_grad, value_grad = carried
        owner_index = (cycle_place - turn_index) % cycle_size
        query_grad, key_grad, value_grad = back_block(
            queries,
            mixed_grad,
            log_total,
            delta,
            key_block,
            value_block,
            owner_index * row_count,
            (query_grad, key_grad, value_grad),
        )
        key_block, value_block = passed_along((key_block, value_block), "ctx", 1)
        key_grad, value_grad = (
            passed_along(key_grad.astype(jnp.bfloat16), "ctx", 1).astype(key_grad.dtype),
            passed_along(value_grad.astype(jnp.bfloat16), "ctx", 1).astype(value_grad.dtype),
        )
        return (key_block, value_block, query_grad, key_grad, value_grad)

    key_block, value_block, query_grad, key_grad, value_grad = lax.fori_loop(
        0, cycle_size - 1, key_turn, (key_rows, values, zero_grad, zero_grad, zero_grad)
    )
    query_grad, key_grad, value_grad = back_block(
        queries,
        mixed_grad,
        log_total,
        delta,
        key_block,
        value_block,
        last_owner * row_count,
        (query_grad, key_grad, value_grad),
    )
    key_grad, value_grad = (
        passed_along(key_grad.astype(jnp.bfloat16), "ctx", 1).astype(key_grad.dtype),
        passed_along(value_grad.astype(jnp.bfloat16), "ctx", 1).astype(value_grad.dtype),
    )
    query_low = query_grad.astype(jnp.bfloat16) * 0.125
    key_low = key_grad.astype(jnp.bfloat16)
    value_low = value_grad.astype(jnp.bfloat16)
    query_weight_grad = jnp.dot(inputs.T, query_low, preferred_element_type=jnp.float32)
    query_bias_grad = jnp.sum(query_low.astype(jnp.float32), axis=0)
    key_weight_grad = jnp.dot(inputs.T, key_low, preferred_element_type=jnp.float32)
    value_weight_grad = jnp.dot(inputs.T, value_low, preferred_element_type=jnp.float32)
    value_bias_grad = jnp.sum(value_low.astype(jnp.float32), axis=0)
    input_grad = (
        hidden_grad
        + jnp.dot(query_low, query_full.T, preferred_element_type=jnp.float32)
        + jnp.dot(key_low, key_full.T, preferred_element_type=jnp.float32)
        + jnp.dot(value_low, value_full.T, preferred_element_type=jnp.float32)
    ).astype(jnp.bfloat16)[None]
    local_grads = (
        query_weight_grad,
        query_bias_grad,
        key_weight_grad,
        value_weight_grad,
        value_bias_grad,
        output_weight_grad,
        output_bias_grad,
        first_gain_grad,
        first_shift_grad,
        inner_weight_grad,
        inner_bias_grad,
        outer_weight_grad,
        outer_bias_grad,
        second_gain_grad,
        second_shift_grad,
    )
    shards = (
        lax.psum_scatter(
            local_grads[0].astype(jnp.bfloat16), "fsdp", scatter_dimension=0, tiled=True
        ).astype(jnp.float32),
        lax.psum_scatter(
            local_grads[1].astype(jnp.bfloat16), "fsdp", scatter_dimension=0, tiled=True
        ).astype(jnp.float32),
        lax.psum_scatter(
            local_grads[2].astype(jnp.bfloat16), "fsdp", scatter_dimension=0, tiled=True
        ).astype(jnp.float32),
        lax.psum_scatter(
            local_grads[3].astype(jnp.bfloat16), "fsdp", scatter_dimension=0, tiled=True
        ).astype(jnp.float32),
        lax.psum_scatter(
            local_grads[4].astype(jnp.bfloat16), "fsdp", scatter_dimension=0, tiled=True
        ).astype(jnp.float32),
        lax.psum_scatter(
            local_grads[5].astype(jnp.bfloat16), "fsdp", scatter_dimension=0, tiled=True
        ).astype(jnp.float32),
        lax.psum_scatter(
            local_grads[6].astype(jnp.bfloat16), "fsdp", scatter_dimension=0, tiled=True
        ).astype(jnp.float32),
        lax.psum_scatter(
            local_grads[7].astype(jnp.bfloat16), "fsdp", scatter_dimension=0, tiled=True
        ).astype(jnp.float32),
        lax.psum_scatter(
            local_grads[8].astype(jnp.bfloat16), "fsdp", scatter_dimension=0, tiled=True
        ).astype(jnp.float32),
        lax.psum_scatter(
            local_grads[9].astype(jnp.bfloat16), "fsdp", scatter_dimension=0, tiled=True
        ).astype(jnp.float32),
        lax.psum_scatter(
            local_grads[10].astype(jnp.bfloat16), "fsdp", scatter_dimension=0, tiled=True
        ).astype(jnp.float32),
        lax.psum_scatter(
            local_grads[11].astype(jnp.bfloat16), "fsdp", scatter_dimension=0, tiled=True
        ).astype(jnp.float32),
        lax.psum_scatter(
            local_grads[12].astype(jnp.bfloat16), "fsdp", scatter_dimension=0, tiled=True
        ).astype(jnp.float32),
        lax.psum_scatter(
            local_grads[13].astype(jnp.bfloat16), "fsdp", scatter_dimension=0, tiled=True
        ).astype(jnp.float32),
        lax.psum_scatter(
            local_grads[14].astype(jnp.bfloat16), "fsdp", scatter_dimension=0, tiled=True
        ).astype(jnp.float32),
    )
    totals = (
        lax.psum(shards[0].astype(jnp.bfloat16), "ctx").astype(jnp.float32),
        lax.psum(shards[1].astype(jnp.bfloat16), "ctx").astype(jnp.float32),
        lax.psum(shards[2].astype(jnp.bfloat16), "ctx").astype(jnp.float32),
        lax.psum(shards[3].astype(jnp.bfloat16), "ctx").astype(jnp.float32),
        lax.psum(shards[4].astype(jnp.bfloat16), "ctx").astype(jnp.float32),
        lax.psum(shards[5].astype(jnp.bfloat16), "ctx").astype(jnp.float32),
        lax.psum(shards[6].astype(jnp.bfloat16), "ctx").astype(jnp.float32),
        lax.psum(shards[7].astype(jnp.bfloat16), "ctx").astype(jnp.float32),
        lax.psum(shards[8].astype(jnp.bfloat16), "ctx").astype(jnp.float32),
        lax.psum(shards[9].astype(jnp.bfloat16), "ctx").astype(jnp.float32),
        lax.psum(shards[10].astype(jnp.bfloat16), "ctx").astype(jnp.float32),
        lax.psum(shards[11].astype(jnp.bfloat16), "ctx").astype(jnp.float32),
        lax.psum(shards[12].astype(jnp.bfloat16), "ctx").astype(jnp.float32),
        lax.psum(shards[13].astype(jnp.bfloat16), "ctx").astype(jnp.float32),
        lax.psum(shards[14].astype(jnp.bfloat16), "ctx").astype(jnp.float32),
    )
    return (
        layer_output,
        input_grad,
        totals[0],
        totals[1],
        totals[2],
        totals[3],
        totals[4],
        totals[5],
        totals[6],
        totals[7],
        totals[8],
        totals[9],
        totals[10],
        totals[11],
        totals[12],
        totals[13],
        totals[14],
    )


def solution(mesh):
    small = mesh.shape["ctx"] == CTX and mesh.shape["fsdp"] == GROUP
    return jax.shard_map(
        small_plane if small else per_device,
        mesh=mesh,
        in_specs=(
            P("fsdp", "ctx", None),
            P(),
            P("fsdp", None),
            P("fsdp"),
            P("fsdp", None),
            P("fsdp", None),
            P("fsdp"),
            P("fsdp", None),
            P("fsdp"),
            P("fsdp"),
            P("fsdp"),
            P("fsdp", None),
            P("fsdp"),
            P("fsdp", None),
            P("fsdp"),
            P("fsdp"),
            P("fsdp"),
            P("fsdp", "ctx", None),
        ),
        out_specs=(
            P("fsdp", "ctx", None),
            P("fsdp", "ctx", None),
            P("fsdp", None),
            P("fsdp"),
            P("fsdp", None),
            P("fsdp", None),
            P("fsdp"),
            P("fsdp", None),
            P("fsdp"),
            P("fsdp"),
            P("fsdp"),
            P("fsdp", None),
            P("fsdp"),
            P("fsdp", None),
            P("fsdp"),
            P("fsdp"),
            P("fsdp"),
        ),
        check_vma=False,
    )
```

```python
import functools

import jax
import jax.numpy as jnp
from jax import lax
from jax.experimental import pallas as pl
from jax.experimental.pallas import tpu as pltpu
from jax.sharding import PartitionSpec as P

D = 768
H = 12
HD = 64


epsilon = 1e-05


def passed_along(value, axis, steps):
    count = lax.axis_size(axis)
    pairs = [(source, (source + steps) % count) for source in range(count)]
    return lax.ppermute(value, axis, pairs)


def normalize(hidden):
    centred = hidden - jnp.mean(hidden, axis=1, keepdims=True)
    scale = lax.rsqrt(jnp.mean(centred * centred, axis=1, keepdims=True) + epsilon)
    return (centred * scale, scale)


def norm_back(upstream, normed, scale, gain):
    gain_grad = jnp.sum(upstream * normed, axis=0)
    shift_grad = jnp.sum(upstream, axis=0)
    scaled = upstream * gain
    hidden_grad = scale * (
        scaled
        - jnp.mean(scaled, axis=1, keepdims=True)
        - normed * jnp.mean(scaled * normed, axis=1, keepdims=True)
    )
    return (hidden_grad, gain_grad, shift_grad)


def gelu_slope(inner):
    return (
        0.5 * (1.0 + lax.erf(inner * 0.7071067811865476))
        + inner * jnp.exp(-0.5 * inner * inner) * 0.3989422804014327
    )


bf16 = jnp.bfloat16
f32 = jnp.float32
FF = 3072
ROWS = 384
CTX = 8
GROUP = 4
LOCAL = 3
SLOTS = 3072
QUERIES = 1536
TILE = 768
CHUNK = 512
WIDE = 640
MESH = pl.DeviceIdType.MESH


def multiple(value, step):
    return pl.multiple_of(value * step, step)


class Place:
    def __init__(self):
        self.c = lax.axis_index("ctx")
        self.z = lax.axis_index("fsdp")
        c = self.c
        self.core = c % 2
        self.p = c // 2
        self.x = self.p % 2
        self.y = c // 4
        self.p_x = self.p + 1 - 2 * self.x
        self.p_y = self.p + 2 - 4 * self.y
        self.p_d = self.p_y + 1 - 2 * self.x
        self.to_core = (c + 1 - 2 * self.core, self.z)
        self.to_x = (2 * self.p_x + self.core, self.z)
        self.to_y = (2 * self.p_y + self.core, self.z)
        self.to_d = (2 * self.p_d + self.core, self.z)

    def to_z(self, step):
        return (self.c, (self.z + step) % GROUP)

    def from_z(self, step):
        return (self.z + GROUP - step) % GROUP


class Net:
    def __init__(self, sends, receives):
        self.sends = sends
        self.receives = receives
        self.index = {}
        self.open = []

    def of(self, name):
        return self.index.setdefault(name, len(self.index))

    def copy(self, name, src, dst, device):
        i = self.of(name)
        return pltpu.make_async_remote_copy(
            src_ref=src,
            dst_ref=dst,
            send_sem=self.sends.at[i],
            recv_sem=self.receives.at[i],
            device_id=device,
            device_id_type=MESH,
        )

    def start(self, name, src, dst, device):
        self.launch(name, lambda: (src, dst, device))

    def launch(self, name, make):
        self.copy(name, *make()).start()
        self.open.append((name, make))

    def landed(self, name, dst, device):
        self.copy(name, dst, dst, device).wait_recv()

    def finish(self, name):
        for opened, make in self.open:
            if opened == name:
                self.copy(name, *make()).wait_send()
        self.open = [pair for pair in self.open if pair[0] != name]

    def drain(self):
        for name, make in self.open:
            self.copy(name, *make()).wait_send()
        self.open = []


def greet(place, with_z=True):
    barrier = pltpu.get_barrier_semaphore()
    partners = [place.to_core, place.to_x, place.to_y, place.to_d]
    if with_z:
        partners += [place.to_z(step) for step in range(1, GROUP)]
    for partner in partners:
        pl.semaphore_signal(barrier, inc=1, device_id=partner, device_id_type=MESH)
    pl.semaphore_wait(barrier, len(partners))


def dot(a, b):
    return jnp.dot(a, b, preferred_element_type=f32)


def dot_nt(a, b):
    return lax.dot_general(a, b, (((1,), (1,)), ((), ())), preferred_element_type=f32)


def dot_tn(a, b):
    return lax.dot_general(a, b, (((0,), (0,)), ((), ())), preferred_element_type=f32)


def parts_of(value):
    high = value.astype(bf16).astype(f32)
    rest = value - high
    middle = rest.astype(bf16).astype(f32)
    return high, middle, rest - middle


def added(a, b):
    return (a.astype(f32) + b.astype(f32)).astype(bf16)


def forward_kernel(
    length,
    x_in,
    wqkv_in,
    vec_in,
    inner_in,
    outer_in,
    wo_in,
    cot_in,
    low_out,
    mg_out,
    gi_out,
    gw_out,
    own_out,
    half_y_out,
    half_x_out,
    hg_out,
    small_out,
    xs_out,
    wqkv_out,
    qt_out,
    ka_out,
    va_out,
    kt_out,
    ot_out,
    lse_out,
    xall,
    wqkv,
    vec,
    qt,
    ka,
    va,
    kt,
    vt,
    ot,
    lse,
    mix,
    mixed,
    acc,
    top,
    iw,
    ow,
    wo,
    cot,
    work,
    first,
    normed,
    second,
    slope,
    act,
    low,
    lower,
    gi,
    gw,
    mg,
    small,
    scales,
    ro,
    ax,
    ay,
    sends,
    receives,
    locals_,
):
    at = Place()
    net = Net(sends, receives)
    c, z, core, p = at.c, at.z, at.core, at.p
    other = 1 - core
    chips = [at.p_d, at.p_x, at.p_y, p]
    devices = [at.to_d, at.to_x, at.to_y]
    slots = []

    def local(src, dst):
        copy = pltpu.make_async_copy(src, dst, locals_.at[len(slots)])
        slots.append(copy)
        copy.start()
        return copy

    def inner_at(ref, chip, side):
        return ref.at[:, pl.ds(multiple(2 * chip + side, 384), 384)]

    def outer_at(ref, chip, side):
        return ref.at[2 * chip + side]

    def wo_at(ref, chip, side):
        return ref.at[chip, :, pl.ds(multiple(side, 384), 384)]

    weights = {
        "wo": (wo_in, wo, wo_at),
        "inner": (inner_in, iw, inner_at),
        "outer": (outer_in, ow, outer_at),
    }

    def block_at(chip, side, part=slice(None)):
        return xall.at[chip, side, part]

    greet(at)

    early, late = pl.ds(0, 2), pl.ds(2, 2)
    net.start("sx0", x_in.at[early], block_at(p, core, early), at.to_x)
    net.start("sy1", x_in.at[late], block_at(p, core, late), at.to_y)
    net.start("sx1", x_in.at[late], block_at(p, core, late), at.to_x)
    net.start("sy0", x_in.at[early], block_at(p, core, early), at.to_y)
    net.start("sc", x_in, block_at(p, core), at.to_core)
    for step in range(1, GROUP):
        net.start(f"vec{step}", vec_in, vec.at[z], at.to_z(step))
    for step in range(1, GROUP):
        net.start(f"wq{step}", wqkv_in.at[core], wqkv.at[z, core], at.to_z(step))
    for name, (src, dst, region) in weights.items():
        for step in range(1, GROUP):
            net.start(
                f"{name}z{step}", region(src, p, core), region(dst.at[z], p, core), at.to_z(step)
            )
    opening = [local(x_in, block_at(p, core)), local(vec_in, vec.at[z]), local(wqkv_in, wqkv.at[z])]
    owned = [
        local(wo_in, wo.at[z]),
        local(inner_in, iw.at[z]),
        local(outer_in, ow.at[z]),
        local(cot_in, cot),
    ]

    row64 = lax.broadcasted_iota(jnp.int32, (64, QUERIES), 0)
    row16 = lax.broadcasted_iota(jnp.int32, (16, SLOTS), 0)
    for h in range(LOCAL):
        qt[h, 64:128, :] = jnp.where(row64 == 0, 1.0, 0.0).astype(bf16)
        vt[h, 64:80, :] = jnp.where(row16 == 0, 1.0, 0.0).astype(bf16)

    for step in range(1, GROUP):
        source = at.from_z(step)
        net.landed(f"wq{step}", wqkv.at[source, core], at.to_z(step))
        net.start(f"wqc{step}", wqkv.at[source, core], wqkv.at[source, core], at.to_core)
    p_x, p_y, p_d = at.p_x, at.p_y, at.p_d

    def hand_on(label, ref, device):
        net.start(label, ref, ref, device)

    net.landed("sx0", block_at(p_x, core, early), at.to_x)
    hand_on("rx0", block_at(p_x, core, early), at.to_y)
    net.landed("sy1", block_at(p_y, core, late), at.to_y)
    hand_on("ry1", block_at(p_y, core, late), at.to_x)
    net.landed("sx1", block_at(p_x, core, late), at.to_x)
    hand_on("cx", block_at(p_x, core), at.to_core)
    net.landed("sy0", block_at(p_y, core, early), at.to_y)
    hand_on("cy", block_at(p_y, core), at.to_core)
    for copy in opening:
        copy.wait()
    for step in range(1, GROUP):
        source = at.from_z(step)
        net.landed(f"vec{step}", vec.at[source], at.to_z(step))
        net.landed(f"wqc{step}", wqkv.at[source, other], at.to_core)

    bias = vec[p][0:1, 0:WIDE].astype(f32)
    lane = lax.broadcasted_iota(jnp.int32, (ROWS, 128), 1)
    row = lax.broadcasted_iota(jnp.int32, (ROWS, 128), 0)
    count = length[0]

    def project(chip, side, column):
        block = 2 * chip + side
        rows = xall[chip, side].reshape(ROWS, D)
        keep = block * ROWS + row < count
        mark = jnp.where(keep, 0.0, -1e30)
        at_rows = pl.ds(multiple(block, ROWS), ROWS)
        width = 384 if column is None else WIDE
        full = wqkv[...].reshape(D, WIDE)
        y = dot(rows, full[:, 0:width]) + bias[:, 0:width]
        for h in range(LOCAL):
            g = y[:, 128 * h : 128 * h + 128]
            ka[h, at_rows, :] = jnp.where(
                lane < 64, g, jnp.where(lane == 64, mark, jnp.where(lane < 68, 1.0, 0.0))
            ).astype(bf16)
            va[h, at_rows, :] = jnp.where(
                lane < 64, pltpu.roll(g, 64, 1), jnp.where(lane < 67, 1.0, 0.0)
            ).astype(bf16)
            turned = g.T.astype(bf16)
            kt[h, :, at_rows] = turned[0:64]
            vt[h, 0:64, at_rows] = turned[64:128]
        if column is not None:
            q = (y[:, 384:WIDE] * 0.125).T.astype(bf16)
            for h in range(LOCAL):
                qt[h, 0:64, 384 * column : 384 * column + 384] = q[64 * h : 64 * h + 64]

    project(p, core, 3)
    net.landed("sc", block_at(p, other), at.to_core)
    project(p, other, None)
    project(p_x, core, 1)
    project(p_y, core, 2)
    net.landed("cx", block_at(p_x, other), at.to_core)
    project(p_x, other, None)
    net.landed("cy", block_at(p_y, other), at.to_core)
    project(p_y, other, None)
    net.landed("rx0", block_at(p_d, core, early), at.to_y)
    net.landed("ry1", block_at(p_d, core, late), at.to_x)
    hand_on("cd", block_at(p_d, core), at.to_core)
    project(p_d, core, 0)
    net.landed("cd", block_at(p_d, other), at.to_core)
    project(p_d, other, None)

    kept = [local(block_at(chips[r], core), xs_out.at[r]) for r in range(4)]
    for src, dst in (
        (wqkv, wqkv_out),
        (qt, qt_out),
        (ka, ka_out),
        (va, va_out),
        (kt, kt_out),
    ):
        local(src, dst)

    def part_of(name, step, chip, side):
        _, dst, region = weights[name]
        return region(dst.at[at.from_z(step)], chip, side)

    def hand(label, name, step, chip, device):
        def make():
            ref = part_of(name, step, chip, core)
            return ref, ref, device

        net.launch(label, make)

    def plane_out(name):
        for step in range(1, GROUP):
            net.landed(f"{name}z{step}", part_of(name, step, p, core), at.to_z(step))
            hand(f"{name}x{step}", name, step, p, at.to_x)
            hand(f"{name}y{step}", name, step, p, at.to_y)
            hand(f"{name}c{step}", name, step, p, at.to_core)

    def plane_relay(name):
        for step in range(1, GROUP):
            net.landed(f"{name}x{step}", part_of(name, step, p_x, core), at.to_x)
            net.landed(f"{name}y{step}", part_of(name, step, p_y, core), at.to_y)
            if (step + (name == "outer")) % 2:
                hand(f"{name}r{step}", name, step, p_y, at.to_x)
            else:
                hand(f"{name}r{step}", name, step, p_x, at.to_y)
            hand(f"{name}cx{step}", name, step, p_x, at.to_core)
            hand(f"{name}cy{step}", name, step, p_y, at.to_core)

    def plane_last(name):
        for step in range(1, GROUP):
            far = part_of(name, step, p_d, core)
            via_x = (step + (name == "outer")) % 2
            net.landed(f"{name}r{step}", far, at.to_x if via_x else at.to_y)
            hand(f"{name}cd{step}", name, step, p_d, at.to_core)

    def plane_in(name):
        for step in range(1, GROUP):
            for tag, chip in (("c", p), ("cx", p_x), ("cy", p_y), ("cd", p_d)):
                net.landed(f"{name}{tag}{step}", part_of(name, step, chip, other), at.to_core)

    plane_out("wo")

    def attend(h, tile):
        cols = pl.ds(TILE * tile, TILE)
        queries = qt[h, :, cols]
        for j in range(SLOTS // CHUNK):
            rows = pl.ds(CHUNK * j, CHUNK)
            scores = dot(ka[h, rows, :], queries)
            peak = jnp.max(scores, axis=0, keepdims=True)
            if j == 0:
                newest = peak
            else:
                newest = jnp.maximum(top[0:1, :], peak)
                factor = jnp.exp(top[0:1, :] - newest)
            probs = jnp.exp(scores - newest).astype(bf16)
            update = dot(vt[h, :, rows], probs)
            if j == 0:
                acc[...] = update
            else:
                acc[...] = acc[...] * factor + update
            top[0:1, :] = newest
        total = acc[64:65, :]
        value = acc[0:64, :] / total
        ot[h, :, cols] = value
        lse[h, 0:1, cols] = top[0:1, :] + jnp.log(total)
        low_value = value.astype(bf16)
        at_head = pl.ds(multiple(h, 64), 64)
        mix[2 * tile, at_head, :] = low_value[:, 0:384]
        mix[2 * tile + 1, at_head, :] = low_value[:, 384:768]

    plan = {
        (0, 1): [lambda: plane_relay("wo"), lambda: plane_out("inner")],
        (0, 2): [lambda: plane_last("wo")],
        (1, 1): [lambda: plane_relay("inner")],
        (1, 2): [lambda: plane_out("outer")],
    }

    def take(steps):
        for step in steps:
            step()

    for tile in range(QUERIES // TILE):

        def head(h, carried, tile=tile):
            for (which, when), steps in plan.items():
                if which == tile:
                    pl.when(h == when)(functools.partial(take, steps))
            attend(h, tile)
            return carried

        lax.fori_loop(0, LOCAL, head, 0)
        if tile == 0:
            net.start("md", mix.at[0], mixed.at[p], at.to_d)
            net.start("mx", mix.at[1], mixed.at[p], at.to_x)
        else:
            net.start("my", mix.at[2], mixed.at[p], at.to_y)
            mixed[p] = mix[3]
    local(ot, ot_out)
    local(lse, lse_out)

    plane_last("inner")
    plane_in("wo")
    for copy in owned:
        copy.wait()
    net.landed("md", mixed.at[p_d], at.to_d)
    net.landed("mx", mixed.at[p_x], at.to_x)
    net.landed("my", mixed.at[p_y], at.to_y)
    table = vec[0].astype(f32) + vec[1].astype(f32) + vec[2].astype(f32) + vec[3].astype(f32)
    output_add, gain_one, shift_one, outer_add, gain_two, shift_two = [
        table[2 + i : 3 + i, :] for i in range(6)
    ]
    heads = mixed[...].reshape(D, ROWS)
    work[...] = dot_tn(heads, wo[...].reshape(D, D))
    low[...] = xall[p, core].reshape(ROWS, D)

    def blocks(step, start=0):
        def one(i, carried):
            return step(pl.ds(multiple(i, 128), 128), i, carried)

        return lax.fori_loop(0, ROWS // 128, one, start)

    def mean(value):
        return jnp.mean(value, axis=1, keepdims=True)

    def column(value):
        return jnp.sum(value, axis=0, keepdims=True)

    def norm(hidden):
        centred = hidden - mean(hidden)
        scale = lax.rsqrt(mean(centred * centred) + 1e-05)
        return centred * scale, scale

    def first_norm(rows, i, carried):
        value, scale = norm(low[rows, :].astype(f32) + work[rows, :] + output_add)
        normed[rows, :] = value
        scales[0, rows, :] = jnp.broadcast_to(scale, (128, 128))
        value = value * gain_one + shift_one
        first[rows, :] = value
        low[rows, :] = value.astype(bf16)
        return carried

    blocks(first_norm)

    plane_in("inner")
    inner_weight = iw[...].reshape(D, FF)
    for q in range(4):
        cols = pl.ds(D * q, D)
        slope[:, cols] = dot(low[...], inner_weight[:, D * q : D * q + D])
        add = vec[q][1:2, :].astype(f32)

        def activate(rows, i, carried, cols=cols, add=add):
            u = slope[rows, cols] + add
            gate = 0.5 * (1.0 + lax.erf(u * 0.7071067811865476))
            act[rows, cols] = (u * gate).astype(bf16)
            slope[rows, cols] = gate + u * jnp.exp(-0.5 * u * u) * 0.3989422804014327
            return carried

        blocks(activate)
        if q == 1:
            plane_relay("outer")
    plane_last("outer")
    plane_in("outer")
    total = None
    for q in range(4):
        term = dot(act[:, D * q : D * q + D], ow[q].reshape(D, D))
        total = term if total is None else total + term
    work[...] = total

    nothing = jnp.zeros((1, D), f32)

    def second_norm(rows, i, carried):
        gains, shifts, biases = carried
        value, scale = norm(first[rows, :] + work[rows, :] + outer_add)
        slot = c * ROWS + i * 128 + lax.broadcasted_iota(jnp.int32, (128, D), 0)
        keep = slot < count
        lower[rows, :] = jnp.where(keep, value * gain_two + shift_two, 0.0).astype(bf16)
        upstream = jnp.where(keep, cot[rows, :].astype(f32), 0.0)
        product = upstream * value
        scaled = upstream * gain_two
        grad = scale * (scaled - mean(scaled) - value * mean(scaled * value))
        second[rows, :] = grad
        cot[rows, :] = grad.astype(bf16)
        return gains + column(product), shifts + column(upstream), biases + column(grad)

    gain_two_grad, shift_two_grad, outer_bias_grad = blocks(second_norm, (nothing,) * 3)
    local(lower, low_out)

    for copy in kept:
        copy.wait()
    for name in ("rx0", "ry1", "cx", "cy", "cd"):
        net.finish(name)
    for q in range(4):
        term = dot_tn(act[:, D * q : D * q + D], cot[...]).astype(bf16)
        xall[q] = term.reshape(2, 4, 96, D)

    def outer_part(chip, side, part=slice(None)):
        j = 2 * chip + side
        return xall.at[:, j // 4, j % 4, part]

    for r in range(4):
        net.start(f"go{r}", outer_part(chips[r], other), ro.at[r], at.to_core)

    upper, under = pl.ds(0, 48), pl.ds(48, 48)

    def outer_add_core():
        for r in range(4):
            net.landed(f"go{r}", ro.at[r], at.to_core)

        def one(t, carried):
            for r in range(4):
                j = 2 * chips[r] + core
                xall[t, j // 4, j % 4] = added(xall[t, j // 4, j % 4], ro[r, t])
            return carried

        lax.fori_loop(0, GROUP, one, 0)
        net.start("ox", outer_part(p_x, core, upper), ax.at[0], at.to_x)
        net.start("oy", outer_part(p_y, core, under), ay.at[0], at.to_y)
        net.start("oxd", outer_part(p_d, core, upper), ax.at[1], at.to_x)
        net.start("oyd", outer_part(p_d, core, under), ay.at[1], at.to_y)

    def outer_add_plane():
        net.landed("ox", ax.at[0], at.to_x)
        net.landed("oxd", ax.at[1], at.to_x)
        net.landed("oy", ay.at[0], at.to_y)
        net.landed("oyd", ay.at[1], at.to_y)

        def one(t, carried):
            for chip, part, ref in (
                (p, upper, ax.at[0]),
                (p_y, upper, ax.at[1]),
                (p, under, ay.at[0]),
                (p_x, under, ay.at[1]),
            ):
                j = 2 * chip + core
                xall[t, j // 4, j % 4, part] = added(xall[t, j // 4, j % 4, part], ref[t])
            return carried

        lax.fori_loop(0, GROUP, one, 0)
        local(outer_part(p, core), own_out)
        local(outer_part(p_y, core, upper), half_y_out)
        local(outer_part(p_x, core, under), half_x_out)

    total = None
    for q in range(4):
        cols = pl.ds(D * q, D)
        work[...] = dot_nt(cot[...], ow[q].reshape(D, D))

        def slopes(rows, i, carried, cols=cols):
            grad = work[rows, :] * slope[rows, cols]
            act[rows, cols] = grad.astype(bf16)
            return carried + column(grad)

        small[q, 1:2, :] = blocks(slopes, nothing)
        grads = act[:, D * q : D * q + D]
        term = dot_nt(grads, inner_weight[:, D * q : D * q + D])
        total = term if total is None else total + term
        if q == 2:
            outer_add_core()
    work[...] = total

    def first_back(rows, i, carried):
        gains, shifts, biases = carried
        value = normed[rows, :]
        upstream = second[rows, :] + work[rows, :]
        scaled = upstream * gain_one
        grad = scales[0, rows, 0:1] * (scaled - mean(scaled) - value * mean(scaled * value))
        first[rows, :] = grad
        lower_grad[rows, :] = grad.astype(bf16)
        return gains + column(upstream * value), shifts + column(upstream), biases + column(grad)

    lower_grad = cot
    gain_one_grad, shift_one_grad, output_bias_grad = blocks(first_back, (nothing,) * 3)
    local(first, hg_out)
    mg[...] = dot_nt(wo[...].reshape(D, D), lower_grad[...]).astype(bf16).reshape(GROUP, 192, ROWS)
    for r in range(3):
        net.start(f"mg{r}", mg.at[chips[r]], mg_out.at[r], devices[r])
    local(mg.at[p], mg_out.at[3])
    for q in range(4):
        grads = act[:, D * q : D * q + D]
        gi[:, :, D * q : D * q + D] = dot_tn(low[...], grads).astype(bf16).reshape(GROUP, 192, D)
    local(gi, gi_out)
    gw[...] = dot(heads, lower_grad[...]).astype(bf16).reshape(GROUP, GROUP, 48, D)
    local(gw, gw_out)
    narrow = [
        output_bias_grad,
        gain_one_grad,
        shift_one_grad,
        outer_bias_grad,
        gain_two_grad,
        shift_two_grad,
    ]
    for t in range(GROUP):
        small[t, 0:1, :] = nothing
        for i, value in enumerate(narrow):
            small[t, 2 + i : 3 + i, :] = value
    local(small, small_out)
    outer_add_plane()
    for r in range(3):
        net.landed(f"mg{r}", mg_out.at[r], devices[r])
    waited = len(opening) + len(owned)
    for copy in slots[waited:]:
        if not any(copy is other_copy for other_copy in kept):
            copy.wait()
    net.drain()


FORWARD_COPIES = 128


def forward_call(*operands):
    any_ = pl.BlockSpec(memory_space=pl.ANY)
    shape = jax.ShapeDtypeStruct
    vmem = pltpu.VMEM
    return pl.pallas_call(
        forward_kernel,
        name="forward_attention",
        out_shape=(
            shape((ROWS, D), bf16),
            shape((4, 192, ROWS), bf16),
            shape((GROUP, 192, FF), bf16),
            shape((GROUP, GROUP, 48, D), bf16),
            shape((GROUP, 96, D), bf16),
            shape((GROUP, 48, D), bf16),
            shape((GROUP, 48, D), bf16),
            shape((ROWS, D), f32),
            shape((GROUP, 8, D), f32),
            shape((4, 4, 96, D), bf16),
            shape((GROUP, 2, 96, WIDE), bf16),
            shape((LOCAL, 128, QUERIES), bf16),
            shape((LOCAL, SLOTS, 128), bf16),
            shape((LOCAL, SLOTS, 128), bf16),
            shape((LOCAL, 64, SLOTS), bf16),
            shape((LOCAL, 64, QUERIES), f32),
            shape((LOCAL, 8, QUERIES), f32),
        ),
        in_specs=[pl.BlockSpec(memory_space=pltpu.SMEM)] + [any_] * 7,
        out_specs=[any_] * 17,
        scratch_shapes=[
            vmem((GROUP, 2, 4, 96, D), bf16),
            vmem((GROUP, 2, 96, WIDE), bf16),
            vmem((GROUP, 16, D), bf16),
            vmem((LOCAL, 128, QUERIES), bf16),
            vmem((LOCAL, SLOTS, 128), bf16),
            vmem((LOCAL, SLOTS, 128), bf16),
            vmem((LOCAL, 64, SLOTS), bf16),
            vmem((LOCAL, 80, SLOTS), bf16),
            vmem((LOCAL, 64, QUERIES), f32),
            vmem((LOCAL, 8, QUERIES), f32),
            vmem((4, 192, ROWS), bf16),
            vmem((GROUP, 192, ROWS), bf16),
            vmem((80, TILE), f32),
            vmem((8, TILE), f32),
            vmem((GROUP, 192, FF), bf16),
            vmem((GROUP, CTX, 96, D), bf16),
            vmem((GROUP, GROUP, 48, D), bf16),
            vmem((ROWS, D), bf16),
            vmem((ROWS, D), f32),
            vmem((ROWS, D), f32),
            vmem((ROWS, D), f32),
            vmem((ROWS, D), f32),
            vmem((ROWS, FF), f32),
            vmem((ROWS, FF), bf16),
            vmem((ROWS, D), bf16),
            vmem((ROWS, D), bf16),
            vmem((GROUP, 192, FF), bf16),
            vmem((GROUP, GROUP, 48, D), bf16),
            vmem((GROUP, 192, ROWS), bf16),
            vmem((GROUP, 8, D), f32),
            vmem((1, ROWS, 128), f32),
            vmem((4, GROUP, 96, D), bf16),
            vmem((2, GROUP, 48, D), bf16),
            vmem((2, GROUP, 48, D), bf16),
            pltpu.SemaphoreType.DMA((FORWARD_COPIES,)),
            pltpu.SemaphoreType.DMA((FORWARD_COPIES,)),
            pltpu.SemaphoreType.DMA((48,)),
        ],
        compiler_params=pltpu.CompilerParams(
            collective_id=0, has_side_effects=True, vmem_limit_bytes=67043328
        ),
    )(*operands)


def split_weights(place_p, query_weight, key_weight, value_weight):
    def columns(weight):
        return lax.dynamic_slice_in_dim(weight, place_p * 192, 192, axis=1)

    rows = query_weight.shape[0]
    pair = jnp.concatenate(
        [columns(key_weight).reshape(rows, 3, 64), columns(value_weight).reshape(rows, 3, 64)],
        axis=2,
    ).reshape(rows, 384)
    fill = jnp.zeros((rows, 64), bf16)
    return jnp.concatenate([pair, columns(query_weight), fill], axis=1).reshape(2, 96, WIDE)


def pack_vectors(query_bias, value_bias, inner_bias, vectors):
    nothing = jnp.zeros((3, 64), bf16)
    first = jnp.concatenate(
        [
            jnp.concatenate([nothing, value_bias.reshape(3, 64)], axis=1).reshape(384),
            query_bias,
            jnp.zeros((192,), bf16),
        ]
    )
    rest = jnp.stack(vectors)[:, None, :]
    mine = lax.broadcasted_iota(jnp.int32, (1, GROUP, 1), 1) == lax.axis_index("fsdp")
    rest = jnp.where(mine, rest, 0).astype(bf16).reshape(len(vectors), D)
    return jnp.concatenate([first[None], inner_bias[None], rest, jnp.zeros((8, D), bf16)])


SPAN = 256


def backward_kernel(
    mg_in,
    ot_in,
    lse_in,
    qt_in,
    ka_in,
    va_in,
    kt_in,
    gi_in,
    gw_in,
    own_in,
    half_y_in,
    half_x_in,
    xs_in,
    wqkv_in,
    hg_in,
    small_in,
    dx_out,
    gqkv_out,
    gi_out,
    go_out,
    gw_out,
    small_out,
    mg,
    ot,
    lse,
    qa,
    qz,
    ka,
    va,
    kt,
    da,
    dz,
    kv,
    rkv,
    dq,
    so,
    si,
    ri,
    aix,
    aiy,
    boy,
    box,
    biy,
    bix,
    zo,
    zi,
    xs,
    wqkv,
    dqkv,
    sdx,
    rdx,
    hg,
    dw,
    dwl,
    rdw,
    rzw,
    small,
    rsz,
    rsc,
    rsp,
    ssum,
    sends,
    receives,
    locals_,
):
    at = Place()
    net = Net(sends, receives)
    c, z, core, p = at.c, at.z, at.core, at.p
    other = 1 - core
    chips = [at.p_d, at.p_x, at.p_y, p]
    devices = [at.to_d, at.to_x, at.to_y]
    slots = []

    def local(src, dst):
        copy = pltpu.make_async_copy(src, dst, locals_.at[len(slots)])
        slots.append(copy)
        copy.start()
        return copy

    greet(at)
    net.start("oy", half_y_in, boy, at.to_y)
    net.start("ox", half_x_in, box, at.to_x)
    loads = [
        local(mg_in, mg),
        local(ot_in, ot),
        local(lse_in, lse),
        local(qt_in, qa),
        local(ka_in, ka),
        local(va_in, va),
        local(kt_in, kt),
    ]

    def i_at(chip, side):
        return gi_in.at[:, :, pl.ds(multiple(2 * chip + side, 384), 384)]

    def w_at(chip, side):
        return gw_in.at[:, chip, :, pl.ds(multiple(side, 384), 384)]

    halves = [local(own_in, so)]
    for r in range(4):
        net.start(f"gi{r}", i_at(chips[r], other), ri.at[r, :, 0:192], at.to_core)
        net.start(f"gw{r}", w_at(chips[r], other), ri.at[r, :, 192:240], at.to_core)
        halves.append(local(i_at(chips[r], core), si.at[r, :, 0:192]))
        halves.append(local(w_at(chips[r], core), si.at[r, :, 192:240]))
    later = [local(wqkv_in, wqkv), local(hg_in, hg), local(small_in, small)]
    for r in range(4):
        later.append(local(xs_in.at[r], xs.at[r]))

    for copy in loads:
        copy.wait()
    row16 = lax.broadcasted_iota(jnp.int32, (16, QUERIES), 0)
    row128 = lax.broadcasted_iota(jnp.int32, (128, QUERIES), 0)
    for h in range(LOCAL):
        high, middle, rest = parts_of(-lse[h, 0:1, :])
        qz[h] = jnp.where(row128 < 64, qa[h].astype(f32), 0.0).astype(bf16)
        qa[h, 64:80, :] = jnp.where(
            row16 == 0,
            1.0,
            jnp.where(
                row16 == 1, high, jnp.where(row16 == 2, middle, jnp.where(row16 == 3, rest, 0.0))
            ),
        ).astype(bf16)
        kv[h] = jnp.zeros((SLOTS, 128), f32)
        dz[h, 0:64, :] = jnp.zeros((64, QUERIES), bf16)
        da[h, 80:128, :] = jnp.zeros((48, QUERIES), bf16)
    row16 = lax.broadcasted_iota(jnp.int32, (16, ROWS), 0)
    for r in range(4):
        cols = pl.ds(ROWS * r, ROWS)
        for h in range(LOCAL):
            grad = mg[r, 64 * h : 64 * h + 64, :]
            delta = jnp.sum(grad.astype(f32) * ot[h, :, cols], axis=0, keepdims=True)
            high, middle, rest = parts_of(-delta)
            da[h, 0:64, cols] = grad
            dz[h, 64:128, cols] = grad
            da[h, 64:80, cols] = jnp.where(
                row16 == 0,
                high,
                jnp.where(row16 == 1, middle, jnp.where(row16 == 2, rest, 0.0)),
            ).astype(bf16)

    upper, under = pl.ds(0, 48), pl.ds(48, 48)
    left, right = pl.ds(0, 128), pl.ds(128, 112)

    def along_shards(step):
        def one(t, carried):
            step(t)
            return carried

        lax.fori_loop(0, GROUP, one, 0)

    def outer_second():
        halves[0].wait()
        net.landed("oy", boy, at.to_y)
        net.landed("ox", box, at.to_x)

        def step(t):
            so[t, upper] = added(so[t, upper], boy[t])
            so[t, under] = added(so[t, under], box[t])

        along_shards(step)
        for i in range(1, GROUP):
            net.launch(
                f"oz{i}", lambda i=i: (so.at[at.to_z(i)[1]], zo.at[i - 1], at.to_z(i))
            )

    def outer_last():
        total = so[z].astype(f32)
        for i in range(1, GROUP):
            net.landed(f"oz{i}", zo.at[i - 1], at.to_z(i))
            total = total + zo[i - 1].astype(f32)
        so[z] = total.astype(bf16)

    def inner_core():
        for copy in halves[1:]:
            copy.wait()
        for r in range(4):
            net.landed(f"gi{r}", ri.at[r, :, 0:192], at.to_core)
            net.landed(f"gw{r}", ri.at[r, :, 192:240], at.to_core)

        def step(t):
            for r in range(4):
                si[r, t] = added(si[r, t], ri[r, t])

        along_shards(step)
        net.launch("ixn", lambda: (si.at[1, :, left], aix.at[0], at.to_x))
        net.launch("iyn", lambda: (si.at[2, :, right], aiy.at[0], at.to_y))
        net.launch("ixd", lambda: (si.at[0, :, left], aix.at[1], at.to_x))
        net.launch("iyd", lambda: (si.at[0, :, right], aiy.at[1], at.to_y))

    def inner_first():
        net.landed("ixn", aix.at[0], at.to_x)
        net.landed("iyn", aiy.at[0], at.to_y)
        net.landed("ixd", aix.at[1], at.to_x)
        net.landed("iyd", aiy.at[1], at.to_y)

        def step(t):
            si[2, t, left] = added(si[2, t, left], aix[1, t])
            si[1, t, right] = added(si[1, t, right], aiy[1, t])
            si[3, t, left] = added(si[3, t, left], aix[0, t])
            si[3, t, right] = added(si[3, t, right], aiy[0, t])

        along_shards(step)
        net.launch("iby", lambda: (si.at[2, :, left], biy, at.to_y))
        net.launch("ibx", lambda: (si.at[1, :, right], bix, at.to_x))

    def inner_second():
        net.landed("iby", biy, at.to_y)
        net.landed("ibx", bix, at.to_x)

        def step(t):
            si[3, t, left] = added(si[3, t, left], biy[t])
            si[3, t, right] = added(si[3, t, right], bix[t])

        along_shards(step)
        for i in range(1, GROUP):
            net.launch(
                f"iz{i}", lambda i=i: (si.at[3, at.to_z(i)[1]], zi.at[i - 1], at.to_z(i))
            )

    def inner_last():
        total = si[3, z].astype(f32)
        for i in range(1, GROUP):
            net.landed(f"iz{i}", zi.at[i - 1], at.to_z(i))
            total = total + zi[i - 1].astype(f32)
        si[3, z] = total.astype(bf16)

    def go_at(chip, side):
        return go_out.at[2 * chip + side]

    def gi_at(chip, side):
        return gi_out.at[:, pl.ds(multiple(2 * chip + side, 384), 384)]

    def gw_at(chip, side):
        return gw_out.at[chip, :, pl.ds(multiple(side, 384), 384)]

    place_of = {"o": go_at, "i": gi_at, "w": gw_at}
    via_x = {"o": False, "i": True, "w": False}
    mine = {
        "o": lambda: so.at[z],
        "i": lambda: si.at[3, z, 0:192],
        "w": lambda: si.at[3, z, 192:240],
    }

    def spread(name):
        place = place_of[name]
        for tag, device in (("x", at.to_x), ("y", at.to_y), ("c", at.to_core)):
            net.launch(
                f"f{name}{tag}", lambda device=device: (mine[name](), place(p, core), device)
            )

    def pass_on(name):
        place = place_of[name]

        def hand(tag, chip, device):
            net.launch(
                f"f{name}{tag}", lambda: (place(chip, core), place(chip, core), device)
            )

        net.landed(f"f{name}x", place(at.p_x, core), at.to_x)
        net.landed(f"f{name}y", place(at.p_y, core), at.to_y)
        if via_x[name]:
            hand("r", at.p_y, at.to_x)
        else:
            hand("r", at.p_x, at.to_y)
        hand("cx", at.p_x, at.to_core)
        hand("cy", at.p_y, at.to_core)

    def finish_spread(name):
        place = place_of[name]
        far = place(at.p_d, core)
        net.landed(f"f{name}r", far, at.to_x if via_x[name] else at.to_y)
        net.start(f"f{name}cd", far, far, at.to_core)

    def close_spread(name):
        place = place_of[name]
        for tag, chip in (("c", p), ("cx", at.p_x), ("cy", at.p_y), ("cd", at.p_d)):
            net.landed(f"f{name}{tag}", place(chip, other), at.to_core)

    def swap_kv(h):
        for r in range(4):
            net.launch(
                f"kv{h}{r}",
                lambda r=r: (
                    kv.at[h, pl.ds(multiple(2 * chips[r] + other, ROWS), ROWS)],
                    rkv.at[h, r],
                    at.to_core,
                ),
            )

    def attend(h, tile):
        cols = pl.ds(multiple(tile, TILE), TILE)
        queries = qa[h, :, cols]
        upstream = da[h, :, cols]
        queries_only = qz[h, :, cols]
        upstream_only = dz[h, :, cols]
        for j in range(SLOTS // SPAN):
            rows = pl.ds(SPAN * j, SPAN)
            probs = jnp.exp(dot(ka[h, rows, :], queries))
            grads = (probs * dot(va[h, rows, :], upstream)).astype(bf16)
            kv[h, rows, :] += dot_nt(grads, queries_only) + dot_nt(
                probs.astype(bf16), upstream_only
            )
            update = dot(kt[h, :, rows], grads)
            if j == 0:
                dq[h, :, cols] = update
            else:
                dq[h, :, cols] += update

    plan = {
        1: [outer_second, inner_core],
        2: [lambda: swap_kv(0)],
        4: [lambda: swap_kv(1), inner_first, outer_last, lambda: spread("o")],
        5: [lambda: pass_on("o")],
    }

    def take(steps):
        for step in steps:
            step()

    def unit(u, carried):
        for when, steps in plan.items():
            pl.when(u == when)(functools.partial(take, steps))
        attend(u // 2, u % 2)
        return carried

    lax.fori_loop(0, 2 * LOCAL, unit, 0)
    swap_kv(2)
    inner_second()
    local(so.at[z], go_at(p, core))
    finish_spread("o")

    for copy in later:
        copy.wait()
    weights = wqkv[...].reshape(D, WIDE)
    for h in range(LOCAL):
        for r in range(4):
            net.landed(f"kv{h}{r}", rkv.at[h, r], at.to_core)
    sums = jnp.zeros((1, WIDE), f32)
    for r in range(4):
        cols = pl.ds(ROWS * r, ROWS)
        rows = pl.ds(multiple(2 * chips[r] + core, ROWS), ROWS)
        for h in range(LOCAL):
            dqkv[r, :, 128 * h : 128 * h + 128] = (kv[h, rows, :] + rkv[h, r]).astype(bf16)
        turned = jnp.concatenate(
            [dq[h, :, cols] for h in range(LOCAL)] + [jnp.zeros((64, ROWS), f32)], axis=0
        )
        dqkv[r, :, 384:WIDE] = (turned.T * 0.125).astype(bf16)
        block = dqkv[r]
        sums = sums + jnp.sum(block.astype(f32), axis=0, keepdims=True)
        update = dot_nt(block, weights)
        if r < 3:
            sdx[r] = update.astype(bf16)
            net.start(f"dx{r}", sdx.at[r], rdx.at[r], devices[r])
        else:
            hg[...] += update
    small[p, 0:1, 0:WIDE] += sums
    for step in range(1, GROUP):
        net.start(f"sz{step}", small.at[at.to_z(step)[1]], rsz.at[step - 1], at.to_z(step))

    total = None
    for r in range(4):
        term = lax.dot_general(
            xs[r].reshape(ROWS, D), dqkv[r], (((0,), (0,)), ((), ())), preferred_element_type=f32
        )
        total = term if total is None else total + term
    dw[...] = total.reshape(GROUP, 2, 96, WIDE)
    dwl[...] = dw[:, other].astype(bf16)
    net.start("dwc", dwl, rdw, at.to_core)

    for step in range(1, GROUP):
        net.landed(f"sz{step}", rsz.at[step - 1], at.to_z(step))
    small[z] = small[z] + rsz[0] + rsz[1] + rsz[2]
    net.start("sc", small.at[z], rsc, at.to_core)
    net.landed("dwc", rdw, at.to_core)
    for t in range(GROUP):
        rdw[t] = added(dw[t, core], rdw[t])
    for step in range(1, GROUP):
        net.start(f"dwz{step}", rdw.at[at.to_z(step)[1]], rzw.at[step - 1], at.to_z(step))
    net.landed("sc", rsc, at.to_core)
    rsc[...] = small[z] + rsc[...]
    for r in range(3):
        net.start(f"sp{r}", rsc, rsp.at[r], devices[r])

    inner_last()
    for name in ("i", "w"):
        spread(name)
        local(mine[name](), place_of[name](p, core))

    for step in range(1, GROUP):
        net.landed(f"dwz{step}", rzw.at[step - 1], at.to_z(step))
    finished = rdw[z].astype(f32)
    for step in range(GROUP - 1):
        finished = finished + rzw[step].astype(f32)
    rdw[z] = finished.astype(bf16)
    for r in range(3):
        net.start(f"fq{r}", rdw.at[z], gqkv_out.at[p, core], devices[r])
    net.start("fqc", rdw.at[z], gqkv_out.at[p, core], at.to_core)
    local(rdw.at[z], gqkv_out.at[p, core])

    for r in range(3):
        net.landed(f"sp{r}", rsp.at[r], devices[r])
    ssum[...] = rsc[...] + rsp[0] + rsp[1] + rsp[2]
    local(ssum, small_out)

    for name in ("i", "w"):
        pass_on(name)
    for r in range(3):
        ref = gqkv_out.at[chips[r], core]
        net.landed(f"fq{r}", ref, devices[r])
        net.start(f"fqc{r}", ref, ref, at.to_core)

    result = hg[...]
    for r in range(3):
        net.landed(f"dx{r}", rdx.at[r], devices[r])
        result = result + rdx[r].astype(f32)
    sdx[3] = result.astype(bf16)
    local(sdx.at[3], dx_out)

    for name in ("i", "w"):
        finish_spread(name)
    for name in ("o", "i", "w"):
        close_spread(name)
    net.landed("fqc", gqkv_out.at[p, other], at.to_core)
    for r in range(3):
        net.landed(f"fqc{r}", gqkv_out.at[chips[r], other], at.to_core)
    done = len(loads) + len(halves) + len(later)
    for copy in slots[done:]:
        copy.wait()
    net.drain()


BACKWARD_COPIES = 96


def backward_call(*operands):
    any_ = pl.BlockSpec(memory_space=pl.ANY)
    shape = jax.ShapeDtypeStruct
    vmem = pltpu.VMEM
    return pl.pallas_call(
        backward_kernel,
        name="backward_attention",
        out_shape=(
            shape((ROWS, D), bf16),
            shape((GROUP, 2, 96, WIDE), bf16),
            shape((192, FF), bf16),
            shape((CTX, 96, D), bf16),
            shape((GROUP, 48, D), bf16),
            shape((8, D), f32),
        ),
        in_specs=[any_] * 16,
        out_specs=[any_] * 6,
        scratch_shapes=[
            vmem((4, 192, ROWS), bf16),
            vmem((LOCAL, 64, QUERIES), f32),
            vmem((LOCAL, 8, QUERIES), f32),
            vmem((LOCAL, 128, QUERIES), bf16),
            vmem((LOCAL, 128, QUERIES), bf16),
            vmem((LOCAL, SLOTS, 128), bf16),
            vmem((LOCAL, SLOTS, 128), bf16),
            vmem((LOCAL, 64, SLOTS), bf16),
            vmem((LOCAL, 128, QUERIES), bf16),
            vmem((LOCAL, 128, QUERIES), bf16),
            vmem((LOCAL, SLOTS, 128), f32),
            vmem((LOCAL, 4, ROWS, 128), f32),
            vmem((LOCAL, 64, QUERIES), f32),
            vmem((GROUP, 96, D), bf16),
            vmem((4, GROUP, 240, 384), bf16),
            vmem((4, GROUP, 240, 384), bf16),
            vmem((2, GROUP, 128, 384), bf16),
            vmem((2, GROUP, 112, 384), bf16),
            vmem((GROUP, 48, D), bf16),
            vmem((GROUP, 48, D), bf16),
            vmem((GROUP, 128, 384), bf16),
            vmem((GROUP, 112, 384), bf16),
            vmem((3, 96, D), bf16),
            vmem((3, 240, 384), bf16),
            vmem((4, 4, 96, D), bf16),
            vmem((GROUP, 2, 96, WIDE), bf16),
            vmem((4, ROWS, WIDE), bf16),
            vmem((4, ROWS, D), bf16),
            vmem((3, ROWS, D), bf16),
            vmem((ROWS, D), f32),
            vmem((GROUP, 2, 96, WIDE), f32),
            vmem((GROUP, 96, WIDE), bf16),
            vmem((GROUP, 96, WIDE), bf16),
            vmem((3, 96, WIDE), bf16),
            vmem((GROUP, 8, D), f32),
            vmem((3, 8, D), f32),
            vmem((8, D), f32),
            vmem((3, 8, D), f32),
            vmem((8, D), f32),
            pltpu.SemaphoreType.DMA((BACKWARD_COPIES,)),
            pltpu.SemaphoreType.DMA((BACKWARD_COPIES,)),
            pltpu.SemaphoreType.DMA((48,)),
        ],
        compiler_params=pltpu.CompilerParams(
            collective_id=1, has_side_effects=True, vmem_limit_bytes=63 << 20
        ),
    )(*operands)


def small_plane(
    states,
    lengths,
    query_weight,
    query_bias,
    key_weight,
    value_weight,
    value_bias,
    output_weight,
    output_bias,
    first_gain,
    first_shift,
    inner_weight,
    inner_bias,
    outer_weight,
    outer_bias,
    second_gain,
    second_shift,
    cotangent,
):
    cycle_place = lax.axis_index("ctx")
    shard = lax.axis_index("fsdp")
    length = lengths[shard]
    wqkv = split_weights(cycle_place // 2, query_weight, key_weight, value_weight)
    vectors = pack_vectors(
        query_bias,
        value_bias,
        inner_bias,
        [output_bias, first_gain, first_shift, outer_bias, second_gain, second_shift],
    )
    low, mg, gi, gw, own, half_y, half_x, hg, small, xs, wall, qt, ka, va, kt, ot, lse = (
        forward_call(
            length[None],
            states.reshape(4, 96, D),
            wqkv,
            vectors,
            inner_weight,
            outer_weight.reshape(CTX, 96, D),
            output_weight.reshape(GROUP, 48, D),
            cotangent[0],
        )
    )
    layer_output = low[None]
    dx, gqkv, gi, go, gw, sums = backward_call(
        mg, ot, lse, qt, ka, va, kt, gi, gw, own, half_y, half_x, xs, wall, hg, small
    )
    gqkv = gqkv.reshape(GROUP, 192, WIDE)
    pairs = gqkv[:, :, :384].reshape(GROUP, 192, LOCAL, 2, 64).transpose(3, 1, 0, 2, 4)
    pairs = pairs.reshape(2, 192, D).astype(jnp.float32)
    query_grad = gqkv[:, :, 384:576].transpose(1, 0, 2).reshape(192, D).astype(jnp.float32)
    narrow = lax.dynamic_slice_in_dim(sums[2:8], shard * 192, 192, axis=1)
    value_bias_grad = sums[0, :384].reshape(LOCAL, 2, 64)[:, 1].reshape(192)
    return (
        layer_output,
        dx[None],
        query_grad,
        sums[0, 384:576],
        pairs[0],
        pairs[1],
        value_bias_grad,
        gw.reshape(192, D).astype(jnp.float32),
        narrow[0],
        narrow[1],
        narrow[2],
        gi.astype(jnp.float32),
        sums[1],
        go.reshape(D, D).astype(jnp.float32),
        narrow[3],
        narrow[4],
        narrow[5],
    )


def keep_state(carried):
    return carried


def per_device(
    states,
    lengths,
    query_weight,
    query_bias,
    key_weight,
    value_weight,
    value_bias,
    output_weight,
    output_bias,
    first_gain,
    first_shift,
    inner_weight,
    inner_bias,
    outer_weight,
    outer_bias,
    second_gain,
    second_shift,
    cotangent,
):
    row_count = states.shape[1]
    cycle_size = lax.axis_size("ctx")
    cycle_place = lax.axis_index("ctx")
    sequence = lax.axis_index("fsdp")
    length = lengths[sequence]
    offsets = jnp.arange(row_count, dtype=jnp.int32)
    row_keep = cycle_place * row_count + offsets < length
    inputs = states[0]
    input_float = inputs.astype(jnp.float32)
    attention_set = (
        lax.all_gather(query_weight, "fsdp", axis=0, tiled=True),
        lax.all_gather(key_weight, "fsdp", axis=0, tiled=True),
        lax.all_gather(value_weight, "fsdp", axis=0, tiled=True),
        lax.all_gather(output_weight, "fsdp", axis=0, tiled=True),
        lax.all_gather(query_bias, "fsdp", axis=0, tiled=True),
        lax.all_gather(value_bias, "fsdp", axis=0, tiled=True),
        lax.all_gather(output_bias, "fsdp", axis=0, tiled=True),
        lax.all_gather(first_gain, "fsdp", axis=0, tiled=True),
        lax.all_gather(first_shift, "fsdp", axis=0, tiled=True),
    )
    query_full = attention_set[0]
    key_full = attention_set[1]
    value_full = attention_set[2]
    output_full = attention_set[3]
    query_add = attention_set[4].astype(jnp.float32)
    value_add = attention_set[5].astype(jnp.float32)
    output_add = attention_set[6].astype(jnp.float32)
    gain_one = attention_set[7].astype(jnp.float32)
    shift_one = attention_set[8].astype(jnp.float32)
    queries = (
        (jnp.dot(inputs, query_full, preferred_element_type=jnp.float32) + query_add) * 0.125
    ).astype(jnp.bfloat16)
    key_rows = jnp.dot(inputs, key_full, preferred_element_type=jnp.float32).astype(jnp.bfloat16)
    values = (jnp.dot(inputs, value_full, preferred_element_type=jnp.float32) + value_add).astype(
        jnp.bfloat16
    )
    query_heads = queries.reshape(row_count, H, HD)

    def forward_block(key_block, value_block, key_start, running_state):

        def forward_compute(carried):
            running, exp_total, accum = carried
            key_keep = key_start + offsets < length
            scores = jnp.einsum(
                "qhd,khd->hqk",
                query_heads,
                key_block.reshape(row_count, H, HD),
                preferred_element_type=jnp.float32,
            )
            scores = jnp.where(key_keep[None, None, :], scores, -1e30)
            newest = jnp.maximum(running, jnp.max(scores, axis=2))
            factor = jnp.exp(running - newest)
            weights = jnp.exp(scores - newest[:, :, None])
            exp_total = exp_total * factor + jnp.sum(weights, axis=2)
            update = jnp.einsum(
                "hqk,khd->qhd",
                weights.astype(jnp.bfloat16),
                value_block.reshape(row_count, H, HD),
                preferred_element_type=jnp.float32,
            )
            accum = accum * factor.T[:, :, None] + update
            return (newest, exp_total, accum)

        return lax.cond(key_start < length, forward_compute, keep_state, running_state)

    start_state = (
        jnp.full((H, row_count), -1e30, jnp.float32),
        jnp.zeros((H, row_count), jnp.float32),
        jnp.zeros((row_count, H, HD), jnp.float32),
    )

    def cycle_turn(turn_index, carried):
        key_block, value_block, running_state = carried
        owner_index = (cycle_place - turn_index) % cycle_size
        running_state = forward_block(
            key_block, value_block, owner_index * row_count, running_state
        )
        key_block, value_block = passed_along((key_block, value_block), "ctx", 1)
        return (key_block, value_block, running_state)

    key_block, value_block, running_state = lax.fori_loop(
        0, cycle_size - 1, cycle_turn, (key_rows, values, start_state)
    )
    last_owner = (cycle_place + 1) % cycle_size
    running, exp_total, accum = forward_block(
        key_block, value_block, last_owner * row_count, running_state
    )
    log_total = running + jnp.log(exp_total)
    attention_value = (accum / exp_total.T[:, :, None]).reshape(row_count, D)
    mixed = attention_value.astype(jnp.bfloat16)
    attended = jnp.dot(mixed, output_full, preferred_element_type=jnp.float32) + output_add
    first_normed, first_scale = normalize(input_float + attended)
    first = first_normed * gain_one + shift_one
    first_low = first.astype(jnp.bfloat16)
    feed_set = (
        lax.all_gather(inner_weight, "fsdp", axis=0, tiled=True),
        lax.all_gather(outer_weight, "fsdp", axis=0, tiled=True),
        lax.all_gather(inner_bias, "fsdp", axis=0, tiled=True),
        lax.all_gather(outer_bias, "fsdp", axis=0, tiled=True),
        lax.all_gather(second_gain, "fsdp", axis=0, tiled=True),
        lax.all_gather(second_shift, "fsdp", axis=0, tiled=True),
    )
    inner_full = feed_set[0]
    outer_full = feed_set[1]
    inner_add = feed_set[2].astype(jnp.float32)
    outer_add = feed_set[3].astype(jnp.float32)
    gain_two = feed_set[4].astype(jnp.float32)
    shift_two = feed_set[5].astype(jnp.float32)
    inner = jnp.dot(first_low, inner_full, preferred_element_type=jnp.float32) + inner_add
    activated = jax.nn.gelu(inner, approximate=False).astype(jnp.bfloat16)
    outer = jnp.dot(activated, outer_full, preferred_element_type=jnp.float32) + outer_add
    second_normed, second_scale = normalize(first + outer)
    second = second_normed * gain_two + shift_two
    layer_output = jnp.where(row_keep[:, None], second, 0.0).astype(jnp.bfloat16)[None]
    query_full = attention_set[0]
    key_full = attention_set[1]
    value_full = attention_set[2]
    output_full = attention_set[3]
    gain_one = attention_set[7].astype(jnp.float32)
    inner_full = feed_set[0]
    outer_full = feed_set[1]
    gain_two = feed_set[4].astype(jnp.float32)
    upstream = jnp.where(row_keep[:, None], cotangent[0].astype(jnp.float32), 0.0)
    second_grad, second_gain_grad, second_shift_grad = norm_back(
        upstream, second_normed, second_scale, gain_two
    )
    outer_low = second_grad.astype(jnp.bfloat16)
    outer_bias_grad = jnp.sum(second_grad, axis=0)
    outer_weight_grad = jnp.dot(activated.T, outer_low, preferred_element_type=jnp.float32)
    inner_grad = jnp.dot(outer_low, outer_full.T, preferred_element_type=jnp.float32) * gelu_slope(
        inner
    )
    inner_low = inner_grad.astype(jnp.bfloat16)
    inner_bias_grad = jnp.sum(inner_grad, axis=0)
    inner_weight_grad = jnp.dot(first_low.T, inner_low, preferred_element_type=jnp.float32)
    first_grad = second_grad + jnp.dot(inner_low, inner_full.T, preferred_element_type=jnp.float32)
    hidden_grad, first_gain_grad, first_shift_grad = norm_back(
        first_grad, first_normed, first_scale, gain_one
    )
    attended_low = hidden_grad.astype(jnp.bfloat16)
    output_bias_grad = jnp.sum(hidden_grad, axis=0)
    output_weight_grad = jnp.dot(mixed.T, attended_low, preferred_element_type=jnp.float32)
    mixed_grad = jnp.dot(attended_low, output_full.T, preferred_element_type=jnp.float32).astype(
        jnp.bfloat16
    )
    delta = jnp.sum(
        (mixed_grad.astype(jnp.float32) * attention_value).reshape(row_count, H, HD), axis=2
    ).T

    def back_block(
        query_block,
        upstream_block,
        log_block,
        delta_block,
        key_block,
        value_block,
        key_start,
        grads,
    ):

        def back_compute(carried):
            query_grad, key_grad, value_grad = carried
            key_keep = key_start + offsets < length
            query_three = query_block.reshape(row_count, H, HD)
            upstream_three = upstream_block.reshape(row_count, H, HD)
            key_three = key_block.reshape(row_count, H, HD)
            value_three = value_block.reshape(row_count, H, HD)
            scores = jnp.einsum(
                "qhd,khd->hqk", query_three, key_three, preferred_element_type=jnp.float32
            )
            weights = jnp.where(
                key_keep[None, None, :], jnp.exp(scores - log_block[:, :, None]), 0.0
            )
            weight_grad = jnp.einsum(
                "qhd,khd->hqk", upstream_three, value_three, preferred_element_type=jnp.float32
            )
            score_grad = (weights * (weight_grad - delta_block[:, :, None])).astype(jnp.bfloat16)
            query_grad = query_grad + jnp.einsum(
                "hqk,khd->qhd", score_grad, key_three, preferred_element_type=jnp.float32
            ).reshape(row_count, D)
            key_grad = key_grad + jnp.einsum(
                "hqk,qhd->khd", score_grad, query_three, preferred_element_type=jnp.float32
            ).reshape(row_count, D)
            value_grad = value_grad + jnp.einsum(
                "hqk,qhd->khd",
                weights.astype(jnp.bfloat16),
                upstream_three,
                preferred_element_type=jnp.float32,
            ).reshape(row_count, D)
            return (query_grad, key_grad, value_grad)

        return lax.cond(key_start < length, back_compute, keep_state, grads)

    zero_grad = jnp.zeros((row_count, D), jnp.float32)

    def key_turn(turn_index, carried):
        key_block, value_block, query_grad, key_grad, value_grad = carried
        owner_index = (cycle_place - turn_index) % cycle_size
        query_grad, key_grad, value_grad = back_block(
            queries,
            mixed_grad,
            log_total,
            delta,
            key_block,
            value_block,
            owner_index * row_count,
            (query_grad, key_grad, value_grad),
        )
        key_block, value_block = passed_along((key_block, value_block), "ctx", 1)
        key_grad, value_grad = (
            passed_along(key_grad.astype(jnp.bfloat16), "ctx", 1).astype(key_grad.dtype),
            passed_along(value_grad.astype(jnp.bfloat16), "ctx", 1).astype(value_grad.dtype),
        )
        return (key_block, value_block, query_grad, key_grad, value_grad)

    key_block, value_block, query_grad, key_grad, value_grad = lax.fori_loop(
        0, cycle_size - 1, key_turn, (key_rows, values, zero_grad, zero_grad, zero_grad)
    )
    query_grad, key_grad, value_grad = back_block(
        queries,
        mixed_grad,
        log_total,
        delta,
        key_block,
        value_block,
        last_owner * row_count,
        (query_grad, key_grad, value_grad),
    )
    key_grad, value_grad = (
        passed_along(key_grad.astype(jnp.bfloat16), "ctx", 1).astype(key_grad.dtype),
        passed_along(value_grad.astype(jnp.bfloat16), "ctx", 1).astype(value_grad.dtype),
    )
    query_low = query_grad.astype(jnp.bfloat16) * 0.125
    key_low = key_grad.astype(jnp.bfloat16)
    value_low = value_grad.astype(jnp.bfloat16)
    query_weight_grad = jnp.dot(inputs.T, query_low, preferred_element_type=jnp.float32)
    query_bias_grad = jnp.sum(query_low.astype(jnp.float32), axis=0)
    key_weight_grad = jnp.dot(inputs.T, key_low, preferred_element_type=jnp.float32)
    value_weight_grad = jnp.dot(inputs.T, value_low, preferred_element_type=jnp.float32)
    value_bias_grad = jnp.sum(value_low.astype(jnp.float32), axis=0)
    input_grad = (
        hidden_grad
        + jnp.dot(query_low, query_full.T, preferred_element_type=jnp.float32)
        + jnp.dot(key_low, key_full.T, preferred_element_type=jnp.float32)
        + jnp.dot(value_low, value_full.T, preferred_element_type=jnp.float32)
    ).astype(jnp.bfloat16)[None]
    local_grads = (
        query_weight_grad,
        query_bias_grad,
        key_weight_grad,
        value_weight_grad,
        value_bias_grad,
        output_weight_grad,
        output_bias_grad,
        first_gain_grad,
        first_shift_grad,
        inner_weight_grad,
        inner_bias_grad,
        outer_weight_grad,
        outer_bias_grad,
        second_gain_grad,
        second_shift_grad,
    )
    shards = (
        lax.psum_scatter(
            local_grads[0].astype(jnp.bfloat16), "fsdp", scatter_dimension=0, tiled=True
        ).astype(jnp.float32),
        lax.psum_scatter(
            local_grads[1].astype(jnp.bfloat16), "fsdp", scatter_dimension=0, tiled=True
        ).astype(jnp.float32),
        lax.psum_scatter(
            local_grads[2].astype(jnp.bfloat16), "fsdp", scatter_dimension=0, tiled=True
        ).astype(jnp.float32),
        lax.psum_scatter(
            local_grads[3].astype(jnp.bfloat16), "fsdp", scatter_dimension=0, tiled=True
        ).astype(jnp.float32),
        lax.psum_scatter(
            local_grads[4].astype(jnp.bfloat16), "fsdp", scatter_dimension=0, tiled=True
        ).astype(jnp.float32),
        lax.psum_scatter(
            local_grads[5].astype(jnp.bfloat16), "fsdp", scatter_dimension=0, tiled=True
        ).astype(jnp.float32),
        lax.psum_scatter(
            local_grads[6].astype(jnp.bfloat16), "fsdp", scatter_dimension=0, tiled=True
        ).astype(jnp.float32),
        lax.psum_scatter(
            local_grads[7].astype(jnp.bfloat16), "fsdp", scatter_dimension=0, tiled=True
        ).astype(jnp.float32),
        lax.psum_scatter(
            local_grads[8].astype(jnp.bfloat16), "fsdp", scatter_dimension=0, tiled=True
        ).astype(jnp.float32),
        lax.psum_scatter(
            local_grads[9].astype(jnp.bfloat16), "fsdp", scatter_dimension=0, tiled=True
        ).astype(jnp.float32),
        lax.psum_scatter(
            local_grads[10].astype(jnp.bfloat16), "fsdp", scatter_dimension=0, tiled=True
        ).astype(jnp.float32),
        lax.psum_scatter(
            local_grads[11].astype(jnp.bfloat16), "fsdp", scatter_dimension=0, tiled=True
        ).astype(jnp.float32),
        lax.psum_scatter(
            local_grads[12].astype(jnp.bfloat16), "fsdp", scatter_dimension=0, tiled=True
        ).astype(jnp.float32),
        lax.psum_scatter(
            local_grads[13].astype(jnp.bfloat16), "fsdp", scatter_dimension=0, tiled=True
        ).astype(jnp.float32),
        lax.psum_scatter(
            local_grads[14].astype(jnp.bfloat16), "fsdp", scatter_dimension=0, tiled=True
        ).astype(jnp.float32),
    )
    totals = (
        lax.psum(shards[0].astype(jnp.bfloat16), "ctx").astype(jnp.float32),
        lax.psum(shards[1].astype(jnp.bfloat16), "ctx").astype(jnp.float32),
        lax.psum(shards[2].astype(jnp.bfloat16), "ctx").astype(jnp.float32),
        lax.psum(shards[3].astype(jnp.bfloat16), "ctx").astype(jnp.float32),
        lax.psum(shards[4].astype(jnp.bfloat16), "ctx").astype(jnp.float32),
        lax.psum(shards[5].astype(jnp.bfloat16), "ctx").astype(jnp.float32),
        lax.psum(shards[6].astype(jnp.bfloat16), "ctx").astype(jnp.float32),
        lax.psum(shards[7].astype(jnp.bfloat16), "ctx").astype(jnp.float32),
        lax.psum(shards[8].astype(jnp.bfloat16), "ctx").astype(jnp.float32),
        lax.psum(shards[9].astype(jnp.bfloat16), "ctx").astype(jnp.float32),
        lax.psum(shards[10].astype(jnp.bfloat16), "ctx").astype(jnp.float32),
        lax.psum(shards[11].astype(jnp.bfloat16), "ctx").astype(jnp.float32),
        lax.psum(shards[12].astype(jnp.bfloat16), "ctx").astype(jnp.float32),
        lax.psum(shards[13].astype(jnp.bfloat16), "ctx").astype(jnp.float32),
        lax.psum(shards[14].astype(jnp.bfloat16), "ctx").astype(jnp.float32),
    )
    return (
        layer_output,
        input_grad,
        totals[0],
        totals[1],
        totals[2],
        totals[3],
        totals[4],
        totals[5],
        totals[6],
        totals[7],
        totals[8],
        totals[9],
        totals[10],
        totals[11],
        totals[12],
        totals[13],
        totals[14],
    )


def solution(mesh):
    small = mesh.shape["ctx"] == CTX and mesh.shape["fsdp"] == GROUP
    return jax.shard_map(
        small_plane if small else per_device,
        mesh=mesh,
        in_specs=(
            P("fsdp", "ctx", None),
            P(),
            P("fsdp", None),
            P("fsdp"),
            P("fsdp", None),
            P("fsdp", None),
            P("fsdp"),
            P("fsdp", None),
            P("fsdp"),
            P("fsdp"),
            P("fsdp"),
            P("fsdp", None),
            P("fsdp"),
            P("fsdp", None),
            P("fsdp"),
            P("fsdp"),
            P("fsdp"),
            P("fsdp", "ctx", None),
        ),
        out_specs=(
            P("fsdp", "ctx", None),
            P("fsdp", "ctx", None),
            P("fsdp", None),
            P("fsdp"),
            P("fsdp", None),
            P("fsdp", None),
            P("fsdp"),
            P("fsdp", None),
            P("fsdp"),
            P("fsdp"),
            P("fsdp"),
            P("fsdp", None),
            P("fsdp"),
            P("fsdp", None),
            P("fsdp"),
            P("fsdp"),
            P("fsdp"),
        ),
        check_vma=False,
    )
```

```python
import functools

import jax
import jax.numpy as jnp
from jax import lax
from jax.experimental import pallas as pl
from jax.experimental.pallas import tpu as pltpu
from jax.sharding import PartitionSpec as P

D = 768
H = 12
HD = 64


epsilon = 1e-05


def passed_along(value, axis, steps):
    count = lax.axis_size(axis)
    pairs = [(source, (source + steps) % count) for source in range(count)]
    return lax.ppermute(value, axis, pairs)


def normalize(hidden):
    centred = hidden - jnp.mean(hidden, axis=1, keepdims=True)
    scale = lax.rsqrt(jnp.mean(centred * centred, axis=1, keepdims=True) + epsilon)
    return (centred * scale, scale)


def norm_back(upstream, normed, scale, gain):
    gain_grad = jnp.sum(upstream * normed, axis=0)
    shift_grad = jnp.sum(upstream, axis=0)
    scaled = upstream * gain
    hidden_grad = scale * (
        scaled
        - jnp.mean(scaled, axis=1, keepdims=True)
        - normed * jnp.mean(scaled * normed, axis=1, keepdims=True)
    )
    return (hidden_grad, gain_grad, shift_grad)


def gelu_slope(inner):
    return (
        0.5 * (1.0 + lax.erf(inner * 0.7071067811865476))
        + inner * jnp.exp(-0.5 * inner * inner) * 0.3989422804014327
    )


bf16 = jnp.bfloat16
f32 = jnp.float32
FF = 3072
ROWS = 384
CTX = 8
GROUP = 4
LOCAL = 3
SLOTS = 3072
QUERIES = 1536
TILE = 768
CHUNK = 512
WIDE = 640
MESH = pl.DeviceIdType.MESH


def multiple(value, step):
    return pl.multiple_of(value * step, step)


class Place:
    def __init__(self):
        self.c = lax.axis_index("ctx")
        self.z = lax.axis_index("fsdp")
        c = self.c
        self.core = c % 2
        self.p = c // 2
        self.x = self.p % 2
        self.y = c // 4
        self.p_x = self.p + 1 - 2 * self.x
        self.p_y = self.p + 2 - 4 * self.y
        self.p_d = self.p_y + 1 - 2 * self.x
        self.to_core = (c + 1 - 2 * self.core, self.z)
        self.to_x = (2 * self.p_x + self.core, self.z)
        self.to_y = (2 * self.p_y + self.core, self.z)
        self.to_d = (2 * self.p_d + self.core, self.z)

    def to_z(self, step):
        return (self.c, (self.z + step) % GROUP)

    def from_z(self, step):
        return (self.z + GROUP - step) % GROUP


class Net:
    def __init__(self, sends, receives):
        self.sends = sends
        self.receives = receives
        self.index = {}
        self.open = []

    def of(self, name):
        return self.index.setdefault(name, len(self.index))

    def copy(self, name, src, dst, device):
        i = self.of(name)
        return pltpu.make_async_remote_copy(
            src_ref=src,
            dst_ref=dst,
            send_sem=self.sends.at[i],
            recv_sem=self.receives.at[i],
            device_id=device,
            device_id_type=MESH,
        )

    def start(self, name, src, dst, device):
        self.launch(name, lambda: (src, dst, device))

    def launch(self, name, make, when=None):
        if when is None:
            self.copy(name, *make()).start()
        else:
            pl.when(when())(lambda: self.copy(name, *make()).start())
        self.open.append((name, make, when))

    def sent(self, name, make, when):
        if when is None:
            self.copy(name, *make()).wait_send()
        else:
            pl.when(when())(lambda: self.copy(name, *make()).wait_send())

    def landed(self, name, dst, device):
        self.copy(name, dst, dst, device).wait_recv()

    def finish(self, name):
        for entry in self.open:
            if entry[0] == name:
                self.sent(*entry)
        self.open = [entry for entry in self.open if entry[0] != name]

    def drain(self):
        for entry in self.open:
            self.sent(*entry)
        self.open = []


def greet(place, with_z=True):
    barrier = pltpu.get_barrier_semaphore()
    partners = [place.to_core, place.to_x, place.to_y, place.to_d]
    if with_z:
        partners += [place.to_z(step) for step in range(1, GROUP)]
    for partner in partners:
        pl.semaphore_signal(barrier, inc=1, device_id=partner, device_id_type=MESH)
    pl.semaphore_wait(barrier, len(partners))


def dot(a, b):
    return jnp.dot(a, b, preferred_element_type=f32)


def dot_nt(a, b):
    return lax.dot_general(a, b, (((1,), (1,)), ((), ())), preferred_element_type=f32)


def dot_tn(a, b):
    return lax.dot_general(a, b, (((0,), (0,)), ((), ())), preferred_element_type=f32)


def parts_of(value):
    high = value.astype(bf16).astype(f32)
    rest = value - high
    middle = rest.astype(bf16).astype(f32)
    return high, middle, rest - middle


def added(a, b):
    return (a.astype(f32) + b.astype(f32)).astype(bf16)


def forward_kernel(
    length,
    x_in,
    wqkv_in,
    vec_in,
    inner_in,
    outer_in,
    wo_in,
    cot_in,
    low_out,
    mg_out,
    gi_out,
    gw_out,
    own_out,
    hg_out,
    small_out,
    xs_out,
    wqkv_out,
    qt_out,
    ka_out,
    va_out,
    kt_out,
    ot_out,
    lse_out,
    xall,
    wqkv,
    vec,
    qt,
    ka,
    va,
    kt,
    vt,
    ot,
    lse,
    mix,
    mixed,
    acc,
    top,
    iw,
    ow,
    wo,
    cot,
    work,
    first,
    normed,
    second,
    slope,
    act,
    low,
    lower,
    gi,
    gw,
    mg,
    small,
    scales,
    ro,
    sends,
    receives,
    locals_,
):
    at = Place()
    net = Net(sends, receives)
    c, z, core, p = at.c, at.z, at.core, at.p
    other = 1 - core
    chips = [at.p_d, at.p_x, at.p_y, p]
    devices = [at.to_d, at.to_x, at.to_y]
    slots = []

    def local(src, dst):
        copy = pltpu.make_async_copy(src, dst, locals_.at[len(slots)])
        slots.append(copy)
        copy.start()
        return copy

    def inner_at(ref, chip, side):
        return ref.at[:, pl.ds(multiple(2 * chip + side, 384), 384)]

    def outer_at(ref, chip, side):
        return ref.at[0, 2 * chip + side]

    def wo_at(ref, chip, side):
        return ref.at[chip, :, pl.ds(multiple(side, 384), 384)]

    weights = {
        "wo": (wo_in, wo, wo_at),
        "inner": (inner_in, iw, inner_at),
        "outer": (outer_in, ow, outer_at),
    }

    def block_at(chip, side, part=slice(None)):
        return xall.at[chip, side, part]

    greet(at)

    early, late = pl.ds(0, 2), pl.ds(2, 2)
    net.start("sx0", x_in.at[early], block_at(p, core, early), at.to_x)
    net.start("sy1", x_in.at[late], block_at(p, core, late), at.to_y)
    net.start("sx1", x_in.at[late], block_at(p, core, late), at.to_x)
    net.start("sy0", x_in.at[early], block_at(p, core, early), at.to_y)
    net.start("sc", x_in, block_at(p, core), at.to_core)
    for step in range(1, GROUP):
        net.start(f"vec{step}", vec_in, vec.at[z], at.to_z(step))
    class Along:
        def __init__(self, name, source, region):
            self.name = name
            self.source = source
            self.region = region

        def send(self):
            name, source, region = self.name, self.source, self.region
            for step in range(1, GROUP):
                when = {1: lambda: z < 3, 2: None, 3: lambda: z > 0}[step]

                def make(step=step):
                    return source, region(z), at.to_z(step)

                net.launch(f"{name}z{step}", make, when)

        def relay(self):
            name, region = self.name, self.region

            def up():
                net.copy(f"{name}z2", region(z - 2), region(z - 2), at.to_z(2)).wait_recv()

            def down():
                net.copy(f"{name}z2", region(z + 2), region(z + 2), at.to_z(2)).wait_recv()

            pl.when(z == 2)(up)
            pl.when(z == 1)(down)
            net.launch(
                f"{name}u", lambda: (region(0), region(0), at.to_z(1)), lambda: z == 2
            )
            net.launch(
                f"{name}d", lambda: (region(3), region(3), at.to_z(3)), lambda: z == 1
            )

        def landed(self, step):
            name, region = self.name, self.region
            ref = region(at.from_z(step))
            if step == 1:
                pl.when(z > 0)(lambda: net.landed(f"{name}z1", region(at.from_z(1)), at.to_z(1)))
                pl.when(z == 0)(lambda: net.landed(f"{name}d", region(3), at.to_z(1)))
            elif step == 3:
                pl.when(z < 3)(lambda: net.landed(f"{name}z3", region(at.from_z(3)), at.to_z(3)))
                pl.when(z == 3)(lambda: net.landed(f"{name}u", region(0), at.to_z(3)))
            else:
                pl.when((z == 0) | (z == 3))(
                    lambda: net.landed(f"{name}z2", region(at.from_z(2)), at.to_z(2))
                )
            return ref

    along = {"wq": Along("wq", wqkv_in.at[core], lambda shard: wqkv.at[shard, core])}
    for name, (src, dst, region) in weights.items():
        along[name] = Along(
            name,
            region(src, p, core),
            lambda shard, dst=dst, region=region: region(dst.at[shard], p, core),
        )

    def far_at(shard, side):
        return ow.at[shard, 1, pl.ds(4 * side, 4)]

    along["far"] = Along(
        "far", outer_in.at[1, pl.ds(4 * core, 4)], lambda shard: far_at(shard, core)
    )
    along["wq"].send()
    opening = [local(x_in, block_at(p, core)), local(vec_in, vec.at[z]), local(wqkv_in, wqkv.at[z])]
    owned = [
        local(wo_in, wo.at[z]),
        local(inner_in, iw.at[z]),
        local(outer_in, ow.at[z]),
        local(cot_in, cot),
    ]

    row64 = lax.broadcasted_iota(jnp.int32, (64, QUERIES), 0)
    row16 = lax.broadcasted_iota(jnp.int32, (16, SLOTS), 0)
    for h in range(LOCAL):
        qt[h, 64:128, :] = jnp.where(row64 == 0, 1.0, 0.0).astype(bf16)
        vt[h, 64:80, :] = jnp.where(row16 == 0, 1.0, 0.0).astype(bf16)

    along["wq"].relay()
    along["wo"].send()
    along["inner"].send()
    p_x, p_y, p_d = at.p_x, at.p_y, at.p_d

    def hand_on(label, ref, device):
        net.start(label, ref, ref, device)

    net.landed("sx0", block_at(p_x, core, early), at.to_x)
    hand_on("rx0", block_at(p_x, core, early), at.to_y)
    net.landed("sy1", block_at(p_y, core, late), at.to_y)
    hand_on("ry1", block_at(p_y, core, late), at.to_x)
    for step in range(1, GROUP):
        source = at.from_z(step)
        along["wq"].landed(step)
        net.start(f"wqc{step}", wqkv.at[source, core], wqkv.at[source, core], at.to_core)
    along["wo"].relay()
    net.landed("sx1", block_at(p_x, core, late), at.to_x)
    hand_on("cx", block_at(p_x, core), at.to_core)
    net.landed("sy0", block_at(p_y, core, early), at.to_y)
    hand_on("cy", block_at(p_y, core), at.to_core)
    for copy in opening:
        copy.wait()
    for step in range(1, GROUP):
        source = at.from_z(step)
        net.landed(f"vec{step}", vec.at[source], at.to_z(step))
        net.landed(f"wqc{step}", wqkv.at[source, other], at.to_core)

    bias = vec[p][0:1, 0:WIDE].astype(f32)
    lane = lax.broadcasted_iota(jnp.int32, (ROWS, 128), 1)
    row = lax.broadcasted_iota(jnp.int32, (ROWS, 128), 0)
    count = length[0]

    def project(chip, side, column):
        block = 2 * chip + side
        rows = xall[chip, side].reshape(ROWS, D)
        keep = block * ROWS + row < count
        mark = jnp.where(keep, 0.0, -1e30)
        at_rows = pl.ds(multiple(block, ROWS), ROWS)
        width = 384 if column is None else WIDE
        full = wqkv[...].reshape(D, WIDE)
        y = dot(rows, full[:, 0:width]) + bias[:, 0:width]
        for h in range(LOCAL):
            g = y[:, 128 * h : 128 * h + 128]
            ka[h, at_rows, :] = jnp.where(
                lane < 64, g, jnp.where(lane == 64, mark, jnp.where(lane < 68, 1.0, 0.0))
            ).astype(bf16)
            va[h, at_rows, :] = jnp.where(
                lane < 64, pltpu.roll(g, 64, 1), jnp.where(lane < 67, 1.0, 0.0)
            ).astype(bf16)
            turned = g.T.astype(bf16)
            kt[h, :, at_rows] = turned[0:64]
            vt[h, 0:64, at_rows] = turned[64:128]
        if column is not None:
            q = (y[:, 384:WIDE] * 0.125).T.astype(bf16)
            for h in range(LOCAL):
                qt[h, 0:64, 384 * column : 384 * column + 384] = q[64 * h : 64 * h + 64]

    project(p, core, 3)
    net.landed("sc", block_at(p, other), at.to_core)
    project(p, other, None)
    along["outer"].send()
    project(p_x, core, 1)
    project(p_y, core, 2)
    net.landed("cx", block_at(p_x, other), at.to_core)
    project(p_x, other, None)
    net.landed("cy", block_at(p_y, other), at.to_core)
    project(p_y, other, None)
    net.landed("rx0", block_at(p_d, core, early), at.to_y)
    net.landed("ry1", block_at(p_d, core, late), at.to_x)
    hand_on("cd", block_at(p_d, core), at.to_core)
    project(p_d, core, 0)
    net.landed("cd", block_at(p_d, other), at.to_core)
    project(p_d, other, None)

    kept = [local(block_at(chips[r], core), xs_out.at[r]) for r in range(4)]
    for src, dst in (
        (wqkv, wqkv_out),
        (qt, qt_out),
        (ka, ka_out),
        (va, va_out),
        (kt, kt_out),
    ):
        local(src, dst)

    def part_of(name, step, chip, side):
        _, dst, region = weights[name]
        return region(dst.at[at.from_z(step)], chip, side)

    def hand(label, name, step, chip, device):
        def make():
            ref = part_of(name, step, chip, core)
            return ref, ref, device

        net.launch(label, make)

    steps_all = tuple(range(1, GROUP))

    def plane_out(name, steps=steps_all):
        for step in steps:
            along[name].landed(step)
            hand(f"{name}x{step}", name, step, p, at.to_x)
            hand(f"{name}y{step}", name, step, p, at.to_y)
            hand(f"{name}c{step}", name, step, p, at.to_core)

    def relay_by_x(name, step):
        return (step + (name == "outer")) % 2 == 1

    def plane_relay(name, steps=steps_all):
        for step in steps:
            net.landed(f"{name}x{step}", part_of(name, step, p_x, core), at.to_x)
            net.landed(f"{name}y{step}", part_of(name, step, p_y, core), at.to_y)
            if relay_by_x(name, step):
                hand(f"{name}r{step}", name, step, p_y, at.to_x)
            else:
                hand(f"{name}r{step}", name, step, p_x, at.to_y)
            hand(f"{name}cx{step}", name, step, p_x, at.to_core)
            hand(f"{name}cy{step}", name, step, p_y, at.to_core)

    def plane_last(name, steps=steps_all):
        for step in steps:
            far = part_of(name, step, p_d, core)
            net.landed(f"{name}r{step}", far, at.to_x if relay_by_x(name, step) else at.to_y)
            hand(f"{name}cd{step}", name, step, p_d, at.to_core)

    def plane_in(name):
        for step in steps_all:
            for tag, chip in (("c", p), ("cx", p_x), ("cy", p_y), ("cd", p_d)):
                net.landed(f"{name}{tag}{step}", part_of(name, step, chip, other), at.to_core)

    plane_out("wo")
    along["inner"].relay()

    def attend(h, tile):
        cols = pl.ds(multiple(tile, TILE), TILE)
        queries = qt[h, :, cols]
        for j in range(SLOTS // CHUNK):
            rows = pl.ds(CHUNK * j, CHUNK)
            scores = dot(ka[h, rows, :], queries)
            peak = jnp.max(scores, axis=0, keepdims=True)
            if j == 0:
                newest = peak
            else:
                newest = jnp.maximum(top[0:1, :], peak)
                factor = jnp.exp(top[0:1, :] - newest)
            probs = jnp.exp(scores - newest).astype(bf16)
            update = dot(vt[h, :, rows], probs)
            if j == 0:
                acc[...] = update
            else:
                acc[...] = acc[...] * factor + update
            top[0:1, :] = newest
        total = acc[64:65, :]
        value = acc[0:64, :] / total
        ot[h, :, cols] = value
        lse[h, 0:1, cols] = top[0:1, :] + jnp.log(total)
        low_value = value.astype(bf16)
        at_head = pl.ds(multiple(h, 64), 64)
        mix[2 * tile, at_head, :] = low_value[:, 0:384]
        mix[2 * tile + 1, at_head, :] = low_value[:, 384:768]

    def send_mixed(name, index, device):
        net.launch(name, lambda: (mix.at[index], mixed.at[p], device))

    plan = {
        1: [
            lambda: plane_out("inner"),
            lambda: plane_relay("wo"),
            along["outer"].relay,
            along["far"].send,
        ],
        2: [lambda: plane_last("wo"), lambda: plane_relay("inner", (1,))],
        3: [
            lambda: send_mixed("md", 0, at.to_d),
            lambda: send_mixed("mx", 1, at.to_x),
            lambda: plane_relay("inner", (2,)),
        ],
        4: [lambda: plane_relay("inner", (3,)), lambda: plane_out("outer")],
        5: [
            along["far"].relay,
            lambda: plane_last("inner"),
        ],
    }

    def take(steps):
        for step in steps:
            step()

    def unit(u, carried):
        for when, steps in plan.items():
            pl.when(u == when)(functools.partial(take, steps))
        attend(u % LOCAL, u // LOCAL)
        return carried

    lax.fori_loop(0, 2 * LOCAL, unit, 0)
    send_mixed("my", 2, at.to_y)
    mixed[p] = mix[3]
    local(ot, ot_out)
    local(lse, lse_out)

    plane_in("wo")
    for copy in owned:
        copy.wait()
    net.landed("md", mixed.at[p_d], at.to_d)
    net.landed("mx", mixed.at[p_x], at.to_x)
    net.landed("my", mixed.at[p_y], at.to_y)
    table = vec[0].astype(f32) + vec[1].astype(f32) + vec[2].astype(f32) + vec[3].astype(f32)
    output_add, gain_one, shift_one, outer_add, gain_two, shift_two = [
        table[2 + i : 3 + i, :] for i in range(6)
    ]
    heads = mixed[...].reshape(D, ROWS)
    work[...] = dot_tn(heads, wo[...].reshape(D, D))
    low[...] = xall[p, core].reshape(ROWS, D)
    plane_relay("outer")

    def blocks(step, start=0):
        def one(i, carried):
            return step(pl.ds(multiple(i, 128), 128), i, carried)

        return lax.fori_loop(0, ROWS // 128, one, start)

    def mean(value):
        return jnp.mean(value, axis=1, keepdims=True)

    def column(value):
        return jnp.sum(value, axis=0, keepdims=True)

    def norm(hidden):
        centred = hidden - mean(hidden)
        scale = lax.rsqrt(mean(centred * centred) + 1e-05)
        return centred * scale, scale

    def first_norm(rows, i, carried):
        value, scale = norm(low[rows, :].astype(f32) + work[rows, :] + output_add)
        normed[rows, :] = value
        scales[0, rows, :] = jnp.broadcast_to(scale, (128, 128))
        value = value * gain_one + shift_one
        first[rows, :] = value
        low[rows, :] = value.astype(bf16)
        return carried

    blocks(first_norm)
    for step in steps_all:
        along["far"].landed(step)
        source = at.from_z(step)
        net.start(f"farc{step}", far_at(source, core), far_at(source, core), at.to_core)

    plane_in("inner")
    inner_weight = iw[...].reshape(D, FF)
    for q in range(4):
        cols = pl.ds(D * q, D)
        slope[:, cols] = dot(low[...], inner_weight[:, D * q : D * q + D])
        add = vec[q][1:2, :].astype(f32)

        def activate(rows, i, carried, cols=cols, add=add):
            u = slope[rows, cols] + add
            gate = 0.5 * (1.0 + lax.erf(u * 0.7071067811865476))
            act[rows, cols] = (u * gate).astype(bf16)
            slope[rows, cols] = gate + u * jnp.exp(-0.5 * u * u) * 0.3989422804014327
            return carried

        blocks(activate)
        if q == 1:
            plane_last("outer")
    plane_in("outer")
    for step in steps_all:
        net.landed(f"farc{step}", far_at(at.from_z(step), other), at.to_core)
    total = None
    for q in range(4):
        term = dot(act[:, D * q : D * q + D], ow[q].reshape(D, D))
        total = term if total is None else total + term
    work[...] = total

    nothing = jnp.zeros((1, D), f32)

    def second_norm(rows, i, carried):
        gains, shifts, biases = carried
        value, scale = norm(first[rows, :] + work[rows, :] + outer_add)
        slot = c * ROWS + i * 128 + lax.broadcasted_iota(jnp.int32, (128, D), 0)
        keep = slot < count
        lower[rows, :] = jnp.where(keep, value * gain_two + shift_two, 0.0).astype(bf16)
        upstream = jnp.where(keep, cot[rows, :].astype(f32), 0.0)
        product = upstream * value
        scaled = upstream * gain_two
        grad = scale * (scaled - mean(scaled) - value * mean(scaled * value))
        second[rows, :] = grad
        cot[rows, :] = grad.astype(bf16)
        return gains + column(product), shifts + column(upstream), biases + column(grad)

    gain_two_grad, shift_two_grad, outer_bias_grad = blocks(second_norm, (nothing,) * 3)
    local(lower, low_out)

    for copy in kept:
        copy.wait()
    for name in ("rx0", "ry1", "cx", "cy", "cd"):
        net.finish(name)
    def outer_row(t, chip, side):
        j = 2 * chip + side
        return xall.at[t, j // 4, j % 4]

    for q in range(4):
        term = dot_tn(act[:, D * q : D * q + D], cot[...]).astype(bf16)
        xall[q] = term.reshape(2, 4, 96, D)
        for r in range(4):
            net.start(f"go{q}{r}", outer_row(q, chips[r], other), ro.at[r, q], at.to_core)

    def outer_add_core():
        for q in range(4):
            for r in range(4):
                net.landed(f"go{q}{r}", ro.at[r, q], at.to_core)

        def one(t, carried):
            for r in range(4):
                ref = outer_row(t, chips[r], core)
                ref[...] = added(ref[...], ro[r, t])
            return carried

        lax.fori_loop(0, GROUP, one, 0)
    total = None
    for q in range(4):
        cols = pl.ds(D * q, D)
        work[...] = dot_nt(cot[...], ow[q].reshape(D, D))

        def slopes(rows, i, carried, cols=cols):
            grad = work[rows, :] * slope[rows, cols]
            act[rows, cols] = grad.astype(bf16)
            return carried + column(grad)

        small[q, 1:2, :] = blocks(slopes, nothing)
        grads = act[:, D * q : D * q + D]
        term = dot_nt(grads, inner_weight[:, D * q : D * q + D])
        total = term if total is None else total + term
        if q == 2:
            outer_add_core()
    work[...] = total

    def first_back(rows, i, carried):
        gains, shifts, biases = carried
        value = normed[rows, :]
        upstream = second[rows, :] + work[rows, :]
        scaled = upstream * gain_one
        grad = scales[0, rows, 0:1] * (scaled - mean(scaled) - value * mean(scaled * value))
        first[rows, :] = grad
        lower_grad[rows, :] = grad.astype(bf16)
        return gains + column(upstream * value), shifts + column(upstream), biases + column(grad)

    lower_grad = cot
    gain_one_grad, shift_one_grad, output_bias_grad = blocks(first_back, (nothing,) * 3)
    local(first, hg_out)
    mg[...] = dot_nt(wo[...].reshape(D, D), lower_grad[...]).astype(bf16).reshape(GROUP, 192, ROWS)
    for r in range(3):
        net.start(f"mg{r}", mg.at[chips[r]], mg_out.at[r], devices[r])
    local(mg.at[p], mg_out.at[3])
    for q in range(4):
        grads = act[:, D * q : D * q + D]
        gi[:, :, D * q : D * q + D] = dot_tn(low[...], grads).astype(bf16).reshape(GROUP, 192, D)
    local(gi, gi_out)
    gw[...] = dot(heads, lower_grad[...]).astype(bf16).reshape(GROUP, GROUP, 48, D)
    local(gw, gw_out)
    narrow = [
        output_bias_grad,
        gain_one_grad,
        shift_one_grad,
        outer_bias_grad,
        gain_two_grad,
        shift_two_grad,
    ]
    for t in range(GROUP):
        small[t, 0:1, :] = nothing
        for i, value in enumerate(narrow):
            small[t, 2 + i : 3 + i, :] = value
    local(small, small_out)
    for r in range(4):
        j = 2 * chips[r] + core
        local(xall.at[:, j // 4, j % 4], own_out.at[r])
    for r in range(3):
        net.landed(f"mg{r}", mg_out.at[r], devices[r])
    waited = len(opening) + len(owned)
    for copy in slots[waited:]:
        if not any(copy is other_copy for other_copy in kept):
            copy.wait()
    net.drain()


FORWARD_COPIES = 140


def forward_call(*operands):
    any_ = pl.BlockSpec(memory_space=pl.ANY)
    shape = jax.ShapeDtypeStruct
    vmem = pltpu.VMEM
    return pl.pallas_call(
        forward_kernel,
        name="forward_attention",
        out_shape=(
            shape((ROWS, D), bf16),
            shape((4, 192, ROWS), bf16),
            shape((GROUP, 192, FF), bf16),
            shape((GROUP, GROUP, 48, D), bf16),
            shape((4, GROUP, 96, D), bf16),
            shape((ROWS, D), f32),
            shape((GROUP, 8, D), f32),
            shape((4, 4, 96, D), bf16),
            shape((GROUP, 2, 96, WIDE), bf16),
            shape((LOCAL, 128, QUERIES), bf16),
            shape((LOCAL, SLOTS, 128), bf16),
            shape((LOCAL, SLOTS, 128), bf16),
            shape((LOCAL, 64, SLOTS), bf16),
            shape((LOCAL, 64, QUERIES), f32),
            shape((LOCAL, 8, QUERIES), f32),
        ),
        in_specs=[pl.BlockSpec(memory_space=pltpu.SMEM)] + [any_] * 7,
        out_specs=[any_] * 15,
        scratch_shapes=[
            vmem((GROUP, 2, 4, 96, D), bf16),
            vmem((GROUP, 2, 96, WIDE), bf16),
            vmem((GROUP, 16, D), bf16),
            vmem((LOCAL, 128, QUERIES), bf16),
            vmem((LOCAL, SLOTS, 128), bf16),
            vmem((LOCAL, SLOTS, 128), bf16),
            vmem((LOCAL, 64, SLOTS), bf16),
            vmem((LOCAL, 80, SLOTS), bf16),
            vmem((LOCAL, 64, QUERIES), f32),
            vmem((LOCAL, 8, QUERIES), f32),
            vmem((4, 192, ROWS), bf16),
            vmem((GROUP, 192, ROWS), bf16),
            vmem((80, TILE), f32),
            vmem((8, TILE), f32),
            vmem((GROUP, 192, FF), bf16),
            vmem((GROUP, 2, CTX, 48, D), bf16),
            vmem((GROUP, GROUP, 48, D), bf16),
            vmem((ROWS, D), bf16),
            vmem((ROWS, D), f32),
            vmem((ROWS, D), f32),
            vmem((ROWS, D), f32),
            vmem((ROWS, D), f32),
            vmem((ROWS, FF), f32),
            vmem((ROWS, FF), bf16),
            vmem((ROWS, D), bf16),
            vmem((ROWS, D), bf16),
            vmem((GROUP, 192, FF), bf16),
            vmem((GROUP, GROUP, 48, D), bf16),
            vmem((GROUP, 192, ROWS), bf16),
            vmem((GROUP, 8, D), f32),
            vmem((1, ROWS, 128), f32),
            vmem((4, GROUP, 96, D), bf16),
            pltpu.SemaphoreType.DMA((FORWARD_COPIES,)),
            pltpu.SemaphoreType.DMA((FORWARD_COPIES,)),
            pltpu.SemaphoreType.DMA((48,)),
        ],
        compiler_params=pltpu.CompilerParams(
            collective_id=0, has_side_effects=True, vmem_limit_bytes=67043328
        ),
    )(*operands)


def split_weights(place_p, query_weight, key_weight, value_weight):
    def columns(weight):
        return lax.dynamic_slice_in_dim(weight, place_p * 192, 192, axis=1)

    rows = query_weight.shape[0]
    pair = jnp.concatenate(
        [columns(key_weight).reshape(rows, 3, 64), columns(value_weight).reshape(rows, 3, 64)],
        axis=2,
    ).reshape(rows, 384)
    fill = jnp.zeros((rows, 64), bf16)
    return jnp.concatenate([pair, columns(query_weight), fill], axis=1).reshape(2, 96, WIDE)


def pack_vectors(query_bias, value_bias, inner_bias, vectors):
    nothing = jnp.zeros((3, 64), bf16)
    first = jnp.concatenate(
        [
            jnp.concatenate([nothing, value_bias.reshape(3, 64)], axis=1).reshape(384),
            query_bias,
            jnp.zeros((192,), bf16),
        ]
    )
    rest = jnp.stack(vectors)[:, None, :]
    mine = lax.broadcasted_iota(jnp.int32, (1, GROUP, 1), 1) == lax.axis_index("fsdp")
    rest = jnp.where(mine, rest, 0).astype(bf16).reshape(len(vectors), D)
    return jnp.concatenate([first[None], inner_bias[None], rest, jnp.zeros((8, D), bf16)])


SPAN = 256


def backward_kernel(
    mg_in,
    ot_in,
    lse_in,
    qt_in,
    ka_in,
    va_in,
    kt_in,
    gi_in,
    gw_in,
    own_in,
    xs_in,
    wqkv_in,
    hg_in,
    small_in,
    dx_out,
    gqkv_out,
    gi_out,
    go_out,
    gw_out,
    small_out,
    mg,
    ot,
    lse,
    qa,
    qz,
    ka,
    va,
    kt,
    da,
    dz,
    kv,
    rkv,
    dq,
    so,
    si,
    ri,
    aix,
    aiy,
    boy,
    box,
    ax,
    ay,
    az,
    su,
    ux,
    uy,
    vx,
    vy,
    done_o,
    biy,
    bix,
    zo,
    zi,
    xs,
    wqkv,
    dqkv,
    sdx,
    rx,
    ry,
    bx,
    by,
    hg,
    dw,
    dwl,
    rdw,
    rzw,
    small,
    rsz,
    rsc,
    rsp,
    ssum,
    sends,
    receives,
    locals_,
):
    at = Place()
    net = Net(sends, receives)
    c, z, core, p = at.c, at.z, at.core, at.p
    other = 1 - core
    chips = [at.p_d, at.p_x, at.p_y, p]
    devices = [at.to_d, at.to_x, at.to_y]
    slots = []

    def local(src, dst):
        copy = pltpu.make_async_copy(src, dst, locals_.at[len(slots)])
        slots.append(copy)
        copy.start()
        return copy

    greet(at)
    upper, under = pl.ds(0, 48), pl.ds(48, 48)
    fore, aft = pl.ds(0, 2), pl.ds(2, 2)
    front, back = pl.ds(0, 384), pl.ds(384, 384)
    net.start("oxn", own_in.at[1, fore, under], ax.at[0], at.to_x)
    net.start("oyn", own_in.at[2, aft, under], ay.at[0], at.to_y)
    net.start("oxd", own_in.at[0, fore, under], ax.at[1], at.to_x)
    net.start("oyd", own_in.at[0, aft, under], ay.at[1], at.to_y)
    for r in range(4):
        for step in range(1, GROUP):
            device = at.to_z(step)
            net.start(f"uz{r}{step}", own_in.at[r, device[1], upper], az.at[r, step - 1], device)
    loads = [
        local(mg_in, mg),
        local(ot_in, ot),
        local(lse_in, lse),
        local(qt_in, qa),
        local(ka_in, ka),
        local(va_in, va),
        local(kt_in, kt),
    ]

    def i_at(chip, side):
        return gi_in.at[:, :, pl.ds(multiple(2 * chip + side, 384), 384)]

    def w_at(chip, side):
        return gw_in.at[:, chip, :, pl.ds(multiple(side, 384), 384)]

    halves = [local(own_in, so)]
    for r in range(4):
        net.start(f"gi{r}", i_at(chips[r], other), ri.at[r, :, 0:192], at.to_core)
        net.start(f"gw{r}", w_at(chips[r], other), ri.at[r, :, 192:240], at.to_core)
        halves.append(local(i_at(chips[r], core), si.at[r, :, 0:192]))
        halves.append(local(w_at(chips[r], core), si.at[r, :, 192:240]))
    later = [local(wqkv_in, wqkv), local(hg_in, hg), local(small_in, small)]
    for r in range(4):
        later.append(local(xs_in.at[r], xs.at[r]))

    for copy in loads:
        copy.wait()
    row16 = lax.broadcasted_iota(jnp.int32, (16, QUERIES), 0)
    row128 = lax.broadcasted_iota(jnp.int32, (128, QUERIES), 0)
    for h in range(LOCAL):
        high, middle, rest = parts_of(-lse[h, 0:1, :])
        qz[h] = jnp.where(row128 < 64, qa[h].astype(f32), 0.0).astype(bf16)
        qa[h, 64:80, :] = jnp.where(
            row16 == 0,
            1.0,
            jnp.where(
                row16 == 1, high, jnp.where(row16 == 2, middle, jnp.where(row16 == 3, rest, 0.0))
            ),
        ).astype(bf16)
        kv[h] = jnp.zeros((SLOTS, 128), f32)
        dz[h, 0:64, :] = jnp.zeros((64, QUERIES), bf16)
        da[h, 80:128, :] = jnp.zeros((48, QUERIES), bf16)
    row16 = lax.broadcasted_iota(jnp.int32, (16, ROWS), 0)
    for r in range(4):
        cols = pl.ds(ROWS * r, ROWS)
        for h in range(LOCAL):
            grad = mg[r, 64 * h : 64 * h + 64, :]
            delta = jnp.sum(grad.astype(f32) * ot[h, :, cols], axis=0, keepdims=True)
            high, middle, rest = parts_of(-delta)
            da[h, 0:64, cols] = grad
            dz[h, 64:128, cols] = grad
            da[h, 64:80, cols] = jnp.where(
                row16 == 0,
                high,
                jnp.where(row16 == 1, middle, jnp.where(row16 == 2, rest, 0.0)),
            ).astype(bf16)

    left, right = pl.ds(0, 128), pl.ds(128, 112)

    def along_shards(step):
        def one(t, carried):
            step(t)
            return carried

        lax.fori_loop(0, GROUP, one, 0)

    upper, under = pl.ds(0, 48), pl.ds(48, 48)

    def outer_first():
        halves[0].wait()
        net.landed("oxn", ax.at[0], at.to_x)
        net.landed("oyn", ay.at[0], at.to_y)
        net.landed("oxd", ax.at[1], at.to_x)
        net.landed("oyd", ay.at[1], at.to_y)
        for t in range(2):
            so[2, t, under] = added(so[2, t, under], ax[1, t])
            so[1, t + 2, under] = added(so[1, t + 2, under], ay[1, t])
            so[3, t, under] = added(so[3, t, under], ax[0, t])
            so[3, t + 2, under] = added(so[3, t + 2, under], ay[0, t])
        net.launch("oby", lambda: (so.at[2, fore, under], boy, at.to_y))
        net.launch("obx", lambda: (so.at[1, aft, under], box, at.to_x))

    def outer_second():
        net.landed("oby", boy, at.to_y)
        net.landed("obx", box, at.to_x)
        for t in range(2):
            so[3, t, under] = added(so[3, t, under], boy[t])
            so[3, t + 2, under] = added(so[3, t + 2, under], box[t])
        for i in range(1, GROUP):
            net.launch(
                f"oz{i}",
                lambda i=i: (so.at[3, at.to_z(i)[1], under], zo.at[i - 1], at.to_z(i)),
            )

    def outer_shards():
        for r in range(4):
            total = so[r, z, upper].astype(f32)
            for i in range(1, GROUP):
                net.landed(f"uz{r}{i}", az.at[r, i - 1], at.to_z(i))
                total = total + az[r, i - 1].astype(f32)
            su[r] = total.astype(bf16)
        net.launch("uxn", lambda: (su.at[1, :, front], ux.at[0], at.to_x))
        net.launch("uyn", lambda: (su.at[2, :, back], uy.at[0], at.to_y))
        net.launch("uxd", lambda: (su.at[0, :, front], ux.at[1], at.to_x))
        net.launch("uyd", lambda: (su.at[0, :, back], uy.at[1], at.to_y))

    def outer_third():
        net.landed("uxn", ux.at[0], at.to_x)
        net.landed("uyn", uy.at[0], at.to_y)
        net.landed("uxd", ux.at[1], at.to_x)
        net.landed("uyd", uy.at[1], at.to_y)
        su[2, :, front] = added(su[2, :, front], ux[1])
        su[1, :, back] = added(su[1, :, back], uy[1])
        net.launch("uby", lambda: (su.at[2, :, front], vy, at.to_y))
        net.launch("ubx", lambda: (su.at[1, :, back], vx, at.to_x))
        su[3, :, front] = added(su[3, :, front], ux[0])
        su[3, :, back] = added(su[3, :, back], uy[0])

    def outer_last():
        total = so[3, z, under].astype(f32)
        for i in range(1, GROUP):
            net.landed(f"oz{i}", zo.at[i - 1], at.to_z(i))
            total = total + zo[i - 1].astype(f32)
        done_o[48:96] = total.astype(bf16)
        net.landed("uby", vy, at.to_y)
        net.landed("ubx", vx, at.to_x)
        done_o[0:48, front] = added(su[3, :, front], vy[...])
        done_o[0:48, back] = added(su[3, :, back], vx[...])

    def inner_core():
        for copy in halves[1:]:
            copy.wait()
        for r in range(4):
            net.landed(f"gi{r}", ri.at[r, :, 0:192], at.to_core)
            net.landed(f"gw{r}", ri.at[r, :, 192:240], at.to_core)

        def step(t):
            for r in range(4):
                si[r, t] = added(si[r, t], ri[r, t])

        along_shards(step)
        net.launch("ixn", lambda: (si.at[1, :, left], aix.at[0], at.to_x))
        net.launch("iyn", lambda: (si.at[2, :, right], aiy.at[0], at.to_y))
        net.launch("ixd", lambda: (si.at[0, :, left], aix.at[1], at.to_x))
        net.launch("iyd", lambda: (si.at[0, :, right], aiy.at[1], at.to_y))

    def inner_first():
        net.landed("ixn", aix.at[0], at.to_x)
        net.landed("iyn", aiy.at[0], at.to_y)
        net.landed("ixd", aix.at[1], at.to_x)
        net.landed("iyd", aiy.at[1], at.to_y)

        def step(t):
            si[2, t, left] = added(si[2, t, left], aix[1, t])
            si[1, t, right] = added(si[1, t, right], aiy[1, t])
            si[3, t, left] = added(si[3, t, left], aix[0, t])
            si[3, t, right] = added(si[3, t, right], aiy[0, t])

        along_shards(step)
        net.launch("iby", lambda: (si.at[2, :, left], biy, at.to_y))
        net.launch("ibx", lambda: (si.at[1, :, right], bix, at.to_x))

    def inner_second():
        net.landed("iby", biy, at.to_y)
        net.landed("ibx", bix, at.to_x)

        def step(t):
            si[3, t, left] = added(si[3, t, left], biy[t])
            si[3, t, right] = added(si[3, t, right], bix[t])

        along_shards(step)
        for i in range(1, GROUP):
            net.launch(
                f"iz{i}", lambda i=i: (si.at[3, at.to_z(i)[1]], zi.at[i - 1], at.to_z(i))
            )

    def inner_last():
        total = si[3, z].astype(f32)
        for i in range(1, GROUP):
            net.landed(f"iz{i}", zi.at[i - 1], at.to_z(i))
            total = total + zi[i - 1].astype(f32)
        si[3, z] = total.astype(bf16)

    def go_at(chip, side):
        return go_out.at[2 * chip + side]

    def gi_at(chip, side):
        return gi_out.at[:, pl.ds(multiple(2 * chip + side, 384), 384)]

    def gw_at(chip, side):
        return gw_out.at[chip, :, pl.ds(multiple(side, 384), 384)]

    place_of = {"o": go_at, "i": gi_at, "w": gw_at}
    via_x = {"o": False, "i": True, "w": False}
    mine = {
        "o": lambda: done_o,
        "i": lambda: si.at[3, z, 0:192],
        "w": lambda: si.at[3, z, 192:240],
    }

    def spread(name):
        place = place_of[name]
        for tag, device in (("x", at.to_x), ("y", at.to_y), ("c", at.to_core)):
            net.launch(
                f"f{name}{tag}", lambda device=device: (mine[name](), place(p, core), device)
            )

    def pass_on(name):
        place = place_of[name]

        def hand(tag, chip, device):
            net.launch(
                f"f{name}{tag}", lambda: (place(chip, core), place(chip, core), device)
            )

        net.landed(f"f{name}x", place(at.p_x, core), at.to_x)
        net.landed(f"f{name}y", place(at.p_y, core), at.to_y)
        if via_x[name]:
            hand("r", at.p_y, at.to_x)
        else:
            hand("r", at.p_x, at.to_y)
        hand("cx", at.p_x, at.to_core)
        hand("cy", at.p_y, at.to_core)

    def finish_spread(name):
        place = place_of[name]
        far = place(at.p_d, core)
        net.landed(f"f{name}r", far, at.to_x if via_x[name] else at.to_y)
        net.start(f"f{name}cd", far, far, at.to_core)

    def close_spread(name):
        place = place_of[name]
        for tag, chip in (("c", p), ("cx", at.p_x), ("cy", at.p_y), ("cd", at.p_d)):
            net.landed(f"f{name}{tag}", place(chip, other), at.to_core)

    def swap_kv(h):
        for r in range(4):
            net.launch(
                f"kv{h}{r}",
                lambda r=r: (
                    kv.at[h, pl.ds(multiple(2 * chips[r] + other, ROWS), ROWS)],
                    rkv.at[h, r],
                    at.to_core,
                ),
            )

    def attend(h, tile):
        cols = pl.ds(multiple(tile, TILE), TILE)
        queries = qa[h, :, cols]
        upstream = da[h, :, cols]
        queries_only = qz[h, :, cols]
        upstream_only = dz[h, :, cols]
        for j in range(SLOTS // SPAN):
            rows = pl.ds(SPAN * j, SPAN)
            probs = jnp.exp(dot(ka[h, rows, :], queries))
            grads = (probs * dot(va[h, rows, :], upstream)).astype(bf16)
            kv[h, rows, :] += dot_nt(grads, queries_only) + dot_nt(
                probs.astype(bf16), upstream_only
            )
            update = dot(kt[h, :, rows], grads)
            if j == 0:
                dq[h, :, cols] = update
            else:
                dq[h, :, cols] += update

    plan = {
        1: [outer_first, inner_core],
        2: [lambda: swap_kv(0), outer_second],
        4: [lambda: swap_kv(1), outer_shards, inner_first],
        5: [outer_third, inner_second],
    }

    def take(steps):
        for step in steps:
            step()

    def unit(u, carried):
        for when, steps in plan.items():
            pl.when(u == when)(functools.partial(take, steps))
        attend(u // 2, u % 2)
        return carried

    lax.fori_loop(0, 2 * LOCAL, unit, 0)
    swap_kv(2)

    for copy in later:
        copy.wait()
    weights = wqkv[...].reshape(D, WIDE)
    for h in range(LOCAL):
        for r in range(4):
            net.landed(f"kv{h}{r}", rkv.at[h, r], at.to_core)
    sums = jnp.zeros((1, WIDE), f32)
    top, low = pl.ds(0, 192), pl.ds(192, 192)
    for r in range(4):
        cols = pl.ds(ROWS * r, ROWS)
        rows = pl.ds(multiple(2 * chips[r] + core, ROWS), ROWS)
        for h in range(LOCAL):
            dqkv[r, :, 128 * h : 128 * h + 128] = (kv[h, rows, :] + rkv[h, r]).astype(bf16)
        turned = jnp.concatenate(
            [dq[h, :, cols] for h in range(LOCAL)] + [jnp.zeros((64, ROWS), f32)], axis=0
        )
        dqkv[r, :, 384:WIDE] = (turned.T * 0.125).astype(bf16)
        block = dqkv[r]
        sums = sums + jnp.sum(block.astype(f32), axis=0, keepdims=True)
        update = dot_nt(block, weights)
        if r < 3:
            sdx[r] = update.astype(bf16)
        else:
            hg[...] += update
        if r == 1:
            net.start("dxn", sdx.at[1, top], rx.at[0], at.to_x)
            net.start("dxd", sdx.at[0, top], rx.at[1], at.to_x)
        if r == 2:
            net.start("dyn", sdx.at[2, low], ry.at[0], at.to_y)
            net.start("dyd", sdx.at[0, low], ry.at[1], at.to_y)
    small[p, 0:1, 0:WIDE] += sums
    for step in range(1, GROUP):
        net.start(f"sz{step}", small.at[at.to_z(step)[1]], rsz.at[step - 1], at.to_z(step))

    outer_last()
    spread("o")
    local(done_o, go_at(p, core))

    total = None
    for r in range(4):
        term = lax.dot_general(
            xs[r].reshape(ROWS, D), dqkv[r], (((0,), (0,)), ((), ())), preferred_element_type=f32
        )
        total = term if total is None else total + term
    dw[...] = total.reshape(GROUP, 2, 96, WIDE)
    dwl[...] = dw[:, other].astype(bf16)
    net.start("dwc", dwl, rdw, at.to_core)

    for step in range(1, GROUP):
        net.landed(f"sz{step}", rsz.at[step - 1], at.to_z(step))
    small[z] = small[z] + rsz[0] + rsz[1] + rsz[2]
    net.start("sc", small.at[z], rsc, at.to_core)
    net.landed("dwc", rdw, at.to_core)
    for t in range(GROUP):
        rdw[t] = added(dw[t, core], rdw[t])
    for step in range(1, GROUP):
        net.start(f"dwz{step}", rdw.at[at.to_z(step)[1]], rzw.at[step - 1], at.to_z(step))
    net.landed("sc", rsc, at.to_core)
    rsc[...] = small[z] + rsc[...]
    for r in range(3):
        net.start(f"sp{r}", rsc, rsp.at[r], devices[r])

    net.landed("dxn", rx.at[0], at.to_x)
    net.landed("dxd", rx.at[1], at.to_x)
    sdx[2, top] = added(sdx[2, top], rx[1])
    net.start("dby", sdx.at[2, top], by, at.to_y)
    net.landed("dyn", ry.at[0], at.to_y)
    net.landed("dyd", ry.at[1], at.to_y)
    sdx[1, low] = added(sdx[1, low], ry[1])
    net.start("dbx", sdx.at[1, low], bx, at.to_x)
    hg[top] += rx[0].astype(f32)
    hg[low] += ry[0].astype(f32)

    inner_last()
    for name in ("i", "w"):
        spread(name)
        local(mine[name](), place_of[name](p, core))

    for step in range(1, GROUP):
        net.landed(f"dwz{step}", rzw.at[step - 1], at.to_z(step))
    finished = rdw[z].astype(f32)
    for step in range(GROUP - 1):
        finished = finished + rzw[step].astype(f32)
    rdw[z] = finished.astype(bf16)
    for r in range(3):
        net.start(f"fq{r}", rdw.at[z], gqkv_out.at[p, core], devices[r])
    net.start("fqc", rdw.at[z], gqkv_out.at[p, core], at.to_core)
    local(rdw.at[z], gqkv_out.at[p, core])

    for r in range(3):
        net.landed(f"sp{r}", rsp.at[r], devices[r])
    ssum[...] = rsc[...] + rsp[0] + rsp[1] + rsp[2]
    local(ssum, small_out)

    for name in ("o", "i", "w"):
        pass_on(name)
    for r in range(3):
        ref = gqkv_out.at[chips[r], core]
        net.landed(f"fq{r}", ref, devices[r])
        net.start(f"fqc{r}", ref, ref, at.to_core)

    net.landed("dby", by, at.to_y)
    net.landed("dbx", bx, at.to_x)
    sdx[3, top] = (hg[top] + by[...].astype(f32)).astype(bf16)
    sdx[3, low] = (hg[low] + bx[...].astype(f32)).astype(bf16)
    local(sdx.at[3], dx_out)

    for name in ("o", "i", "w"):
        finish_spread(name)
    for name in ("o", "i", "w"):
        close_spread(name)
    net.landed("fqc", gqkv_out.at[p, other], at.to_core)
    for r in range(3):
        net.landed(f"fqc{r}", gqkv_out.at[chips[r], other], at.to_core)
    done = len(loads) + len(halves) + len(later)
    for copy in slots[done:]:
        copy.wait()
    net.drain()


BACKWARD_COPIES = 110


def backward_call(*operands):
    any_ = pl.BlockSpec(memory_space=pl.ANY)
    shape = jax.ShapeDtypeStruct
    vmem = pltpu.VMEM
    return pl.pallas_call(
        backward_kernel,
        name="backward_attention",
        out_shape=(
            shape((ROWS, D), bf16),
            shape((GROUP, 2, 96, WIDE), bf16),
            shape((192, FF), bf16),
            shape((CTX, 96, D), bf16),
            shape((GROUP, 48, D), bf16),
            shape((8, D), f32),
        ),
        in_specs=[any_] * 14,
        out_specs=[any_] * 6,
        scratch_shapes=[
            vmem((4, 192, ROWS), bf16),
            vmem((LOCAL, 64, QUERIES), f32),
            vmem((LOCAL, 8, QUERIES), f32),
            vmem((LOCAL, 128, QUERIES), bf16),
            vmem((LOCAL, 128, QUERIES), bf16),
            vmem((LOCAL, SLOTS, 128), bf16),
            vmem((LOCAL, SLOTS, 128), bf16),
            vmem((LOCAL, 64, SLOTS), bf16),
            vmem((LOCAL, 128, QUERIES), bf16),
            vmem((LOCAL, 128, QUERIES), bf16),
            vmem((LOCAL, SLOTS, 128), f32),
            vmem((LOCAL, 4, ROWS, 128), f32),
            vmem((LOCAL, 64, QUERIES), f32),
            vmem((4, GROUP, 96, D), bf16),
            vmem((4, GROUP, 240, 384), bf16),
            vmem((4, GROUP, 240, 384), bf16),
            vmem((2, GROUP, 128, 384), bf16),
            vmem((2, GROUP, 112, 384), bf16),
            vmem((2, 48, D), bf16),
            vmem((2, 48, D), bf16),
            vmem((2, 2, 48, D), bf16),
            vmem((2, 2, 48, D), bf16),
            vmem((4, 3, 48, D), bf16),
            vmem((4, 48, D), bf16),
            vmem((2, 48, 384), bf16),
            vmem((2, 48, 384), bf16),
            vmem((48, 384), bf16),
            vmem((48, 384), bf16),
            vmem((96, D), bf16),
            vmem((GROUP, 128, 384), bf16),
            vmem((GROUP, 112, 384), bf16),
            vmem((3, 48, D), bf16),
            vmem((3, 240, 384), bf16),
            vmem((4, 4, 96, D), bf16),
            vmem((GROUP, 2, 96, WIDE), bf16),
            vmem((4, ROWS, WIDE), bf16),
            vmem((4, ROWS, D), bf16),
            vmem((2, 192, D), bf16),
            vmem((2, 192, D), bf16),
            vmem((192, D), bf16),
            vmem((192, D), bf16),
            vmem((ROWS, D), f32),
            vmem((GROUP, 2, 96, WIDE), f32),
            vmem((GROUP, 96, WIDE), bf16),
            vmem((GROUP, 96, WIDE), bf16),
            vmem((3, 96, WIDE), bf16),
            vmem((GROUP, 8, D), f32),
            vmem((3, 8, D), f32),
            vmem((8, D), f32),
            vmem((3, 8, D), f32),
            vmem((8, D), f32),
            pltpu.SemaphoreType.DMA((BACKWARD_COPIES,)),
            pltpu.SemaphoreType.DMA((BACKWARD_COPIES,)),
            pltpu.SemaphoreType.DMA((48,)),
        ],
        compiler_params=pltpu.CompilerParams(
            collective_id=1, has_side_effects=True, vmem_limit_bytes=63 << 20
        ),
    )(*operands)


def small_plane(
    states,
    lengths,
    query_weight,
    query_bias,
    key_weight,
    value_weight,
    value_bias,
    output_weight,
    output_bias,
    first_gain,
    first_shift,
    inner_weight,
    inner_bias,
    outer_weight,
    outer_bias,
    second_gain,
    second_shift,
    cotangent,
):
    cycle_place = lax.axis_index("ctx")
    shard = lax.axis_index("fsdp")
    length = lengths[shard]
    wqkv = split_weights(cycle_place // 2, query_weight, key_weight, value_weight)
    vectors = pack_vectors(
        query_bias,
        value_bias,
        inner_bias,
        [output_bias, first_gain, first_shift, outer_bias, second_gain, second_shift],
    )
    low, mg, gi, gw, own, hg, small, xs, wall, qt, ka, va, kt, ot, lse = (
        forward_call(
            length[None],
            states.reshape(4, 96, D),
            wqkv,
            vectors,
            inner_weight,
            outer_weight.reshape(2, CTX, 48, D),
            output_weight.reshape(GROUP, 48, D),
            cotangent[0],
        )
    )
    layer_output = low[None]
    dx, gqkv, gi, go, gw, sums = backward_call(
        mg, ot, lse, qt, ka, va, kt, gi, gw, own, xs, wall, hg, small
    )
    gqkv = gqkv.reshape(GROUP, 192, WIDE)
    pairs = gqkv[:, :, :384].reshape(GROUP, 192, LOCAL, 2, 64).transpose(3, 1, 0, 2, 4)
    pairs = pairs.reshape(2, 192, D).astype(jnp.float32)
    query_grad = gqkv[:, :, 384:576].transpose(1, 0, 2).reshape(192, D).astype(jnp.float32)
    narrow = lax.dynamic_slice_in_dim(sums[2:8], shard * 192, 192, axis=1)
    value_bias_grad = sums[0, :384].reshape(LOCAL, 2, 64)[:, 1].reshape(192)
    return (
        layer_output,
        dx[None],
        query_grad,
        sums[0, 384:576],
        pairs[0],
        pairs[1],
        value_bias_grad,
        gw.reshape(192, D).astype(jnp.float32),
        narrow[0],
        narrow[1],
        narrow[2],
        gi.astype(jnp.float32),
        sums[1],
        go.reshape(D, D).astype(jnp.float32),
        narrow[3],
        narrow[4],
        narrow[5],
    )


def keep_state(carried):
    return carried


def per_device(
    states,
    lengths,
    query_weight,
    query_bias,
    key_weight,
    value_weight,
    value_bias,
    output_weight,
    output_bias,
    first_gain,
    first_shift,
    inner_weight,
    inner_bias,
    outer_weight,
    outer_bias,
    second_gain,
    second_shift,
    cotangent,
):
    row_count = states.shape[1]
    cycle_size = lax.axis_size("ctx")
    cycle_place = lax.axis_index("ctx")
    sequence = lax.axis_index("fsdp")
    length = lengths[sequence]
    offsets = jnp.arange(row_count, dtype=jnp.int32)
    row_keep = cycle_place * row_count + offsets < length
    inputs = states[0]
    input_float = inputs.astype(jnp.float32)
    attention_set = (
        lax.all_gather(query_weight, "fsdp", axis=0, tiled=True),
        lax.all_gather(key_weight, "fsdp", axis=0, tiled=True),
        lax.all_gather(value_weight, "fsdp", axis=0, tiled=True),
        lax.all_gather(output_weight, "fsdp", axis=0, tiled=True),
        lax.all_gather(query_bias, "fsdp", axis=0, tiled=True),
        lax.all_gather(value_bias, "fsdp", axis=0, tiled=True),
        lax.all_gather(output_bias, "fsdp", axis=0, tiled=True),
        lax.all_gather(first_gain, "fsdp", axis=0, tiled=True),
        lax.all_gather(first_shift, "fsdp", axis=0, tiled=True),
    )
    query_full = attention_set[0]
    key_full = attention_set[1]
    value_full = attention_set[2]
    output_full = attention_set[3]
    query_add = attention_set[4].astype(jnp.float32)
    value_add = attention_set[5].astype(jnp.float32)
    output_add = attention_set[6].astype(jnp.float32)
    gain_one = attention_set[7].astype(jnp.float32)
    shift_one = attention_set[8].astype(jnp.float32)
    queries = (
        (jnp.dot(inputs, query_full, preferred_element_type=jnp.float32) + query_add) * 0.125
    ).astype(jnp.bfloat16)
    key_rows = jnp.dot(inputs, key_full, preferred_element_type=jnp.float32).astype(jnp.bfloat16)
    values = (jnp.dot(inputs, value_full, preferred_element_type=jnp.float32) + value_add).astype(
        jnp.bfloat16
    )
    query_heads = queries.reshape(row_count, H, HD)

    def forward_block(key_block, value_block, key_start, running_state):

        def forward_compute(carried):
            running, exp_total, accum = carried
            key_keep = key_start + offsets < length
            scores = jnp.einsum(
                "qhd,khd->hqk",
                query_heads,
                key_block.reshape(row_count, H, HD),
                preferred_element_type=jnp.float32,
            )
            scores = jnp.where(key_keep[None, None, :], scores, -1e30)
            newest = jnp.maximum(running, jnp.max(scores, axis=2))
            factor = jnp.exp(running - newest)
            weights = jnp.exp(scores - newest[:, :, None])
            exp_total = exp_total * factor + jnp.sum(weights, axis=2)
            update = jnp.einsum(
                "hqk,khd->qhd",
                weights.astype(jnp.bfloat16),
                value_block.reshape(row_count, H, HD),
                preferred_element_type=jnp.float32,
            )
            accum = accum * factor.T[:, :, None] + update
            return (newest, exp_total, accum)

        return lax.cond(key_start < length, forward_compute, keep_state, running_state)

    start_state = (
        jnp.full((H, row_count), -1e30, jnp.float32),
        jnp.zeros((H, row_count), jnp.float32),
        jnp.zeros((row_count, H, HD), jnp.float32),
    )

    def cycle_turn(turn_index, carried):
        key_block, value_block, running_state = carried
        owner_index = (cycle_place - turn_index) % cycle_size
        running_state = forward_block(
            key_block, value_block, owner_index * row_count, running_state
        )
        key_block, value_block = passed_along((key_block, value_block), "ctx", 1)
        return (key_block, value_block, running_state)

    key_block, value_block, running_state = lax.fori_loop(
        0, cycle_size - 1, cycle_turn, (key_rows, values, start_state)
    )
    last_owner = (cycle_place + 1) % cycle_size
    running, exp_total, accum = forward_block(
        key_block, value_block, last_owner * row_count, running_state
    )
    log_total = running + jnp.log(exp_total)
    attention_value = (accum / exp_total.T[:, :, None]).reshape(row_count, D)
    mixed = attention_value.astype(jnp.bfloat16)
    attended = jnp.dot(mixed, output_full, preferred_element_type=jnp.float32) + output_add
    first_normed, first_scale = normalize(input_float + attended)
    first = first_normed * gain_one + shift_one
    first_low = first.astype(jnp.bfloat16)
    feed_set = (
        lax.all_gather(inner_weight, "fsdp", axis=0, tiled=True),
        lax.all_gather(outer_weight, "fsdp", axis=0, tiled=True),
        lax.all_gather(inner_bias, "fsdp", axis=0, tiled=True),
        lax.all_gather(outer_bias, "fsdp", axis=0, tiled=True),
        lax.all_gather(second_gain, "fsdp", axis=0, tiled=True),
        lax.all_gather(second_shift, "fsdp", axis=0, tiled=True),
    )
    inner_full = feed_set[0]
    outer_full = feed_set[1]
    inner_add = feed_set[2].astype(jnp.float32)
    outer_add = feed_set[3].astype(jnp.float32)
    gain_two = feed_set[4].astype(jnp.float32)
    shift_two = feed_set[5].astype(jnp.float32)
    inner = jnp.dot(first_low, inner_full, preferred_element_type=jnp.float32) + inner_add
    activated = jax.nn.gelu(inner, approximate=False).astype(jnp.bfloat16)
    outer = jnp.dot(activated, outer_full, preferred_element_type=jnp.float32) + outer_add
    second_normed, second_scale = normalize(first + outer)
    second = second_normed * gain_two + shift_two
    layer_output = jnp.where(row_keep[:, None], second, 0.0).astype(jnp.bfloat16)[None]
    query_full = attention_set[0]
    key_full = attention_set[1]
    value_full = attention_set[2]
    output_full = attention_set[3]
    gain_one = attention_set[7].astype(jnp.float32)
    inner_full = feed_set[0]
    outer_full = feed_set[1]
    gain_two = feed_set[4].astype(jnp.float32)
    upstream = jnp.where(row_keep[:, None], cotangent[0].astype(jnp.float32), 0.0)
    second_grad, second_gain_grad, second_shift_grad = norm_back(
        upstream, second_normed, second_scale, gain_two
    )
    outer_low = second_grad.astype(jnp.bfloat16)
    outer_bias_grad = jnp.sum(second_grad, axis=0)
    outer_weight_grad = jnp.dot(activated.T, outer_low, preferred_element_type=jnp.float32)
    inner_grad = jnp.dot(outer_low, outer_full.T, preferred_element_type=jnp.float32) * gelu_slope(
        inner
    )
    inner_low = inner_grad.astype(jnp.bfloat16)
    inner_bias_grad = jnp.sum(inner_grad, axis=0)
    inner_weight_grad = jnp.dot(first_low.T, inner_low, preferred_element_type=jnp.float32)
    first_grad = second_grad + jnp.dot(inner_low, inner_full.T, preferred_element_type=jnp.float32)
    hidden_grad, first_gain_grad, first_shift_grad = norm_back(
        first_grad, first_normed, first_scale, gain_one
    )
    attended_low = hidden_grad.astype(jnp.bfloat16)
    output_bias_grad = jnp.sum(hidden_grad, axis=0)
    output_weight_grad = jnp.dot(mixed.T, attended_low, preferred_element_type=jnp.float32)
    mixed_grad = jnp.dot(attended_low, output_full.T, preferred_element_type=jnp.float32).astype(
        jnp.bfloat16
    )
    delta = jnp.sum(
        (mixed_grad.astype(jnp.float32) * attention_value).reshape(row_count, H, HD), axis=2
    ).T

    def back_block(
        query_block,
        upstream_block,
        log_block,
        delta_block,
        key_block,
        value_block,
        key_start,
        grads,
    ):

        def back_compute(carried):
            query_grad, key_grad, value_grad = carried
            key_keep = key_start + offsets < length
            query_three = query_block.reshape(row_count, H, HD)
            upstream_three = upstream_block.reshape(row_count, H, HD)
            key_three = key_block.reshape(row_count, H, HD)
            value_three = value_block.reshape(row_count, H, HD)
            scores = jnp.einsum(
                "qhd,khd->hqk", query_three, key_three, preferred_element_type=jnp.float32
            )
            weights = jnp.where(
                key_keep[None, None, :], jnp.exp(scores - log_block[:, :, None]), 0.0
            )
            weight_grad = jnp.einsum(
                "qhd,khd->hqk", upstream_three, value_three, preferred_element_type=jnp.float32
            )
            score_grad = (weights * (weight_grad - delta_block[:, :, None])).astype(jnp.bfloat16)
            query_grad = query_grad + jnp.einsum(
                "hqk,khd->qhd", score_grad, key_three, preferred_element_type=jnp.float32
            ).reshape(row_count, D)
            key_grad = key_grad + jnp.einsum(
                "hqk,qhd->khd", score_grad, query_three, preferred_element_type=jnp.float32
            ).reshape(row_count, D)
            value_grad = value_grad + jnp.einsum(
                "hqk,qhd->khd",
                weights.astype(jnp.bfloat16),
                upstream_three,
                preferred_element_type=jnp.float32,
            ).reshape(row_count, D)
            return (query_grad, key_grad, value_grad)

        return lax.cond(key_start < length, back_compute, keep_state, grads)

    zero_grad = jnp.zeros((row_count, D), jnp.float32)

    def key_turn(turn_index, carried):
        key_block, value_block, query_grad, key_grad, value_grad = carried
        owner_index = (cycle_place - turn_index) % cycle_size
        query_grad, key_grad, value_grad = back_block(
            queries,
            mixed_grad,
            log_total,
            delta,
            key_block,
            value_block,
            owner_index * row_count,
            (query_grad, key_grad, value_grad),
        )
        key_block, value_block = passed_along((key_block, value_block), "ctx", 1)
        key_grad, value_grad = (
            passed_along(key_grad.astype(jnp.bfloat16), "ctx", 1).astype(key_grad.dtype),
            passed_along(value_grad.astype(jnp.bfloat16), "ctx", 1).astype(value_grad.dtype),
        )
        return (key_block, value_block, query_grad, key_grad, value_grad)

    key_block, value_block, query_grad, key_grad, value_grad = lax.fori_loop(
        0, cycle_size - 1, key_turn, (key_rows, values, zero_grad, zero_grad, zero_grad)
    )
    query_grad, key_grad, value_grad = back_block(
        queries,
        mixed_grad,
        log_total,
        delta,
        key_block,
        value_block,
        last_owner * row_count,
        (query_grad, key_grad, value_grad),
    )
    key_grad, value_grad = (
        passed_along(key_grad.astype(jnp.bfloat16), "ctx", 1).astype(key_grad.dtype),
        passed_along(value_grad.astype(jnp.bfloat16), "ctx", 1).astype(value_grad.dtype),
    )
    query_low = query_grad.astype(jnp.bfloat16) * 0.125
    key_low = key_grad.astype(jnp.bfloat16)
    value_low = value_grad.astype(jnp.bfloat16)
    query_weight_grad = jnp.dot(inputs.T, query_low, preferred_element_type=jnp.float32)
    query_bias_grad = jnp.sum(query_low.astype(jnp.float32), axis=0)
    key_weight_grad = jnp.dot(inputs.T, key_low, preferred_element_type=jnp.float32)
    value_weight_grad = jnp.dot(inputs.T, value_low, preferred_element_type=jnp.float32)
    value_bias_grad = jnp.sum(value_low.astype(jnp.float32), axis=0)
    input_grad = (
        hidden_grad
        + jnp.dot(query_low, query_full.T, preferred_element_type=jnp.float32)
        + jnp.dot(key_low, key_full.T, preferred_element_type=jnp.float32)
        + jnp.dot(value_low, value_full.T, preferred_element_type=jnp.float32)
    ).astype(jnp.bfloat16)[None]
    local_grads = (
        query_weight_grad,
        query_bias_grad,
        key_weight_grad,
        value_weight_grad,
        value_bias_grad,
        output_weight_grad,
        output_bias_grad,
        first_gain_grad,
        first_shift_grad,
        inner_weight_grad,
        inner_bias_grad,
        outer_weight_grad,
        outer_bias_grad,
        second_gain_grad,
        second_shift_grad,
    )
    shards = (
        lax.psum_scatter(
            local_grads[0].astype(jnp.bfloat16), "fsdp", scatter_dimension=0, tiled=True
        ).astype(jnp.float32),
        lax.psum_scatter(
            local_grads[1].astype(jnp.bfloat16), "fsdp", scatter_dimension=0, tiled=True
        ).astype(jnp.float32),
        lax.psum_scatter(
            local_grads[2].astype(jnp.bfloat16), "fsdp", scatter_dimension=0, tiled=True
        ).astype(jnp.float32),
        lax.psum_scatter(
            local_grads[3].astype(jnp.bfloat16), "fsdp", scatter_dimension=0, tiled=True
        ).astype(jnp.float32),
        lax.psum_scatter(
            local_grads[4].astype(jnp.bfloat16), "fsdp", scatter_dimension=0, tiled=True
        ).astype(jnp.float32),
        lax.psum_scatter(
            local_grads[5].astype(jnp.bfloat16), "fsdp", scatter_dimension=0, tiled=True
        ).astype(jnp.float32),
        lax.psum_scatter(
            local_grads[6].astype(jnp.bfloat16), "fsdp", scatter_dimension=0, tiled=True
        ).astype(jnp.float32),
        lax.psum_scatter(
            local_grads[7].astype(jnp.bfloat16), "fsdp", scatter_dimension=0, tiled=True
        ).astype(jnp.float32),
        lax.psum_scatter(
            local_grads[8].astype(jnp.bfloat16), "fsdp", scatter_dimension=0, tiled=True
        ).astype(jnp.float32),
        lax.psum_scatter(
            local_grads[9].astype(jnp.bfloat16), "fsdp", scatter_dimension=0, tiled=True
        ).astype(jnp.float32),
        lax.psum_scatter(
            local_grads[10].astype(jnp.bfloat16), "fsdp", scatter_dimension=0, tiled=True
        ).astype(jnp.float32),
        lax.psum_scatter(
            local_grads[11].astype(jnp.bfloat16), "fsdp", scatter_dimension=0, tiled=True
        ).astype(jnp.float32),
        lax.psum_scatter(
            local_grads[12].astype(jnp.bfloat16), "fsdp", scatter_dimension=0, tiled=True
        ).astype(jnp.float32),
        lax.psum_scatter(
            local_grads[13].astype(jnp.bfloat16), "fsdp", scatter_dimension=0, tiled=True
        ).astype(jnp.float32),
        lax.psum_scatter(
            local_grads[14].astype(jnp.bfloat16), "fsdp", scatter_dimension=0, tiled=True
        ).astype(jnp.float32),
    )
    totals = (
        lax.psum(shards[0].astype(jnp.bfloat16), "ctx").astype(jnp.float32),
        lax.psum(shards[1].astype(jnp.bfloat16), "ctx").astype(jnp.float32),
        lax.psum(shards[2].astype(jnp.bfloat16), "ctx").astype(jnp.float32),
        lax.psum(shards[3].astype(jnp.bfloat16), "ctx").astype(jnp.float32),
        lax.psum(shards[4].astype(jnp.bfloat16), "ctx").astype(jnp.float32),
        lax.psum(shards[5].astype(jnp.bfloat16), "ctx").astype(jnp.float32),
        lax.psum(shards[6].astype(jnp.bfloat16), "ctx").astype(jnp.float32),
        lax.psum(shards[7].astype(jnp.bfloat16), "ctx").astype(jnp.float32),
        lax.psum(shards[8].astype(jnp.bfloat16), "ctx").astype(jnp.float32),
        lax.psum(shards[9].astype(jnp.bfloat16), "ctx").astype(jnp.float32),
        lax.psum(shards[10].astype(jnp.bfloat16), "ctx").astype(jnp.float32),
        lax.psum(shards[11].astype(jnp.bfloat16), "ctx").astype(jnp.float32),
        lax.psum(shards[12].astype(jnp.bfloat16), "ctx").astype(jnp.float32),
        lax.psum(shards[13].astype(jnp.bfloat16), "ctx").astype(jnp.float32),
        lax.psum(shards[14].astype(jnp.bfloat16), "ctx").astype(jnp.float32),
    )
    return (
        layer_output,
        input_grad,
        totals[0],
        totals[1],
        totals[2],
        totals[3],
        totals[4],
        totals[5],
        totals[6],
        totals[7],
        totals[8],
        totals[9],
        totals[10],
        totals[11],
        totals[12],
        totals[13],
        totals[14],
    )


def solution(mesh):
    small = mesh.shape["ctx"] == CTX and mesh.shape["fsdp"] == GROUP
    return jax.shard_map(
        small_plane if small else per_device,
        mesh=mesh,
        in_specs=(
            P("fsdp", "ctx", None),
            P(),
            P("fsdp", None),
            P("fsdp"),
            P("fsdp", None),
            P("fsdp", None),
            P("fsdp"),
            P("fsdp", None),
            P("fsdp"),
            P("fsdp"),
            P("fsdp"),
            P("fsdp", None),
            P("fsdp"),
            P("fsdp", None),
            P("fsdp"),
            P("fsdp"),
            P("fsdp"),
            P("fsdp", "ctx", None),
        ),
        out_specs=(
            P("fsdp", "ctx", None),
            P("fsdp", "ctx", None),
            P("fsdp", None),
            P("fsdp"),
            P("fsdp", None),
            P("fsdp", None),
            P("fsdp"),
            P("fsdp", None),
            P("fsdp"),
            P("fsdp"),
            P("fsdp"),
            P("fsdp", None),
            P("fsdp"),
            P("fsdp", None),
            P("fsdp"),
            P("fsdp"),
            P("fsdp"),
        ),
        check_vma=False,
    )
```

```python
import functools

import jax
import jax.numpy as jnp
from jax import lax
from jax.experimental import pallas as pl
from jax.experimental.pallas import tpu as pltpu
from jax.sharding import PartitionSpec as P

RING = "ctx"
FSDP = "fsdp"
D = 768
H = 12
HD = 64


epsilon = 1e-05


def passed_along(value, axis, steps):
    count = lax.axis_size(axis)
    pairs = [(source, (source + steps) % count) for source in range(count)]
    return lax.ppermute(value, axis, pairs)


def normalize(hidden):
    centred = hidden - jnp.mean(hidden, axis=1, keepdims=True)
    scale = lax.rsqrt(jnp.mean(centred * centred, axis=1, keepdims=True) + epsilon)
    return (centred * scale, scale)


def norm_back(upstream, normed, scale, gain):
    gain_grad = jnp.sum(upstream * normed, axis=0)
    shift_grad = jnp.sum(upstream, axis=0)
    scaled = upstream * gain
    hidden_grad = scale * (
        scaled
        - jnp.mean(scaled, axis=1, keepdims=True)
        - normed * jnp.mean(scaled * normed, axis=1, keepdims=True)
    )
    return (hidden_grad, gain_grad, shift_grad)


def gelu_slope(inner):
    return (
        0.5 * (1.0 + lax.erf(inner * 0.7071067811865476))
        + inner * jnp.exp(-0.5 * inner * inner) * 0.3989422804014327
    )


bf16 = jnp.bfloat16
f32 = jnp.float32
FF = 3072
ROWS = 384
CTX = 8
GROUP = 4
LOCAL = 3
SLOTS = 3072
QUERIES = 1536
TILE = 768
CHUNK = 512
WIDE = 640
MESH = pl.DeviceIdType.MESH


def multiple(value, step):
    return pl.multiple_of(value * step, step)


class Place:
    def __init__(self):
        self.c = lax.axis_index(RING)
        self.z = lax.axis_index(FSDP)
        c = self.c
        self.core = c % 2
        self.p = c // 2
        self.x = self.p % 2
        self.y = c // 4
        self.p_x = self.p + 1 - 2 * self.x
        self.p_y = self.p + 2 - 4 * self.y
        self.p_d = self.p_y + 1 - 2 * self.x
        self.to_core = (c + 1 - 2 * self.core, self.z)
        self.to_x = (2 * self.p_x + self.core, self.z)
        self.to_y = (2 * self.p_y + self.core, self.z)
        self.to_d = (2 * self.p_d + self.core, self.z)

    def to_z(self, step):
        return (self.c, (self.z + step) % GROUP)

    def from_z(self, step):
        return (self.z + GROUP - step) % GROUP


class Net:
    def __init__(self, sends, receives):
        self.sends = sends
        self.receives = receives
        self.index = {}
        self.open = []

    def of(self, name):
        return self.index.setdefault(name, len(self.index))

    def copy(self, name, src, dst, device):
        i = self.of(name)
        return pltpu.make_async_remote_copy(
            src_ref=src,
            dst_ref=dst,
            send_sem=self.sends.at[i],
            recv_sem=self.receives.at[i],
            device_id=device,
            device_id_type=MESH,
        )

    def start(self, name, src, dst, device):
        self.launch(name, lambda: (src, dst, device))

    def launch(self, name, make, when=None):
        if when is None:
            self.copy(name, *make()).start()
        else:
            pl.when(when())(lambda: self.copy(name, *make()).start())
        self.open.append((name, make, when))

    def sent(self, name, make, when):
        if when is None:
            self.copy(name, *make()).wait_send()
        else:
            pl.when(when())(lambda: self.copy(name, *make()).wait_send())

    def landed(self, name, dst, device):
        self.copy(name, dst, dst, device).wait_recv()

    def finish(self, name):
        for entry in self.open:
            if entry[0] == name:
                self.sent(*entry)
        self.open = [entry for entry in self.open if entry[0] != name]

    def drain(self):
        for entry in self.open:
            self.sent(*entry)
        self.open = []


def greet(place, with_z=True):
    barrier = pltpu.get_barrier_semaphore()
    partners = [place.to_core, place.to_x, place.to_y, place.to_d]
    if with_z:
        partners += [place.to_z(step) for step in range(1, GROUP)]
    for partner in partners:
        pl.semaphore_signal(barrier, inc=1, device_id=partner, device_id_type=MESH)
    pl.semaphore_wait(barrier, len(partners))


def dot(a, b):
    return jnp.dot(a, b, preferred_element_type=f32)


def dot_nt(a, b):
    return lax.dot_general(a, b, (((1,), (1,)), ((), ())), preferred_element_type=f32)


def dot_tn(a, b):
    return lax.dot_general(a, b, (((0,), (0,)), ((), ())), preferred_element_type=f32)


def parts_of(value):
    high = value.astype(bf16).astype(f32)
    rest = value - high
    middle = rest.astype(bf16).astype(f32)
    return high, middle, rest - middle


def added(a, b):
    return (a.astype(f32) + b.astype(f32)).astype(bf16)


def forward_kernel(
    lengths,
    x_in,
    wqkv_in,
    vec_in,
    inner_in,
    outer_in,
    wo_in,
    cot_in,
    low_out,
    mg_out,
    gi_out,
    gw_out,
    own_out,
    hg_out,
    small_out,
    xs_out,
    wqkv_out,
    qt_out,
    ka_out,
    va_out,
    kt_out,
    ot_out,
    lse_out,
    xall,
    wqkv,
    vec,
    qt,
    ka,
    va,
    kt,
    vt,
    ot,
    lse,
    mix,
    mixed,
    acc,
    top,
    iw,
    ow,
    wo,
    cot,
    work,
    first,
    normed,
    second,
    slope,
    act,
    low,
    lower,
    gi,
    gw,
    mg,
    small,
    scales,
    ro,
    sends,
    receives,
    locals_,
):
    at = Place()
    net = Net(sends, receives)
    c, z, core, p = at.c, at.z, at.core, at.p
    other = 1 - core
    chips = [at.p_d, at.p_x, at.p_y, p]
    devices = [at.to_d, at.to_x, at.to_y]
    slots = []

    def local(src, dst):
        copy = pltpu.make_async_copy(src, dst, locals_.at[len(slots)])
        slots.append(copy)
        copy.start()
        return copy

    def inner_at(ref, chip, side):
        return ref.at[:, pl.ds(multiple(2 * chip + side, 384), 384)]

    def outer_at(ref, chip, side):
        return ref.at[0, 2 * chip + side]

    def wo_at(ref, chip, side):
        return ref.at[chip, :, pl.ds(multiple(side, 384), 384)]

    weights = {
        "wo": (wo_in, wo, wo_at),
        "inner": (inner_in, iw, inner_at),
        "outer": (outer_in, ow, outer_at),
    }

    def block_at(chip, side, part=slice(None)):
        return xall.at[chip, side, part]

    greet(at)

    early, late = pl.ds(0, 2), pl.ds(2, 2)
    net.start("sx0", x_in.at[early], block_at(p, core, early), at.to_x)
    net.start("sy1", x_in.at[late], block_at(p, core, late), at.to_y)
    net.start("sx1", x_in.at[late], block_at(p, core, late), at.to_x)
    net.start("sy0", x_in.at[early], block_at(p, core, early), at.to_y)
    net.start("sc", x_in, block_at(p, core), at.to_core)
    for step in range(1, GROUP):
        net.start(("vec", step), vec_in, vec.at[z], at.to_z(step))
    class Along:
        def __init__(self, name, source, region):
            self.name = name
            self.source = source
            self.region = region

        def send(self):
            name, source, region = self.name, self.source, self.region
            for step in range(1, GROUP):
                when = {1: lambda: z < 3, 2: None, 3: lambda: z > 0}[step]

                def make(step=step):
                    return source, region(z), at.to_z(step)

                net.launch((name, "z", step), make, when)

        def relay(self):
            name, region = self.name, self.region

            def up():
                net.copy((name, "z", 2), region(z - 2), region(z - 2), at.to_z(2)).wait_recv()

            def down():
                net.copy((name, "z", 2), region(z + 2), region(z + 2), at.to_z(2)).wait_recv()

            pl.when(z == 2)(up)
            pl.when(z == 1)(down)
            net.launch(
                (name, "u"), lambda: (region(0), region(0), at.to_z(1)), lambda: z == 2
            )
            net.launch(
                (name, "d"), lambda: (region(3), region(3), at.to_z(3)), lambda: z == 1
            )

        def landed(self, step):
            name, region = self.name, self.region
            ref = region(at.from_z(step))
            if step == 1:
                pl.when(z > 0)(lambda: net.landed((name, "z", 1), region(at.from_z(1)), at.to_z(1)))
                pl.when(z == 0)(lambda: net.landed((name, "d"), region(3), at.to_z(1)))
            elif step == 3:
                pl.when(z < 3)(lambda: net.landed((name, "z", 3), region(at.from_z(3)), at.to_z(3)))
                pl.when(z == 3)(lambda: net.landed((name, "u"), region(0), at.to_z(3)))
            else:
                pl.when((z == 0) | (z == 3))(
                    lambda: net.landed((name, "z", 2), region(at.from_z(2)), at.to_z(2))
                )
            return ref

    along = {"wq": Along("wq", wqkv_in.at[core], lambda shard: wqkv.at[shard, core])}
    for name, (src, dst, region) in weights.items():
        along[name] = Along(
            name,
            region(src, p, core),
            lambda shard, dst=dst, region=region: region(dst.at[shard], p, core),
        )

    def far_at(shard, side):
        return ow.at[shard, 1, pl.ds(4 * side, 4)]

    along["far"] = Along(
        "far", outer_in.at[1, pl.ds(4 * core, 4)], lambda shard: far_at(shard, core)
    )
    along["wq"].send()
    opening = [local(x_in, block_at(p, core)), local(vec_in, vec.at[z]), local(wqkv_in, wqkv.at[z])]
    owned = [
        local(wo_in, wo.at[z]),
        local(inner_in, iw.at[z]),
        local(outer_in, ow.at[z]),
        local(cot_in, cot),
    ]

    row64 = lax.broadcasted_iota(jnp.int32, (64, QUERIES), 0)
    row16 = lax.broadcasted_iota(jnp.int32, (16, SLOTS), 0)
    for h in range(LOCAL):
        qt[h, 64:128, :] = jnp.where(row64 == 0, 1.0, 0.0).astype(bf16)
        vt[h, 64:80, :] = jnp.where(row16 == 0, 1.0, 0.0).astype(bf16)

    along["wq"].relay()
    along["wo"].send()
    along["inner"].send()
    p_x, p_y, p_d = at.p_x, at.p_y, at.p_d

    def hand_on(label, ref, device):
        net.start(label, ref, ref, device)

    net.landed("sx0", block_at(p_x, core, early), at.to_x)
    hand_on("rx0", block_at(p_x, core, early), at.to_y)
    net.landed("sy1", block_at(p_y, core, late), at.to_y)
    hand_on("ry1", block_at(p_y, core, late), at.to_x)
    for step in range(1, GROUP):
        source = at.from_z(step)
        along["wq"].landed(step)
        net.start(("wqc", step), wqkv.at[source, core], wqkv.at[source, core], at.to_core)
    along["wo"].relay()
    net.landed("sx1", block_at(p_x, core, late), at.to_x)
    hand_on("cx", block_at(p_x, core), at.to_core)
    net.landed("sy0", block_at(p_y, core, early), at.to_y)
    hand_on("cy", block_at(p_y, core), at.to_core)
    for copy in opening:
        copy.wait()
    for step in range(1, GROUP):
        source = at.from_z(step)
        net.landed(("vec", step), vec.at[source], at.to_z(step))
        net.landed(("wqc", step), wqkv.at[source, other], at.to_core)

    bias = vec[p][0:1, 0:WIDE].astype(f32)
    lane = lax.broadcasted_iota(jnp.int32, (ROWS, 128), 1)
    row = lax.broadcasted_iota(jnp.int32, (ROWS, 128), 0)
    count = lengths[z]

    def project(chip, side, column):
        block = 2 * chip + side
        rows = xall[chip, side].reshape(ROWS, D)
        keep = block * ROWS + row < count
        mark = jnp.where(keep, 0.0, -1e30)
        at_rows = pl.ds(multiple(block, ROWS), ROWS)
        width = 384 if column is None else WIDE
        full = wqkv[...].reshape(D, WIDE)
        y = dot(rows, full[:, 0:width]) + bias[:, 0:width]
        for h in range(LOCAL):
            g = y[:, 128 * h : 128 * h + 128]
            ka[h, at_rows, :] = jnp.where(
                lane < 64, g, jnp.where(lane == 64, mark, jnp.where(lane < 68, 1.0, 0.0))
            ).astype(bf16)
            va[h, at_rows, :] = jnp.where(
                lane < 64, pltpu.roll(g, 64, 1), jnp.where(lane < 67, 1.0, 0.0)
            ).astype(bf16)
            turned = g.T.astype(bf16)
            kt[h, :, at_rows] = turned[0:64]
            vt[h, 0:64, at_rows] = turned[64:128]
        if column is not None:
            q = (y[:, 384:WIDE] * 0.125).T.astype(bf16)
            for h in range(LOCAL):
                qt[h, 0:64, pl.ds(multiple(column, ROWS), ROWS)] = q[64 * h : 64 * h + 64]

    def chip_of(i):
        return p + (i % 2) * (1 - 2 * at.x) + (i // 2) * (2 - 4 * at.y)

    def project_own(i, carried):
        project(chip_of(i), core, 3 * (1 - (i + 1) // 2) + i * ((i + 1) // 2))
        return carried

    def project_other(i, carried):
        project(chip_of(i), other, None)
        return carried

    along["outer"].send()
    lax.fori_loop(0, 3, project_own, 0)
    net.landed("sc", block_at(p, other), at.to_core)
    net.landed("cx", block_at(p_x, other), at.to_core)
    net.landed("cy", block_at(p_y, other), at.to_core)
    lax.fori_loop(0, 3, project_other, 0)
    net.landed("rx0", block_at(p_d, core, early), at.to_y)
    net.landed("ry1", block_at(p_d, core, late), at.to_x)
    hand_on("cd", block_at(p_d, core), at.to_core)
    project(p_d, core, 0)
    net.landed("cd", block_at(p_d, other), at.to_core)
    project(p_d, other, None)

    kept = [local(block_at(chips[r], core), xs_out.at[r]) for r in range(4)]
    for src, dst in (
        (wqkv, wqkv_out),
        (qt, qt_out),
        (ka, ka_out),
        (va, va_out),
        (kt, kt_out),
    ):
        local(src, dst)

    def part_of(name, step, chip, side):
        _, dst, region = weights[name]
        return region(dst.at[at.from_z(step)], chip, side)

    def hand(label, name, step, chip, device):
        def make():
            ref = part_of(name, step, chip, core)
            return ref, ref, device

        net.launch(label, make)

    steps_all = tuple(range(1, GROUP))

    def plane_out(name, steps=steps_all):
        for step in steps:
            along[name].landed(step)
            hand((name, "x", step), name, step, p, at.to_x)
            hand((name, "y", step), name, step, p, at.to_y)
            hand((name, "c", step), name, step, p, at.to_core)

    def relay_by_x(name, step):
        return (step + (name == "outer")) % 2 == 1

    def plane_relay(name, steps=steps_all):
        for step in steps:
            net.landed((name, "x", step), part_of(name, step, p_x, core), at.to_x)
            net.landed((name, "y", step), part_of(name, step, p_y, core), at.to_y)
            if relay_by_x(name, step):
                hand((name, "r", step), name, step, p_y, at.to_x)
            else:
                hand((name, "r", step), name, step, p_x, at.to_y)
            hand((name, "cx", step), name, step, p_x, at.to_core)
            hand((name, "cy", step), name, step, p_y, at.to_core)

    def plane_last(name, steps=steps_all):
        for step in steps:
            far = part_of(name, step, p_d, core)
            net.landed((name, "r", step), far, at.to_x if relay_by_x(name, step) else at.to_y)
            hand((name, "cd", step), name, step, p_d, at.to_core)

    def plane_in(name):
        for step in steps_all:
            for tag, chip in (("c", p), ("cx", p_x), ("cy", p_y), ("cd", p_d)):
                net.landed((name, tag, step), part_of(name, step, chip, other), at.to_core)

    plane_out("wo")
    along["inner"].relay()

    def attend(h, tile):
        cols = pl.ds(multiple(tile, TILE), TILE)
        queries = qt[h, :, cols]
        top[0:1, :] = jnp.full((1, TILE), -3e38, f32)
        acc[...] = jnp.zeros((80, TILE), f32)

        def some(half, carried):
            for j in range(SLOTS // CHUNK // 2):
                rows = pl.ds(multiple(half * (SLOTS // CHUNK // 2) + j, CHUNK), CHUNK)
                scores = dot(ka[h, rows, :], queries)
                before = top[0:1, :]
                newest = jnp.maximum(before, jnp.max(scores, axis=0, keepdims=True))
                probs = jnp.exp(scores - newest).astype(bf16)
                acc[...] = acc[...] * jnp.exp(before - newest) + dot(vt[h, :, rows], probs)
                top[0:1, :] = newest
            return carried

        lax.fori_loop(0, 2, some, 0)
        total = acc[64:65, :]
        value = acc[0:64, :] / total
        ot[h, :, cols] = value
        lse[h, 0:1, cols] = top[0:1, :] + jnp.log(total)
        low_value = value.astype(bf16)
        at_head = pl.ds(multiple(h, 64), 64)
        mix[2 * tile, at_head, :] = low_value[:, 0:384]
        mix[2 * tile + 1, at_head, :] = low_value[:, 384:768]

    def send_mixed(name, index, device):
        net.launch(name, lambda: (mix.at[index], mixed.at[p], device))

    plan = {
        1: [
            lambda: plane_out("inner"),
            lambda: plane_relay("wo"),
            along["outer"].relay,
            along["far"].send,
        ],
        2: [lambda: plane_last("wo"), lambda: plane_relay("inner", (1,))],
        3: [
            lambda: send_mixed("md", 0, at.to_d),
            lambda: send_mixed("mx", 1, at.to_x),
            lambda: plane_relay("inner", (2,)),
        ],
        4: [lambda: plane_relay("inner", (3,)), lambda: plane_out("outer")],
        5: [
            along["far"].relay,
            lambda: plane_last("inner"),
        ],
    }

    def take(steps):
        for step in steps:
            step()

    def unit(u, carried):
        for when, steps in plan.items():
            pl.when(u == when)(functools.partial(take, steps))
        attend(u % LOCAL, u // LOCAL)
        return carried

    lax.fori_loop(0, 2 * LOCAL, unit, 0)
    send_mixed("my", 2, at.to_y)
    mixed[p] = mix[3]
    local(ot, ot_out)
    local(lse, lse_out)

    plane_in("wo")
    for copy in owned:
        copy.wait()
    net.landed("md", mixed.at[p_d], at.to_d)
    net.landed("mx", mixed.at[p_x], at.to_x)
    net.landed("my", mixed.at[p_y], at.to_y)
    table = vec[0].astype(f32) + vec[1].astype(f32) + vec[2].astype(f32) + vec[3].astype(f32)
    output_add, gain_one, shift_one, outer_add, gain_two, shift_two = [
        table[2 + i : 3 + i, :] for i in range(6)
    ]
    heads = mixed[...].reshape(D, ROWS)
    work[...] = dot_tn(heads, wo[...].reshape(D, D))
    low[...] = xall[p, core].reshape(ROWS, D)
    plane_relay("outer")

    def blocks(step, start=0):
        def one(i, carried):
            return step(pl.ds(multiple(i, 128), 128), i, carried)

        return lax.fori_loop(0, ROWS // 128, one, start)

    def mean(value):
        return jnp.mean(value, axis=1, keepdims=True)

    def column(value):
        return jnp.sum(value, axis=0, keepdims=True)

    def norm(hidden):
        centred = hidden - mean(hidden)
        scale = lax.rsqrt(mean(centred * centred) + 1e-05)
        return centred * scale, scale

    def first_norm(rows, i, carried):
        value, scale = norm(low[rows, :].astype(f32) + work[rows, :] + output_add)
        normed[rows, :] = value
        scales[0, rows, :] = jnp.broadcast_to(scale, (128, 128))
        value = value * gain_one + shift_one
        first[rows, :] = value
        low[rows, :] = value.astype(bf16)
        return carried

    blocks(first_norm)
    for step in steps_all:
        along["far"].landed(step)
        source = at.from_z(step)
        net.start(("farc", step), far_at(source, core), far_at(source, core), at.to_core)

    plane_in("inner")
    inner_weight = iw[...].reshape(D, FF)
    for q in range(4):
        cols = pl.ds(D * q, D)
        slope[:, cols] = dot(low[...], inner_weight[:, D * q : D * q + D])
        add = vec[q][1:2, :].astype(f32)

        def activate(rows, i, carried, cols=cols, add=add):
            u = slope[rows, cols] + add
            gate = 0.5 * (1.0 + lax.erf(u * 0.7071067811865476))
            act[rows, cols] = (u * gate).astype(bf16)
            slope[rows, cols] = gate + u * jnp.exp(-0.5 * u * u) * 0.3989422804014327
            return carried

        blocks(activate)
        if q == 1:
            plane_last("outer")
    plane_in("outer")
    for step in steps_all:
        net.landed(("farc", step), far_at(at.from_z(step), other), at.to_core)
    total = None
    for q in range(4):
        term = dot(act[:, D * q : D * q + D], ow[q].reshape(D, D))
        total = term if total is None else total + term
    work[...] = total

    nothing = jnp.zeros((1, D), f32)

    def second_norm(rows, i, carried):
        gains, shifts, biases = carried
        value, scale = norm(first[rows, :] + work[rows, :] + outer_add)
        slot = c * ROWS + i * 128 + lax.broadcasted_iota(jnp.int32, (128, D), 0)
        keep = slot < count
        lower[rows, :] = jnp.where(keep, value * gain_two + shift_two, 0.0).astype(bf16)
        upstream = jnp.where(keep, cot[rows, :].astype(f32), 0.0)
        product = upstream * value
        scaled = upstream * gain_two
        grad = scale * (scaled - mean(scaled) - value * mean(scaled * value))
        second[rows, :] = grad
        cot[rows, :] = grad.astype(bf16)
        return gains + column(product), shifts + column(upstream), biases + column(grad)

    gain_two_grad, shift_two_grad, outer_bias_grad = blocks(second_norm, (nothing,) * 3)
    local(lower, low_out)

    for copy in kept:
        copy.wait()
    for name in ("rx0", "ry1", "cx", "cy", "cd"):
        net.finish(name)
    def outer_row(t, chip, side):
        j = 2 * chip + side
        return xall.at[t, j // 4, j % 4]

    for q in range(4):
        term = dot_tn(act[:, D * q : D * q + D], cot[...]).astype(bf16)
        xall[q] = term.reshape(2, 4, 96, D)
        for r in range(4):
            net.start(("go", q, r), outer_row(q, chips[r], other), ro.at[r, q], at.to_core)

    def outer_add_core():
        for q in range(4):
            for r in range(4):
                net.landed(("go", q, r), ro.at[r, q], at.to_core)

        def one(t, carried):
            for r in range(4):
                ref = outer_row(t, chips[r], core)
                ref[...] = added(ref[...], ro[r, t])
            return carried

        lax.fori_loop(0, GROUP, one, 0)
    total = None
    for q in range(4):
        cols = pl.ds(D * q, D)
        work[...] = dot_nt(cot[...], ow[q].reshape(D, D))

        def slopes(rows, i, carried, cols=cols):
            grad = work[rows, :] * slope[rows, cols]
            act[rows, cols] = grad.astype(bf16)
            return carried + column(grad)

        small[q, 1:2, :] = blocks(slopes, nothing)
        grads = act[:, D * q : D * q + D]
        term = dot_nt(grads, inner_weight[:, D * q : D * q + D])
        total = term if total is None else total + term
        if q == 2:
            outer_add_core()
    work[...] = total

    def first_back(rows, i, carried):
        gains, shifts, biases = carried
        value = normed[rows, :]
        upstream = second[rows, :] + work[rows, :]
        scaled = upstream * gain_one
        grad = scales[0, rows, 0:1] * (scaled - mean(scaled) - value * mean(scaled * value))
        first[rows, :] = grad
        lower_grad[rows, :] = grad.astype(bf16)
        return gains + column(upstream * value), shifts + column(upstream), biases + column(grad)

    lower_grad = cot
    gain_one_grad, shift_one_grad, output_bias_grad = blocks(first_back, (nothing,) * 3)
    local(first, hg_out)
    mg[...] = dot_nt(wo[...].reshape(D, D), lower_grad[...]).astype(bf16).reshape(GROUP, 192, ROWS)
    for r in range(3):
        net.start(("mg", r), mg.at[chips[r]], mg_out.at[r], devices[r])
    local(mg.at[p], mg_out.at[3])
    for q in range(4):
        grads = act[:, D * q : D * q + D]
        gi[:, :, D * q : D * q + D] = dot_tn(low[...], grads).astype(bf16).reshape(GROUP, 192, D)
    local(gi, gi_out)
    gw[...] = dot(heads, lower_grad[...]).astype(bf16).reshape(GROUP, GROUP, 48, D)
    local(gw, gw_out)
    narrow = [
        output_bias_grad,
        gain_one_grad,
        shift_one_grad,
        outer_bias_grad,
        gain_two_grad,
        shift_two_grad,
    ]
    for t in range(GROUP):
        small[t, 0:1, :] = nothing
        for i, value in enumerate(narrow):
            small[t, 2 + i : 3 + i, :] = value
    local(small, small_out)
    for r in range(4):
        j = 2 * chips[r] + core
        local(xall.at[:, j // 4, j % 4], own_out.at[r])
    for r in range(3):
        net.landed(("mg", r), mg_out.at[r], devices[r])
    waited = len(opening) + len(owned)
    for copy in slots[waited:]:
        if not any(copy is other_copy for other_copy in kept):
            copy.wait()
    net.drain()


FORWARD_COPIES = 140


def forward_call(*operands):
    any_ = pl.BlockSpec(memory_space=pl.ANY)
    shape = jax.ShapeDtypeStruct
    vmem = pltpu.VMEM
    return pl.pallas_call(
        forward_kernel,
        name="forward_attention",
        out_shape=(
            shape((ROWS, D), bf16),
            shape((4, 192, ROWS), bf16),
            shape((GROUP, 192, FF), bf16),
            shape((GROUP, GROUP, 48, D), bf16),
            shape((4, GROUP, 96, D), bf16),
            shape((ROWS, D), f32),
            shape((GROUP, 8, D), f32),
            shape((4, 4, 96, D), bf16),
            shape((GROUP, 2, 96, WIDE), bf16),
            shape((LOCAL, 128, QUERIES), bf16),
            shape((LOCAL, SLOTS, 128), bf16),
            shape((LOCAL, SLOTS, 128), bf16),
            shape((LOCAL, 64, SLOTS), bf16),
            shape((LOCAL, 64, QUERIES), f32),
            shape((LOCAL, 8, QUERIES), f32),
        ),
        in_specs=[pl.BlockSpec(memory_space=pltpu.SMEM)] + [any_] * 7,
        out_specs=[any_] * 15,
        scratch_shapes=[
            vmem((GROUP, 2, 4, 96, D), bf16),
            vmem((GROUP, 2, 96, WIDE), bf16),
            vmem((GROUP, 16, D), bf16),
            vmem((LOCAL, 128, QUERIES), bf16),
            vmem((LOCAL, SLOTS, 128), bf16),
            vmem((LOCAL, SLOTS, 128), bf16),
            vmem((LOCAL, 64, SLOTS), bf16),
            vmem((LOCAL, 80, SLOTS), bf16),
            vmem((LOCAL, 64, QUERIES), f32),
            vmem((LOCAL, 8, QUERIES), f32),
            vmem((4, 192, ROWS), bf16),
            vmem((GROUP, 192, ROWS), bf16),
            vmem((80, TILE), f32),
            vmem((8, TILE), f32),
            vmem((GROUP, 192, FF), bf16),
            vmem((GROUP, 2, CTX, 48, D), bf16),
            vmem((GROUP, GROUP, 48, D), bf16),
            vmem((ROWS, D), bf16),
            vmem((ROWS, D), f32),
            vmem((ROWS, D), f32),
            vmem((ROWS, D), f32),
            vmem((ROWS, D), f32),
            vmem((ROWS, FF), f32),
            vmem((ROWS, FF), bf16),
            vmem((ROWS, D), bf16),
            vmem((ROWS, D), bf16),
            vmem((GROUP, 192, FF), bf16),
            vmem((GROUP, GROUP, 48, D), bf16),
            vmem((GROUP, 192, ROWS), bf16),
            vmem((GROUP, 8, D), f32),
            vmem((1, ROWS, 128), f32),
            vmem((4, GROUP, 96, D), bf16),
            pltpu.SemaphoreType.DMA((FORWARD_COPIES,)),
            pltpu.SemaphoreType.DMA((FORWARD_COPIES,)),
            pltpu.SemaphoreType.DMA((48,)),
        ],
        compiler_params=pltpu.CompilerParams(
            collective_id=0, has_side_effects=True, vmem_limit_bytes=67043328
        ),
    )(*operands)


def split_weights(place_p, query_weight, key_weight, value_weight):
    def columns(weight):
        return lax.dynamic_slice_in_dim(weight, place_p * 192, 192, axis=1)

    rows = query_weight.shape[0]
    pair = jnp.concatenate(
        [columns(key_weight).reshape(rows, 3, 64), columns(value_weight).reshape(rows, 3, 64)],
        axis=2,
    ).reshape(rows, 384)
    fill = jnp.zeros((rows, 64), bf16)
    return jnp.concatenate([pair, columns(query_weight), fill], axis=1).reshape(2, 96, WIDE)


def pack_vectors(query_bias, value_bias, inner_bias, vectors):
    nothing = jnp.zeros((3, 64), bf16)
    first = jnp.concatenate(
        [
            jnp.concatenate([nothing, value_bias.reshape(3, 64)], axis=1).reshape(384),
            query_bias,
            jnp.zeros((192,), bf16),
        ]
    )
    rest = jnp.stack(vectors)[:, None, :]
    mine = lax.broadcasted_iota(jnp.int32, (1, GROUP, 1), 1) == lax.axis_index(FSDP)
    rest = jnp.where(mine, rest, 0).astype(bf16).reshape(len(vectors), D)
    return jnp.concatenate([first[None], inner_bias[None], rest, jnp.zeros((8, D), bf16)])


SPAN = 256


def backward_kernel(
    mg_in,
    ot_in,
    lse_in,
    qt_in,
    ka_in,
    va_in,
    kt_in,
    gi_in,
    gw_in,
    own_in,
    xs_in,
    wqkv_in,
    hg_in,
    small_in,
    dx_out,
    gqkv_out,
    gi_out,
    go_out,
    gw_out,
    small_out,
    mg,
    ot,
    lse,
    qa,
    qz,
    ka,
    va,
    kt,
    da,
    dz,
    kv,
    rkv,
    dq,
    so,
    si,
    ri,
    aix,
    aiy,
    boy,
    box,
    ax,
    ay,
    az,
    su,
    ux,
    uy,
    vx,
    vy,
    done_o,
    biy,
    bix,
    zo,
    zi,
    xs,
    wqkv,
    dqkv,
    sdx,
    rx,
    ry,
    bx,
    by,
    hg,
    dw,
    dwl,
    rdw,
    rzw,
    small,
    rsz,
    rsc,
    rsp,
    ssum,
    sends,
    receives,
    locals_,
):
    at = Place()
    net = Net(sends, receives)
    c, z, core, p = at.c, at.z, at.core, at.p
    other = 1 - core
    chips = [at.p_d, at.p_x, at.p_y, p]
    devices = [at.to_d, at.to_x, at.to_y]
    slots = []

    def local(src, dst):
        copy = pltpu.make_async_copy(src, dst, locals_.at[len(slots)])
        slots.append(copy)
        copy.start()
        return copy

    greet(at)
    upper, under = pl.ds(0, 48), pl.ds(48, 48)
    fore, aft = pl.ds(0, 2), pl.ds(2, 2)
    front, back = pl.ds(0, 384), pl.ds(384, 384)
    net.start("oxn", own_in.at[1, fore, under], ax.at[0], at.to_x)
    net.start("oyn", own_in.at[2, aft, under], ay.at[0], at.to_y)
    net.start("oxd", own_in.at[0, fore, under], ax.at[1], at.to_x)
    net.start("oyd", own_in.at[0, aft, under], ay.at[1], at.to_y)
    for r in range(4):
        for step in range(1, GROUP):
            device = at.to_z(step)
            net.start(("uz", r, step), own_in.at[r, device[1], upper], az.at[r, step - 1], device)
    loads = [
        local(mg_in, mg),
        local(ot_in, ot),
        local(lse_in, lse),
        local(qt_in, qa),
        local(ka_in, ka),
        local(va_in, va),
        local(kt_in, kt),
    ]

    def i_at(chip, side):
        return gi_in.at[:, :, pl.ds(multiple(2 * chip + side, 384), 384)]

    def w_at(chip, side):
        return gw_in.at[:, chip, :, pl.ds(multiple(side, 384), 384)]

    halves = [local(own_in, so)]
    for r in range(4):
        net.start(("gi", r), i_at(chips[r], other), ri.at[r, :, 0:192], at.to_core)
        net.start(("gw", r), w_at(chips[r], other), ri.at[r, :, 192:240], at.to_core)
        halves.append(local(i_at(chips[r], core), si.at[r, :, 0:192]))
        halves.append(local(w_at(chips[r], core), si.at[r, :, 192:240]))
    later = [local(wqkv_in, wqkv), local(hg_in, hg), local(small_in, small)]
    for r in range(4):
        later.append(local(xs_in.at[r], xs.at[r]))

    for copy in loads:
        copy.wait()
    row16 = lax.broadcasted_iota(jnp.int32, (16, QUERIES), 0)
    row128 = lax.broadcasted_iota(jnp.int32, (128, QUERIES), 0)
    for h in range(LOCAL):
        high, middle, rest = parts_of(-lse[h, 0:1, :])
        qz[h] = jnp.where(row128 < 64, qa[h].astype(f32), 0.0).astype(bf16)
        qa[h, 64:80, :] = jnp.where(
            row16 == 0,
            1.0,
            jnp.where(
                row16 == 1, high, jnp.where(row16 == 2, middle, jnp.where(row16 == 3, rest, 0.0))
            ),
        ).astype(bf16)
        kv[h] = jnp.zeros((SLOTS, 128), f32)
        dz[h, 0:64, :] = jnp.zeros((64, QUERIES), bf16)
        da[h, 80:128, :] = jnp.zeros((48, QUERIES), bf16)
    row16 = lax.broadcasted_iota(jnp.int32, (16, ROWS), 0)
    for r in range(4):
        cols = pl.ds(ROWS * r, ROWS)
        for h in range(LOCAL):
            grad = mg[r, 64 * h : 64 * h + 64, :]
            delta = jnp.sum(grad.astype(f32) * ot[h, :, cols], axis=0, keepdims=True)
            high, middle, rest = parts_of(-delta)
            da[h, 0:64, cols] = grad
            dz[h, 64:128, cols] = grad
            da[h, 64:80, cols] = jnp.where(
                row16 == 0,
                high,
                jnp.where(row16 == 1, middle, jnp.where(row16 == 2, rest, 0.0)),
            ).astype(bf16)

    left, right = pl.ds(0, 128), pl.ds(128, 112)

    def along_shards(step):
        def one(t, carried):
            step(t)
            return carried

        lax.fori_loop(0, GROUP, one, 0)

    upper, under = pl.ds(0, 48), pl.ds(48, 48)

    def outer_first():
        halves[0].wait()
        net.landed("oxn", ax.at[0], at.to_x)
        net.landed("oyn", ay.at[0], at.to_y)
        net.landed("oxd", ax.at[1], at.to_x)
        net.landed("oyd", ay.at[1], at.to_y)
        for t in range(2):
            so[2, t, under] = added(so[2, t, under], ax[1, t])
            so[1, t + 2, under] = added(so[1, t + 2, under], ay[1, t])
            so[3, t, under] = added(so[3, t, under], ax[0, t])
            so[3, t + 2, under] = added(so[3, t + 2, under], ay[0, t])
        net.launch("oby", lambda: (so.at[2, fore, under], boy, at.to_y))
        net.launch("obx", lambda: (so.at[1, aft, under], box, at.to_x))

    def outer_second():
        net.landed("oby", boy, at.to_y)
        net.landed("obx", box, at.to_x)
        for t in range(2):
            so[3, t, under] = added(so[3, t, under], boy[t])
            so[3, t + 2, under] = added(so[3, t + 2, under], box[t])
        for i in range(1, GROUP):
            net.launch(
                ("oz", i),
                lambda i=i: (so.at[3, at.to_z(i)[1], under], zo.at[i - 1], at.to_z(i)),
            )

    def outer_shards():
        for r in range(4):
            total = so[r, z, upper].astype(f32)
            for i in range(1, GROUP):
                net.landed(("uz", r, i), az.at[r, i - 1], at.to_z(i))
                total = total + az[r, i - 1].astype(f32)
            su[r] = total.astype(bf16)
        net.launch("uxn", lambda: (su.at[1, :, front], ux.at[0], at.to_x))
        net.launch("uyn", lambda: (su.at[2, :, back], uy.at[0], at.to_y))
        net.launch("uxd", lambda: (su.at[0, :, front], ux.at[1], at.to_x))
        net.launch("uyd", lambda: (su.at[0, :, back], uy.at[1], at.to_y))

    def outer_third():
        net.landed("uxn", ux.at[0], at.to_x)
        net.landed("uyn", uy.at[0], at.to_y)
        net.landed("uxd", ux.at[1], at.to_x)
        net.landed("uyd", uy.at[1], at.to_y)
        su[2, :, front] = added(su[2, :, front], ux[1])
        su[1, :, back] = added(su[1, :, back], uy[1])
        net.launch("uby", lambda: (su.at[2, :, front], vy, at.to_y))
        net.launch("ubx", lambda: (su.at[1, :, back], vx, at.to_x))
        su[3, :, front] = added(su[3, :, front], ux[0])
        su[3, :, back] = added(su[3, :, back], uy[0])

    def outer_last():
        total = so[3, z, under].astype(f32)
        for i in range(1, GROUP):
            net.landed(("oz", i), zo.at[i - 1], at.to_z(i))
            total = total + zo[i - 1].astype(f32)
        done_o[48:96] = total.astype(bf16)
        net.landed("uby", vy, at.to_y)
        net.landed("ubx", vx, at.to_x)
        done_o[0:48, front] = added(su[3, :, front], vy[...])
        done_o[0:48, back] = added(su[3, :, back], vx[...])

    def inner_core():
        for copy in halves[1:]:
            copy.wait()
        for r in range(4):
            net.landed(("gi", r), ri.at[r, :, 0:192], at.to_core)
            net.landed(("gw", r), ri.at[r, :, 192:240], at.to_core)

        def step(t):
            for r in range(4):
                si[r, t] = added(si[r, t], ri[r, t])

        along_shards(step)
        net.launch("ixn", lambda: (si.at[1, :, left], aix.at[0], at.to_x))
        net.launch("iyn", lambda: (si.at[2, :, right], aiy.at[0], at.to_y))
        net.launch("ixd", lambda: (si.at[0, :, left], aix.at[1], at.to_x))
        net.launch("iyd", lambda: (si.at[0, :, right], aiy.at[1], at.to_y))

    def inner_first():
        net.landed("ixn", aix.at[0], at.to_x)
        net.landed("iyn", aiy.at[0], at.to_y)
        net.landed("ixd", aix.at[1], at.to_x)
        net.landed("iyd", aiy.at[1], at.to_y)

        def step(t):
            si[2, t, left] = added(si[2, t, left], aix[1, t])
            si[1, t, right] = added(si[1, t, right], aiy[1, t])
            si[3, t, left] = added(si[3, t, left], aix[0, t])
            si[3, t, right] = added(si[3, t, right], aiy[0, t])

        along_shards(step)
        net.launch("iby", lambda: (si.at[2, :, left], biy, at.to_y))
        net.launch("ibx", lambda: (si.at[1, :, right], bix, at.to_x))

    def inner_second():
        net.landed("iby", biy, at.to_y)
        net.landed("ibx", bix, at.to_x)

        def step(t):
            si[3, t, left] = added(si[3, t, left], biy[t])
            si[3, t, right] = added(si[3, t, right], bix[t])

        along_shards(step)
        for i in range(1, GROUP):
            net.launch(
                ("iz", i), lambda i=i: (si.at[3, at.to_z(i)[1]], zi.at[i - 1], at.to_z(i))
            )

    def inner_last():
        total = si[3, z].astype(f32)
        for i in range(1, GROUP):
            net.landed(("iz", i), zi.at[i - 1], at.to_z(i))
            total = total + zi[i - 1].astype(f32)
        si[3, z] = total.astype(bf16)

    def go_at(chip, side):
        return go_out.at[2 * chip + side]

    def gi_at(chip, side):
        return gi_out.at[:, pl.ds(multiple(2 * chip + side, 384), 384)]

    def gw_at(chip, side):
        return gw_out.at[chip, :, pl.ds(multiple(side, 384), 384)]

    place_of = {"o": go_at, "i": gi_at, "w": gw_at}
    via_x = {"o": False, "i": True, "w": False}
    mine = {
        "o": lambda: done_o,
        "i": lambda: si.at[3, z, 0:192],
        "w": lambda: si.at[3, z, 192:240],
    }

    def spread(name):
        place = place_of[name]
        for tag, device in (("x", at.to_x), ("y", at.to_y), ("c", at.to_core)):
            net.launch(
                ("f", name, tag), lambda device=device: (mine[name](), place(p, core), device)
            )

    def pass_on(name):
        place = place_of[name]

        def hand(tag, chip, device):
            net.launch(
                ("f", name, tag), lambda: (place(chip, core), place(chip, core), device)
            )

        net.landed(("f", name, "x"), place(at.p_x, core), at.to_x)
        net.landed(("f", name, "y"), place(at.p_y, core), at.to_y)
        if via_x[name]:
            hand("r", at.p_y, at.to_x)
        else:
            hand("r", at.p_x, at.to_y)
        hand("cx", at.p_x, at.to_core)
        hand("cy", at.p_y, at.to_core)

    def finish_spread(name):
        place = place_of[name]
        far = place(at.p_d, core)
        net.landed(("f", name, "r"), far, at.to_x if via_x[name] else at.to_y)
        net.start(("f", name, "cd"), far, far, at.to_core)

    def close_spread(name):
        place = place_of[name]
        for tag, chip in (("c", p), ("cx", at.p_x), ("cy", at.p_y), ("cd", at.p_d)):
            net.landed(("f", name, tag), place(chip, other), at.to_core)

    def swap_kv(h):
        for r in range(4):
            net.launch(
                ("kv", h, r),
                lambda r=r: (
                    kv.at[h, pl.ds(multiple(2 * chips[r] + other, ROWS), ROWS)],
                    rkv.at[h, r],
                    at.to_core,
                ),
            )

    def attend(h, tile):
        cols = pl.ds(multiple(tile, TILE), TILE)
        queries = qa[h, :, cols]
        upstream = da[h, :, cols]
        queries_only = qz[h, :, cols]
        upstream_only = dz[h, :, cols]
        dq[h, :, cols] = jnp.zeros((64, TILE), f32)

        def some(half, carried):
            for j in range(SLOTS // SPAN // 2):
                rows = pl.ds(multiple(half * (SLOTS // SPAN // 2) + j, SPAN), SPAN)
                probs = jnp.exp(dot(ka[h, rows, :], queries))
                grads = (probs * dot(va[h, rows, :], upstream)).astype(bf16)
                kv[h, rows, :] += dot_nt(grads, queries_only) + dot_nt(
                    probs.astype(bf16), upstream_only
                )
                dq[h, :, cols] += dot(kt[h, :, rows], grads)
            return carried

        lax.fori_loop(0, 2, some, 0)

    plan = {
        1: [outer_first, inner_core],
        2: [lambda: swap_kv(0), outer_second],
        4: [lambda: swap_kv(1), outer_shards, inner_first],
        5: [outer_third, inner_second],
    }

    def take(steps):
        for step in steps:
            step()

    def unit(u, carried):
        for when, steps in plan.items():
            pl.when(u == when)(functools.partial(take, steps))
        attend(u // 2, u % 2)
        return carried

    lax.fori_loop(0, 2 * LOCAL, unit, 0)
    swap_kv(2)

    for copy in later:
        copy.wait()
    weights = wqkv[...].reshape(D, WIDE)
    for h in range(LOCAL):
        for r in range(4):
            net.landed(("kv", h, r), rkv.at[h, r], at.to_core)
    sums = jnp.zeros((1, WIDE), f32)
    top, low = pl.ds(0, 192), pl.ds(192, 192)
    for r in range(4):
        cols = pl.ds(ROWS * r, ROWS)
        rows = pl.ds(multiple(2 * chips[r] + core, ROWS), ROWS)
        for h in range(LOCAL):
            dqkv[r, :, 128 * h : 128 * h + 128] = (kv[h, rows, :] + rkv[h, r]).astype(bf16)
        turned = jnp.concatenate(
            [dq[h, :, cols] for h in range(LOCAL)] + [jnp.zeros((64, ROWS), f32)], axis=0
        )
        dqkv[r, :, 384:WIDE] = (turned.T * 0.125).astype(bf16)
        block = dqkv[r]
        sums = sums + jnp.sum(block.astype(f32), axis=0, keepdims=True)
        update = dot_nt(block, weights)
        if r < 3:
            sdx[r] = update.astype(bf16)
        else:
            hg[...] += update
        if r == 1:
            net.start("dxn", sdx.at[1, top], rx.at[0], at.to_x)
            net.start("dxd", sdx.at[0, top], rx.at[1], at.to_x)
        if r == 2:
            net.start("dyn", sdx.at[2, low], ry.at[0], at.to_y)
            net.start("dyd", sdx.at[0, low], ry.at[1], at.to_y)
    small[p, 0:1, 0:WIDE] += sums
    for step in range(1, GROUP):
        net.start(("sz", step), small.at[at.to_z(step)[1]], rsz.at[step - 1], at.to_z(step))

    outer_last()
    spread("o")
    local(done_o, go_at(p, core))

    total = None
    for r in range(4):
        term = lax.dot_general(
            xs[r].reshape(ROWS, D), dqkv[r], (((0,), (0,)), ((), ())), preferred_element_type=f32
        )
        total = term if total is None else total + term
    dw[...] = total.reshape(GROUP, 2, 96, WIDE)
    dwl[...] = dw[:, other].astype(bf16)
    net.start("dwc", dwl, rdw, at.to_core)

    for step in range(1, GROUP):
        net.landed(("sz", step), rsz.at[step - 1], at.to_z(step))
    small[z] = small[z] + rsz[0] + rsz[1] + rsz[2]
    net.start("sc", small.at[z], rsc, at.to_core)
    net.landed("dwc", rdw, at.to_core)
    for t in range(GROUP):
        rdw[t] = added(dw[t, core], rdw[t])
    for step in range(1, GROUP):
        net.start(("dwz", step), rdw.at[at.to_z(step)[1]], rzw.at[step - 1], at.to_z(step))
    net.landed("sc", rsc, at.to_core)
    rsc[...] = small[z] + rsc[...]
    for r in range(3):
        net.start(("sp", r), rsc, rsp.at[r], devices[r])

    net.landed("dxn", rx.at[0], at.to_x)
    net.landed("dxd", rx.at[1], at.to_x)
    sdx[2, top] = added(sdx[2, top], rx[1])
    net.start("dby", sdx.at[2, top], by, at.to_y)
    net.landed("dyn", ry.at[0], at.to_y)
    net.landed("dyd", ry.at[1], at.to_y)
    sdx[1, low] = added(sdx[1, low], ry[1])
    net.start("dbx", sdx.at[1, low], bx, at.to_x)
    hg[top] += rx[0].astype(f32)
    hg[low] += ry[0].astype(f32)

    inner_last()
    for name in ("i", "w"):
        spread(name)
        local(mine[name](), place_of[name](p, core))

    for step in range(1, GROUP):
        net.landed(("dwz", step), rzw.at[step - 1], at.to_z(step))
    finished = rdw[z].astype(f32)
    for step in range(GROUP - 1):
        finished = finished + rzw[step].astype(f32)
    rdw[z] = finished.astype(bf16)
    for r in range(3):
        net.start(("fq", r), rdw.at[z], gqkv_out.at[p, core], devices[r])
    net.start("fqc", rdw.at[z], gqkv_out.at[p, core], at.to_core)
    local(rdw.at[z], gqkv_out.at[p, core])

    for r in range(3):
        net.landed(("sp", r), rsp.at[r], devices[r])
    ssum[...] = rsc[...] + rsp[0] + rsp[1] + rsp[2]
    local(ssum, small_out)

    for name in ("o", "i", "w"):
        pass_on(name)
    for r in range(3):
        ref = gqkv_out.at[chips[r], core]
        net.landed(("fq", r), ref, devices[r])
        net.start(("fqc", r), ref, ref, at.to_core)

    net.landed("dby", by, at.to_y)
    net.landed("dbx", bx, at.to_x)
    sdx[3, top] = (hg[top] + by[...].astype(f32)).astype(bf16)
    sdx[3, low] = (hg[low] + bx[...].astype(f32)).astype(bf16)
    local(sdx.at[3], dx_out)

    for name in ("o", "i", "w"):
        finish_spread(name)
    for name in ("o", "i", "w"):
        close_spread(name)
    net.landed("fqc", gqkv_out.at[p, other], at.to_core)
    for r in range(3):
        net.landed(("fqc", r), gqkv_out.at[chips[r], other], at.to_core)
    done = len(loads) + len(halves) + len(later)
    for copy in slots[done:]:
        copy.wait()
    net.drain()


BACKWARD_COPIES = 110


def backward_call(*operands):
    any_ = pl.BlockSpec(memory_space=pl.ANY)
    shape = jax.ShapeDtypeStruct
    vmem = pltpu.VMEM
    return pl.pallas_call(
        backward_kernel,
        name="backward_attention",
        out_shape=(
            shape((ROWS, D), bf16),
            shape((GROUP, 2, 96, WIDE), bf16),
            shape((192, FF), bf16),
            shape((CTX, 96, D), bf16),
            shape((GROUP, 48, D), bf16),
            shape((8, D), f32),
        ),
        in_specs=[any_] * 14,
        out_specs=[any_] * 6,
        scratch_shapes=[
            vmem((4, 192, ROWS), bf16),
            vmem((LOCAL, 64, QUERIES), f32),
            vmem((LOCAL, 8, QUERIES), f32),
            vmem((LOCAL, 128, QUERIES), bf16),
            vmem((LOCAL, 128, QUERIES), bf16),
            vmem((LOCAL, SLOTS, 128), bf16),
            vmem((LOCAL, SLOTS, 128), bf16),
            vmem((LOCAL, 64, SLOTS), bf16),
            vmem((LOCAL, 128, QUERIES), bf16),
            vmem((LOCAL, 128, QUERIES), bf16),
            vmem((LOCAL, SLOTS, 128), f32),
            vmem((LOCAL, 4, ROWS, 128), f32),
            vmem((LOCAL, 64, QUERIES), f32),
            vmem((4, GROUP, 96, D), bf16),
            vmem((4, GROUP, 240, 384), bf16),
            vmem((4, GROUP, 240, 384), bf16),
            vmem((2, GROUP, 128, 384), bf16),
            vmem((2, GROUP, 112, 384), bf16),
            vmem((2, 48, D), bf16),
            vmem((2, 48, D), bf16),
            vmem((2, 2, 48, D), bf16),
            vmem((2, 2, 48, D), bf16),
            vmem((4, 3, 48, D), bf16),
            vmem((4, 48, D), bf16),
            vmem((2, 48, 384), bf16),
            vmem((2, 48, 384), bf16),
            vmem((48, 384), bf16),
            vmem((48, 384), bf16),
            vmem((96, D), bf16),
            vmem((GROUP, 128, 384), bf16),
            vmem((GROUP, 112, 384), bf16),
            vmem((3, 48, D), bf16),
            vmem((3, 240, 384), bf16),
            vmem((4, 4, 96, D), bf16),
            vmem((GROUP, 2, 96, WIDE), bf16),
            vmem((4, ROWS, WIDE), bf16),
            vmem((4, ROWS, D), bf16),
            vmem((2, 192, D), bf16),
            vmem((2, 192, D), bf16),
            vmem((192, D), bf16),
            vmem((192, D), bf16),
            vmem((ROWS, D), f32),
            vmem((GROUP, 2, 96, WIDE), f32),
            vmem((GROUP, 96, WIDE), bf16),
            vmem((GROUP, 96, WIDE), bf16),
            vmem((3, 96, WIDE), bf16),
            vmem((GROUP, 8, D), f32),
            vmem((3, 8, D), f32),
            vmem((8, D), f32),
            vmem((3, 8, D), f32),
            vmem((8, D), f32),
            pltpu.SemaphoreType.DMA((BACKWARD_COPIES,)),
            pltpu.SemaphoreType.DMA((BACKWARD_COPIES,)),
            pltpu.SemaphoreType.DMA((48,)),
        ],
        compiler_params=pltpu.CompilerParams(
            collective_id=1, has_side_effects=True, vmem_limit_bytes=63 << 20
        ),
    )(*operands)


def finish_kernel(
    low_in, dx_in, gqkv_in, gi_in, go_in, gw_in,
    low_out, dx_out, q_out, k_out, v_out, gi_out, go_out, gw_out,
    low, dx, gqkv, gi, go, gw, q, k, v, wide_i, wide_o, wide_w, reads, writes,
):
    loads = [
        pltpu.make_async_copy(src, dst, reads.at[i])
        for i, (src, dst) in enumerate(
            ((gi_in, gi), (go_in, go), (gw_in, gw), (gqkv_in, gqkv), (low_in, low), (dx_in, dx))
        )
    ]
    for copy in loads:
        copy.start()
    stores = []

    def store(src, dst):
        copy = pltpu.make_async_copy(src, dst, writes.at[len(stores)])
        stores.append(copy)
        copy.start()

    for copy, narrow, wide, dst in (
        (loads[0], gi, wide_i, gi_out),
        (loads[1], go, wide_o, go_out),
        (loads[2], gw, wide_w, gw_out),
    ):
        copy.wait()
        wide[...] = narrow[...].astype(f32)
        store(wide, dst)
    loads[3].wait()
    lane = lax.broadcasted_iota(jnp.int32, (192, 128), 1)

    def piece(chip, tile, side, wanted):
        value = gqkv[chip, :, 128 * tile : 128 * tile + 128].astype(f32)
        return value if side == wanted else pltpu.roll(value, 64, 1)

    for tile in range(6):
        cols = pl.ds(128 * tile, 128)
        left, right = [divmod(g, LOCAL) for g in (2 * tile, 2 * tile + 1)]
        for ref, place in (
            (k, lambda h: (h, 0)),
            (v, lambda h: (h, 1)),
            (q, lambda h: (3 + h // 2, h % 2)),
        ):
            a = piece(left[0], *place(left[1]), 0)
            b = piece(right[0], *place(right[1]), 1)
            ref[:, cols] = jnp.where(lane < 64, a, b)
    for src, dst in ((q, q_out), (k, k_out), (v, v_out)):
        store(src, dst)
    loads[4].wait()
    store(low, low_out)
    loads[5].wait()
    store(dx, dx_out)
    for copy in stores:
        copy.wait()


def finish_call(*operands):
    any_ = pl.BlockSpec(memory_space=pl.ANY)
    vmem = pltpu.VMEM
    square, wide = (192, D), (192, FF)
    shapes = [((ROWS, D), bf16)] * 2 + [(square, f32)] * 3
    shapes += [(wide, f32), ((D, D), f32), (square, f32)]
    return pl.pallas_call(
        finish_kernel,
        name="finish",
        out_shape=[jax.ShapeDtypeStruct(*pair) for pair in shapes],
        in_specs=[any_] * 6,
        out_specs=[any_] * 8,
        scratch_shapes=[
            vmem((ROWS, D), bf16),
            vmem((ROWS, D), bf16),
            vmem((GROUP, 192, WIDE), bf16),
            vmem(wide, bf16),
            vmem((D, D), bf16),
            vmem(square, bf16),
            vmem(square, f32),
            vmem(square, f32),
            vmem(square, f32),
            vmem(wide, f32),
            vmem((D, D), f32),
            vmem(square, f32),
            pltpu.SemaphoreType.DMA((6,)),
            pltpu.SemaphoreType.DMA((8,)),
        ],
        compiler_params=pltpu.CompilerParams(vmem_limit_bytes=67043328),
    )(*operands)


def small_plane(
    states,
    lengths,
    query_weight,
    query_bias,
    key_weight,
    value_weight,
    value_bias,
    output_weight,
    output_bias,
    first_gain,
    first_shift,
    inner_weight,
    inner_bias,
    outer_weight,
    outer_bias,
    second_gain,
    second_shift,
    cotangent,
):
    cycle_place = lax.axis_index(RING)
    shard = lax.axis_index(FSDP)
    wqkv = split_weights(cycle_place // 2, query_weight, key_weight, value_weight)
    vectors = pack_vectors(
        query_bias,
        value_bias,
        inner_bias,
        [output_bias, first_gain, first_shift, outer_bias, second_gain, second_shift],
    )
    low, mg, gi, gw, own, hg, small, xs, wall, qt, ka, va, kt, ot, lse = (
        forward_call(
            lengths,
            states.reshape(4, 96, D),
            wqkv,
            vectors,
            inner_weight,
            outer_weight.reshape(2, CTX, 48, D),
            output_weight.reshape(GROUP, 48, D),
            cotangent[0],
        )
    )
    dx, gqkv, gi, go, gw, sums = backward_call(
        mg, ot, lse, qt, ka, va, kt, gi, gw, own, xs, wall, hg, small
    )
    low, dx, gq, gk, gv, gi, go, gw = finish_call(
        low,
        dx,
        gqkv.reshape(GROUP, 192, WIDE),
        gi,
        go.reshape(D, D),
        gw.reshape(192, D),
    )
    narrow = lax.dynamic_slice_in_dim(sums[2:8], shard * 192, 192, axis=1)
    value_bias_grad = sums[0, :384].reshape(LOCAL, 2, 64)[:, 1].reshape(192)
    return (
        low[None],
        dx[None],
        gq,
        sums[0, 384:576],
        gk,
        gv,
        value_bias_grad,
        gw,
        narrow[0],
        narrow[1],
        narrow[2],
        gi,
        sums[1],
        go,
        narrow[3],
        narrow[4],
        narrow[5],
    )


def keep_state(carried):
    return carried


def per_device(
    states,
    lengths,
    query_weight,
    query_bias,
    key_weight,
    value_weight,
    value_bias,
    output_weight,
    output_bias,
    first_gain,
    first_shift,
    inner_weight,
    inner_bias,
    outer_weight,
    outer_bias,
    second_gain,
    second_shift,
    cotangent,
):
    row_count = states.shape[1]
    cycle_size = lax.axis_size(RING)
    cycle_place = lax.axis_index(RING)
    sequence = lax.axis_index(FSDP)
    length = lengths[sequence]
    offsets = jnp.arange(row_count, dtype=jnp.int32)
    row_keep = cycle_place * row_count + offsets < length
    inputs = states[0]
    input_float = inputs.astype(jnp.float32)
    attention_set = (
        lax.all_gather(query_weight, FSDP, axis=0, tiled=True),
        lax.all_gather(key_weight, FSDP, axis=0, tiled=True),
        lax.all_gather(value_weight, FSDP, axis=0, tiled=True),
        lax.all_gather(output_weight, FSDP, axis=0, tiled=True),
        lax.all_gather(query_bias, FSDP, axis=0, tiled=True),
        lax.all_gather(value_bias, FSDP, axis=0, tiled=True),
        lax.all_gather(output_bias, FSDP, axis=0, tiled=True),
        lax.all_gather(first_gain, FSDP, axis=0, tiled=True),
        lax.all_gather(first_shift, FSDP, axis=0, tiled=True),
    )
    query_full = attention_set[0]
    key_full = attention_set[1]
    value_full = attention_set[2]
    output_full = attention_set[3]
    query_add = attention_set[4].astype(jnp.float32)
    value_add = attention_set[5].astype(jnp.float32)
    output_add = attention_set[6].astype(jnp.float32)
    gain_one = attention_set[7].astype(jnp.float32)
    shift_one = attention_set[8].astype(jnp.float32)
    queries = (
        (jnp.dot(inputs, query_full, preferred_element_type=jnp.float32) + query_add) * 0.125
    ).astype(jnp.bfloat16)
    key_rows = jnp.dot(inputs, key_full, preferred_element_type=jnp.float32).astype(jnp.bfloat16)
    values = (jnp.dot(inputs, value_full, preferred_element_type=jnp.float32) + value_add).astype(
        jnp.bfloat16
    )
    query_heads = queries.reshape(row_count, H, HD)

    def forward_block(key_block, value_block, key_start, running_state):

        def forward_compute(carried):
            running, exp_total, accum = carried
            key_keep = key_start + offsets < length
            scores = jnp.einsum(
                "qhd,khd->hqk",
                query_heads,
                key_block.reshape(row_count, H, HD),
                preferred_element_type=jnp.float32,
            )
            scores = jnp.where(key_keep[None, None, :], scores, -1e30)
            newest = jnp.maximum(running, jnp.max(scores, axis=2))
            factor = jnp.exp(running - newest)
            weights = jnp.exp(scores - newest[:, :, None])
            exp_total = exp_total * factor + jnp.sum(weights, axis=2)
            update = jnp.einsum(
                "hqk,khd->qhd",
                weights.astype(jnp.bfloat16),
                value_block.reshape(row_count, H, HD),
                preferred_element_type=jnp.float32,
            )
            accum = accum * factor.T[:, :, None] + update
            return (newest, exp_total, accum)

        return lax.cond(key_start < length, forward_compute, keep_state, running_state)

    start_state = (
        jnp.full((H, row_count), -1e30, jnp.float32),
        jnp.zeros((H, row_count), jnp.float32),
        jnp.zeros((row_count, H, HD), jnp.float32),
    )

    def cycle_turn(turn_index, carried):
        key_block, value_block, running_state = carried
        owner_index = (cycle_place - turn_index) % cycle_size
        running_state = forward_block(
            key_block, value_block, owner_index * row_count, running_state
        )
        key_block, value_block = passed_along((key_block, value_block), RING, 1)
        return (key_block, value_block, running_state)

    key_block, value_block, running_state = lax.fori_loop(
        0, cycle_size - 1, cycle_turn, (key_rows, values, start_state)
    )
    last_owner = (cycle_place + 1) % cycle_size
    running, exp_total, accum = forward_block(
        key_block, value_block, last_owner * row_count, running_state
    )
    log_total = running + jnp.log(exp_total)
    attention_value = (accum / exp_total.T[:, :, None]).reshape(row_count, D)
    mixed = attention_value.astype(jnp.bfloat16)
    attended = jnp.dot(mixed, output_full, preferred_element_type=jnp.float32) + output_add
    first_normed, first_scale = normalize(input_float + attended)
    first = first_normed * gain_one + shift_one
    first_low = first.astype(jnp.bfloat16)
    feed_set = (
        lax.all_gather(inner_weight, FSDP, axis=0, tiled=True),
        lax.all_gather(outer_weight, FSDP, axis=0, tiled=True),
        lax.all_gather(inner_bias, FSDP, axis=0, tiled=True),
        lax.all_gather(outer_bias, FSDP, axis=0, tiled=True),
        lax.all_gather(second_gain, FSDP, axis=0, tiled=True),
        lax.all_gather(second_shift, FSDP, axis=0, tiled=True),
    )
    inner_full = feed_set[0]
    outer_full = feed_set[1]
    inner_add = feed_set[2].astype(jnp.float32)
    outer_add = feed_set[3].astype(jnp.float32)
    gain_two = feed_set[4].astype(jnp.float32)
    shift_two = feed_set[5].astype(jnp.float32)
    inner = jnp.dot(first_low, inner_full, preferred_element_type=jnp.float32) + inner_add
    activated = jax.nn.gelu(inner, approximate=False).astype(jnp.bfloat16)
    outer = jnp.dot(activated, outer_full, preferred_element_type=jnp.float32) + outer_add
    second_normed, second_scale = normalize(first + outer)
    second = second_normed * gain_two + shift_two
    layer_output = jnp.where(row_keep[:, None], second, 0.0).astype(jnp.bfloat16)[None]
    query_full = attention_set[0]
    key_full = attention_set[1]
    value_full = attention_set[2]
    output_full = attention_set[3]
    gain_one = attention_set[7].astype(jnp.float32)
    inner_full = feed_set[0]
    outer_full = feed_set[1]
    gain_two = feed_set[4].astype(jnp.float32)
    upstream = jnp.where(row_keep[:, None], cotangent[0].astype(jnp.float32), 0.0)
    second_grad, second_gain_grad, second_shift_grad = norm_back(
        upstream, second_normed, second_scale, gain_two
    )
    outer_low = second_grad.astype(jnp.bfloat16)
    outer_bias_grad = jnp.sum(second_grad, axis=0)
    outer_weight_grad = jnp.dot(activated.T, outer_low, preferred_element_type=jnp.float32)
    inner_grad = jnp.dot(outer_low, outer_full.T, preferred_element_type=jnp.float32) * gelu_slope(
        inner
    )
    inner_low = inner_grad.astype(jnp.bfloat16)
    inner_bias_grad = jnp.sum(inner_grad, axis=0)
    inner_weight_grad = jnp.dot(first_low.T, inner_low, preferred_element_type=jnp.float32)
    first_grad = second_grad + jnp.dot(inner_low, inner_full.T, preferred_element_type=jnp.float32)
    hidden_grad, first_gain_grad, first_shift_grad = norm_back(
        first_grad, first_normed, first_scale, gain_one
    )
    attended_low = hidden_grad.astype(jnp.bfloat16)
    output_bias_grad = jnp.sum(hidden_grad, axis=0)
    output_weight_grad = jnp.dot(mixed.T, attended_low, preferred_element_type=jnp.float32)
    mixed_grad = jnp.dot(attended_low, output_full.T, preferred_element_type=jnp.float32).astype(
        jnp.bfloat16
    )
    delta = jnp.sum(
        (mixed_grad.astype(jnp.float32) * attention_value).reshape(row_count, H, HD), axis=2
    ).T

    def back_block(
        query_block,
        upstream_block,
        log_block,
        delta_block,
        key_block,
        value_block,
        key_start,
        grads,
    ):

        def back_compute(carried):
            query_grad, key_grad, value_grad = carried
            key_keep = key_start + offsets < length
            query_three = query_block.reshape(row_count, H, HD)
            upstream_three = upstream_block.reshape(row_count, H, HD)
            key_three = key_block.reshape(row_count, H, HD)
            value_three = value_block.reshape(row_count, H, HD)
            scores = jnp.einsum(
                "qhd,khd->hqk", query_three, key_three, preferred_element_type=jnp.float32
            )
            weights = jnp.where(
                key_keep[None, None, :], jnp.exp(scores - log_block[:, :, None]), 0.0
            )
            weight_grad = jnp.einsum(
                "qhd,khd->hqk", upstream_three, value_three, preferred_element_type=jnp.float32
            )
            score_grad = (weights * (weight_grad - delta_block[:, :, None])).astype(jnp.bfloat16)
            query_grad = query_grad + jnp.einsum(
                "hqk,khd->qhd", score_grad, key_three, preferred_element_type=jnp.float32
            ).reshape(row_count, D)
            key_grad = key_grad + jnp.einsum(
                "hqk,qhd->khd", score_grad, query_three, preferred_element_type=jnp.float32
            ).reshape(row_count, D)
            value_grad = value_grad + jnp.einsum(
                "hqk,qhd->khd",
                weights.astype(jnp.bfloat16),
                upstream_three,
                preferred_element_type=jnp.float32,
            ).reshape(row_count, D)
            return (query_grad, key_grad, value_grad)

        return lax.cond(key_start < length, back_compute, keep_state, grads)

    zero_grad = jnp.zeros((row_count, D), jnp.float32)

    def key_turn(turn_index, carried):
        key_block, value_block, query_grad, key_grad, value_grad = carried
        owner_index = (cycle_place - turn_index) % cycle_size
        query_grad, key_grad, value_grad = back_block(
            queries,
            mixed_grad,
            log_total,
            delta,
            key_block,
            value_block,
            owner_index * row_count,
            (query_grad, key_grad, value_grad),
        )
        key_block, value_block = passed_along((key_block, value_block), RING, 1)
        key_grad, value_grad = (
            passed_along(key_grad.astype(jnp.bfloat16), RING, 1).astype(key_grad.dtype),
            passed_along(value_grad.astype(jnp.bfloat16), RING, 1).astype(value_grad.dtype),
        )
        return (key_block, value_block, query_grad, key_grad, value_grad)

    key_block, value_block, query_grad, key_grad, value_grad = lax.fori_loop(
        0, cycle_size - 1, key_turn, (key_rows, values, zero_grad, zero_grad, zero_grad)
    )
    query_grad, key_grad, value_grad = back_block(
        queries,
        mixed_grad,
        log_total,
        delta,
        key_block,
        value_block,
        last_owner * row_count,
        (query_grad, key_grad, value_grad),
    )
    key_grad, value_grad = (
        passed_along(key_grad.astype(jnp.bfloat16), RING, 1).astype(key_grad.dtype),
        passed_along(value_grad.astype(jnp.bfloat16), RING, 1).astype(value_grad.dtype),
    )
    query_low = query_grad.astype(jnp.bfloat16) * 0.125
    key_low = key_grad.astype(jnp.bfloat16)
    value_low = value_grad.astype(jnp.bfloat16)
    query_weight_grad = jnp.dot(inputs.T, query_low, preferred_element_type=jnp.float32)
    query_bias_grad = jnp.sum(query_low.astype(jnp.float32), axis=0)
    key_weight_grad = jnp.dot(inputs.T, key_low, preferred_element_type=jnp.float32)
    value_weight_grad = jnp.dot(inputs.T, value_low, preferred_element_type=jnp.float32)
    value_bias_grad = jnp.sum(value_low.astype(jnp.float32), axis=0)
    input_grad = (
        hidden_grad
        + jnp.dot(query_low, query_full.T, preferred_element_type=jnp.float32)
        + jnp.dot(key_low, key_full.T, preferred_element_type=jnp.float32)
        + jnp.dot(value_low, value_full.T, preferred_element_type=jnp.float32)
    ).astype(jnp.bfloat16)[None]
    local_grads = (
        query_weight_grad,
        query_bias_grad,
        key_weight_grad,
        value_weight_grad,
        value_bias_grad,
        output_weight_grad,
        output_bias_grad,
        first_gain_grad,
        first_shift_grad,
        inner_weight_grad,
        inner_bias_grad,
        outer_weight_grad,
        outer_bias_grad,
        second_gain_grad,
        second_shift_grad,
    )
    shards = (
        lax.psum_scatter(
            local_grads[0].astype(jnp.bfloat16), FSDP, scatter_dimension=0, tiled=True
        ).astype(jnp.float32),
        lax.psum_scatter(
            local_grads[1].astype(jnp.bfloat16), FSDP, scatter_dimension=0, tiled=True
        ).astype(jnp.float32),
        lax.psum_scatter(
            local_grads[2].astype(jnp.bfloat16), FSDP, scatter_dimension=0, tiled=True
        ).astype(jnp.float32),
        lax.psum_scatter(
            local_grads[3].astype(jnp.bfloat16), FSDP, scatter_dimension=0, tiled=True
        ).astype(jnp.float32),
        lax.psum_scatter(
            local_grads[4].astype(jnp.bfloat16), FSDP, scatter_dimension=0, tiled=True
        ).astype(jnp.float32),
        lax.psum_scatter(
            local_grads[5].astype(jnp.bfloat16), FSDP, scatter_dimension=0, tiled=True
        ).astype(jnp.float32),
        lax.psum_scatter(
            local_grads[6].astype(jnp.bfloat16), FSDP, scatter_dimension=0, tiled=True
        ).astype(jnp.float32),
        lax.psum_scatter(
            local_grads[7].astype(jnp.bfloat16), FSDP, scatter_dimension=0, tiled=True
        ).astype(jnp.float32),
        lax.psum_scatter(
            local_grads[8].astype(jnp.bfloat16), FSDP, scatter_dimension=0, tiled=True
        ).astype(jnp.float32),
        lax.psum_scatter(
            local_grads[9].astype(jnp.bfloat16), FSDP, scatter_dimension=0, tiled=True
        ).astype(jnp.float32),
        lax.psum_scatter(
            local_grads[10].astype(jnp.bfloat16), FSDP, scatter_dimension=0, tiled=True
        ).astype(jnp.float32),
        lax.psum_scatter(
            local_grads[11].astype(jnp.bfloat16), FSDP, scatter_dimension=0, tiled=True
        ).astype(jnp.float32),
        lax.psum_scatter(
            local_grads[12].astype(jnp.bfloat16), FSDP, scatter_dimension=0, tiled=True
        ).astype(jnp.float32),
        lax.psum_scatter(
            local_grads[13].astype(jnp.bfloat16), FSDP, scatter_dimension=0, tiled=True
        ).astype(jnp.float32),
        lax.psum_scatter(
            local_grads[14].astype(jnp.bfloat16), FSDP, scatter_dimension=0, tiled=True
        ).astype(jnp.float32),
    )
    totals = (
        lax.psum(shards[0].astype(jnp.bfloat16), RING).astype(jnp.float32),
        lax.psum(shards[1].astype(jnp.bfloat16), RING).astype(jnp.float32),
        lax.psum(shards[2].astype(jnp.bfloat16), RING).astype(jnp.float32),
        lax.psum(shards[3].astype(jnp.bfloat16), RING).astype(jnp.float32),
        lax.psum(shards[4].astype(jnp.bfloat16), RING).astype(jnp.float32),
        lax.psum(shards[5].astype(jnp.bfloat16), RING).astype(jnp.float32),
        lax.psum(shards[6].astype(jnp.bfloat16), RING).astype(jnp.float32),
        lax.psum(shards[7].astype(jnp.bfloat16), RING).astype(jnp.float32),
        lax.psum(shards[8].astype(jnp.bfloat16), RING).astype(jnp.float32),
        lax.psum(shards[9].astype(jnp.bfloat16), RING).astype(jnp.float32),
        lax.psum(shards[10].astype(jnp.bfloat16), RING).astype(jnp.float32),
        lax.psum(shards[11].astype(jnp.bfloat16), RING).astype(jnp.float32),
        lax.psum(shards[12].astype(jnp.bfloat16), RING).astype(jnp.float32),
        lax.psum(shards[13].astype(jnp.bfloat16), RING).astype(jnp.float32),
        lax.psum(shards[14].astype(jnp.bfloat16), RING).astype(jnp.float32),
    )
    return (
        layer_output,
        input_grad,
        totals[0],
        totals[1],
        totals[2],
        totals[3],
        totals[4],
        totals[5],
        totals[6],
        totals[7],
        totals[8],
        totals[9],
        totals[10],
        totals[11],
        totals[12],
        totals[13],
        totals[14],
    )


def solution(mesh):
    small = mesh.shape[RING] == CTX and mesh.shape[FSDP] == GROUP
    return jax.shard_map(
        small_plane if small else per_device,
        mesh=mesh,
        in_specs=(
            P(FSDP, RING, None),
            P(),
            P(FSDP, None),
            P(FSDP),
            P(FSDP, None),
            P(FSDP, None),
            P(FSDP),
            P(FSDP, None),
            P(FSDP),
            P(FSDP),
            P(FSDP),
            P(FSDP, None),
            P(FSDP),
            P(FSDP, None),
            P(FSDP),
            P(FSDP),
            P(FSDP),
            P(FSDP, RING, None),
        ),
        out_specs=(
            P(FSDP, RING, None),
            P(FSDP, RING, None),
            P(FSDP, None),
            P(FSDP),
            P(FSDP, None),
            P(FSDP, None),
            P(FSDP),
            P(FSDP, None),
            P(FSDP),
            P(FSDP),
            P(FSDP),
            P(FSDP, None),
            P(FSDP),
            P(FSDP, None),
            P(FSDP),
            P(FSDP),
            P(FSDP),
        ),
        check_vma=False,
    )
```

```python
import functools

import jax
import jax.numpy as jnp
from jax import lax
from jax.experimental import pallas as pl
from jax.experimental.pallas import tpu as pltpu
from jax.sharding import PartitionSpec as P

RING = "ctx"
FSDP = "fsdp"
D = 768
H = 12
HD = 64


epsilon = 1e-05


def passed_along(value, axis, steps):
    count = lax.axis_size(axis)
    pairs = [(source, (source + steps) % count) for source in range(count)]
    return lax.ppermute(value, axis, pairs)


def normalize(hidden):
    centred = hidden - jnp.mean(hidden, axis=1, keepdims=True)
    scale = lax.rsqrt(jnp.mean(centred * centred, axis=1, keepdims=True) + epsilon)
    return (centred * scale, scale)


def norm_back(upstream, normed, scale, gain):
    gain_grad = jnp.sum(upstream * normed, axis=0)
    shift_grad = jnp.sum(upstream, axis=0)
    scaled = upstream * gain
    hidden_grad = scale * (
        scaled
        - jnp.mean(scaled, axis=1, keepdims=True)
        - normed * jnp.mean(scaled * normed, axis=1, keepdims=True)
    )
    return (hidden_grad, gain_grad, shift_grad)


def gelu_slope(inner):
    return (
        0.5 * (1.0 + lax.erf(inner * 0.7071067811865476))
        + inner * jnp.exp(-0.5 * inner * inner) * 0.3989422804014327
    )


bf16 = jnp.bfloat16
f32 = jnp.float32
FF = 3072
ROWS = 384
CTX = 8
GROUP = 4
LOCAL = 3
SLOTS = 3072
QUERIES = 1536
TILE = 768
CHUNK = 512
WIDE = 640
MESH = pl.DeviceIdType.MESH


def multiple(value, step):
    return pl.multiple_of(value * step, step)


class Place:
    def __init__(self):
        self.c = lax.axis_index(RING)
        self.z = lax.axis_index(FSDP)
        c = self.c
        self.core = c % 2
        self.p = c // 2
        self.x = self.p % 2
        self.y = c // 4
        self.p_x = self.p + 1 - 2 * self.x
        self.p_y = self.p + 2 - 4 * self.y
        self.p_d = self.p_y + 1 - 2 * self.x
        self.to_core = (c + 1 - 2 * self.core, self.z)
        self.to_x = (2 * self.p_x + self.core, self.z)
        self.to_y = (2 * self.p_y + self.core, self.z)
        self.to_d = (2 * self.p_d + self.core, self.z)

    def to_z(self, step):
        return (self.c, (self.z + step) % GROUP)

    def from_z(self, step):
        return (self.z + GROUP - step) % GROUP


class Net:
    def __init__(self, sends, receives):
        self.sends = sends
        self.receives = receives
        self.index = {}
        self.open = []

    def of(self, name):
        return self.index.setdefault(name, len(self.index))

    def copy(self, name, src, dst, device):
        i = self.of(name)
        return pltpu.make_async_remote_copy(
            src_ref=src,
            dst_ref=dst,
            send_sem=self.sends.at[i],
            recv_sem=self.receives.at[i],
            device_id=device,
            device_id_type=MESH,
        )

    def start(self, name, src, dst, device):
        self.launch(name, lambda: (src, dst, device))

    def launch(self, name, make, when=None):
        if when is None:
            self.copy(name, *make()).start()
        else:
            pl.when(when())(lambda: self.copy(name, *make()).start())
        self.open.append((name, make, when))

    def sent(self, name, make, when):
        if when is None:
            self.copy(name, *make()).wait_send()
        else:
            pl.when(when())(lambda: self.copy(name, *make()).wait_send())

    def landed(self, name, dst, device):
        self.copy(name, dst, dst, device).wait_recv()

    def finish(self, name):
        for entry in self.open:
            if entry[0] == name:
                self.sent(*entry)
        self.open = [entry for entry in self.open if entry[0] != name]

    def drain(self):
        for entry in self.open:
            self.sent(*entry)
        self.open = []


def greet(place, with_z=True):
    barrier = pltpu.get_barrier_semaphore()
    partners = [place.to_core, place.to_x, place.to_y, place.to_d]
    if with_z:
        partners += [place.to_z(step) for step in range(1, GROUP)]
    for partner in partners:
        pl.semaphore_signal(barrier, inc=1, device_id=partner, device_id_type=MESH)
    pl.semaphore_wait(barrier, len(partners))


def dot(a, b):
    return jnp.dot(a, b, preferred_element_type=f32)


def dot_nt(a, b):
    return lax.dot_general(a, b, (((1,), (1,)), ((), ())), preferred_element_type=f32)


def dot_tn(a, b):
    return lax.dot_general(a, b, (((0,), (0,)), ((), ())), preferred_element_type=f32)


def parts_of(value):
    high = value.astype(bf16).astype(f32)
    rest = value - high
    middle = rest.astype(bf16).astype(f32)
    return high, middle, rest - middle


def added(a, b):
    return (a.astype(f32) + b.astype(f32)).astype(bf16)


def forward_kernel(
    lengths,
    x_in,
    wqkv_in,
    vec_in,
    inner_in,
    outer_in,
    wo_in,
    cot_in,
    low_out,
    mg_out,
    gi_out,
    gw_out,
    own_out,
    summed_out,
    hg_out,
    small_out,
    xs_out,
    wqkv_out,
    qt_out,
    ka_out,
    va_out,
    kt_out,
    ot_out,
    lse_out,
    xall,
    wqkv,
    vec,
    qt,
    ka,
    va,
    kt,
    vt,
    ot,
    lse,
    mix,
    mixed,
    acc,
    top,
    iw,
    ow,
    wo,
    cot,
    work,
    first,
    normed,
    second,
    slope,
    act,
    low,
    lower,
    gi,
    gw,
    mg,
    small,
    scales,
    ro,
    ax,
    ay,
    az,
    summed,
    sends,
    receives,
    locals_,
):
    at = Place()
    net = Net(sends, receives)
    c, z, core, p = at.c, at.z, at.core, at.p
    other = 1 - core
    chips = [at.p_d, at.p_x, at.p_y, p]
    devices = [at.to_d, at.to_x, at.to_y]
    slots = []

    def local(src, dst):
        copy = pltpu.make_async_copy(src, dst, locals_.at[len(slots)])
        slots.append(copy)
        copy.start()
        return copy

    def inner_at(ref, chip, side):
        return ref.at[:, pl.ds(multiple(2 * chip + side, 384), 384)]

    def outer_at(ref, chip, side):
        return ref.at[0, 2 * chip + side]

    def wo_at(ref, chip, side):
        return ref.at[chip, :, pl.ds(multiple(side, 384), 384)]

    weights = {
        "wo": (wo_in, wo, wo_at),
        "inner": (inner_in, iw, inner_at),
        "outer": (outer_in, ow, outer_at),
    }

    def block_at(chip, side, part=slice(None)):
        return xall.at[chip, side, part]

    greet(at)

    early, late = pl.ds(0, 2), pl.ds(2, 2)
    net.start("sx0", x_in.at[early], block_at(p, core, early), at.to_x)
    net.start("sy1", x_in.at[late], block_at(p, core, late), at.to_y)
    net.start("sx1", x_in.at[late], block_at(p, core, late), at.to_x)
    net.start("sy0", x_in.at[early], block_at(p, core, early), at.to_y)
    net.start("sc", x_in, block_at(p, core), at.to_core)
    for step in range(1, GROUP):
        net.start(("vec", step), vec_in, vec.at[z], at.to_z(step))
    class Along:
        def __init__(self, name, source, region):
            self.name = name
            self.source = source
            self.region = region

        def send(self):
            name, source, region = self.name, self.source, self.region
            for step in (2, 1, 3):
                when = {1: lambda: z < 3, 2: None, 3: lambda: z > 0}[step]

                def make(step=step):
                    return source, region(z), at.to_z(step)

                net.launch((name, "z", step), make, when)

        def relay(self):
            name, region = self.name, self.region

            def up():
                net.copy((name, "z", 2), region(z - 2), region(z - 2), at.to_z(2)).wait_recv()

            def down():
                net.copy((name, "z", 2), region(z + 2), region(z + 2), at.to_z(2)).wait_recv()

            pl.when(z == 2)(up)
            pl.when(z == 1)(down)
            net.launch(
                (name, "u"), lambda: (region(0), region(0), at.to_z(1)), lambda: z == 2
            )
            net.launch(
                (name, "d"), lambda: (region(3), region(3), at.to_z(3)), lambda: z == 1
            )

        def landed(self, step):
            name, region = self.name, self.region
            ref = region(at.from_z(step))
            if step == 1:
                pl.when(z > 0)(lambda: net.landed((name, "z", 1), region(at.from_z(1)), at.to_z(1)))
                pl.when(z == 0)(lambda: net.landed((name, "d"), region(3), at.to_z(1)))
            elif step == 3:
                pl.when(z < 3)(lambda: net.landed((name, "z", 3), region(at.from_z(3)), at.to_z(3)))
                pl.when(z == 3)(lambda: net.landed((name, "u"), region(0), at.to_z(3)))
            else:
                pl.when((z == 0) | (z == 3))(
                    lambda: net.landed((name, "z", 2), region(at.from_z(2)), at.to_z(2))
                )
            return ref

    along = {"wq": Along("wq", wqkv_in.at[core], lambda shard: wqkv.at[shard, core])}
    for name, (src, dst, region) in weights.items():
        along[name] = Along(
            name,
            region(src, p, core),
            lambda shard, dst=dst, region=region: region(dst.at[shard], p, core),
        )

    def far_at(shard, side):
        return ow.at[shard, 1, pl.ds(4 * side, 4)]

    along["far"] = Along(
        "far", outer_in.at[1, pl.ds(4 * core, 4)], lambda shard: far_at(shard, core)
    )
    along["wq"].send()
    opening = [local(x_in, block_at(p, core)), local(vec_in, vec.at[z]), local(wqkv_in, wqkv.at[z])]
    owned = [
        local(wo_in, wo.at[z]),
        local(inner_in, iw.at[z]),
        local(outer_in, ow.at[z]),
        local(cot_in, cot),
    ]

    row64 = lax.broadcasted_iota(jnp.int32, (64, QUERIES), 0)
    row16 = lax.broadcasted_iota(jnp.int32, (16, SLOTS), 0)
    for h in range(LOCAL):
        qt[h, 64:128, :] = jnp.where(row64 == 0, 1.0, 0.0).astype(bf16)
        vt[h, 64:80, :] = jnp.where(row16 == 0, 1.0, 0.0).astype(bf16)

    along["wq"].relay()
    along["wo"].send()
    along["inner"].send()
    p_x, p_y, p_d = at.p_x, at.p_y, at.p_d

    def hand_on(label, ref, device):
        net.start(label, ref, ref, device)

    net.landed("sx0", block_at(p_x, core, early), at.to_x)
    hand_on("rx0", block_at(p_x, core, early), at.to_y)
    net.landed("sy1", block_at(p_y, core, late), at.to_y)
    hand_on("ry1", block_at(p_y, core, late), at.to_x)
    for step in range(1, GROUP):
        source = at.from_z(step)
        along["wq"].landed(step)
        net.start(("wqc", step), wqkv.at[source, core], wqkv.at[source, core], at.to_core)
    along["wo"].relay()
    net.landed("sx1", block_at(p_x, core, late), at.to_x)
    hand_on("cx", block_at(p_x, core), at.to_core)
    net.landed("sy0", block_at(p_y, core, early), at.to_y)
    hand_on("cy", block_at(p_y, core), at.to_core)
    for copy in opening:
        copy.wait()
    for step in range(1, GROUP):
        source = at.from_z(step)
        net.landed(("vec", step), vec.at[source], at.to_z(step))
        net.landed(("wqc", step), wqkv.at[source, other], at.to_core)

    bias = vec[p][0:1, 0:WIDE].astype(f32)
    lane = lax.broadcasted_iota(jnp.int32, (ROWS, 128), 1)
    row = lax.broadcasted_iota(jnp.int32, (ROWS, 128), 0)
    count = lengths[z]

    def project(chip, side, column):
        block = 2 * chip + side
        rows = xall[chip, side].reshape(ROWS, D)
        keep = block * ROWS + row < count
        mark = jnp.where(keep, 0.0, -1e30)
        at_rows = pl.ds(multiple(block, ROWS), ROWS)
        width = 384 if column is None else WIDE
        full = wqkv[...].reshape(D, WIDE)
        y = dot(rows, full[:, 0:width]) + bias[:, 0:width]
        for h in range(LOCAL):
            g = y[:, 128 * h : 128 * h + 128]
            ka[h, at_rows, :] = jnp.where(
                lane < 64, g, jnp.where(lane == 64, mark, jnp.where(lane < 68, 1.0, 0.0))
            ).astype(bf16)
            va[h, at_rows, :] = jnp.where(
                lane < 64, pltpu.roll(g, 64, 1), jnp.where(lane < 67, 1.0, 0.0)
            ).astype(bf16)
            turned = g.T.astype(bf16)
            kt[h, :, at_rows] = turned[0:64]
            vt[h, 0:64, at_rows] = turned[64:128]
        if column is not None:
            q = (y[:, 384:WIDE] * 0.125).T.astype(bf16)
            for h in range(LOCAL):
                qt[h, 0:64, pl.ds(multiple(column, ROWS), ROWS)] = q[64 * h : 64 * h + 64]

    def chip_of(i):
        return p + (i % 2) * (1 - 2 * at.x) + (i // 2) * (2 - 4 * at.y)

    def project_own(i, carried):
        project(chip_of(i), core, 3 * (1 - (i + 1) // 2) + i * ((i + 1) // 2))
        return carried

    def project_other(i, carried):
        project(chip_of(i), other, None)
        return carried

    along["outer"].send()
    lax.fori_loop(0, 3, project_own, 0)
    net.landed("sc", block_at(p, other), at.to_core)
    net.landed("cx", block_at(p_x, other), at.to_core)
    net.landed("cy", block_at(p_y, other), at.to_core)
    lax.fori_loop(0, 3, project_other, 0)
    net.landed("rx0", block_at(p_d, core, early), at.to_y)
    net.landed("ry1", block_at(p_d, core, late), at.to_x)
    hand_on("cd", block_at(p_d, core), at.to_core)
    project(p_d, core, 0)
    net.landed("cd", block_at(p_d, other), at.to_core)
    project(p_d, other, None)

    kept = [local(block_at(chips[r], core), xs_out.at[r]) for r in range(4)]
    for src, dst in (
        (wqkv, wqkv_out),
        (qt, qt_out),
        (ka, ka_out),
        (va, va_out),
        (kt, kt_out),
    ):
        local(src, dst)

    def part_of(name, step, chip, side):
        _, dst, region = weights[name]
        return region(dst.at[at.from_z(step)], chip, side)

    def hand(label, name, step, chip, device):
        def make():
            ref = part_of(name, step, chip, core)
            return ref, ref, device

        net.launch(label, make)

    steps_all = tuple(range(1, GROUP))

    def plane_out(name, steps=steps_all):
        for step in steps:
            along[name].landed(step)
            hand((name, "x", step), name, step, p, at.to_x)
            hand((name, "y", step), name, step, p, at.to_y)
            hand((name, "c", step), name, step, p, at.to_core)

    def relay_by_x(name, step):
        return (step + (name == "outer")) % 2 == 1

    def plane_relay(name, steps=steps_all):
        for step in steps:
            net.landed((name, "x", step), part_of(name, step, p_x, core), at.to_x)
            net.landed((name, "y", step), part_of(name, step, p_y, core), at.to_y)
            if relay_by_x(name, step):
                hand((name, "r", step), name, step, p_y, at.to_x)
            else:
                hand((name, "r", step), name, step, p_x, at.to_y)
            hand((name, "cx", step), name, step, p_x, at.to_core)
            hand((name, "cy", step), name, step, p_y, at.to_core)

    def plane_last(name, steps=steps_all):
        for step in steps:
            far = part_of(name, step, p_d, core)
            net.landed((name, "r", step), far, at.to_x if relay_by_x(name, step) else at.to_y)
            hand((name, "cd", step), name, step, p_d, at.to_core)

    def plane_in(name):
        for step in steps_all:
            for tag, chip in (("c", p), ("cx", p_x), ("cy", p_y), ("cd", p_d)):
                net.landed((name, tag, step), part_of(name, step, chip, other), at.to_core)

    plane_out("wo")
    along["inner"].relay()

    def attend(h, tile):
        cols = pl.ds(multiple(tile, TILE), TILE)
        queries = qt[h, :, cols]
        top[0:1, :] = jnp.full((1, TILE), -3e38, f32)
        acc[...] = jnp.zeros((80, TILE), f32)

        def some(half, carried):
            for j in range(SLOTS // CHUNK // 2):
                rows = pl.ds(multiple(half * (SLOTS // CHUNK // 2) + j, CHUNK), CHUNK)
                scores = dot(ka[h, rows, :], queries)
                before = top[0:1, :]
                newest = jnp.maximum(before, jnp.max(scores, axis=0, keepdims=True))
                probs = jnp.exp(scores - newest).astype(bf16)
                acc[...] = acc[...] * jnp.exp(before - newest) + dot(vt[h, :, rows], probs)
                top[0:1, :] = newest
            return carried

        lax.fori_loop(0, 2, some, 0)
        total = acc[64:65, :]
        value = acc[0:64, :] / total
        ot[h, :, cols] = value
        lse[h, 0:1, cols] = top[0:1, :] + jnp.log(total)
        low_value = value.astype(bf16)
        at_head = pl.ds(multiple(h, 64), 64)
        mix[2 * tile, at_head, :] = low_value[:, 0:384]
        mix[2 * tile + 1, at_head, :] = low_value[:, 384:768]

    def send_mixed(name, index, device):
        net.launch(name, lambda: (mix.at[index], mixed.at[p], device))

    plan = {
        1: [lambda: plane_relay("wo"), lambda: plane_out("inner")],
        2: [
            lambda: plane_last("wo"),
            along["outer"].relay,
            along["far"].send,
            lambda: plane_relay("inner", (1,)),
        ],
        3: [
            lambda: send_mixed("md", 0, at.to_d),
            lambda: send_mixed("mx", 1, at.to_x),
            lambda: plane_relay("inner", (2,)),
        ],
        4: [lambda: plane_relay("inner", (3,))],
        5: [lambda: plane_out("outer"), lambda: plane_last("inner")],
    }

    def take(steps):
        for step in steps:
            step()

    def unit(u, carried):
        for when, steps in plan.items():
            pl.when(u == when)(functools.partial(take, steps))
        attend(u % LOCAL, u // LOCAL)
        return carried

    lax.fori_loop(0, 2 * LOCAL, unit, 0)
    send_mixed("my", 2, at.to_y)
    along["far"].relay()
    mixed[p] = mix[3]
    local(ot, ot_out)
    local(lse, lse_out)

    plane_in("wo")
    for copy in owned:
        copy.wait()
    net.landed("md", mixed.at[p_d], at.to_d)
    net.landed("mx", mixed.at[p_x], at.to_x)
    net.landed("my", mixed.at[p_y], at.to_y)
    table = vec[0].astype(f32) + vec[1].astype(f32) + vec[2].astype(f32) + vec[3].astype(f32)
    output_add, gain_one, shift_one, outer_add, gain_two, shift_two = [
        table[2 + i : 3 + i, :] for i in range(6)
    ]
    heads = mixed[...].reshape(D, ROWS)
    work[...] = dot_tn(heads, wo[...].reshape(D, D))
    low[...] = xall[p, core].reshape(ROWS, D)

    def blocks(step, start=0):
        def one(i, carried):
            return step(pl.ds(multiple(i, 128), 128), i, carried)

        return lax.fori_loop(0, ROWS // 128, one, start)

    def mean(value):
        return jnp.mean(value, axis=1, keepdims=True)

    def column(value):
        return jnp.sum(value, axis=0, keepdims=True)

    def norm(hidden):
        centred = hidden - mean(hidden)
        scale = lax.rsqrt(mean(centred * centred) + 1e-05)
        return centred * scale, scale

    def first_norm(rows, i, carried):
        value, scale = norm(low[rows, :].astype(f32) + work[rows, :] + output_add)
        normed[rows, :] = value
        scales[0, rows, :] = jnp.broadcast_to(scale, (128, 128))
        value = value * gain_one + shift_one
        first[rows, :] = value
        low[rows, :] = value.astype(bf16)
        return carried

    blocks(first_norm)
    plane_relay("outer")
    for step in steps_all:
        along["far"].landed(step)
        source = at.from_z(step)
        net.start(("farc", step), far_at(source, core), far_at(source, core), at.to_core)

    plane_in("inner")
    inner_weight = iw[...].reshape(D, FF)
    for q in range(4):
        cols = pl.ds(D * q, D)
        slope[:, cols] = dot(low[...], inner_weight[:, D * q : D * q + D])
        add = vec[q][1:2, :].astype(f32)

        def activate(rows, i, carried, cols=cols, add=add):
            u = slope[rows, cols] + add
            gate = 0.5 * (1.0 + lax.erf(u * 0.7071067811865476))
            act[rows, cols] = (u * gate).astype(bf16)
            slope[rows, cols] = gate + u * jnp.exp(-0.5 * u * u) * 0.3989422804014327
            return carried

        blocks(activate)
        if q == 1:
            plane_last("outer")
    plane_in("outer")
    for step in steps_all:
        net.landed(("farc", step), far_at(at.from_z(step), other), at.to_core)
    total = None
    for q in range(4):
        term = dot(act[:, D * q : D * q + D], ow[q].reshape(D, D))
        total = term if total is None else total + term
    work[...] = total

    nothing = jnp.zeros((1, D), f32)

    def second_norm(rows, i, carried):
        gains, shifts, biases = carried
        value, scale = norm(first[rows, :] + work[rows, :] + outer_add)
        slot = c * ROWS + i * 128 + lax.broadcasted_iota(jnp.int32, (128, D), 0)
        keep = slot < count
        lower[rows, :] = jnp.where(keep, value * gain_two + shift_two, 0.0).astype(bf16)
        upstream = jnp.where(keep, cot[rows, :].astype(f32), 0.0)
        product = upstream * value
        scaled = upstream * gain_two
        grad = scale * (scaled - mean(scaled) - value * mean(scaled * value))
        second[rows, :] = grad
        cot[rows, :] = grad.astype(bf16)
        return gains + column(product), shifts + column(upstream), biases + column(grad)

    gain_two_grad, shift_two_grad, outer_bias_grad = blocks(second_norm, (nothing,) * 3)
    local(lower, low_out)

    for copy in kept:
        copy.wait()
    for name in ("rx0", "ry1", "cx", "cy", "cd"):
        net.finish(name)
    def outer_row(t, chip, side):
        j = 2 * chip + side
        return xall.at[t, j // 4, j % 4]

    for q in range(4):
        term = dot_tn(act[:, D * q : D * q + D], cot[...]).astype(bf16)
        xall[q] = term.reshape(2, 4, 96, D)
        for r in range(4):
            net.start(("go", q, r), outer_row(q, chips[r], other), ro.at[r, q], at.to_core)

    upper, under = pl.ds(0, 48), pl.ds(48, 48)

    def outer_pair(chip, shard):
        j = 2 * chip + core
        return xall.at[pl.ds(shard, 2), j // 4, j % 4, under]

    def outer_add_core():
        for q in range(4):
            for r in range(4):
                net.landed(("go", q, r), ro.at[r, q], at.to_core)

        def one(t, carried):
            for r in range(4):
                ref = outer_row(t, chips[r], core)
                ref[...] = added(ref[...], ro[r, t])
            return carried

        lax.fori_loop(0, GROUP, one, 0)
        net.start("oxn", outer_pair(p_x, 0), ax.at[0], at.to_x)
        net.start("oyn", outer_pair(p_y, 2), ay.at[0], at.to_y)
        net.start("oxd", outer_pair(p_d, 0), ax.at[1], at.to_x)
        net.start("oyd", outer_pair(p_d, 2), ay.at[1], at.to_y)

        for r in range(2):
            for step in (2, 1, 3):
                device = at.to_z(step)
                net.start(
                    ("uz", r, step),
                    outer_row(device[1], chips[r], core).at[upper],
                    az.at[r, step - 1],
                    device,
                )

    def outer_add_shards():
        for r in range(2):
            total = outer_row(z, chips[r], core).at[upper][...].astype(f32)
            for step in steps_all:
                net.landed(("uz", r, step), az.at[r, step - 1], at.to_z(step))
                total = total + az[r, step - 1].astype(f32)
            summed[r] = total.astype(bf16)
        local(summed, summed_out)

    def outer_add_plane():
        net.landed("oxn", ax.at[0], at.to_x)
        net.landed("oyn", ay.at[0], at.to_y)
        net.landed("oxd", ax.at[1], at.to_x)
        net.landed("oyd", ay.at[1], at.to_y)
        for t in range(2):
            for shard, chip, ref in (
                (t, p, ax.at[0, t]),
                (t, p_y, ax.at[1, t]),
                (t + 2, p, ay.at[0, t]),
                (t + 2, p_x, ay.at[1, t]),
            ):
                row = outer_row(shard, chip, core).at[under]
                row[...] = added(row[...], ref[...])

    total = None
    for q in range(4):
        cols = pl.ds(D * q, D)
        work[...] = dot_nt(cot[...], ow[q].reshape(D, D))

        def slopes(rows, i, carried, cols=cols):
            grad = work[rows, :] * slope[rows, cols]
            act[rows, cols] = grad.astype(bf16)
            return carried + column(grad)

        small[q, 1:2, :] = blocks(slopes, nothing)
        grads = act[:, D * q : D * q + D]
        term = dot_nt(grads, inner_weight[:, D * q : D * q + D])
        total = term if total is None else total + term
        if q == 0:
            outer_add_core()
    work[...] = total

    def first_back(rows, i, carried):
        gains, shifts, biases = carried
        value = normed[rows, :]
        upstream = second[rows, :] + work[rows, :]
        scaled = upstream * gain_one
        grad = scales[0, rows, 0:1] * (scaled - mean(scaled) - value * mean(scaled * value))
        first[rows, :] = grad
        lower_grad[rows, :] = grad.astype(bf16)
        return gains + column(upstream * value), shifts + column(upstream), biases + column(grad)

    lower_grad = cot
    gain_one_grad, shift_one_grad, output_bias_grad = blocks(first_back, (nothing,) * 3)
    local(first, hg_out)
    mg[...] = dot_nt(wo[...].reshape(D, D), lower_grad[...]).astype(bf16).reshape(GROUP, 192, ROWS)
    for r in range(3):
        net.start(("mg", r), mg.at[chips[r]], mg_out.at[r], devices[r])
    local(mg.at[p], mg_out.at[3])
    for q in range(4):
        grads = act[:, D * q : D * q + D]
        gi[:, :, D * q : D * q + D] = dot_tn(low[...], grads).astype(bf16).reshape(GROUP, 192, D)
    local(gi, gi_out)
    gw[...] = dot(heads, lower_grad[...]).astype(bf16).reshape(GROUP, GROUP, 48, D)
    local(gw, gw_out)
    narrow = [
        output_bias_grad,
        gain_one_grad,
        shift_one_grad,
        outer_bias_grad,
        gain_two_grad,
        shift_two_grad,
    ]
    for t in range(GROUP):
        small[t, 0:1, :] = nothing
        for i, value in enumerate(narrow):
            small[t, 2 + i : 3 + i, :] = value
    local(small, small_out)
    outer_add_plane()
    outer_add_shards()
    for r in range(4):
        j = 2 * chips[r] + core
        local(xall.at[:, j // 4, j % 4], own_out.at[r])
    for r in range(3):
        net.landed(("mg", r), mg_out.at[r], devices[r])
    waited = len(opening) + len(owned)
    for copy in slots[waited:]:
        if not any(copy is other_copy for other_copy in kept):
            copy.wait()
    net.drain()


FORWARD_COPIES = 140


def forward_call(*operands):
    any_ = pl.BlockSpec(memory_space=pl.ANY)
    shape = jax.ShapeDtypeStruct
    vmem = pltpu.VMEM
    return pl.pallas_call(
        forward_kernel,
        name="forward_attention",
        out_shape=(
            shape((ROWS, D), bf16),
            shape((4, 192, ROWS), bf16),
            shape((GROUP, 192, FF), bf16),
            shape((GROUP, GROUP, 48, D), bf16),
            shape((4, GROUP, 96, D), bf16),
            shape((2, 48, D), bf16),
            shape((ROWS, D), f32),
            shape((GROUP, 8, D), f32),
            shape((4, 4, 96, D), bf16),
            shape((GROUP, 2, 96, WIDE), bf16),
            shape((LOCAL, 128, QUERIES), bf16),
            shape((LOCAL, SLOTS, 128), bf16),
            shape((LOCAL, SLOTS, 128), bf16),
            shape((LOCAL, 64, SLOTS), bf16),
            shape((LOCAL, 64, QUERIES), f32),
            shape((LOCAL, 8, QUERIES), f32),
        ),
        in_specs=[pl.BlockSpec(memory_space=pltpu.SMEM)] + [any_] * 7,
        out_specs=[any_] * 16,
        scratch_shapes=[
            vmem((GROUP, 2, 4, 96, D), bf16),
            vmem((GROUP, 2, 96, WIDE), bf16),
            vmem((GROUP, 16, D), bf16),
            vmem((LOCAL, 128, QUERIES), bf16),
            vmem((LOCAL, SLOTS, 128), bf16),
            vmem((LOCAL, SLOTS, 128), bf16),
            vmem((LOCAL, 64, SLOTS), bf16),
            vmem((LOCAL, 80, SLOTS), bf16),
            vmem((LOCAL, 64, QUERIES), f32),
            vmem((LOCAL, 8, QUERIES), f32),
            vmem((4, 192, ROWS), bf16),
            vmem((GROUP, 192, ROWS), bf16),
            vmem((80, TILE), f32),
            vmem((8, TILE), f32),
            vmem((GROUP, 192, FF), bf16),
            vmem((GROUP, 2, CTX, 48, D), bf16),
            vmem((GROUP, GROUP, 48, D), bf16),
            vmem((ROWS, D), bf16),
            vmem((ROWS, D), f32),
            vmem((ROWS, D), f32),
            vmem((ROWS, D), f32),
            vmem((ROWS, D), f32),
            vmem((ROWS, FF), f32),
            vmem((ROWS, FF), bf16),
            vmem((ROWS, D), bf16),
            vmem((ROWS, D), bf16),
            vmem((GROUP, 192, FF), bf16),
            vmem((GROUP, GROUP, 48, D), bf16),
            vmem((GROUP, 192, ROWS), bf16),
            vmem((GROUP, 8, D), f32),
            vmem((1, ROWS, 128), f32),
            vmem((4, GROUP, 96, D), bf16),
            vmem((2, 2, 48, D), bf16),
            vmem((2, 2, 48, D), bf16),
            vmem((2, 3, 48, D), bf16),
            vmem((2, 48, D), bf16),
            pltpu.SemaphoreType.DMA((FORWARD_COPIES,)),
            pltpu.SemaphoreType.DMA((FORWARD_COPIES,)),
            pltpu.SemaphoreType.DMA((48,)),
        ],
        compiler_params=pltpu.CompilerParams(
            collective_id=0, has_side_effects=True, vmem_limit_bytes=67043328
        ),
    )(*operands)


def split_weights(place_p, query_weight, key_weight, value_weight):
    def columns(weight):
        return lax.dynamic_slice_in_dim(weight, place_p * 192, 192, axis=1)

    rows = query_weight.shape[0]
    pair = jnp.concatenate(
        [columns(key_weight).reshape(rows, 3, 64), columns(value_weight).reshape(rows, 3, 64)],
        axis=2,
    ).reshape(rows, 384)
    fill = jnp.zeros((rows, 64), bf16)
    return jnp.concatenate([pair, columns(query_weight), fill], axis=1).reshape(2, 96, WIDE)


def pack_vectors(query_bias, value_bias, inner_bias, vectors):
    nothing = jnp.zeros((3, 64), bf16)
    first = jnp.concatenate(
        [
            jnp.concatenate([nothing, value_bias.reshape(3, 64)], axis=1).reshape(384),
            query_bias,
            jnp.zeros((192,), bf16),
        ]
    )
    rest = jnp.stack(vectors)[:, None, :]
    mine = lax.broadcasted_iota(jnp.int32, (1, GROUP, 1), 1) == lax.axis_index(FSDP)
    rest = jnp.where(mine, rest, 0).astype(bf16).reshape(len(vectors), D)
    return jnp.concatenate([first[None], inner_bias[None], rest, jnp.zeros((8, D), bf16)])


SPAN = 256


def backward_kernel(
    mg_in,
    ot_in,
    lse_in,
    qt_in,
    ka_in,
    va_in,
    kt_in,
    gi_in,
    gw_in,
    own_in,
    summed_in,
    xs_in,
    wqkv_in,
    hg_in,
    small_in,
    dx_out,
    gqkv_out,
    gi_out,
    go_out,
    gw_out,
    small_out,
    mg,
    ot,
    lse,
    qa,
    qz,
    ka,
    va,
    kt,
    da,
    dz,
    kv,
    rkv,
    dq,
    so,
    si,
    ri,
    aix,
    aiy,
    boy,
    box,
    az,
    su,
    ux,
    uy,
    vx,
    vy,
    done_o,
    biy,
    bix,
    zo,
    zi,
    xs,
    wqkv,
    dqkv,
    sdx,
    rx,
    ry,
    bx,
    by,
    hg,
    dw,
    dwl,
    rdw,
    rzw,
    small,
    rsz,
    rsc,
    rsp,
    ssum,
    sends,
    receives,
    locals_,
):
    at = Place()
    net = Net(sends, receives)
    c, z, core, p = at.c, at.z, at.core, at.p
    other = 1 - core
    chips = [at.p_d, at.p_x, at.p_y, p]
    devices = [at.to_d, at.to_x, at.to_y]
    slots = []

    def local(src, dst):
        copy = pltpu.make_async_copy(src, dst, locals_.at[len(slots)])
        slots.append(copy)
        copy.start()
        return copy

    greet(at)
    upper, under = pl.ds(0, 48), pl.ds(48, 48)
    fore, aft = pl.ds(0, 2), pl.ds(2, 2)
    front, back = pl.ds(0, 384), pl.ds(384, 384)
    net.start("oby", own_in.at[2, fore, under], boy, at.to_y)
    net.start("obx", own_in.at[1, aft, under], box, at.to_x)
    for r in range(2, 4):
        for step in (2, 1, 3):
            device = at.to_z(step)
            net.start(
                ("uz", r, step), own_in.at[r, device[1], upper], az.at[r - 2, step - 1], device
            )
    loads = [
        local(mg_in, mg),
        local(ot_in, ot),
        local(lse_in, lse),
        local(qt_in, qa),
        local(ka_in, ka),
        local(va_in, va),
        local(kt_in, kt),
    ]

    def i_at(chip, side):
        return gi_in.at[:, :, pl.ds(multiple(2 * chip + side, 384), 384)]

    def w_at(chip, side):
        return gw_in.at[:, chip, :, pl.ds(multiple(side, 384), 384)]

    halves = [local(own_in, so), local(summed_in, su.at[pl.ds(0, 2)])]
    for r in range(4):
        net.start(("gi", r), i_at(chips[r], other), ri.at[r, :, 0:192], at.to_core)
        net.start(("gw", r), w_at(chips[r], other), ri.at[r, :, 192:240], at.to_core)
        halves.append(local(i_at(chips[r], core), si.at[r, :, 0:192]))
        halves.append(local(w_at(chips[r], core), si.at[r, :, 192:240]))
    later = [local(wqkv_in, wqkv), local(hg_in, hg), local(small_in, small)]
    for r in range(4):
        later.append(local(xs_in.at[r], xs.at[r]))

    for copy in loads:
        copy.wait()
    row16 = lax.broadcasted_iota(jnp.int32, (16, QUERIES), 0)
    row128 = lax.broadcasted_iota(jnp.int32, (128, QUERIES), 0)
    for h in range(LOCAL):
        high, middle, rest = parts_of(-lse[h, 0:1, :])
        qz[h] = jnp.where(row128 < 64, qa[h].astype(f32), 0.0).astype(bf16)
        qa[h, 64:80, :] = jnp.where(
            row16 == 0,
            1.0,
            jnp.where(
                row16 == 1, high, jnp.where(row16 == 2, middle, jnp.where(row16 == 3, rest, 0.0))
            ),
        ).astype(bf16)
        kv[h] = jnp.zeros((SLOTS, 128), f32)
        dz[h, 0:64, :] = jnp.zeros((64, QUERIES), bf16)
        da[h, 80:128, :] = jnp.zeros((48, QUERIES), bf16)
    row16 = lax.broadcasted_iota(jnp.int32, (16, ROWS), 0)
    for r in range(4):
        cols = pl.ds(ROWS * r, ROWS)
        for h in range(LOCAL):
            grad = mg[r, 64 * h : 64 * h + 64, :]
            delta = jnp.sum(grad.astype(f32) * ot[h, :, cols], axis=0, keepdims=True)
            high, middle, rest = parts_of(-delta)
            da[h, 0:64, cols] = grad
            dz[h, 64:128, cols] = grad
            da[h, 64:80, cols] = jnp.where(
                row16 == 0,
                high,
                jnp.where(row16 == 1, middle, jnp.where(row16 == 2, rest, 0.0)),
            ).astype(bf16)

    left, right = pl.ds(0, 128), pl.ds(128, 112)

    def along_shards(step):
        def one(t, carried):
            step(t)
            return carried

        lax.fori_loop(0, GROUP, one, 0)

    upper, under = pl.ds(0, 48), pl.ds(48, 48)

    def outer_second():
        halves[0].wait()
        net.landed("oby", boy, at.to_y)
        net.landed("obx", box, at.to_x)
        for t in range(2):
            so[3, t, under] = added(so[3, t, under], boy[t])
            so[3, t + 2, under] = added(so[3, t + 2, under], box[t])
        for i in range(1, GROUP):
            net.launch(
                ("oz", i),
                lambda i=i: (so.at[3, at.to_z(i)[1], under], zo.at[i - 1], at.to_z(i)),
            )

    def outer_shards():
        halves[1].wait()
        for r in range(2, 4):
            total = so[r, z, upper].astype(f32)
            for i in range(1, GROUP):
                net.landed(("uz", r, i), az.at[r - 2, i - 1], at.to_z(i))
                total = total + az[r - 2, i - 1].astype(f32)
            su[r] = total.astype(bf16)
        net.launch("uxn", lambda: (su.at[1, :, front], ux.at[0], at.to_x))
        net.launch("uyn", lambda: (su.at[2, :, back], uy.at[0], at.to_y))
        net.launch("uxd", lambda: (su.at[0, :, front], ux.at[1], at.to_x))
        net.launch("uyd", lambda: (su.at[0, :, back], uy.at[1], at.to_y))

    def outer_third():
        net.landed("uxn", ux.at[0], at.to_x)
        net.landed("uyn", uy.at[0], at.to_y)
        net.landed("uxd", ux.at[1], at.to_x)
        net.landed("uyd", uy.at[1], at.to_y)
        su[2, :, front] = added(su[2, :, front], ux[1])
        su[1, :, back] = added(su[1, :, back], uy[1])
        net.launch("uby", lambda: (su.at[2, :, front], vy, at.to_y))
        net.launch("ubx", lambda: (su.at[1, :, back], vx, at.to_x))
        su[3, :, front] = added(su[3, :, front], ux[0])
        su[3, :, back] = added(su[3, :, back], uy[0])

    def outer_last():
        total = so[3, z, under].astype(f32)
        for i in range(1, GROUP):
            net.landed(("oz", i), zo.at[i - 1], at.to_z(i))
            total = total + zo[i - 1].astype(f32)
        done_o[48:96] = total.astype(bf16)
        net.landed("uby", vy, at.to_y)
        net.landed("ubx", vx, at.to_x)
        done_o[0:48, front] = added(su[3, :, front], vy[...])
        done_o[0:48, back] = added(su[3, :, back], vx[...])

    def inner_core():
        for copy in halves[2:]:
            copy.wait()
        for r in range(4):
            net.landed(("gi", r), ri.at[r, :, 0:192], at.to_core)
            net.landed(("gw", r), ri.at[r, :, 192:240], at.to_core)

        def step(t):
            for r in range(4):
                si[r, t] = added(si[r, t], ri[r, t])

        along_shards(step)
        net.launch("ixn", lambda: (si.at[1, :, left], aix.at[0], at.to_x))
        net.launch("iyn", lambda: (si.at[2, :, right], aiy.at[0], at.to_y))
        net.launch("ixd", lambda: (si.at[0, :, left], aix.at[1], at.to_x))
        net.launch("iyd", lambda: (si.at[0, :, right], aiy.at[1], at.to_y))

    def inner_first():
        net.landed("ixn", aix.at[0], at.to_x)
        net.landed("iyn", aiy.at[0], at.to_y)
        net.landed("ixd", aix.at[1], at.to_x)
        net.landed("iyd", aiy.at[1], at.to_y)

        def step(t):
            si[2, t, left] = added(si[2, t, left], aix[1, t])
            si[1, t, right] = added(si[1, t, right], aiy[1, t])
            si[3, t, left] = added(si[3, t, left], aix[0, t])
            si[3, t, right] = added(si[3, t, right], aiy[0, t])

        along_shards(step)
        net.launch("iby", lambda: (si.at[2, :, left], biy, at.to_y))
        net.launch("ibx", lambda: (si.at[1, :, right], bix, at.to_x))

    def inner_second():
        net.landed("iby", biy, at.to_y)
        net.landed("ibx", bix, at.to_x)

        def step(t):
            si[3, t, left] = added(si[3, t, left], biy[t])
            si[3, t, right] = added(si[3, t, right], bix[t])

        along_shards(step)
        for i in range(1, GROUP):
            net.launch(
                ("iz", i), lambda i=i: (si.at[3, at.to_z(i)[1]], zi.at[i - 1], at.to_z(i))
            )

    def inner_last():
        total = si[3, z].astype(f32)
        for i in range(1, GROUP):
            net.landed(("iz", i), zi.at[i - 1], at.to_z(i))
            total = total + zi[i - 1].astype(f32)
        si[3, z] = total.astype(bf16)

    def go_at(chip, side):
        return go_out.at[2 * chip + side]

    def gi_at(chip, side):
        return gi_out.at[:, pl.ds(multiple(2 * chip + side, 384), 384)]

    def gw_at(chip, side):
        return gw_out.at[chip, :, pl.ds(multiple(side, 384), 384)]

    place_of = {"o": go_at, "i": gi_at, "w": gw_at}
    via_x = {"o": False, "i": True, "w": False}
    mine = {
        "o": lambda: done_o,
        "i": lambda: si.at[3, z, 0:192],
        "w": lambda: si.at[3, z, 192:240],
    }

    def spread(name):
        place = place_of[name]
        for tag, device in (("x", at.to_x), ("y", at.to_y), ("c", at.to_core)):
            net.launch(
                ("f", name, tag), lambda device=device: (mine[name](), place(p, core), device)
            )

    def pass_on(name):
        place = place_of[name]

        def hand(tag, chip, device):
            net.launch(
                ("f", name, tag), lambda: (place(chip, core), place(chip, core), device)
            )

        net.landed(("f", name, "x"), place(at.p_x, core), at.to_x)
        net.landed(("f", name, "y"), place(at.p_y, core), at.to_y)
        if via_x[name]:
            hand("r", at.p_y, at.to_x)
        else:
            hand("r", at.p_x, at.to_y)
        hand("cx", at.p_x, at.to_core)
        hand("cy", at.p_y, at.to_core)

    def finish_spread(name):
        place = place_of[name]
        far = place(at.p_d, core)
        net.landed(("f", name, "r"), far, at.to_x if via_x[name] else at.to_y)
        net.start(("f", name, "cd"), far, far, at.to_core)

    def close_spread(name):
        place = place_of[name]
        for tag, chip in (("c", p), ("cx", at.p_x), ("cy", at.p_y), ("cd", at.p_d)):
            net.landed(("f", name, tag), place(chip, other), at.to_core)

    def swap_kv(h):
        for r in range(4):
            net.launch(
                ("kv", h, r),
                lambda r=r: (
                    kv.at[h, pl.ds(multiple(2 * chips[r] + other, ROWS), ROWS)],
                    rkv.at[h, r],
                    at.to_core,
                ),
            )

    def attend(h, tile):
        cols = pl.ds(multiple(tile, TILE), TILE)
        queries = qa[h, :, cols]
        upstream = da[h, :, cols]
        queries_only = qz[h, :, cols]
        upstream_only = dz[h, :, cols]
        dq[h, :, cols] = jnp.zeros((64, TILE), f32)

        def some(half, carried):
            for j in range(SLOTS // SPAN // 2):
                rows = pl.ds(multiple(half * (SLOTS // SPAN // 2) + j, SPAN), SPAN)
                probs = jnp.exp(dot(ka[h, rows, :], queries))
                grads = (probs * dot(va[h, rows, :], upstream)).astype(bf16)
                kv[h, rows, :] += dot_nt(grads, queries_only) + dot_nt(
                    probs.astype(bf16), upstream_only
                )
                dq[h, :, cols] += dot(kt[h, :, rows], grads)
            return carried

        lax.fori_loop(0, 2, some, 0)

    plan = {
        1: [inner_core, outer_second],
        2: [lambda: swap_kv(0)],
        3: [outer_shards],
        4: [lambda: swap_kv(1), inner_first, outer_third],
        5: [outer_last, lambda: spread("o"), inner_second],
    }

    def take(steps):
        for step in steps:
            step()

    def unit(u, carried):
        for when, steps in plan.items():
            pl.when(u == when)(functools.partial(take, steps))
        attend(u // 2, u % 2)
        return carried

    lax.fori_loop(0, 2 * LOCAL, unit, 0)
    swap_kv(2)
    pass_on("o")
    local(done_o, go_at(p, core))

    for copy in later:
        copy.wait()
    weights = wqkv[...].reshape(D, WIDE)
    for h in range(LOCAL):
        for r in range(4):
            net.landed(("kv", h, r), rkv.at[h, r], at.to_core)
    sums = jnp.zeros((1, WIDE), f32)
    top, low = pl.ds(0, 192), pl.ds(192, 192)
    for r in range(4):
        cols = pl.ds(ROWS * r, ROWS)
        rows = pl.ds(multiple(2 * chips[r] + core, ROWS), ROWS)
        for h in range(LOCAL):
            dqkv[r, :, 128 * h : 128 * h + 128] = (kv[h, rows, :] + rkv[h, r]).astype(bf16)
        turned = jnp.concatenate(
            [dq[h, :, cols] for h in range(LOCAL)] + [jnp.zeros((64, ROWS), f32)], axis=0
        )
        dqkv[r, :, 384:WIDE] = (turned.T * 0.125).astype(bf16)
        block = dqkv[r]
        sums = sums + jnp.sum(block.astype(f32), axis=0, keepdims=True)
        update = dot_nt(block, weights)
        if r < 3:
            sdx[r] = update.astype(bf16)
        else:
            hg[...] += update
        if r == 1:
            net.start("dxn", sdx.at[1, top], rx.at[0], at.to_x)
            net.start("dxd", sdx.at[0, top], rx.at[1], at.to_x)
        if r == 2:
            net.start("dyn", sdx.at[2, low], ry.at[0], at.to_y)
            net.start("dyd", sdx.at[0, low], ry.at[1], at.to_y)
    small[p, 0:1, 0:WIDE] += sums
    for step in range(1, GROUP):
        net.start(("sz", step), small.at[at.to_z(step)[1]], rsz.at[step - 1], at.to_z(step))

    total = None
    for r in range(4):
        term = lax.dot_general(
            xs[r].reshape(ROWS, D), dqkv[r], (((0,), (0,)), ((), ())), preferred_element_type=f32
        )
        total = term if total is None else total + term
    dw[...] = total.reshape(GROUP, 2, 96, WIDE)
    dwl[...] = dw[:, other].astype(bf16)
    net.start("dwc", dwl, rdw, at.to_core)

    for step in range(1, GROUP):
        net.landed(("sz", step), rsz.at[step - 1], at.to_z(step))
    small[z] = small[z] + rsz[0] + rsz[1] + rsz[2]
    net.start("sc", small.at[z], rsc, at.to_core)
    net.landed("dwc", rdw, at.to_core)
    for t in range(GROUP):
        rdw[t] = added(dw[t, core], rdw[t])
    for step in range(1, GROUP):
        net.start(("dwz", step), rdw.at[at.to_z(step)[1]], rzw.at[step - 1], at.to_z(step))
    net.landed("sc", rsc, at.to_core)
    rsc[...] = small[z] + rsc[...]
    for r in range(3):
        net.start(("sp", r), rsc, rsp.at[r], devices[r])

    net.landed("dxn", rx.at[0], at.to_x)
    net.landed("dxd", rx.at[1], at.to_x)
    sdx[2, top] = added(sdx[2, top], rx[1])
    net.start("dby", sdx.at[2, top], by, at.to_y)
    net.landed("dyn", ry.at[0], at.to_y)
    net.landed("dyd", ry.at[1], at.to_y)
    sdx[1, low] = added(sdx[1, low], ry[1])
    net.start("dbx", sdx.at[1, low], bx, at.to_x)
    hg[top] += rx[0].astype(f32)
    hg[low] += ry[0].astype(f32)

    inner_last()
    for name in ("i", "w"):
        spread(name)
        local(mine[name](), place_of[name](p, core))

    for step in range(1, GROUP):
        net.landed(("dwz", step), rzw.at[step - 1], at.to_z(step))
    finished = rdw[z].astype(f32)
    for step in range(GROUP - 1):
        finished = finished + rzw[step].astype(f32)
    rdw[z] = finished.astype(bf16)
    for r in range(3):
        net.start(("fq", r), rdw.at[z], gqkv_out.at[p, core], devices[r])
    net.start("fqc", rdw.at[z], gqkv_out.at[p, core], at.to_core)
    local(rdw.at[z], gqkv_out.at[p, core])

    for r in range(3):
        net.landed(("sp", r), rsp.at[r], devices[r])
    ssum[...] = rsc[...] + rsp[0] + rsp[1] + rsp[2]
    local(ssum, small_out)

    for name in ("i", "w"):
        pass_on(name)
    for r in range(3):
        ref = gqkv_out.at[chips[r], core]
        net.landed(("fq", r), ref, devices[r])
        net.start(("fqc", r), ref, ref, at.to_core)

    net.landed("dby", by, at.to_y)
    net.landed("dbx", bx, at.to_x)
    sdx[3, top] = (hg[top] + by[...].astype(f32)).astype(bf16)
    sdx[3, low] = (hg[low] + bx[...].astype(f32)).astype(bf16)
    local(sdx.at[3], dx_out)

    for name in ("o", "i", "w"):
        finish_spread(name)
    for name in ("o", "i", "w"):
        close_spread(name)
    net.landed("fqc", gqkv_out.at[p, other], at.to_core)
    for r in range(3):
        net.landed(("fqc", r), gqkv_out.at[chips[r], other], at.to_core)
    done = len(loads) + len(halves) + len(later)
    for copy in slots[done:]:
        copy.wait()
    net.drain()


BACKWARD_COPIES = 110


def backward_call(*operands):
    any_ = pl.BlockSpec(memory_space=pl.ANY)
    shape = jax.ShapeDtypeStruct
    vmem = pltpu.VMEM
    return pl.pallas_call(
        backward_kernel,
        name="backward_attention",
        out_shape=(
            shape((ROWS, D), bf16),
            shape((GROUP, 2, 96, WIDE), bf16),
            shape((192, FF), bf16),
            shape((CTX, 96, D), bf16),
            shape((GROUP, 48, D), bf16),
            shape((8, D), f32),
        ),
        in_specs=[any_] * 15,
        out_specs=[any_] * 6,
        scratch_shapes=[
            vmem((4, 192, ROWS), bf16),
            vmem((LOCAL, 64, QUERIES), f32),
            vmem((LOCAL, 8, QUERIES), f32),
            vmem((LOCAL, 128, QUERIES), bf16),
            vmem((LOCAL, 128, QUERIES), bf16),
            vmem((LOCAL, SLOTS, 128), bf16),
            vmem((LOCAL, SLOTS, 128), bf16),
            vmem((LOCAL, 64, SLOTS), bf16),
            vmem((LOCAL, 128, QUERIES), bf16),
            vmem((LOCAL, 128, QUERIES), bf16),
            vmem((LOCAL, SLOTS, 128), f32),
            vmem((LOCAL, 4, ROWS, 128), f32),
            vmem((LOCAL, 64, QUERIES), f32),
            vmem((4, GROUP, 96, D), bf16),
            vmem((4, GROUP, 240, 384), bf16),
            vmem((4, GROUP, 240, 384), bf16),
            vmem((2, GROUP, 128, 384), bf16),
            vmem((2, GROUP, 112, 384), bf16),
            vmem((2, 48, D), bf16),
            vmem((2, 48, D), bf16),
            vmem((2, 3, 48, D), bf16),
            vmem((4, 48, D), bf16),
            vmem((2, 48, 384), bf16),
            vmem((2, 48, 384), bf16),
            vmem((48, 384), bf16),
            vmem((48, 384), bf16),
            vmem((96, D), bf16),
            vmem((GROUP, 128, 384), bf16),
            vmem((GROUP, 112, 384), bf16),
            vmem((3, 48, D), bf16),
            vmem((3, 240, 384), bf16),
            vmem((4, 4, 96, D), bf16),
            vmem((GROUP, 2, 96, WIDE), bf16),
            vmem((4, ROWS, WIDE), bf16),
            vmem((4, ROWS, D), bf16),
            vmem((2, 192, D), bf16),
            vmem((2, 192, D), bf16),
            vmem((192, D), bf16),
            vmem((192, D), bf16),
            vmem((ROWS, D), f32),
            vmem((GROUP, 2, 96, WIDE), f32),
            vmem((GROUP, 96, WIDE), bf16),
            vmem((GROUP, 96, WIDE), bf16),
            vmem((3, 96, WIDE), bf16),
            vmem((GROUP, 8, D), f32),
            vmem((3, 8, D), f32),
            vmem((8, D), f32),
            vmem((3, 8, D), f32),
            vmem((8, D), f32),
            pltpu.SemaphoreType.DMA((BACKWARD_COPIES,)),
            pltpu.SemaphoreType.DMA((BACKWARD_COPIES,)),
            pltpu.SemaphoreType.DMA((48,)),
        ],
        compiler_params=pltpu.CompilerParams(
            collective_id=1, has_side_effects=True, vmem_limit_bytes=63 << 20
        ),
    )(*operands)


def finish_kernel(
    low_in, dx_in, gqkv_in, gi_in, go_in, gw_in,
    low_out, dx_out, q_out, k_out, v_out, gi_out, go_out, gw_out,
    low, dx, gqkv, gi, go, gw, q, k, v, wide_i, wide_o, wide_w, reads, writes,
):
    loads = [
        pltpu.make_async_copy(src, dst, reads.at[i])
        for i, (src, dst) in enumerate(
            ((gi_in, gi), (go_in, go), (gw_in, gw), (gqkv_in, gqkv), (low_in, low), (dx_in, dx))
        )
    ]
    for copy in loads:
        copy.start()
    stores = []

    def store(src, dst):
        copy = pltpu.make_async_copy(src, dst, writes.at[len(stores)])
        stores.append(copy)
        copy.start()

    for copy, narrow, wide, dst in (
        (loads[0], gi, wide_i, gi_out),
        (loads[1], go, wide_o, go_out),
        (loads[2], gw, wide_w, gw_out),
    ):
        copy.wait()
        wide[...] = narrow[...].astype(f32)
        store(wide, dst)
    loads[3].wait()
    lane = lax.broadcasted_iota(jnp.int32, (192, 128), 1)

    def piece(chip, tile, side, wanted):
        value = gqkv[chip, :, 128 * tile : 128 * tile + 128].astype(f32)
        return value if side == wanted else pltpu.roll(value, 64, 1)

    for tile in range(6):
        cols = pl.ds(128 * tile, 128)
        left, right = [divmod(g, LOCAL) for g in (2 * tile, 2 * tile + 1)]
        for ref, place in (
            (k, lambda h: (h, 0)),
            (v, lambda h: (h, 1)),
            (q, lambda h: (3 + h // 2, h % 2)),
        ):
            a = piece(left[0], *place(left[1]), 0)
            b = piece(right[0], *place(right[1]), 1)
            ref[:, cols] = jnp.where(lane < 64, a, b)
    for src, dst in ((q, q_out), (k, k_out), (v, v_out)):
        store(src, dst)
    loads[4].wait()
    store(low, low_out)
    loads[5].wait()
    store(dx, dx_out)
    for copy in stores:
        copy.wait()


def finish_call(*operands):
    any_ = pl.BlockSpec(memory_space=pl.ANY)
    vmem = pltpu.VMEM
    square, wide = (192, D), (192, FF)
    shapes = [((ROWS, D), bf16)] * 2 + [(square, f32)] * 3
    shapes += [(wide, f32), ((D, D), f32), (square, f32)]
    return pl.pallas_call(
        finish_kernel,
        name="finish",
        out_shape=[jax.ShapeDtypeStruct(*pair) for pair in shapes],
        in_specs=[any_] * 6,
        out_specs=[any_] * 8,
        scratch_shapes=[
            vmem((ROWS, D), bf16),
            vmem((ROWS, D), bf16),
            vmem((GROUP, 192, WIDE), bf16),
            vmem(wide, bf16),
            vmem((D, D), bf16),
            vmem(square, bf16),
            vmem(square, f32),
            vmem(square, f32),
            vmem(square, f32),
            vmem(wide, f32),
            vmem((D, D), f32),
            vmem(square, f32),
            pltpu.SemaphoreType.DMA((6,)),
            pltpu.SemaphoreType.DMA((8,)),
        ],
        compiler_params=pltpu.CompilerParams(vmem_limit_bytes=67043328),
    )(*operands)


def small_plane(
    states,
    lengths,
    query_weight,
    query_bias,
    key_weight,
    value_weight,
    value_bias,
    output_weight,
    output_bias,
    first_gain,
    first_shift,
    inner_weight,
    inner_bias,
    outer_weight,
    outer_bias,
    second_gain,
    second_shift,
    cotangent,
):
    cycle_place = lax.axis_index(RING)
    shard = lax.axis_index(FSDP)
    wqkv = split_weights(cycle_place // 2, query_weight, key_weight, value_weight)
    vectors = pack_vectors(
        query_bias,
        value_bias,
        inner_bias,
        [output_bias, first_gain, first_shift, outer_bias, second_gain, second_shift],
    )
    low, mg, gi, gw, own, summed, hg, small, xs, wall, qt, ka, va, kt, ot, lse = (
        forward_call(
            lengths,
            states.reshape(4, 96, D),
            wqkv,
            vectors,
            inner_weight,
            outer_weight.reshape(2, CTX, 48, D),
            output_weight.reshape(GROUP, 48, D),
            cotangent[0],
        )
    )
    dx, gqkv, gi, go, gw, sums = backward_call(
        mg, ot, lse, qt, ka, va, kt, gi, gw, own, summed, xs, wall, hg, small
    )
    low, dx, gq, gk, gv, gi, go, gw = finish_call(
        low,
        dx,
        gqkv.reshape(GROUP, 192, WIDE),
        gi,
        go.reshape(D, D),
        gw.reshape(192, D),
    )
    narrow = lax.dynamic_slice_in_dim(sums[2:8], shard * 192, 192, axis=1)
    value_bias_grad = sums[0, :384].reshape(LOCAL, 2, 64)[:, 1].reshape(192)
    return (
        low[None],
        dx[None],
        gq,
        sums[0, 384:576],
        gk,
        gv,
        value_bias_grad,
        gw,
        narrow[0],
        narrow[1],
        narrow[2],
        gi,
        sums[1],
        go,
        narrow[3],
        narrow[4],
        narrow[5],
    )


def keep_state(carried):
    return carried


def per_device(
    states,
    lengths,
    query_weight,
    query_bias,
    key_weight,
    value_weight,
    value_bias,
    output_weight,
    output_bias,
    first_gain,
    first_shift,
    inner_weight,
    inner_bias,
    outer_weight,
    outer_bias,
    second_gain,
    second_shift,
    cotangent,
):
    row_count = states.shape[1]
    cycle_size = lax.axis_size(RING)
    cycle_place = lax.axis_index(RING)
    sequence = lax.axis_index(FSDP)
    length = lengths[sequence]
    offsets = jnp.arange(row_count, dtype=jnp.int32)
    row_keep = cycle_place * row_count + offsets < length
    inputs = states[0]
    input_float = inputs.astype(jnp.float32)
    attention_set = (
        lax.all_gather(query_weight, FSDP, axis=0, tiled=True),
        lax.all_gather(key_weight, FSDP, axis=0, tiled=True),
        lax.all_gather(value_weight, FSDP, axis=0, tiled=True),
        lax.all_gather(output_weight, FSDP, axis=0, tiled=True),
        lax.all_gather(query_bias, FSDP, axis=0, tiled=True),
        lax.all_gather(value_bias, FSDP, axis=0, tiled=True),
        lax.all_gather(output_bias, FSDP, axis=0, tiled=True),
        lax.all_gather(first_gain, FSDP, axis=0, tiled=True),
        lax.all_gather(first_shift, FSDP, axis=0, tiled=True),
    )
    query_full = attention_set[0]
    key_full = attention_set[1]
    value_full = attention_set[2]
    output_full = attention_set[3]
    query_add = attention_set[4].astype(jnp.float32)
    value_add = attention_set[5].astype(jnp.float32)
    output_add = attention_set[6].astype(jnp.float32)
    gain_one = attention_set[7].astype(jnp.float32)
    shift_one = attention_set[8].astype(jnp.float32)
    queries = (
        (jnp.dot(inputs, query_full, preferred_element_type=jnp.float32) + query_add) * 0.125
    ).astype(jnp.bfloat16)
    key_rows = jnp.dot(inputs, key_full, preferred_element_type=jnp.float32).astype(jnp.bfloat16)
    values = (jnp.dot(inputs, value_full, preferred_element_type=jnp.float32) + value_add).astype(
        jnp.bfloat16
    )
    query_heads = queries.reshape(row_count, H, HD)

    def forward_block(key_block, value_block, key_start, running_state):

        def forward_compute(carried):
            running, exp_total, accum = carried
            key_keep = key_start + offsets < length
            scores = jnp.einsum(
                "qhd,khd->hqk",
                query_heads,
                key_block.reshape(row_count, H, HD),
                preferred_element_type=jnp.float32,
            )
            scores = jnp.where(key_keep[None, None, :], scores, -1e30)
            newest = jnp.maximum(running, jnp.max(scores, axis=2))
            factor = jnp.exp(running - newest)
            weights = jnp.exp(scores - newest[:, :, None])
            exp_total = exp_total * factor + jnp.sum(weights, axis=2)
            update = jnp.einsum(
                "hqk,khd->qhd",
                weights.astype(jnp.bfloat16),
                value_block.reshape(row_count, H, HD),
                preferred_element_type=jnp.float32,
            )
            accum = accum * factor.T[:, :, None] + update
            return (newest, exp_total, accum)

        return lax.cond(key_start < length, forward_compute, keep_state, running_state)

    start_state = (
        jnp.full((H, row_count), -1e30, jnp.float32),
        jnp.zeros((H, row_count), jnp.float32),
        jnp.zeros((row_count, H, HD), jnp.float32),
    )

    def cycle_turn(turn_index, carried):
        key_block, value_block, running_state = carried
        owner_index = (cycle_place - turn_index) % cycle_size
        running_state = forward_block(
            key_block, value_block, owner_index * row_count, running_state
        )
        key_block, value_block = passed_along((key_block, value_block), RING, 1)
        return (key_block, value_block, running_state)

    key_block, value_block, running_state = lax.fori_loop(
        0, cycle_size - 1, cycle_turn, (key_rows, values, start_state)
    )
    last_owner = (cycle_place + 1) % cycle_size
    running, exp_total, accum = forward_block(
        key_block, value_block, last_owner * row_count, running_state
    )
    log_total = running + jnp.log(exp_total)
    attention_value = (accum / exp_total.T[:, :, None]).reshape(row_count, D)
    mixed = attention_value.astype(jnp.bfloat16)
    attended = jnp.dot(mixed, output_full, preferred_element_type=jnp.float32) + output_add
    first_normed, first_scale = normalize(input_float + attended)
    first = first_normed * gain_one + shift_one
    first_low = first.astype(jnp.bfloat16)
    feed_set = (
        lax.all_gather(inner_weight, FSDP, axis=0, tiled=True),
        lax.all_gather(outer_weight, FSDP, axis=0, tiled=True),
        lax.all_gather(inner_bias, FSDP, axis=0, tiled=True),
        lax.all_gather(outer_bias, FSDP, axis=0, tiled=True),
        lax.all_gather(second_gain, FSDP, axis=0, tiled=True),
        lax.all_gather(second_shift, FSDP, axis=0, tiled=True),
    )
    inner_full = feed_set[0]
    outer_full = feed_set[1]
    inner_add = feed_set[2].astype(jnp.float32)
    outer_add = feed_set[3].astype(jnp.float32)
    gain_two = feed_set[4].astype(jnp.float32)
    shift_two = feed_set[5].astype(jnp.float32)
    inner = jnp.dot(first_low, inner_full, preferred_element_type=jnp.float32) + inner_add
    activated = jax.nn.gelu(inner, approximate=False).astype(jnp.bfloat16)
    outer = jnp.dot(activated, outer_full, preferred_element_type=jnp.float32) + outer_add
    second_normed, second_scale = normalize(first + outer)
    second = second_normed * gain_two + shift_two
    layer_output = jnp.where(row_keep[:, None], second, 0.0).astype(jnp.bfloat16)[None]
    query_full = attention_set[0]
    key_full = attention_set[1]
    value_full = attention_set[2]
    output_full = attention_set[3]
    gain_one = attention_set[7].astype(jnp.float32)
    inner_full = feed_set[0]
    outer_full = feed_set[1]
    gain_two = feed_set[4].astype(jnp.float32)
    upstream = jnp.where(row_keep[:, None], cotangent[0].astype(jnp.float32), 0.0)
    second_grad, second_gain_grad, second_shift_grad = norm_back(
        upstream, second_normed, second_scale, gain_two
    )
    outer_low = second_grad.astype(jnp.bfloat16)
    outer_bias_grad = jnp.sum(second_grad, axis=0)
    outer_weight_grad = jnp.dot(activated.T, outer_low, preferred_element_type=jnp.float32)
    inner_grad = jnp.dot(outer_low, outer_full.T, preferred_element_type=jnp.float32) * gelu_slope(
        inner
    )
    inner_low = inner_grad.astype(jnp.bfloat16)
    inner_bias_grad = jnp.sum(inner_grad, axis=0)
    inner_weight_grad = jnp.dot(first_low.T, inner_low, preferred_element_type=jnp.float32)
    first_grad = second_grad + jnp.dot(inner_low, inner_full.T, preferred_element_type=jnp.float32)
    hidden_grad, first_gain_grad, first_shift_grad = norm_back(
        first_grad, first_normed, first_scale, gain_one
    )
    attended_low = hidden_grad.astype(jnp.bfloat16)
    output_bias_grad = jnp.sum(hidden_grad, axis=0)
    output_weight_grad = jnp.dot(mixed.T, attended_low, preferred_element_type=jnp.float32)
    mixed_grad = jnp.dot(attended_low, output_full.T, preferred_element_type=jnp.float32).astype(
        jnp.bfloat16
    )
    delta = jnp.sum(
        (mixed_grad.astype(jnp.float32) * attention_value).reshape(row_count, H, HD), axis=2
    ).T

    def back_block(
        query_block,
        upstream_block,
        log_block,
        delta_block,
        key_block,
        value_block,
        key_start,
        grads,
    ):

        def back_compute(carried):
            query_grad, key_grad, value_grad = carried
            key_keep = key_start + offsets < length
            query_three = query_block.reshape(row_count, H, HD)
            upstream_three = upstream_block.reshape(row_count, H, HD)
            key_three = key_block.reshape(row_count, H, HD)
            value_three = value_block.reshape(row_count, H, HD)
            scores = jnp.einsum(
                "qhd,khd->hqk", query_three, key_three, preferred_element_type=jnp.float32
            )
            weights = jnp.where(
                key_keep[None, None, :], jnp.exp(scores - log_block[:, :, None]), 0.0
            )
            weight_grad = jnp.einsum(
                "qhd,khd->hqk", upstream_three, value_three, preferred_element_type=jnp.float32
            )
            score_grad = (weights * (weight_grad - delta_block[:, :, None])).astype(jnp.bfloat16)
            query_grad = query_grad + jnp.einsum(
                "hqk,khd->qhd", score_grad, key_three, preferred_element_type=jnp.float32
            ).reshape(row_count, D)
            key_grad = key_grad + jnp.einsum(
                "hqk,qhd->khd", score_grad, query_three, preferred_element_type=jnp.float32
            ).reshape(row_count, D)
            value_grad = value_grad + jnp.einsum(
                "hqk,qhd->khd",
                weights.astype(jnp.bfloat16),
                upstream_three,
                preferred_element_type=jnp.float32,
            ).reshape(row_count, D)
            return (query_grad, key_grad, value_grad)

        return lax.cond(key_start < length, back_compute, keep_state, grads)

    zero_grad = jnp.zeros((row_count, D), jnp.float32)

    def key_turn(turn_index, carried):
        key_block, value_block, query_grad, key_grad, value_grad = carried
        owner_index = (cycle_place - turn_index) % cycle_size
        query_grad, key_grad, value_grad = back_block(
            queries,
            mixed_grad,
            log_total,
            delta,
            key_block,
            value_block,
            owner_index * row_count,
            (query_grad, key_grad, value_grad),
        )
        key_block, value_block = passed_along((key_block, value_block), RING, 1)
        key_grad, value_grad = (
            passed_along(key_grad.astype(jnp.bfloat16), RING, 1).astype(key_grad.dtype),
            passed_along(value_grad.astype(jnp.bfloat16), RING, 1).astype(value_grad.dtype),
        )
        return (key_block, value_block, query_grad, key_grad, value_grad)

    key_block, value_block, query_grad, key_grad, value_grad = lax.fori_loop(
        0, cycle_size - 1, key_turn, (key_rows, values, zero_grad, zero_grad, zero_grad)
    )
    query_grad, key_grad, value_grad = back_block(
        queries,
        mixed_grad,
        log_total,
        delta,
        key_block,
        value_block,
        last_owner * row_count,
        (query_grad, key_grad, value_grad),
    )
    key_grad, value_grad = (
        passed_along(key_grad.astype(jnp.bfloat16), RING, 1).astype(key_grad.dtype),
        passed_along(value_grad.astype(jnp.bfloat16), RING, 1).astype(value_grad.dtype),
    )
    query_low = query_grad.astype(jnp.bfloat16) * 0.125
    key_low = key_grad.astype(jnp.bfloat16)
    value_low = value_grad.astype(jnp.bfloat16)
    query_weight_grad = jnp.dot(inputs.T, query_low, preferred_element_type=jnp.float32)
    query_bias_grad = jnp.sum(query_low.astype(jnp.float32), axis=0)
    key_weight_grad = jnp.dot(inputs.T, key_low, preferred_element_type=jnp.float32)
    value_weight_grad = jnp.dot(inputs.T, value_low, preferred_element_type=jnp.float32)
    value_bias_grad = jnp.sum(value_low.astype(jnp.float32), axis=0)
    input_grad = (
        hidden_grad
        + jnp.dot(query_low, query_full.T, preferred_element_type=jnp.float32)
        + jnp.dot(key_low, key_full.T, preferred_element_type=jnp.float32)
        + jnp.dot(value_low, value_full.T, preferred_element_type=jnp.float32)
    ).astype(jnp.bfloat16)[None]
    local_grads = (
        query_weight_grad,
        query_bias_grad,
        key_weight_grad,
        value_weight_grad,
        value_bias_grad,
        output_weight_grad,
        output_bias_grad,
        first_gain_grad,
        first_shift_grad,
        inner_weight_grad,
        inner_bias_grad,
        outer_weight_grad,
        outer_bias_grad,
        second_gain_grad,
        second_shift_grad,
    )
    shards = (
        lax.psum_scatter(
            local_grads[0].astype(jnp.bfloat16), FSDP, scatter_dimension=0, tiled=True
        ).astype(jnp.float32),
        lax.psum_scatter(
            local_grads[1].astype(jnp.bfloat16), FSDP, scatter_dimension=0, tiled=True
        ).astype(jnp.float32),
        lax.psum_scatter(
            local_grads[2].astype(jnp.bfloat16), FSDP, scatter_dimension=0, tiled=True
        ).astype(jnp.float32),
        lax.psum_scatter(
            local_grads[3].astype(jnp.bfloat16), FSDP, scatter_dimension=0, tiled=True
        ).astype(jnp.float32),
        lax.psum_scatter(
            local_grads[4].astype(jnp.bfloat16), FSDP, scatter_dimension=0, tiled=True
        ).astype(jnp.float32),
        lax.psum_scatter(
            local_grads[5].astype(jnp.bfloat16), FSDP, scatter_dimension=0, tiled=True
        ).astype(jnp.float32),
        lax.psum_scatter(
            local_grads[6].astype(jnp.bfloat16), FSDP, scatter_dimension=0, tiled=True
        ).astype(jnp.float32),
        lax.psum_scatter(
            local_grads[7].astype(jnp.bfloat16), FSDP, scatter_dimension=0, tiled=True
        ).astype(jnp.float32),
        lax.psum_scatter(
            local_grads[8].astype(jnp.bfloat16), FSDP, scatter_dimension=0, tiled=True
        ).astype(jnp.float32),
        lax.psum_scatter(
            local_grads[9].astype(jnp.bfloat16), FSDP, scatter_dimension=0, tiled=True
        ).astype(jnp.float32),
        lax.psum_scatter(
            local_grads[10].astype(jnp.bfloat16), FSDP, scatter_dimension=0, tiled=True
        ).astype(jnp.float32),
        lax.psum_scatter(
            local_grads[11].astype(jnp.bfloat16), FSDP, scatter_dimension=0, tiled=True
        ).astype(jnp.float32),
        lax.psum_scatter(
            local_grads[12].astype(jnp.bfloat16), FSDP, scatter_dimension=0, tiled=True
        ).astype(jnp.float32),
        lax.psum_scatter(
            local_grads[13].astype(jnp.bfloat16), FSDP, scatter_dimension=0, tiled=True
        ).astype(jnp.float32),
        lax.psum_scatter(
            local_grads[14].astype(jnp.bfloat16), FSDP, scatter_dimension=0, tiled=True
        ).astype(jnp.float32),
    )
    totals = (
        lax.psum(shards[0].astype(jnp.bfloat16), RING).astype(jnp.float32),
        lax.psum(shards[1].astype(jnp.bfloat16), RING).astype(jnp.float32),
        lax.psum(shards[2].astype(jnp.bfloat16), RING).astype(jnp.float32),
        lax.psum(shards[3].astype(jnp.bfloat16), RING).astype(jnp.float32),
        lax.psum(shards[4].astype(jnp.bfloat16), RING).astype(jnp.float32),
        lax.psum(shards[5].astype(jnp.bfloat16), RING).astype(jnp.float32),
        lax.psum(shards[6].astype(jnp.bfloat16), RING).astype(jnp.float32),
        lax.psum(shards[7].astype(jnp.bfloat16), RING).astype(jnp.float32),
        lax.psum(shards[8].astype(jnp.bfloat16), RING).astype(jnp.float32),
        lax.psum(shards[9].astype(jnp.bfloat16), RING).astype(jnp.float32),
        lax.psum(shards[10].astype(jnp.bfloat16), RING).astype(jnp.float32),
        lax.psum(shards[11].astype(jnp.bfloat16), RING).astype(jnp.float32),
        lax.psum(shards[12].astype(jnp.bfloat16), RING).astype(jnp.float32),
        lax.psum(shards[13].astype(jnp.bfloat16), RING).astype(jnp.float32),
        lax.psum(shards[14].astype(jnp.bfloat16), RING).astype(jnp.float32),
    )
    return (
        layer_output,
        input_grad,
        totals[0],
        totals[1],
        totals[2],
        totals[3],
        totals[4],
        totals[5],
        totals[6],
        totals[7],
        totals[8],
        totals[9],
        totals[10],
        totals[11],
        totals[12],
        totals[13],
        totals[14],
    )


def solution(mesh):
    small = mesh.shape[RING] == CTX and mesh.shape[FSDP] == GROUP
    return jax.shard_map(
        small_plane if small else per_device,
        mesh=mesh,
        in_specs=(
            P(FSDP, RING, None),
            P(),
            P(FSDP, None),
            P(FSDP),
            P(FSDP, None),
            P(FSDP, None),
            P(FSDP),
            P(FSDP, None),
            P(FSDP),
            P(FSDP),
            P(FSDP),
            P(FSDP, None),
            P(FSDP),
            P(FSDP, None),
            P(FSDP),
            P(FSDP),
            P(FSDP),
            P(FSDP, RING, None),
        ),
        out_specs=(
            P(FSDP, RING, None),
            P(FSDP, RING, None),
            P(FSDP, None),
            P(FSDP),
            P(FSDP, None),
            P(FSDP, None),
            P(FSDP),
            P(FSDP, None),
            P(FSDP),
            P(FSDP),
            P(FSDP),
            P(FSDP, None),
            P(FSDP),
            P(FSDP, None),
            P(FSDP),
            P(FSDP),
            P(FSDP),
        ),
        check_vma=False,
    )
```

```python
import functools

import jax
import jax.numpy as jnp
from jax import lax
from jax.experimental import pallas as pl
from jax.experimental.pallas import tpu as pltpu
from jax.sharding import PartitionSpec as P

RING = "ctx"
FSDP = "fsdp"
D = 768
H = 12
HD = 64


epsilon = 1e-05


def passed_along(value, axis, steps):
    count = lax.axis_size(axis)
    pairs = [(source, (source + steps) % count) for source in range(count)]
    return lax.ppermute(value, axis, pairs)


def normalize(hidden):
    centred = hidden - jnp.mean(hidden, axis=1, keepdims=True)
    scale = lax.rsqrt(jnp.mean(centred * centred, axis=1, keepdims=True) + epsilon)
    return (centred * scale, scale)


def norm_back(upstream, normed, scale, gain):
    gain_grad = jnp.sum(upstream * normed, axis=0)
    shift_grad = jnp.sum(upstream, axis=0)
    scaled = upstream * gain
    hidden_grad = scale * (
        scaled
        - jnp.mean(scaled, axis=1, keepdims=True)
        - normed * jnp.mean(scaled * normed, axis=1, keepdims=True)
    )
    return (hidden_grad, gain_grad, shift_grad)


def gelu_slope(inner):
    return (
        0.5 * (1.0 + lax.erf(inner * 0.7071067811865476))
        + inner * jnp.exp(-0.5 * inner * inner) * 0.3989422804014327
    )


bf16 = jnp.bfloat16
f32 = jnp.float32
FF = 3072
ROWS = 384
CTX = 8
GROUP = 4
LOCAL = 3
SLOTS = 3072
QUERIES = 1536
TILE = 768
CHUNK = 512
WIDE = 640
MESH = pl.DeviceIdType.MESH


def multiple(value, step):
    return pl.multiple_of(value * step, step)


class Place:
    def __init__(self):
        self.c = lax.axis_index(RING)
        self.z = lax.axis_index(FSDP)
        c = self.c
        self.core = c % 2
        self.p = c // 2
        self.x = self.p % 2
        self.y = c // 4
        self.p_x = self.p + 1 - 2 * self.x
        self.p_y = self.p + 2 - 4 * self.y
        self.p_d = self.p_y + 1 - 2 * self.x
        self.to_core = (c + 1 - 2 * self.core, self.z)
        self.to_x = (2 * self.p_x + self.core, self.z)
        self.to_y = (2 * self.p_y + self.core, self.z)
        self.to_d = (2 * self.p_d + self.core, self.z)

    def to_z(self, step):
        return (self.c, (self.z + step) % GROUP)

    def from_z(self, step):
        return (self.z + GROUP - step) % GROUP


class Net:
    def __init__(self, sends, receives):
        self.sends = sends
        self.receives = receives
        self.index = {}
        self.open = []

    def of(self, name):
        return self.index.setdefault(name, len(self.index))

    def copy(self, name, src, dst, device):
        i = self.of(name)
        return pltpu.make_async_remote_copy(
            src_ref=src,
            dst_ref=dst,
            send_sem=self.sends.at[i],
            recv_sem=self.receives.at[i],
            device_id=device,
            device_id_type=MESH,
        )

    def start(self, name, src, dst, device):
        self.launch(name, lambda: (src, dst, device))

    def launch(self, name, make, when=None):
        if when is None:
            self.copy(name, *make()).start()
        else:
            pl.when(when())(lambda: self.copy(name, *make()).start())
        self.open.append((name, make, when))

    def sent(self, name, make, when):
        if when is None:
            self.copy(name, *make()).wait_send()
        else:
            pl.when(when())(lambda: self.copy(name, *make()).wait_send())

    def landed(self, name, dst, device):
        self.copy(name, dst, dst, device).wait_recv()

    def finish(self, name):
        for entry in self.open:
            if entry[0] == name:
                self.sent(*entry)
        self.open = [entry for entry in self.open if entry[0] != name]

    def drain(self):
        for entry in self.open:
            self.sent(*entry)
        self.open = []


def greet(place, with_z=True):
    barrier = pltpu.get_barrier_semaphore()
    partners = [place.to_core, place.to_x, place.to_y, place.to_d]
    if with_z:
        partners += [place.to_z(step) for step in range(1, GROUP)]
    for partner in partners:
        pl.semaphore_signal(barrier, inc=1, device_id=partner, device_id_type=MESH)
    pl.semaphore_wait(barrier, len(partners))


def dot(a, b):
    return jnp.dot(a, b, preferred_element_type=f32)


def dot_nt(a, b):
    return lax.dot_general(a, b, (((1,), (1,)), ((), ())), preferred_element_type=f32)


def dot_tn(a, b):
    return lax.dot_general(a, b, (((0,), (0,)), ((), ())), preferred_element_type=f32)


def parts_of(value):
    high = value.astype(bf16).astype(f32)
    rest = value - high
    middle = rest.astype(bf16).astype(f32)
    return high, middle, rest - middle


def added(a, b):
    return (a.astype(f32) + b.astype(f32)).astype(bf16)


def forward_kernel(
    lengths,
    x_in,
    wqkv_in,
    vec_in,
    inner_in,
    outer_in,
    wo_in,
    cot_in,
    low_out,
    mg_out,
    gi_out,
    gw_out,
    own_out,
    summed_out,
    hg_out,
    small_out,
    xs_out,
    wqkv_out,
    qt_out,
    ka_out,
    va_out,
    kt_out,
    ot_out,
    lse_out,
    xall,
    wqkv,
    vec,
    qt,
    ka,
    va,
    kt,
    vt,
    ot,
    lse,
    mix,
    mixed,
    acc,
    top,
    iw,
    ow,
    wo,
    cot,
    work,
    first,
    normed,
    second,
    slope,
    act,
    low,
    lower,
    gi,
    gw,
    mg,
    small,
    scales,
    ro,
    ax,
    ay,
    az,
    summed,
    sends,
    receives,
    locals_,
):
    at = Place()
    net = Net(sends, receives)
    c, z, core, p = at.c, at.z, at.core, at.p
    other = 1 - core
    chips = [at.p_d, at.p_x, at.p_y, p]
    devices = [at.to_d, at.to_x, at.to_y]
    slots = []

    def local(src, dst):
        copy = pltpu.make_async_copy(src, dst, locals_.at[len(slots)])
        slots.append(copy)
        copy.start()
        return copy

    def inner_at(ref, chip, side):
        return ref.at[:, pl.ds(multiple(2 * chip + side, 384), 384)]

    def outer_at(ref, chip, side):
        return ref.at[0, 2 * chip + side]

    def wo_at(ref, chip, side):
        return ref.at[chip, :, pl.ds(multiple(side, 384), 384)]

    weights = {
        "wo": (wo_in, wo, wo_at),
        "inner": (inner_in, iw, inner_at),
        "outer": (outer_in, ow, outer_at),
    }

    def block_at(chip, side, part=slice(None)):
        return xall.at[chip, side, part]

    greet(at)

    early, late = pl.ds(0, 2), pl.ds(2, 2)
    net.start("sx0", x_in.at[early], block_at(p, core, early), at.to_x)
    net.start("sy1", x_in.at[late], block_at(p, core, late), at.to_y)
    net.start("sx1", x_in.at[late], block_at(p, core, late), at.to_x)
    net.start("sy0", x_in.at[early], block_at(p, core, early), at.to_y)
    net.start("sc", x_in, block_at(p, core), at.to_core)
    for step in range(1, GROUP):
        net.start(("vec", step), vec_in, vec.at[z], at.to_z(step))
    class Along:
        def __init__(self, name, source, region):
            self.name = name
            self.source = source
            self.region = region

        def send(self):
            name, source, region = self.name, self.source, self.region
            for step in (2, 1, 3):
                when = {1: lambda: z < 3, 2: None, 3: lambda: z > 0}[step]

                def make(step=step):
                    return source, region(z), at.to_z(step)

                net.launch((name, "z", step), make, when)

        def relay(self):
            name, region = self.name, self.region

            def up():
                net.copy((name, "z", 2), region(z - 2), region(z - 2), at.to_z(2)).wait_recv()

            def down():
                net.copy((name, "z", 2), region(z + 2), region(z + 2), at.to_z(2)).wait_recv()

            pl.when(z == 2)(up)
            pl.when(z == 1)(down)
            net.launch(
                (name, "u"), lambda: (region(0), region(0), at.to_z(1)), lambda: z == 2
            )
            net.launch(
                (name, "d"), lambda: (region(3), region(3), at.to_z(3)), lambda: z == 1
            )

        def landed(self, step):
            name, region = self.name, self.region
            ref = region(at.from_z(step))
            if step == 1:
                pl.when(z > 0)(lambda: net.landed((name, "z", 1), region(at.from_z(1)), at.to_z(1)))
                pl.when(z == 0)(lambda: net.landed((name, "d"), region(3), at.to_z(1)))
            elif step == 3:
                pl.when(z < 3)(lambda: net.landed((name, "z", 3), region(at.from_z(3)), at.to_z(3)))
                pl.when(z == 3)(lambda: net.landed((name, "u"), region(0), at.to_z(3)))
            else:
                pl.when((z == 0) | (z == 3))(
                    lambda: net.landed((name, "z", 2), region(at.from_z(2)), at.to_z(2))
                )
            return ref

    along = {"wq": Along("wq", wqkv_in.at[core], lambda shard: wqkv.at[shard, core])}
    for name, (src, dst, region) in weights.items():
        along[name] = Along(
            name,
            region(src, p, core),
            lambda shard, dst=dst, region=region: region(dst.at[shard], p, core),
        )

    def far_at(shard, side):
        return ow.at[shard, 1, pl.ds(4 * side, 4)]

    along["far"] = Along(
        "far", outer_in.at[1, pl.ds(4 * core, 4)], lambda shard: far_at(shard, core)
    )
    along["wq"].send()
    opening = [local(x_in, block_at(p, core)), local(vec_in, vec.at[z]), local(wqkv_in, wqkv.at[z])]
    owned = [
        local(wo_in, wo.at[z]),
        local(inner_in, iw.at[z]),
        local(outer_in, ow.at[z]),
        local(cot_in, cot),
    ]

    row64 = lax.broadcasted_iota(jnp.int32, (64, QUERIES), 0)
    row16 = lax.broadcasted_iota(jnp.int32, (16, SLOTS), 0)
    for h in range(LOCAL):
        qt[h, 64:128, :] = jnp.where(row64 == 0, 1.0, 0.0).astype(bf16)
        vt[h, 64:80, :] = jnp.where(row16 == 0, 1.0, 0.0).astype(bf16)

    along["wq"].relay()
    along["wo"].send()
    along["inner"].send()
    p_x, p_y, p_d = at.p_x, at.p_y, at.p_d

    def hand_on(label, ref, device):
        net.start(label, ref, ref, device)

    net.landed("sx0", block_at(p_x, core, early), at.to_x)
    hand_on("rx0", block_at(p_x, core, early), at.to_y)
    net.landed("sy1", block_at(p_y, core, late), at.to_y)
    hand_on("ry1", block_at(p_y, core, late), at.to_x)
    for step in range(1, GROUP):
        source = at.from_z(step)
        along["wq"].landed(step)
        net.start(("wqc", step), wqkv.at[source, core], wqkv.at[source, core], at.to_core)
    along["wo"].relay()
    net.landed("sx1", block_at(p_x, core, late), at.to_x)
    hand_on("cx", block_at(p_x, core), at.to_core)
    net.landed("sy0", block_at(p_y, core, early), at.to_y)
    hand_on("cy", block_at(p_y, core), at.to_core)
    for copy in opening:
        copy.wait()
    for step in range(1, GROUP):
        source = at.from_z(step)
        net.landed(("vec", step), vec.at[source], at.to_z(step))
        net.landed(("wqc", step), wqkv.at[source, other], at.to_core)

    bias = vec[p][0:1, 0:WIDE].astype(f32)
    lane = lax.broadcasted_iota(jnp.int32, (ROWS, 128), 1)
    row = lax.broadcasted_iota(jnp.int32, (ROWS, 128), 0)
    count = lengths[z]

    def project(chip, side, column):
        block = 2 * chip + side
        rows = xall[chip, side].reshape(ROWS, D)
        keep = block * ROWS + row < count
        mark = jnp.where(keep, 0.0, -1e30)
        at_rows = pl.ds(multiple(block, ROWS), ROWS)
        width = 384 if column is None else WIDE
        full = wqkv[...].reshape(D, WIDE)
        y = dot(rows, full[:, 0:width]) + bias[:, 0:width]
        for h in range(LOCAL):
            g = y[:, 128 * h : 128 * h + 128]
            ka[h, at_rows, :] = jnp.where(
                lane < 64, g, jnp.where(lane == 64, mark, jnp.where(lane < 68, 1.0, 0.0))
            ).astype(bf16)
            va[h, at_rows, :] = jnp.where(
                lane < 64, pltpu.roll(g, 64, 1), jnp.where(lane < 67, 1.0, 0.0)
            ).astype(bf16)
            turned = g.T.astype(bf16)
            kt[h, :, at_rows] = turned[0:64]
            vt[h, 0:64, at_rows] = turned[64:128]
        if column is not None:
            q = (y[:, 384:WIDE] * 0.125).T.astype(bf16)
            for h in range(LOCAL):
                qt[h, 0:64, pl.ds(multiple(column, ROWS), ROWS)] = q[64 * h : 64 * h + 64]

    def chip_of(i):
        return p + (i % 2) * (1 - 2 * at.x) + (i // 2) * (2 - 4 * at.y)

    def project_own(i, carried):
        project(chip_of(i), core, 3 * (1 - (i + 1) // 2) + i * ((i + 1) // 2))
        return carried

    def project_other(i, carried):
        project(chip_of(i), other, None)
        return carried

    along["outer"].send()
    lax.fori_loop(0, 3, project_own, 0)
    net.landed("sc", block_at(p, other), at.to_core)
    net.landed("cx", block_at(p_x, other), at.to_core)
    net.landed("cy", block_at(p_y, other), at.to_core)
    lax.fori_loop(0, 3, project_other, 0)
    net.landed("rx0", block_at(p_d, core, early), at.to_y)
    net.landed("ry1", block_at(p_d, core, late), at.to_x)
    hand_on("cd", block_at(p_d, core), at.to_core)
    project(p_d, core, 0)
    net.landed("cd", block_at(p_d, other), at.to_core)
    project(p_d, other, None)

    kept = [local(block_at(chips[r], core), xs_out.at[r]) for r in range(4)]
    for src, dst in (
        (wqkv, wqkv_out),
        (qt, qt_out),
        (ka, ka_out),
        (va, va_out),
        (kt, kt_out),
    ):
        local(src, dst)

    def part_of(name, step, chip, side):
        _, dst, region = weights[name]
        return region(dst.at[at.from_z(step)], chip, side)

    def hand(label, name, step, chip, device):
        def make():
            ref = part_of(name, step, chip, core)
            return ref, ref, device

        net.launch(label, make)

    steps_all = tuple(range(1, GROUP))

    def plane_out(name, steps=steps_all):
        for step in steps:
            along[name].landed(step)
            hand((name, "x", step), name, step, p, at.to_x)
            hand((name, "y", step), name, step, p, at.to_y)
            hand((name, "c", step), name, step, p, at.to_core)

    def relay_by_x(name, step):
        return (step + (name == "outer")) % 2 == 1

    def plane_relay(name, steps=steps_all):
        for step in steps:
            net.landed((name, "x", step), part_of(name, step, p_x, core), at.to_x)
            net.landed((name, "y", step), part_of(name, step, p_y, core), at.to_y)
            if relay_by_x(name, step):
                hand((name, "r", step), name, step, p_y, at.to_x)
            else:
                hand((name, "r", step), name, step, p_x, at.to_y)
            hand((name, "cx", step), name, step, p_x, at.to_core)
            hand((name, "cy", step), name, step, p_y, at.to_core)

    def plane_last(name, steps=steps_all):
        for step in steps:
            far = part_of(name, step, p_d, core)
            net.landed((name, "r", step), far, at.to_x if relay_by_x(name, step) else at.to_y)
            hand((name, "cd", step), name, step, p_d, at.to_core)

    def plane_in(name):
        for step in steps_all:
            for tag, chip in (("c", p), ("cx", p_x), ("cy", p_y), ("cd", p_d)):
                net.landed((name, tag, step), part_of(name, step, chip, other), at.to_core)

    plane_out("wo")
    along["inner"].relay()

    def attend(h, tile):
        cols = pl.ds(multiple(tile, TILE), TILE)
        queries = qt[h, :, cols]
        top[0:1, :] = jnp.full((1, TILE), -3e38, f32)
        acc[...] = jnp.zeros((80, TILE), f32)

        def some(half, carried):
            for j in range(SLOTS // CHUNK // 2):
                rows = pl.ds(multiple(half * (SLOTS // CHUNK // 2) + j, CHUNK), CHUNK)
                scores = dot(ka[h, rows, :], queries)
                before = top[0:1, :]
                newest = jnp.maximum(before, jnp.max(scores, axis=0, keepdims=True))
                probs = jnp.exp(scores - newest).astype(bf16)
                acc[...] = acc[...] * jnp.exp(before - newest) + dot(vt[h, :, rows], probs)
                top[0:1, :] = newest
            return carried

        lax.fori_loop(0, 2, some, 0)
        total = acc[64:65, :]
        value = acc[0:64, :] / total
        ot[h, :, cols] = value
        lse[h, 0:1, cols] = top[0:1, :] + jnp.log(total)
        low_value = value.astype(bf16)
        at_head = pl.ds(multiple(h, 64), 64)
        mix[2 * tile, at_head, :] = low_value[:, 0:384]
        mix[2 * tile + 1, at_head, :] = low_value[:, 384:768]

    def send_mixed(name, index, device):
        net.launch(name, lambda: (mix.at[index], mixed.at[p], device))

    plan = {
        1: [lambda: plane_relay("wo"), lambda: plane_out("inner")],
        2: [
            lambda: plane_last("wo"),
            along["outer"].relay,
            along["far"].send,
            lambda: plane_relay("inner", (1,)),
        ],
        3: [
            lambda: send_mixed("md", 0, at.to_d),
            lambda: send_mixed("mx", 1, at.to_x),
            lambda: plane_relay("inner", (2,)),
        ],
        4: [lambda: plane_relay("inner", (3,))],
        5: [lambda: plane_out("outer"), lambda: plane_last("inner")],
    }

    def take(steps):
        for step in steps:
            step()

    def unit(u, carried):
        for when, steps in plan.items():
            pl.when(u == when)(functools.partial(take, steps))
        attend(u % LOCAL, u // LOCAL)
        return carried

    lax.fori_loop(0, 2 * LOCAL, unit, 0)
    send_mixed("my", 2, at.to_y)
    along["far"].relay()
    mixed[p] = mix[3]
    local(ot, ot_out)
    local(lse, lse_out)

    plane_in("wo")
    for copy in owned:
        copy.wait()
    net.landed("md", mixed.at[p_d], at.to_d)
    net.landed("mx", mixed.at[p_x], at.to_x)
    net.landed("my", mixed.at[p_y], at.to_y)
    table = vec[0].astype(f32) + vec[1].astype(f32) + vec[2].astype(f32) + vec[3].astype(f32)
    output_add, gain_one, shift_one, outer_add, gain_two, shift_two = [
        table[2 + i : 3 + i, :] for i in range(6)
    ]
    heads = mixed[...].reshape(D, ROWS)
    work[...] = dot_tn(heads, wo[...].reshape(D, D))
    low[...] = xall[p, core].reshape(ROWS, D)

    def blocks(step, start=0):
        def one(i, carried):
            return step(pl.ds(multiple(i, 128), 128), i, carried)

        return lax.fori_loop(0, ROWS // 128, one, start)

    def mean(value):
        return jnp.mean(value, axis=1, keepdims=True)

    def column(value):
        return jnp.sum(value, axis=0, keepdims=True)

    def norm(hidden):
        centred = hidden - mean(hidden)
        scale = lax.rsqrt(mean(centred * centred) + 1e-05)
        return centred * scale, scale

    def first_norm(rows, i, carried):
        value, scale = norm(low[rows, :].astype(f32) + work[rows, :] + output_add)
        normed[rows, :] = value
        scales[0, rows, :] = jnp.broadcast_to(scale, (128, 128))
        value = value * gain_one + shift_one
        first[rows, :] = value
        low[rows, :] = value.astype(bf16)
        return carried

    blocks(first_norm)
    plane_relay("outer")
    for step in steps_all:
        along["far"].landed(step)
        source = at.from_z(step)
        net.start(("farc", step), far_at(source, core), far_at(source, core), at.to_core)

    plane_in("inner")
    inner_weight = iw[...].reshape(D, FF)
    for q in range(4):
        cols = pl.ds(D * q, D)
        slope[:, cols] = dot(low[...], inner_weight[:, D * q : D * q + D])
        add = vec[q][1:2, :].astype(f32)

        def activate(rows, i, carried, cols=cols, add=add):
            u = slope[rows, cols] + add
            gate = 0.5 * (1.0 + lax.erf(u * 0.7071067811865476))
            act[rows, cols] = (u * gate).astype(bf16)
            slope[rows, cols] = gate + u * jnp.exp(-0.5 * u * u) * 0.3989422804014327
            return carried

        blocks(activate)
        if q == 1:
            plane_last("outer")
    plane_in("outer")
    for step in steps_all:
        net.landed(("farc", step), far_at(at.from_z(step), other), at.to_core)
    total = None
    for q in range(4):
        term = dot(act[:, D * q : D * q + D], ow[q].reshape(D, D))
        total = term if total is None else total + term
    work[...] = total

    nothing = jnp.zeros((1, D), f32)

    def second_norm(rows, i, carried):
        gains, shifts, biases = carried
        value, scale = norm(first[rows, :] + work[rows, :] + outer_add)
        slot = c * ROWS + i * 128 + lax.broadcasted_iota(jnp.int32, (128, D), 0)
        keep = slot < count
        lower[rows, :] = jnp.where(keep, value * gain_two + shift_two, 0.0).astype(bf16)
        upstream = jnp.where(keep, cot[rows, :].astype(f32), 0.0)
        product = upstream * value
        scaled = upstream * gain_two
        grad = scale * (scaled - mean(scaled) - value * mean(scaled * value))
        second[rows, :] = grad
        cot[rows, :] = grad.astype(bf16)
        return gains + column(product), shifts + column(upstream), biases + column(grad)

    gain_two_grad, shift_two_grad, outer_bias_grad = blocks(second_norm, (nothing,) * 3)
    local(lower, low_out)

    for copy in kept:
        copy.wait()
    for name in ("rx0", "ry1", "cx", "cy", "cd"):
        net.finish(name)
    def outer_row(t, chip, side):
        j = 2 * chip + side
        return xall.at[t, j // 4, j % 4]

    for q in range(4):
        term = dot_tn(act[:, D * q : D * q + D], cot[...]).astype(bf16)
        xall[q] = term.reshape(2, 4, 96, D)
        for r in range(4):
            net.start(("go", q, r), outer_row(q, chips[r], other), ro.at[r, q], at.to_core)

    upper, under = pl.ds(0, 48), pl.ds(48, 48)

    def outer_pair(chip, shard):
        j = 2 * chip + core
        return xall.at[pl.ds(shard, 2), j // 4, j % 4, under]

    def outer_add_core():
        for q in range(4):
            for r in range(4):
                net.landed(("go", q, r), ro.at[r, q], at.to_core)

        def one(t, carried):
            for r in range(4):
                ref = outer_row(t, chips[r], core)
                ref[...] = added(ref[...], ro[r, t])
            return carried

        lax.fori_loop(0, GROUP, one, 0)
        net.start("oxn", outer_pair(p_x, 0), ax.at[0], at.to_x)
        net.start("oyn", outer_pair(p_y, 2), ay.at[0], at.to_y)
        net.start("oxd", outer_pair(p_d, 0), ax.at[1], at.to_x)
        net.start("oyd", outer_pair(p_d, 2), ay.at[1], at.to_y)

        for r in range(2):
            for step in (2, 1, 3):
                device = at.to_z(step)
                net.start(
                    ("uz", r, step),
                    outer_row(device[1], chips[r], core).at[upper],
                    az.at[r, step - 1],
                    device,
                )

    def outer_add_shards():
        for r in range(2):
            total = outer_row(z, chips[r], core).at[upper][...].astype(f32)
            for step in steps_all:
                net.landed(("uz", r, step), az.at[r, step - 1], at.to_z(step))
                total = total + az[r, step - 1].astype(f32)
            summed[r] = total.astype(bf16)
        local(summed, summed_out)

    def outer_add_plane():
        net.landed("oxn", ax.at[0], at.to_x)
        net.landed("oyn", ay.at[0], at.to_y)
        net.landed("oxd", ax.at[1], at.to_x)
        net.landed("oyd", ay.at[1], at.to_y)
        for t in range(2):
            for shard, chip, ref in (
                (t, p, ax.at[0, t]),
                (t, p_y, ax.at[1, t]),
                (t + 2, p, ay.at[0, t]),
                (t + 2, p_x, ay.at[1, t]),
            ):
                row = outer_row(shard, chip, core).at[under]
                row[...] = added(row[...], ref[...])

    total = None
    for q in range(4):
        cols = pl.ds(D * q, D)
        work[...] = dot_nt(cot[...], ow[q].reshape(D, D))

        def slopes(rows, i, carried, cols=cols):
            grad = work[rows, :] * slope[rows, cols]
            act[rows, cols] = grad.astype(bf16)
            return carried + column(grad)

        small[q, 1:2, :] = blocks(slopes, nothing)
        grads = act[:, D * q : D * q + D]
        term = dot_nt(grads, inner_weight[:, D * q : D * q + D])
        total = term if total is None else total + term
        if q == 0:
            outer_add_core()
    work[...] = total

    def first_back(rows, i, carried):
        gains, shifts, biases = carried
        value = normed[rows, :]
        upstream = second[rows, :] + work[rows, :]
        scaled = upstream * gain_one
        grad = scales[0, rows, 0:1] * (scaled - mean(scaled) - value * mean(scaled * value))
        first[rows, :] = grad
        lower_grad[rows, :] = grad.astype(bf16)
        return gains + column(upstream * value), shifts + column(upstream), biases + column(grad)

    lower_grad = cot
    gain_one_grad, shift_one_grad, output_bias_grad = blocks(first_back, (nothing,) * 3)
    local(first, hg_out)
    mg[...] = dot_nt(wo[...].reshape(D, D), lower_grad[...]).astype(bf16).reshape(GROUP, 192, ROWS)
    for r in range(3):
        net.start(("mg", r), mg.at[chips[r]], mg_out.at[r], devices[r])
    local(mg.at[p], mg_out.at[3])
    for q in range(4):
        grads = act[:, D * q : D * q + D]
        gi[:, :, D * q : D * q + D] = dot_tn(low[...], grads).astype(bf16).reshape(GROUP, 192, D)
    local(gi, gi_out)
    gw[...] = dot(heads, lower_grad[...]).astype(bf16).reshape(GROUP, GROUP, 48, D)
    local(gw, gw_out)
    narrow = [
        output_bias_grad,
        gain_one_grad,
        shift_one_grad,
        outer_bias_grad,
        gain_two_grad,
        shift_two_grad,
    ]
    for t in range(GROUP):
        small[t, 0:1, :] = nothing
        for i, value in enumerate(narrow):
            small[t, 2 + i : 3 + i, :] = value
    local(small, small_out)
    outer_add_plane()
    outer_add_shards()
    for r in range(4):
        j = 2 * chips[r] + core
        local(xall.at[:, j // 4, j % 4], own_out.at[r])
    for r in range(3):
        net.landed(("mg", r), mg_out.at[r], devices[r])
    waited = len(opening) + len(owned)
    for copy in slots[waited:]:
        if not any(copy is other_copy for other_copy in kept):
            copy.wait()
    net.drain()


FORWARD_COPIES = 140


def forward_call(*operands):
    any_ = pl.BlockSpec(memory_space=pl.ANY)
    shape = jax.ShapeDtypeStruct
    vmem = pltpu.VMEM
    return pl.pallas_call(
        forward_kernel,
        name="forward_attention",
        out_shape=(
            shape((ROWS, D), bf16),
            shape((4, 192, ROWS), bf16),
            shape((GROUP, 192, FF), bf16),
            shape((GROUP, GROUP, 48, D), bf16),
            shape((4, GROUP, 96, D), bf16),
            shape((2, 48, D), bf16),
            shape((ROWS, D), f32),
            shape((GROUP, 8, D), f32),
            shape((4, 4, 96, D), bf16),
            shape((GROUP, 2, 96, WIDE), bf16),
            shape((LOCAL, 128, QUERIES), bf16),
            shape((LOCAL, SLOTS, 128), bf16),
            shape((LOCAL, SLOTS, 128), bf16),
            shape((LOCAL, 64, SLOTS), bf16),
            shape((LOCAL, 64, QUERIES), f32),
            shape((LOCAL, 8, QUERIES), f32),
        ),
        in_specs=[pl.BlockSpec(memory_space=pltpu.SMEM)] + [any_] * 7,
        out_specs=[any_] * 16,
        scratch_shapes=[
            vmem((GROUP, 2, 4, 96, D), bf16),
            vmem((GROUP, 2, 96, WIDE), bf16),
            vmem((GROUP, 16, D), bf16),
            vmem((LOCAL, 128, QUERIES), bf16),
            vmem((LOCAL, SLOTS, 128), bf16),
            vmem((LOCAL, SLOTS, 128), bf16),
            vmem((LOCAL, 64, SLOTS), bf16),
            vmem((LOCAL, 80, SLOTS), bf16),
            vmem((LOCAL, 64, QUERIES), f32),
            vmem((LOCAL, 8, QUERIES), f32),
            vmem((4, 192, ROWS), bf16),
            vmem((GROUP, 192, ROWS), bf16),
            vmem((80, TILE), f32),
            vmem((8, TILE), f32),
            vmem((GROUP, 192, FF), bf16),
            vmem((GROUP, 2, CTX, 48, D), bf16),
            vmem((GROUP, GROUP, 48, D), bf16),
            vmem((ROWS, D), bf16),
            vmem((ROWS, D), f32),
            vmem((ROWS, D), f32),
            vmem((ROWS, D), f32),
            vmem((ROWS, D), f32),
            vmem((ROWS, FF), f32),
            vmem((ROWS, FF), bf16),
            vmem((ROWS, D), bf16),
            vmem((ROWS, D), bf16),
            vmem((GROUP, 192, FF), bf16),
            vmem((GROUP, GROUP, 48, D), bf16),
            vmem((GROUP, 192, ROWS), bf16),
            vmem((GROUP, 8, D), f32),
            vmem((1, ROWS, 128), f32),
            vmem((4, GROUP, 96, D), bf16),
            vmem((2, 2, 48, D), bf16),
            vmem((2, 2, 48, D), bf16),
            vmem((2, 3, 48, D), bf16),
            vmem((2, 48, D), bf16),
            pltpu.SemaphoreType.DMA((FORWARD_COPIES,)),
            pltpu.SemaphoreType.DMA((FORWARD_COPIES,)),
            pltpu.SemaphoreType.DMA((48,)),
        ],
        compiler_params=pltpu.CompilerParams(
            collective_id=0, has_side_effects=True, vmem_limit_bytes=67043328
        ),
    )(*operands)


def split_weights(place_p, query_weight, key_weight, value_weight):
    def columns(weight):
        return lax.dynamic_slice_in_dim(weight, place_p * 192, 192, axis=1)

    rows = query_weight.shape[0]
    pair = jnp.concatenate(
        [columns(key_weight).reshape(rows, 3, 64), columns(value_weight).reshape(rows, 3, 64)],
        axis=2,
    ).reshape(rows, 384)
    fill = jnp.zeros((rows, 64), bf16)
    return jnp.concatenate([pair, columns(query_weight), fill], axis=1).reshape(2, 96, WIDE)


def pack_vectors(query_bias, value_bias, inner_bias, vectors):
    nothing = jnp.zeros((3, 64), bf16)
    first = jnp.concatenate(
        [
            jnp.concatenate([nothing, value_bias.reshape(3, 64)], axis=1).reshape(384),
            query_bias,
            jnp.zeros((192,), bf16),
        ]
    )
    rest = jnp.stack(vectors)[:, None, :]
    mine = lax.broadcasted_iota(jnp.int32, (1, GROUP, 1), 1) == lax.axis_index(FSDP)
    rest = jnp.where(mine, rest, 0).astype(bf16).reshape(len(vectors), D)
    return jnp.concatenate([first[None], inner_bias[None], rest, jnp.zeros((8, D), bf16)])


SPAN = 256


def backward_kernel(
    mg_in,
    ot_in,
    lse_in,
    qt_in,
    ka_in,
    va_in,
    kt_in,
    gi_in,
    gw_in,
    own_in,
    summed_in,
    xs_in,
    wqkv_in,
    hg_in,
    small_in,
    dx_out,
    gqkv_out,
    gi_out,
    go_out,
    gw_out,
    small_out,
    mg,
    ot,
    lse,
    qa,
    qz,
    ka,
    va,
    kt,
    da,
    dz,
    kv,
    rkv,
    dq,
    so,
    si,
    ri,
    aix,
    aiy,
    boy,
    box,
    az,
    su,
    ux,
    uy,
    vx,
    vy,
    done_o,
    biy,
    bix,
    zo,
    zi,
    xs,
    wqkv,
    dqkv,
    sdx,
    rx,
    ry,
    bx,
    by,
    hg,
    dw,
    dwl,
    rdw,
    rzw,
    small,
    rsz,
    rsc,
    rsp,
    ssum,
    sends,
    receives,
    locals_,
):
    at = Place()
    net = Net(sends, receives)
    c, z, core, p = at.c, at.z, at.core, at.p
    other = 1 - core
    chips = [at.p_d, at.p_x, at.p_y, p]
    devices = [at.to_d, at.to_x, at.to_y]
    slots = []

    def local(src, dst):
        copy = pltpu.make_async_copy(src, dst, locals_.at[len(slots)])
        slots.append(copy)
        copy.start()
        return copy

    greet(at)
    upper, under = pl.ds(0, 48), pl.ds(48, 48)
    fore, aft = pl.ds(0, 2), pl.ds(2, 2)
    front, back = pl.ds(0, 384), pl.ds(384, 384)
    net.start("oby", own_in.at[2, fore, under], boy, at.to_y)
    net.start("obx", own_in.at[1, aft, under], box, at.to_x)
    for r in range(2, 4):
        for step in (2, 1, 3):
            device = at.to_z(step)
            net.start(
                ("uz", r, step), own_in.at[r, device[1], upper], az.at[r - 2, step - 1], device
            )
    loads = [
        local(mg_in, mg),
        local(ot_in, ot),
        local(lse_in, lse),
        local(qt_in, qa),
        local(ka_in, ka),
        local(va_in, va),
        local(kt_in, kt),
    ]

    def i_at(chip, side):
        return gi_in.at[:, :, pl.ds(multiple(2 * chip + side, 384), 384)]

    def w_at(chip, side):
        return gw_in.at[:, chip, :, pl.ds(multiple(side, 384), 384)]

    halves = [local(own_in, so), local(summed_in, su.at[pl.ds(0, 2)])]
    for r in range(4):
        net.start(("gi", r), i_at(chips[r], other), ri.at[r, :, 0:192], at.to_core)
        net.start(("gw", r), w_at(chips[r], other), ri.at[r, :, 192:240], at.to_core)
        halves.append(local(i_at(chips[r], core), si.at[r, :, 0:192]))
        halves.append(local(w_at(chips[r], core), si.at[r, :, 192:240]))
    later = [local(wqkv_in, wqkv), local(hg_in, hg), local(small_in, small)]
    for r in range(4):
        later.append(local(xs_in.at[r], xs.at[r]))

    for copy in loads:
        copy.wait()
    row16 = lax.broadcasted_iota(jnp.int32, (16, QUERIES), 0)
    row128 = lax.broadcasted_iota(jnp.int32, (128, QUERIES), 0)
    for h in range(LOCAL):
        high, middle, rest = parts_of(-lse[h, 0:1, :])
        qz[h] = jnp.where(row128 < 64, qa[h].astype(f32), 0.0).astype(bf16)
        qa[h, 64:80, :] = jnp.where(
            row16 == 0,
            1.0,
            jnp.where(
                row16 == 1, high, jnp.where(row16 == 2, middle, jnp.where(row16 == 3, rest, 0.0))
            ),
        ).astype(bf16)
        kv[h] = jnp.zeros((SLOTS, 128), f32)
        dz[h, 0:64, :] = jnp.zeros((64, QUERIES), bf16)
        da[h, 80:128, :] = jnp.zeros((48, QUERIES), bf16)
    row16 = lax.broadcasted_iota(jnp.int32, (16, ROWS), 0)
    for r in range(4):
        cols = pl.ds(ROWS * r, ROWS)
        for h in range(LOCAL):
            grad = mg[r, 64 * h : 64 * h + 64, :]
            delta = jnp.sum(grad.astype(f32) * ot[h, :, cols], axis=0, keepdims=True)
            high, middle, rest = parts_of(-delta)
            da[h, 0:64, cols] = grad
            dz[h, 64:128, cols] = grad
            da[h, 64:80, cols] = jnp.where(
                row16 == 0,
                high,
                jnp.where(row16 == 1, middle, jnp.where(row16 == 2, rest, 0.0)),
            ).astype(bf16)

    left, right = pl.ds(0, 128), pl.ds(128, 112)

    def along_shards(step):
        def one(t, carried):
            step(t)
            return carried

        lax.fori_loop(0, GROUP, one, 0)

    upper, under = pl.ds(0, 48), pl.ds(48, 48)

    def outer_second():
        halves[0].wait()
        net.landed("oby", boy, at.to_y)
        net.landed("obx", box, at.to_x)
        for t in range(2):
            so[3, t, under] = added(so[3, t, under], boy[t])
            so[3, t + 2, under] = added(so[3, t + 2, under], box[t])
        for i in range(1, GROUP):
            net.launch(
                ("oz", i),
                lambda i=i: (so.at[3, at.to_z(i)[1], under], zo.at[i - 1], at.to_z(i)),
            )

    def outer_shards():
        halves[1].wait()
        for r in range(2, 4):
            total = so[r, z, upper].astype(f32)
            for i in range(1, GROUP):
                net.landed(("uz", r, i), az.at[r - 2, i - 1], at.to_z(i))
                total = total + az[r - 2, i - 1].astype(f32)
            su[r] = total.astype(bf16)
        net.launch("uxn", lambda: (su.at[1, :, front], ux.at[0], at.to_x))
        net.launch("uyn", lambda: (su.at[2, :, back], uy.at[0], at.to_y))
        net.launch("uxd", lambda: (su.at[0, :, front], ux.at[1], at.to_x))
        net.launch("uyd", lambda: (su.at[0, :, back], uy.at[1], at.to_y))

    def outer_third():
        net.landed("uxn", ux.at[0], at.to_x)
        net.landed("uyn", uy.at[0], at.to_y)
        net.landed("uxd", ux.at[1], at.to_x)
        net.landed("uyd", uy.at[1], at.to_y)
        su[2, :, front] = added(su[2, :, front], ux[1])
        su[1, :, back] = added(su[1, :, back], uy[1])
        net.launch("uby", lambda: (su.at[2, :, front], vy, at.to_y))
        net.launch("ubx", lambda: (su.at[1, :, back], vx, at.to_x))
        su[3, :, front] = added(su[3, :, front], ux[0])
        su[3, :, back] = added(su[3, :, back], uy[0])

    def outer_last():
        total = so[3, z, under].astype(f32)
        for i in range(1, GROUP):
            net.landed(("oz", i), zo.at[i - 1], at.to_z(i))
            total = total + zo[i - 1].astype(f32)
        done_o[48:96] = total.astype(bf16)
        net.landed("uby", vy, at.to_y)
        net.landed("ubx", vx, at.to_x)
        done_o[0:48, front] = added(su[3, :, front], vy[...])
        done_o[0:48, back] = added(su[3, :, back], vx[...])

    def inner_core():
        for copy in halves[2:]:
            copy.wait()
        for r in range(4):
            net.landed(("gi", r), ri.at[r, :, 0:192], at.to_core)
            net.landed(("gw", r), ri.at[r, :, 192:240], at.to_core)

        def step(t):
            for r in range(4):
                si[r, t] = added(si[r, t], ri[r, t])

        along_shards(step)
        net.launch("ixn", lambda: (si.at[1, :, left], aix.at[0], at.to_x))
        net.launch("iyn", lambda: (si.at[2, :, right], aiy.at[0], at.to_y))
        net.launch("ixd", lambda: (si.at[0, :, left], aix.at[1], at.to_x))
        net.launch("iyd", lambda: (si.at[0, :, right], aiy.at[1], at.to_y))

    def inner_first():
        net.landed("ixn", aix.at[0], at.to_x)
        net.landed("iyn", aiy.at[0], at.to_y)
        net.landed("ixd", aix.at[1], at.to_x)
        net.landed("iyd", aiy.at[1], at.to_y)

        def step(t):
            si[2, t, left] = added(si[2, t, left], aix[1, t])
            si[1, t, right] = added(si[1, t, right], aiy[1, t])
            si[3, t, left] = added(si[3, t, left], aix[0, t])
            si[3, t, right] = added(si[3, t, right], aiy[0, t])

        along_shards(step)
        net.launch("iby", lambda: (si.at[2, :, left], biy, at.to_y))
        net.launch("ibx", lambda: (si.at[1, :, right], bix, at.to_x))

    def inner_second():
        net.landed("iby", biy, at.to_y)
        net.landed("ibx", bix, at.to_x)

        def step(t):
            si[3, t, left] = added(si[3, t, left], biy[t])
            si[3, t, right] = added(si[3, t, right], bix[t])

        along_shards(step)
        for i in range(1, GROUP):
            net.launch(
                ("iz", i), lambda i=i: (si.at[3, at.to_z(i)[1]], zi.at[i - 1], at.to_z(i))
            )

    def inner_last():
        total = si[3, z].astype(f32)
        for i in range(1, GROUP):
            net.landed(("iz", i), zi.at[i - 1], at.to_z(i))
            total = total + zi[i - 1].astype(f32)
        si[3, z] = total.astype(bf16)

    def go_at(chip, side):
        return go_out.at[2 * chip + side]

    def gi_at(chip, side):
        return gi_out.at[:, pl.ds(multiple(2 * chip + side, 384), 384)]

    def gw_at(chip, side):
        return gw_out.at[chip, :, pl.ds(multiple(side, 384), 384)]

    place_of = {"o": go_at, "i": gi_at, "w": gw_at}
    via_x = {"o": False, "i": True, "w": False}
    mine = {
        "o": lambda: done_o,
        "i": lambda: si.at[3, z, 0:192],
        "w": lambda: si.at[3, z, 192:240],
    }

    def spread(name):
        place = place_of[name]
        for tag, device in (("x", at.to_x), ("y", at.to_y), ("c", at.to_core)):
            net.launch(
                ("f", name, tag), lambda device=device: (mine[name](), place(p, core), device)
            )

    def pass_on(name):
        place = place_of[name]

        def hand(tag, chip, device):
            net.launch(
                ("f", name, tag), lambda: (place(chip, core), place(chip, core), device)
            )

        net.landed(("f", name, "x"), place(at.p_x, core), at.to_x)
        net.landed(("f", name, "y"), place(at.p_y, core), at.to_y)
        if via_x[name]:
            hand("r", at.p_y, at.to_x)
        else:
            hand("r", at.p_x, at.to_y)
        hand("cx", at.p_x, at.to_core)
        hand("cy", at.p_y, at.to_core)

    def finish_spread(name):
        place = place_of[name]
        far = place(at.p_d, core)
        net.landed(("f", name, "r"), far, at.to_x if via_x[name] else at.to_y)
        net.start(("f", name, "cd"), far, far, at.to_core)

    def close_spread(name):
        place = place_of[name]
        for tag, chip in (("c", p), ("cx", at.p_x), ("cy", at.p_y), ("cd", at.p_d)):
            net.landed(("f", name, tag), place(chip, other), at.to_core)

    def swap_kv(h):
        for r in range(4):
            net.launch(
                ("kv", h, r),
                lambda r=r: (
                    kv.at[h, pl.ds(multiple(2 * chips[r] + other, ROWS), ROWS)],
                    rkv.at[h, r],
                    at.to_core,
                ),
            )

    def attend(h, tile):
        cols = pl.ds(multiple(tile, TILE), TILE)
        queries = qa[h, :, cols]
        upstream = da[h, :, cols]
        queries_only = qz[h, :, cols]
        upstream_only = dz[h, :, cols]
        dq[h, :, cols] = jnp.zeros((64, TILE), f32)

        def some(half, carried):
            for j in range(SLOTS // SPAN // 2):
                rows = pl.ds(multiple(half * (SLOTS // SPAN // 2) + j, SPAN), SPAN)
                probs = jnp.exp(dot(ka[h, rows, :], queries))
                grads = (probs * dot(va[h, rows, :], upstream)).astype(bf16)
                kv[h, rows, :] += dot_nt(grads, queries_only) + dot_nt(
                    probs.astype(bf16), upstream_only
                )
                dq[h, :, cols] += dot(kt[h, :, rows], grads)
            return carried

        lax.fori_loop(0, 2, some, 0)

    plan = {
        1: [inner_core, outer_second],
        2: [lambda: swap_kv(0)],
        3: [outer_shards],
        4: [lambda: swap_kv(1), inner_first, outer_third],
        5: [outer_last, lambda: spread("o"), inner_second],
    }

    def take(steps):
        for step in steps:
            step()

    def unit(u, carried):
        for when, steps in plan.items():
            pl.when(u == when)(functools.partial(take, steps))
        attend(u // 2, u % 2)
        return carried

    lax.fori_loop(0, 2 * LOCAL, unit, 0)
    swap_kv(2)
    pass_on("o")
    local(done_o, go_at(p, core))

    for copy in later:
        copy.wait()
    weights = wqkv[...].reshape(D, WIDE)
    for h in range(LOCAL):
        for r in range(4):
            net.landed(("kv", h, r), rkv.at[h, r], at.to_core)
    sums = jnp.zeros((1, WIDE), f32)
    top, low = pl.ds(0, 192), pl.ds(192, 192)
    for r in range(4):
        cols = pl.ds(ROWS * r, ROWS)
        rows = pl.ds(multiple(2 * chips[r] + core, ROWS), ROWS)
        for h in range(LOCAL):
            dqkv[r, :, 128 * h : 128 * h + 128] = (kv[h, rows, :] + rkv[h, r]).astype(bf16)
        turned = jnp.concatenate(
            [dq[h, :, cols] for h in range(LOCAL)] + [jnp.zeros((64, ROWS), f32)], axis=0
        )
        dqkv[r, :, 384:WIDE] = (turned.T * 0.125).astype(bf16)
        block = dqkv[r]
        sums = sums + jnp.sum(block.astype(f32), axis=0, keepdims=True)
        update = dot_nt(block, weights)
        if r < 3:
            sdx[r] = update.astype(bf16)
        else:
            hg[...] += update
        if r == 1:
            net.start("dxn", sdx.at[1, top], rx.at[0], at.to_x)
            net.start("dxd", sdx.at[0, top], rx.at[1], at.to_x)
        if r == 2:
            net.start("dyn", sdx.at[2, low], ry.at[0], at.to_y)
            net.start("dyd", sdx.at[0, low], ry.at[1], at.to_y)
    small[p, 0:1, 0:WIDE] += sums
    for step in range(1, GROUP):
        net.start(("sz", step), small.at[at.to_z(step)[1]], rsz.at[step - 1], at.to_z(step))

    total = None
    for r in range(4):
        term = lax.dot_general(
            xs[r].reshape(ROWS, D), dqkv[r], (((0,), (0,)), ((), ())), preferred_element_type=f32
        )
        total = term if total is None else total + term
    dw[...] = total.reshape(GROUP, 2, 96, WIDE)
    dwl[...] = dw[:, other].astype(bf16)
    net.start("dwc", dwl, rdw, at.to_core)

    for step in range(1, GROUP):
        net.landed(("sz", step), rsz.at[step - 1], at.to_z(step))
    small[z] = small[z] + rsz[0] + rsz[1] + rsz[2]
    net.start("sc", small.at[z], rsc, at.to_core)
    net.landed("dwc", rdw, at.to_core)
    for t in range(GROUP):
        rdw[t] = added(dw[t, core], rdw[t])
    for step in range(1, GROUP):
        net.start(("dwz", step), rdw.at[at.to_z(step)[1]], rzw.at[step - 1], at.to_z(step))
    net.landed("sc", rsc, at.to_core)
    rsc[...] = small[z] + rsc[...]
    for r in range(3):
        net.start(("sp", r), rsc, rsp.at[r], devices[r])

    inner_last()
    for name in ("i", "w"):
        spread(name)
        local(mine[name](), place_of[name](p, core))

    net.landed("dxn", rx.at[0], at.to_x)
    net.landed("dxd", rx.at[1], at.to_x)
    sdx[2, top] = added(sdx[2, top], rx[1])
    net.start("dby", sdx.at[2, top], by, at.to_y)
    net.landed("dyn", ry.at[0], at.to_y)
    net.landed("dyd", ry.at[1], at.to_y)
    sdx[1, low] = added(sdx[1, low], ry[1])
    net.start("dbx", sdx.at[1, low], bx, at.to_x)
    hg[top] += rx[0].astype(f32)
    hg[low] += ry[0].astype(f32)

    for step in range(1, GROUP):
        net.landed(("dwz", step), rzw.at[step - 1], at.to_z(step))
    finished = rdw[z].astype(f32)
    for step in range(GROUP - 1):
        finished = finished + rzw[step].astype(f32)
    rdw[z] = finished.astype(bf16)
    for r in range(3):
        net.start(("fq", r), rdw.at[z], gqkv_out.at[p, core], devices[r])
    net.start("fqc", rdw.at[z], gqkv_out.at[p, core], at.to_core)
    local(rdw.at[z], gqkv_out.at[p, core])

    for r in range(3):
        net.landed(("sp", r), rsp.at[r], devices[r])
    ssum[...] = rsc[...] + rsp[0] + rsp[1] + rsp[2]
    local(ssum, small_out)

    for name in ("i", "w"):
        pass_on(name)
    for r in range(3):
        ref = gqkv_out.at[chips[r], core]
        net.landed(("fq", r), ref, devices[r])
        net.start(("fqc", r), ref, ref, at.to_core)

    net.landed("dby", by, at.to_y)
    net.landed("dbx", bx, at.to_x)
    sdx[3, top] = (hg[top] + by[...].astype(f32)).astype(bf16)
    sdx[3, low] = (hg[low] + bx[...].astype(f32)).astype(bf16)
    local(sdx.at[3], dx_out)

    for name in ("o", "i", "w"):
        finish_spread(name)
    for name in ("o", "i", "w"):
        close_spread(name)
    net.landed("fqc", gqkv_out.at[p, other], at.to_core)
    for r in range(3):
        net.landed(("fqc", r), gqkv_out.at[chips[r], other], at.to_core)
    done = len(loads) + len(halves) + len(later)
    for copy in slots[done:]:
        copy.wait()
    net.drain()


BACKWARD_COPIES = 110


def backward_call(*operands):
    any_ = pl.BlockSpec(memory_space=pl.ANY)
    shape = jax.ShapeDtypeStruct
    vmem = pltpu.VMEM
    return pl.pallas_call(
        backward_kernel,
        name="backward_attention",
        out_shape=(
            shape((ROWS, D), bf16),
            shape((GROUP, 2, 96, WIDE), bf16),
            shape((192, FF), bf16),
            shape((CTX, 96, D), bf16),
            shape((GROUP, 48, D), bf16),
            shape((8, D), f32),
        ),
        in_specs=[any_] * 15,
        out_specs=[any_] * 6,
        scratch_shapes=[
            vmem((4, 192, ROWS), bf16),
            vmem((LOCAL, 64, QUERIES), f32),
            vmem((LOCAL, 8, QUERIES), f32),
            vmem((LOCAL, 128, QUERIES), bf16),
            vmem((LOCAL, 128, QUERIES), bf16),
            vmem((LOCAL, SLOTS, 128), bf16),
            vmem((LOCAL, SLOTS, 128), bf16),
            vmem((LOCAL, 64, SLOTS), bf16),
            vmem((LOCAL, 128, QUERIES), bf16),
            vmem((LOCAL, 128, QUERIES), bf16),
            vmem((LOCAL, SLOTS, 128), f32),
            vmem((LOCAL, 4, ROWS, 128), f32),
            vmem((LOCAL, 64, QUERIES), f32),
            vmem((4, GROUP, 96, D), bf16),
            vmem((4, GROUP, 240, 384), bf16),
            vmem((4, GROUP, 240, 384), bf16),
            vmem((2, GROUP, 128, 384), bf16),
            vmem((2, GROUP, 112, 384), bf16),
            vmem((2, 48, D), bf16),
            vmem((2, 48, D), bf16),
            vmem((2, 3, 48, D), bf16),
            vmem((4, 48, D), bf16),
            vmem((2, 48, 384), bf16),
            vmem((2, 48, 384), bf16),
            vmem((48, 384), bf16),
            vmem((48, 384), bf16),
            vmem((96, D), bf16),
            vmem((GROUP, 128, 384), bf16),
            vmem((GROUP, 112, 384), bf16),
            vmem((3, 48, D), bf16),
            vmem((3, 240, 384), bf16),
            vmem((4, 4, 96, D), bf16),
            vmem((GROUP, 2, 96, WIDE), bf16),
            vmem((4, ROWS, WIDE), bf16),
            vmem((4, ROWS, D), bf16),
            vmem((2, 192, D), bf16),
            vmem((2, 192, D), bf16),
            vmem((192, D), bf16),
            vmem((192, D), bf16),
            vmem((ROWS, D), f32),
            vmem((GROUP, 2, 96, WIDE), f32),
            vmem((GROUP, 96, WIDE), bf16),
            vmem((GROUP, 96, WIDE), bf16),
            vmem((3, 96, WIDE), bf16),
            vmem((GROUP, 8, D), f32),
            vmem((3, 8, D), f32),
            vmem((8, D), f32),
            vmem((3, 8, D), f32),
            vmem((8, D), f32),
            pltpu.SemaphoreType.DMA((BACKWARD_COPIES,)),
            pltpu.SemaphoreType.DMA((BACKWARD_COPIES,)),
            pltpu.SemaphoreType.DMA((48,)),
        ],
        compiler_params=pltpu.CompilerParams(
            collective_id=1, has_side_effects=True, vmem_limit_bytes=63 << 20
        ),
    )(*operands)


def finish_kernel(
    low_in, dx_in, gqkv_in, gi_in, go_in, gw_in,
    low_out, dx_out, q_out, k_out, v_out, gi_out, go_out, gw_out,
    low, dx, gqkv, gi, go, gw, q, k, v, wide_i, wide_o, wide_w, reads, writes,
):
    loads = [
        pltpu.make_async_copy(src, dst, reads.at[i])
        for i, (src, dst) in enumerate(
            ((gi_in, gi), (go_in, go), (gw_in, gw), (gqkv_in, gqkv), (low_in, low), (dx_in, dx))
        )
    ]
    for copy in loads:
        copy.start()
    stores = []

    def store(src, dst):
        copy = pltpu.make_async_copy(src, dst, writes.at[len(stores)])
        stores.append(copy)
        copy.start()

    for copy, narrow, wide, dst in (
        (loads[0], gi, wide_i, gi_out),
        (loads[1], go, wide_o, go_out),
        (loads[2], gw, wide_w, gw_out),
    ):
        copy.wait()
        wide[...] = narrow[...].astype(f32)
        store(wide, dst)
    loads[3].wait()
    lane = lax.broadcasted_iota(jnp.int32, (192, 128), 1)

    def piece(chip, tile, side, wanted):
        value = gqkv[chip, :, 128 * tile : 128 * tile + 128].astype(f32)
        return value if side == wanted else pltpu.roll(value, 64, 1)

    for tile in range(6):
        cols = pl.ds(128 * tile, 128)
        left, right = [divmod(g, LOCAL) for g in (2 * tile, 2 * tile + 1)]
        for ref, place in (
            (k, lambda h: (h, 0)),
            (v, lambda h: (h, 1)),
            (q, lambda h: (3 + h // 2, h % 2)),
        ):
            a = piece(left[0], *place(left[1]), 0)
            b = piece(right[0], *place(right[1]), 1)
            ref[:, cols] = jnp.where(lane < 64, a, b)
    for src, dst in ((q, q_out), (k, k_out), (v, v_out)):
        store(src, dst)
    loads[4].wait()
    store(low, low_out)
    loads[5].wait()
    store(dx, dx_out)
    for copy in stores:
        copy.wait()


def finish_call(*operands):
    any_ = pl.BlockSpec(memory_space=pl.ANY)
    vmem = pltpu.VMEM
    square, wide = (192, D), (192, FF)
    shapes = [((ROWS, D), bf16)] * 2 + [(square, f32)] * 3
    shapes += [(wide, f32), ((D, D), f32), (square, f32)]
    return pl.pallas_call(
        finish_kernel,
        name="finish",
        out_shape=[jax.ShapeDtypeStruct(*pair) for pair in shapes],
        in_specs=[any_] * 6,
        out_specs=[any_] * 8,
        scratch_shapes=[
            vmem((ROWS, D), bf16),
            vmem((ROWS, D), bf16),
            vmem((GROUP, 192, WIDE), bf16),
            vmem(wide, bf16),
            vmem((D, D), bf16),
            vmem(square, bf16),
            vmem(square, f32),
            vmem(square, f32),
            vmem(square, f32),
            vmem(wide, f32),
            vmem((D, D), f32),
            vmem(square, f32),
            pltpu.SemaphoreType.DMA((6,)),
            pltpu.SemaphoreType.DMA((8,)),
        ],
        compiler_params=pltpu.CompilerParams(vmem_limit_bytes=67043328),
    )(*operands)


def small_plane(
    states,
    lengths,
    query_weight,
    query_bias,
    key_weight,
    value_weight,
    value_bias,
    output_weight,
    output_bias,
    first_gain,
    first_shift,
    inner_weight,
    inner_bias,
    outer_weight,
    outer_bias,
    second_gain,
    second_shift,
    cotangent,
):
    cycle_place = lax.axis_index(RING)
    shard = lax.axis_index(FSDP)
    wqkv = split_weights(cycle_place // 2, query_weight, key_weight, value_weight)
    vectors = pack_vectors(
        query_bias,
        value_bias,
        inner_bias,
        [output_bias, first_gain, first_shift, outer_bias, second_gain, second_shift],
    )
    low, mg, gi, gw, own, summed, hg, small, xs, wall, qt, ka, va, kt, ot, lse = (
        forward_call(
            lengths,
            states.reshape(4, 96, D),
            wqkv,
            vectors,
            inner_weight,
            outer_weight.reshape(2, CTX, 48, D),
            output_weight.reshape(GROUP, 48, D),
            cotangent[0],
        )
    )
    dx, gqkv, gi, go, gw, sums = backward_call(
        mg, ot, lse, qt, ka, va, kt, gi, gw, own, summed, xs, wall, hg, small
    )
    low, dx, gq, gk, gv, gi, go, gw = finish_call(
        low,
        dx,
        gqkv.reshape(GROUP, 192, WIDE),
        gi,
        go.reshape(D, D),
        gw.reshape(192, D),
    )
    narrow = lax.dynamic_slice_in_dim(sums[2:8], shard * 192, 192, axis=1)
    value_bias_grad = sums[0, :384].reshape(LOCAL, 2, 64)[:, 1].reshape(192)
    return (
        low[None],
        dx[None],
        gq,
        sums[0, 384:576],
        gk,
        gv,
        value_bias_grad,
        gw,
        narrow[0],
        narrow[1],
        narrow[2],
        gi,
        sums[1],
        go,
        narrow[3],
        narrow[4],
        narrow[5],
    )


def keep_state(carried):
    return carried


def per_device(
    states,
    lengths,
    query_weight,
    query_bias,
    key_weight,
    value_weight,
    value_bias,
    output_weight,
    output_bias,
    first_gain,
    first_shift,
    inner_weight,
    inner_bias,
    outer_weight,
    outer_bias,
    second_gain,
    second_shift,
    cotangent,
):
    row_count = states.shape[1]
    cycle_size = lax.axis_size(RING)
    cycle_place = lax.axis_index(RING)
    sequence = lax.axis_index(FSDP)
    length = lengths[sequence]
    offsets = jnp.arange(row_count, dtype=jnp.int32)
    row_keep = cycle_place * row_count + offsets < length
    inputs = states[0]
    input_float = inputs.astype(jnp.float32)
    attention_set = (
        lax.all_gather(query_weight, FSDP, axis=0, tiled=True),
        lax.all_gather(key_weight, FSDP, axis=0, tiled=True),
        lax.all_gather(value_weight, FSDP, axis=0, tiled=True),
        lax.all_gather(output_weight, FSDP, axis=0, tiled=True),
        lax.all_gather(query_bias, FSDP, axis=0, tiled=True),
        lax.all_gather(value_bias, FSDP, axis=0, tiled=True),
        lax.all_gather(output_bias, FSDP, axis=0, tiled=True),
        lax.all_gather(first_gain, FSDP, axis=0, tiled=True),
        lax.all_gather(first_shift, FSDP, axis=0, tiled=True),
    )
    query_full = attention_set[0]
    key_full = attention_set[1]
    value_full = attention_set[2]
    output_full = attention_set[3]
    query_add = attention_set[4].astype(jnp.float32)
    value_add = attention_set[5].astype(jnp.float32)
    output_add = attention_set[6].astype(jnp.float32)
    gain_one = attention_set[7].astype(jnp.float32)
    shift_one = attention_set[8].astype(jnp.float32)
    queries = (
        (jnp.dot(inputs, query_full, preferred_element_type=jnp.float32) + query_add) * 0.125
    ).astype(jnp.bfloat16)
    key_rows = jnp.dot(inputs, key_full, preferred_element_type=jnp.float32).astype(jnp.bfloat16)
    values = (jnp.dot(inputs, value_full, preferred_element_type=jnp.float32) + value_add).astype(
        jnp.bfloat16
    )
    query_heads = queries.reshape(row_count, H, HD)

    def forward_block(key_block, value_block, key_start, running_state):

        def forward_compute(carried):
            running, exp_total, accum = carried
            key_keep = key_start + offsets < length
            scores = jnp.einsum(
                "qhd,khd->hqk",
                query_heads,
                key_block.reshape(row_count, H, HD),
                preferred_element_type=jnp.float32,
            )
            scores = jnp.where(key_keep[None, None, :], scores, -1e30)
            newest = jnp.maximum(running, jnp.max(scores, axis=2))
            factor = jnp.exp(running - newest)
            weights = jnp.exp(scores - newest[:, :, None])
            exp_total = exp_total * factor + jnp.sum(weights, axis=2)
            update = jnp.einsum(
                "hqk,khd->qhd",
                weights.astype(jnp.bfloat16),
                value_block.reshape(row_count, H, HD),
                preferred_element_type=jnp.float32,
            )
            accum = accum * factor.T[:, :, None] + update
            return (newest, exp_total, accum)

        return lax.cond(key_start < length, forward_compute, keep_state, running_state)

    start_state = (
        jnp.full((H, row_count), -1e30, jnp.float32),
        jnp.zeros((H, row_count), jnp.float32),
        jnp.zeros((row_count, H, HD), jnp.float32),
    )

    def cycle_turn(turn_index, carried):
        key_block, value_block, running_state = carried
        owner_index = (cycle_place - turn_index) % cycle_size
        running_state = forward_block(
            key_block, value_block, owner_index * row_count, running_state
        )
        key_block, value_block = passed_along((key_block, value_block), RING, 1)
        return (key_block, value_block, running_state)

    key_block, value_block, running_state = lax.fori_loop(
        0, cycle_size - 1, cycle_turn, (key_rows, values, start_state)
    )
    last_owner = (cycle_place + 1) % cycle_size
    running, exp_total, accum = forward_block(
        key_block, value_block, last_owner * row_count, running_state
    )
    log_total = running + jnp.log(exp_total)
    attention_value = (accum / exp_total.T[:, :, None]).reshape(row_count, D)
    mixed = attention_value.astype(jnp.bfloat16)
    attended = jnp.dot(mixed, output_full, preferred_element_type=jnp.float32) + output_add
    first_normed, first_scale = normalize(input_float + attended)
    first = first_normed * gain_one + shift_one
    first_low = first.astype(jnp.bfloat16)
    feed_set = (
        lax.all_gather(inner_weight, FSDP, axis=0, tiled=True),
        lax.all_gather(outer_weight, FSDP, axis=0, tiled=True),
        lax.all_gather(inner_bias, FSDP, axis=0, tiled=True),
        lax.all_gather(outer_bias, FSDP, axis=0, tiled=True),
        lax.all_gather(second_gain, FSDP, axis=0, tiled=True),
        lax.all_gather(second_shift, FSDP, axis=0, tiled=True),
    )
    inner_full = feed_set[0]
    outer_full = feed_set[1]
    inner_add = feed_set[2].astype(jnp.float32)
    outer_add = feed_set[3].astype(jnp.float32)
    gain_two = feed_set[4].astype(jnp.float32)
    shift_two = feed_set[5].astype(jnp.float32)
    inner = jnp.dot(first_low, inner_full, preferred_element_type=jnp.float32) + inner_add
    activated = jax.nn.gelu(inner, approximate=False).astype(jnp.bfloat16)
    outer = jnp.dot(activated, outer_full, preferred_element_type=jnp.float32) + outer_add
    second_normed, second_scale = normalize(first + outer)
    second = second_normed * gain_two + shift_two
    layer_output = jnp.where(row_keep[:, None], second, 0.0).astype(jnp.bfloat16)[None]
    query_full = attention_set[0]
    key_full = attention_set[1]
    value_full = attention_set[2]
    output_full = attention_set[3]
    gain_one = attention_set[7].astype(jnp.float32)
    inner_full = feed_set[0]
    outer_full = feed_set[1]
    gain_two = feed_set[4].astype(jnp.float32)
    upstream = jnp.where(row_keep[:, None], cotangent[0].astype(jnp.float32), 0.0)
    second_grad, second_gain_grad, second_shift_grad = norm_back(
        upstream, second_normed, second_scale, gain_two
    )
    outer_low = second_grad.astype(jnp.bfloat16)
    outer_bias_grad = jnp.sum(second_grad, axis=0)
    outer_weight_grad = jnp.dot(activated.T, outer_low, preferred_element_type=jnp.float32)
    inner_grad = jnp.dot(outer_low, outer_full.T, preferred_element_type=jnp.float32) * gelu_slope(
        inner
    )
    inner_low = inner_grad.astype(jnp.bfloat16)
    inner_bias_grad = jnp.sum(inner_grad, axis=0)
    inner_weight_grad = jnp.dot(first_low.T, inner_low, preferred_element_type=jnp.float32)
    first_grad = second_grad + jnp.dot(inner_low, inner_full.T, preferred_element_type=jnp.float32)
    hidden_grad, first_gain_grad, first_shift_grad = norm_back(
        first_grad, first_normed, first_scale, gain_one
    )
    attended_low = hidden_grad.astype(jnp.bfloat16)
    output_bias_grad = jnp.sum(hidden_grad, axis=0)
    output_weight_grad = jnp.dot(mixed.T, attended_low, preferred_element_type=jnp.float32)
    mixed_grad = jnp.dot(attended_low, output_full.T, preferred_element_type=jnp.float32).astype(
        jnp.bfloat16
    )
    delta = jnp.sum(
        (mixed_grad.astype(jnp.float32) * attention_value).reshape(row_count, H, HD), axis=2
    ).T

    def back_block(
        query_block,
        upstream_block,
        log_block,
        delta_block,
        key_block,
        value_block,
        key_start,
        grads,
    ):

        def back_compute(carried):
            query_grad, key_grad, value_grad = carried
            key_keep = key_start + offsets < length
            query_three = query_block.reshape(row_count, H, HD)
            upstream_three = upstream_block.reshape(row_count, H, HD)
            key_three = key_block.reshape(row_count, H, HD)
            value_three = value_block.reshape(row_count, H, HD)
            scores = jnp.einsum(
                "qhd,khd->hqk", query_three, key_three, preferred_element_type=jnp.float32
            )
            weights = jnp.where(
                key_keep[None, None, :], jnp.exp(scores - log_block[:, :, None]), 0.0
            )
            weight_grad = jnp.einsum(
                "qhd,khd->hqk", upstream_three, value_three, preferred_element_type=jnp.float32
            )
            score_grad = (weights * (weight_grad - delta_block[:, :, None])).astype(jnp.bfloat16)
            query_grad = query_grad + jnp.einsum(
                "hqk,khd->qhd", score_grad, key_three, preferred_element_type=jnp.float32
            ).reshape(row_count, D)
            key_grad = key_grad + jnp.einsum(
                "hqk,qhd->khd", score_grad, query_three, preferred_element_type=jnp.float32
            ).reshape(row_count, D)
            value_grad = value_grad + jnp.einsum(
                "hqk,qhd->khd",
                weights.astype(jnp.bfloat16),
                upstream_three,
                preferred_element_type=jnp.float32,
            ).reshape(row_count, D)
            return (query_grad, key_grad, value_grad)

        return lax.cond(key_start < length, back_compute, keep_state, grads)

    zero_grad = jnp.zeros((row_count, D), jnp.float32)

    def key_turn(turn_index, carried):
        key_block, value_block, query_grad, key_grad, value_grad = carried
        owner_index = (cycle_place - turn_index) % cycle_size
        query_grad, key_grad, value_grad = back_block(
            queries,
            mixed_grad,
            log_total,
            delta,
            key_block,
            value_block,
            owner_index * row_count,
            (query_grad, key_grad, value_grad),
        )
        key_block, value_block = passed_along((key_block, value_block), RING, 1)
        key_grad, value_grad = (
            passed_along(key_grad.astype(jnp.bfloat16), RING, 1).astype(key_grad.dtype),
            passed_along(value_grad.astype(jnp.bfloat16), RING, 1).astype(value_grad.dtype),
        )
        return (key_block, value_block, query_grad, key_grad, value_grad)

    key_block, value_block, query_grad, key_grad, value_grad = lax.fori_loop(
        0, cycle_size - 1, key_turn, (key_rows, values, zero_grad, zero_grad, zero_grad)
    )
    query_grad, key_grad, value_grad = back_block(
        queries,
        mixed_grad,
        log_total,
        delta,
        key_block,
        value_block,
        last_owner * row_count,
        (query_grad, key_grad, value_grad),
    )
    key_grad, value_grad = (
        passed_along(key_grad.astype(jnp.bfloat16), RING, 1).astype(key_grad.dtype),
        passed_along(value_grad.astype(jnp.bfloat16), RING, 1).astype(value_grad.dtype),
    )
    query_low = query_grad.astype(jnp.bfloat16) * 0.125
    key_low = key_grad.astype(jnp.bfloat16)
    value_low = value_grad.astype(jnp.bfloat16)
    query_weight_grad = jnp.dot(inputs.T, query_low, preferred_element_type=jnp.float32)
    query_bias_grad = jnp.sum(query_low.astype(jnp.float32), axis=0)
    key_weight_grad = jnp.dot(inputs.T, key_low, preferred_element_type=jnp.float32)
    value_weight_grad = jnp.dot(inputs.T, value_low, preferred_element_type=jnp.float32)
    value_bias_grad = jnp.sum(value_low.astype(jnp.float32), axis=0)
    input_grad = (
        hidden_grad
        + jnp.dot(query_low, query_full.T, preferred_element_type=jnp.float32)
        + jnp.dot(key_low, key_full.T, preferred_element_type=jnp.float32)
        + jnp.dot(value_low, value_full.T, preferred_element_type=jnp.float32)
    ).astype(jnp.bfloat16)[None]
    local_grads = (
        query_weight_grad,
        query_bias_grad,
        key_weight_grad,
        value_weight_grad,
        value_bias_grad,
        output_weight_grad,
        output_bias_grad,
        first_gain_grad,
        first_shift_grad,
        inner_weight_grad,
        inner_bias_grad,
        outer_weight_grad,
        outer_bias_grad,
        second_gain_grad,
        second_shift_grad,
    )
    shards = (
        lax.psum_scatter(
            local_grads[0].astype(jnp.bfloat16), FSDP, scatter_dimension=0, tiled=True
        ).astype(jnp.float32),
        lax.psum_scatter(
            local_grads[1].astype(jnp.bfloat16), FSDP, scatter_dimension=0, tiled=True
        ).astype(jnp.float32),
        lax.psum_scatter(
            local_grads[2].astype(jnp.bfloat16), FSDP, scatter_dimension=0, tiled=True
        ).astype(jnp.float32),
        lax.psum_scatter(
            local_grads[3].astype(jnp.bfloat16), FSDP, scatter_dimension=0, tiled=True
        ).astype(jnp.float32),
        lax.psum_scatter(
            local_grads[4].astype(jnp.bfloat16), FSDP, scatter_dimension=0, tiled=True
        ).astype(jnp.float32),
        lax.psum_scatter(
            local_grads[5].astype(jnp.bfloat16), FSDP, scatter_dimension=0, tiled=True
        ).astype(jnp.float32),
        lax.psum_scatter(
            local_grads[6].astype(jnp.bfloat16), FSDP, scatter_dimension=0, tiled=True
        ).astype(jnp.float32),
        lax.psum_scatter(
            local_grads[7].astype(jnp.bfloat16), FSDP, scatter_dimension=0, tiled=True
        ).astype(jnp.float32),
        lax.psum_scatter(
            local_grads[8].astype(jnp.bfloat16), FSDP, scatter_dimension=0, tiled=True
        ).astype(jnp.float32),
        lax.psum_scatter(
            local_grads[9].astype(jnp.bfloat16), FSDP, scatter_dimension=0, tiled=True
        ).astype(jnp.float32),
        lax.psum_scatter(
            local_grads[10].astype(jnp.bfloat16), FSDP, scatter_dimension=0, tiled=True
        ).astype(jnp.float32),
        lax.psum_scatter(
            local_grads[11].astype(jnp.bfloat16), FSDP, scatter_dimension=0, tiled=True
        ).astype(jnp.float32),
        lax.psum_scatter(
            local_grads[12].astype(jnp.bfloat16), FSDP, scatter_dimension=0, tiled=True
        ).astype(jnp.float32),
        lax.psum_scatter(
            local_grads[13].astype(jnp.bfloat16), FSDP, scatter_dimension=0, tiled=True
        ).astype(jnp.float32),
        lax.psum_scatter(
            local_grads[14].astype(jnp.bfloat16), FSDP, scatter_dimension=0, tiled=True
        ).astype(jnp.float32),
    )
    totals = (
        lax.psum(shards[0].astype(jnp.bfloat16), RING).astype(jnp.float32),
        lax.psum(shards[1].astype(jnp.bfloat16), RING).astype(jnp.float32),
        lax.psum(shards[2].astype(jnp.bfloat16), RING).astype(jnp.float32),
        lax.psum(shards[3].astype(jnp.bfloat16), RING).astype(jnp.float32),
        lax.psum(shards[4].astype(jnp.bfloat16), RING).astype(jnp.float32),
        lax.psum(shards[5].astype(jnp.bfloat16), RING).astype(jnp.float32),
        lax.psum(shards[6].astype(jnp.bfloat16), RING).astype(jnp.float32),
        lax.psum(shards[7].astype(jnp.bfloat16), RING).astype(jnp.float32),
        lax.psum(shards[8].astype(jnp.bfloat16), RING).astype(jnp.float32),
        lax.psum(shards[9].astype(jnp.bfloat16), RING).astype(jnp.float32),
        lax.psum(shards[10].astype(jnp.bfloat16), RING).astype(jnp.float32),
        lax.psum(shards[11].astype(jnp.bfloat16), RING).astype(jnp.float32),
        lax.psum(shards[12].astype(jnp.bfloat16), RING).astype(jnp.float32),
        lax.psum(shards[13].astype(jnp.bfloat16), RING).astype(jnp.float32),
        lax.psum(shards[14].astype(jnp.bfloat16), RING).astype(jnp.float32),
    )
    return (
        layer_output,
        input_grad,
        totals[0],
        totals[1],
        totals[2],
        totals[3],
        totals[4],
        totals[5],
        totals[6],
        totals[7],
        totals[8],
        totals[9],
        totals[10],
        totals[11],
        totals[12],
        totals[13],
        totals[14],
    )


def solution(mesh):
    small = mesh.shape[RING] == CTX and mesh.shape[FSDP] == GROUP
    return jax.shard_map(
        small_plane if small else per_device,
        mesh=mesh,
        in_specs=(
            P(FSDP, RING, None),
            P(),
            P(FSDP, None),
            P(FSDP),
            P(FSDP, None),
            P(FSDP, None),
            P(FSDP),
            P(FSDP, None),
            P(FSDP),
            P(FSDP),
            P(FSDP),
            P(FSDP, None),
            P(FSDP),
            P(FSDP, None),
            P(FSDP),
            P(FSDP),
            P(FSDP),
            P(FSDP, RING, None),
        ),
        out_specs=(
            P(FSDP, RING, None),
            P(FSDP, RING, None),
            P(FSDP, None),
            P(FSDP),
            P(FSDP, None),
            P(FSDP, None),
            P(FSDP),
            P(FSDP, None),
            P(FSDP),
            P(FSDP),
            P(FSDP),
            P(FSDP, None),
            P(FSDP),
            P(FSDP, None),
            P(FSDP),
            P(FSDP),
            P(FSDP),
        ),
        check_vma=False,
    )
```

```python
import functools

import jax
import jax.numpy as jnp
from jax import lax
from jax.experimental import pallas as pl
from jax.experimental.pallas import tpu as pltpu
from jax.sharding import PartitionSpec as P

RING = "ctx"
FSDP = "fsdp"
D = 768
H = 12
HD = 64


epsilon = 1e-05


def passed_along(value, axis, steps):
    count = lax.axis_size(axis)
    pairs = [(source, (source + steps) % count) for source in range(count)]
    return lax.ppermute(value, axis, pairs)


def normalize(hidden):
    centred = hidden - jnp.mean(hidden, axis=1, keepdims=True)
    scale = lax.rsqrt(jnp.mean(centred * centred, axis=1, keepdims=True) + epsilon)
    return (centred * scale, scale)


def norm_back(upstream, normed, scale, gain):
    gain_grad = jnp.sum(upstream * normed, axis=0)
    shift_grad = jnp.sum(upstream, axis=0)
    scaled = upstream * gain
    hidden_grad = scale * (
        scaled
        - jnp.mean(scaled, axis=1, keepdims=True)
        - normed * jnp.mean(scaled * normed, axis=1, keepdims=True)
    )
    return (hidden_grad, gain_grad, shift_grad)


def gelu_slope(inner):
    return (
        0.5 * (1.0 + lax.erf(inner * 0.7071067811865476))
        + inner * jnp.exp(-0.5 * inner * inner) * 0.3989422804014327
    )


bf16 = jnp.bfloat16
f32 = jnp.float32
FF = 3072
ROWS = 384
CTX = 8
GROUP = 4
LOCAL = 3
SLOTS = 3072
QUERIES = 1536
TILE = 768
CHUNK = 512
WIDE = 640
MESH = pl.DeviceIdType.MESH


def multiple(value, step):
    return pl.multiple_of(value * step, step)


class Place:
    def __init__(self):
        self.c = lax.axis_index(RING)
        self.z = lax.axis_index(FSDP)
        c = self.c
        self.core = c % 2
        self.p = c // 2
        self.x = self.p % 2
        self.y = c // 4
        self.p_x = self.p + 1 - 2 * self.x
        self.p_y = self.p + 2 - 4 * self.y
        self.p_d = self.p_y + 1 - 2 * self.x
        self.to_core = (c + 1 - 2 * self.core, self.z)
        self.to_x = (2 * self.p_x + self.core, self.z)
        self.to_y = (2 * self.p_y + self.core, self.z)
        self.to_d = (2 * self.p_d + self.core, self.z)

    def to_z(self, step):
        return (self.c, (self.z + step) % GROUP)

    def from_z(self, step):
        return (self.z + GROUP - step) % GROUP


class Net:
    def __init__(self, sends, receives):
        self.sends = sends
        self.receives = receives
        self.index = {}
        self.open = []

    def of(self, name):
        return self.index.setdefault(name, len(self.index))

    def copy(self, name, src, dst, device):
        i = self.of(name)
        return pltpu.make_async_remote_copy(
            src_ref=src,
            dst_ref=dst,
            send_sem=self.sends.at[i],
            recv_sem=self.receives.at[i],
            device_id=device,
            device_id_type=MESH,
        )

    def start(self, name, src, dst, device):
        self.launch(name, lambda: (src, dst, device))

    def launch(self, name, make, when=None):
        if when is None:
            self.copy(name, *make()).start()
        else:
            pl.when(when())(lambda: self.copy(name, *make()).start())
        self.open.append((name, make, when))

    def sent(self, name, make, when):
        if when is None:
            self.copy(name, *make()).wait_send()
        else:
            pl.when(when())(lambda: self.copy(name, *make()).wait_send())

    def landed(self, name, dst, device):
        self.copy(name, dst, dst, device).wait_recv()

    def finish(self, name):
        for entry in self.open:
            if entry[0] == name:
                self.sent(*entry)
        self.open = [entry for entry in self.open if entry[0] != name]

    def drain(self):
        for entry in self.open:
            self.sent(*entry)
        self.open = []


def greet(place, with_z=True):
    barrier = pltpu.get_barrier_semaphore()
    partners = [place.to_core, place.to_x, place.to_y, place.to_d]
    if with_z:
        partners += [place.to_z(step) for step in range(1, GROUP)]
    for partner in partners:
        pl.semaphore_signal(barrier, inc=1, device_id=partner, device_id_type=MESH)
    pl.semaphore_wait(barrier, len(partners))


def dot(a, b):
    return jnp.dot(a, b, preferred_element_type=f32)


def dot_nt(a, b):
    return lax.dot_general(a, b, (((1,), (1,)), ((), ())), preferred_element_type=f32)


def dot_tn(a, b):
    return lax.dot_general(a, b, (((0,), (0,)), ((), ())), preferred_element_type=f32)


def parts_of(value):
    high = value.astype(bf16).astype(f32)
    rest = value - high
    middle = rest.astype(bf16).astype(f32)
    return high, middle, rest - middle


def added(a, b):
    return (a.astype(f32) + b.astype(f32)).astype(bf16)


def forward_kernel(
    lengths,
    x_in,
    wqkv_in,
    vec_in,
    inner_in,
    outer_in,
    wo_in,
    cot_in,
    low_out,
    mg_out,
    gi_out,
    gw_out,
    own_out,
    summed_out,
    hg_out,
    small_out,
    xs_out,
    wqkv_out,
    qt_out,
    ka_out,
    va_out,
    kt_out,
    ot_out,
    lse_out,
    xall,
    wqkv,
    vec,
    qt,
    ka,
    va,
    kt,
    vt,
    ot,
    lse,
    mix,
    mixed,
    acc,
    top,
    iw,
    ow,
    wo,
    cot,
    work,
    first,
    normed,
    second,
    slope,
    act,
    low,
    lower,
    gi,
    gw,
    mg,
    small,
    scales,
    ro,
    ax,
    ay,
    az,
    summed,
    sends,
    receives,
    locals_,
):
    at = Place()
    net = Net(sends, receives)
    c, z, core, p = at.c, at.z, at.core, at.p
    other = 1 - core
    chips = [at.p_d, at.p_x, at.p_y, p]
    devices = [at.to_d, at.to_x, at.to_y]
    slots = []

    def local(src, dst):
        copy = pltpu.make_async_copy(src, dst, locals_.at[len(slots)])
        slots.append(copy)
        copy.start()
        return copy

    def inner_at(ref, chip, side):
        return ref.at[:, pl.ds(multiple(2 * chip + side, 384), 384)]

    def outer_at(ref, chip, side):
        return ref.at[0, 2 * chip + side]

    def wo_at(ref, chip, side):
        return ref.at[chip, :, pl.ds(multiple(side, 384), 384)]

    weights = {
        "wo": (wo_in, wo, wo_at),
        "inner": (inner_in, iw, inner_at),
        "outer": (outer_in, ow, outer_at),
    }

    def block_at(chip, side, part=slice(None)):
        return xall.at[chip, side, part]

    greet(at)

    early, late = pl.ds(0, 2), pl.ds(2, 2)
    net.start("sx0", x_in.at[early], block_at(p, core, early), at.to_x)
    net.start("sy1", x_in.at[late], block_at(p, core, late), at.to_y)
    net.start("sx1", x_in.at[late], block_at(p, core, late), at.to_x)
    net.start("sy0", x_in.at[early], block_at(p, core, early), at.to_y)
    net.start("sc", x_in, block_at(p, core), at.to_core)
    for step in range(1, GROUP):
        net.start(("vec", step), vec_in, vec.at[z], at.to_z(step))
    class Along:
        def __init__(self, name, source, region):
            self.name = name
            self.source = source
            self.region = region

        def send(self):
            name, source, region = self.name, self.source, self.region
            for step in (2, 1, 3):
                when = {1: lambda: z < 3, 2: None, 3: lambda: z > 0}[step]

                def make(step=step):
                    return source, region(z), at.to_z(step)

                net.launch((name, "z", step), make, when)

        def relay(self):
            name, region = self.name, self.region

            def up():
                net.copy((name, "z", 2), region(z - 2), region(z - 2), at.to_z(2)).wait_recv()

            def down():
                net.copy((name, "z", 2), region(z + 2), region(z + 2), at.to_z(2)).wait_recv()

            pl.when(z == 2)(up)
            pl.when(z == 1)(down)
            net.launch(
                (name, "u"), lambda: (region(0), region(0), at.to_z(1)), lambda: z == 2
            )
            net.launch(
                (name, "d"), lambda: (region(3), region(3), at.to_z(3)), lambda: z == 1
            )

        def landed(self, step):
            name, region = self.name, self.region
            ref = region(at.from_z(step))
            if step == 1:
                pl.when(z > 0)(lambda: net.landed((name, "z", 1), region(at.from_z(1)), at.to_z(1)))
                pl.when(z == 0)(lambda: net.landed((name, "d"), region(3), at.to_z(1)))
            elif step == 3:
                pl.when(z < 3)(lambda: net.landed((name, "z", 3), region(at.from_z(3)), at.to_z(3)))
                pl.when(z == 3)(lambda: net.landed((name, "u"), region(0), at.to_z(3)))
            else:
                pl.when((z == 0) | (z == 3))(
                    lambda: net.landed((name, "z", 2), region(at.from_z(2)), at.to_z(2))
                )
            return ref

    along = {"wq": Along("wq", wqkv_in.at[core], lambda shard: wqkv.at[shard, core])}
    for name, (src, dst, region) in weights.items():
        along[name] = Along(
            name,
            region(src, p, core),
            lambda shard, dst=dst, region=region: region(dst.at[shard], p, core),
        )

    def far_at(shard, side):
        return ow.at[shard, 1, pl.ds(4 * side, 4)]

    along["far"] = Along(
        "far", outer_in.at[1, pl.ds(4 * core, 4)], lambda shard: far_at(shard, core)
    )
    along["wq"].send()
    opening = [local(x_in, block_at(p, core)), local(vec_in, vec.at[z]), local(wqkv_in, wqkv.at[z])]
    owned = [
        local(wo_in, wo.at[z]),
        local(inner_in, iw.at[z]),
        local(outer_in, ow.at[z]),
        local(cot_in, cot),
    ]

    row64 = lax.broadcasted_iota(jnp.int32, (64, QUERIES), 0)
    row16 = lax.broadcasted_iota(jnp.int32, (16, SLOTS), 0)
    for h in range(LOCAL):
        qt[h, 64:128, :] = jnp.where(row64 == 0, 1.0, 0.0).astype(bf16)
        vt[h, 64:80, :] = jnp.where(row16 == 0, 1.0, 0.0).astype(bf16)

    along["wq"].relay()
    along["wo"].send()
    along["inner"].send()
    p_x, p_y, p_d = at.p_x, at.p_y, at.p_d

    def hand_on(label, ref, device):
        net.start(label, ref, ref, device)

    net.landed("sx0", block_at(p_x, core, early), at.to_x)
    hand_on("rx0", block_at(p_x, core, early), at.to_y)
    net.landed("sy1", block_at(p_y, core, late), at.to_y)
    hand_on("ry1", block_at(p_y, core, late), at.to_x)
    for step in range(1, GROUP):
        source = at.from_z(step)
        along["wq"].landed(step)
        net.start(("wqc", step), wqkv.at[source, core], wqkv.at[source, core], at.to_core)
    along["wo"].relay()
    net.landed("sx1", block_at(p_x, core, late), at.to_x)
    hand_on("cx", block_at(p_x, core), at.to_core)
    net.landed("sy0", block_at(p_y, core, early), at.to_y)
    hand_on("cy", block_at(p_y, core), at.to_core)
    for copy in opening:
        copy.wait()
    for step in range(1, GROUP):
        source = at.from_z(step)
        net.landed(("vec", step), vec.at[source], at.to_z(step))
        net.landed(("wqc", step), wqkv.at[source, other], at.to_core)

    bias = vec[p][0:1, 0:WIDE].astype(f32)
    lane = lax.broadcasted_iota(jnp.int32, (ROWS, 128), 1)
    row = lax.broadcasted_iota(jnp.int32, (ROWS, 128), 0)
    count = lengths[z]

    def project(chip, side, column):
        block = 2 * chip + side
        rows = xall[chip, side].reshape(ROWS, D)
        keep = block * ROWS + row < count
        mark = jnp.where(keep, 0.0, -1e30)
        at_rows = pl.ds(multiple(block, ROWS), ROWS)
        width = 384 if column is None else WIDE
        full = wqkv[...].reshape(D, WIDE)
        y = dot(rows, full[:, 0:width]) + bias[:, 0:width]
        for h in range(LOCAL):
            g = y[:, 128 * h : 128 * h + 128]
            ka[h, at_rows, :] = jnp.where(
                lane < 64, g, jnp.where(lane == 64, mark, jnp.where(lane < 68, 1.0, 0.0))
            ).astype(bf16)
            va[h, at_rows, :] = jnp.where(
                lane < 64, pltpu.roll(g, 64, 1), jnp.where(lane < 67, 1.0, 0.0)
            ).astype(bf16)
            turned = g.T.astype(bf16)
            kt[h, :, at_rows] = turned[0:64]
            vt[h, 0:64, at_rows] = turned[64:128]
        if column is not None:
            q = (y[:, 384:WIDE] * 0.125).T.astype(bf16)
            for h in range(LOCAL):
                qt[h, 0:64, pl.ds(multiple(column, ROWS), ROWS)] = q[64 * h : 64 * h + 64]

    def chip_of(i):
        return p + (i % 2) * (1 - 2 * at.x) + (i // 2) * (2 - 4 * at.y)

    def project_own(i, carried):
        project(chip_of(i), core, 3 * (1 - (i + 1) // 2) + i * ((i + 1) // 2))
        return carried

    def project_other(i, carried):
        project(chip_of(i), other, None)
        return carried

    along["outer"].send()
    lax.fori_loop(0, 3, project_own, 0)
    net.landed("sc", block_at(p, other), at.to_core)
    net.landed("cx", block_at(p_x, other), at.to_core)
    net.landed("cy", block_at(p_y, other), at.to_core)
    lax.fori_loop(0, 3, project_other, 0)
    net.landed("rx0", block_at(p_d, core, early), at.to_y)
    net.landed("ry1", block_at(p_d, core, late), at.to_x)
    hand_on("cd", block_at(p_d, core), at.to_core)
    project(p_d, core, 0)
    net.landed("cd", block_at(p_d, other), at.to_core)
    project(p_d, other, None)

    kept = [local(block_at(chips[r], core), xs_out.at[r]) for r in range(4)]
    for src, dst in (
        (wqkv, wqkv_out),
        (qt, qt_out),
        (ka, ka_out),
        (va, va_out),
        (kt, kt_out),
    ):
        local(src, dst)

    def part_of(name, step, chip, side):
        _, dst, region = weights[name]
        return region(dst.at[at.from_z(step)], chip, side)

    def hand(label, name, step, chip, device):
        def make():
            ref = part_of(name, step, chip, core)
            return ref, ref, device

        net.launch(label, make)

    steps_all = tuple(range(1, GROUP))

    def plane_out(name, steps=steps_all):
        for step in steps:
            along[name].landed(step)
            hand((name, "x", step), name, step, p, at.to_x)
            hand((name, "y", step), name, step, p, at.to_y)
            hand((name, "c", step), name, step, p, at.to_core)

    def relay_by_x(name, step):
        return (step + (name == "outer")) % 2 == 1

    def plane_relay(name, steps=steps_all):
        for step in steps:
            net.landed((name, "x", step), part_of(name, step, p_x, core), at.to_x)
            net.landed((name, "y", step), part_of(name, step, p_y, core), at.to_y)
            if relay_by_x(name, step):
                hand((name, "r", step), name, step, p_y, at.to_x)
            else:
                hand((name, "r", step), name, step, p_x, at.to_y)
            hand((name, "cx", step), name, step, p_x, at.to_core)
            hand((name, "cy", step), name, step, p_y, at.to_core)

    def plane_last(name, steps=steps_all):
        for step in steps:
            far = part_of(name, step, p_d, core)
            net.landed((name, "r", step), far, at.to_x if relay_by_x(name, step) else at.to_y)
            hand((name, "cd", step), name, step, p_d, at.to_core)

    def plane_in(name):
        for step in steps_all:
            for tag, chip in (("c", p), ("cx", p_x), ("cy", p_y), ("cd", p_d)):
                net.landed((name, tag, step), part_of(name, step, chip, other), at.to_core)

    plane_out("wo")
    along["inner"].relay()

    def attend(h, tile):
        cols = pl.ds(multiple(tile, TILE), TILE)
        queries = qt[h, :, cols]
        top[0:1, :] = jnp.full((1, TILE), -3e38, f32)
        acc[...] = jnp.zeros((80, TILE), f32)

        def some(half, carried):
            for j in range(SLOTS // CHUNK // 2):
                rows = pl.ds(multiple(half * (SLOTS // CHUNK // 2) + j, CHUNK), CHUNK)
                scores = dot(ka[h, rows, :], queries)
                before = top[0:1, :]
                newest = jnp.maximum(before, jnp.max(scores, axis=0, keepdims=True))
                probs = jnp.exp(scores - newest).astype(bf16)
                acc[...] = acc[...] * jnp.exp(before - newest) + dot(vt[h, :, rows], probs)
                top[0:1, :] = newest
            return carried

        lax.fori_loop(0, 2, some, 0)
        total = acc[64:65, :]
        value = acc[0:64, :] / total
        ot[h, :, cols] = value
        lse[h, 0:1, cols] = top[0:1, :] + jnp.log(total)
        low_value = value.astype(bf16)
        at_head = pl.ds(multiple(h, 64), 64)
        mix[2 * tile, at_head, :] = low_value[:, 0:384]
        mix[2 * tile + 1, at_head, :] = low_value[:, 384:768]

    def send_mixed(name, index, device):
        net.launch(name, lambda: (mix.at[index], mixed.at[p], device))

    plan = {
        1: [lambda: plane_relay("wo"), lambda: plane_out("inner")],
        2: [
            lambda: plane_last("wo"),
            along["outer"].relay,
            along["far"].send,
            lambda: plane_relay("inner", (1,)),
        ],
        3: [
            lambda: send_mixed("md", 0, at.to_d),
            lambda: send_mixed("mx", 1, at.to_x),
            lambda: plane_relay("inner", (2,)),
        ],
        4: [lambda: plane_relay("inner", (3,))],
        5: [lambda: plane_out("outer"), lambda: plane_last("inner")],
    }

    def take(steps):
        for step in steps:
            step()

    def unit(u, carried):
        for when, steps in plan.items():
            pl.when(u == when)(functools.partial(take, steps))
        attend(u % LOCAL, u // LOCAL)
        return carried

    lax.fori_loop(0, 2 * LOCAL, unit, 0)
    send_mixed("my", 2, at.to_y)
    along["far"].relay()
    mixed[p] = mix[3]
    local(ot, ot_out)
    local(lse, lse_out)

    plane_in("wo")
    for copy in owned:
        copy.wait()
    net.landed("md", mixed.at[p_d], at.to_d)
    net.landed("mx", mixed.at[p_x], at.to_x)
    net.landed("my", mixed.at[p_y], at.to_y)
    table = vec[0].astype(f32) + vec[1].astype(f32) + vec[2].astype(f32) + vec[3].astype(f32)
    output_add, gain_one, shift_one, outer_add, gain_two, shift_two = [
        table[2 + i : 3 + i, :] for i in range(6)
    ]
    heads = mixed[...].reshape(D, ROWS)
    work[...] = dot_tn(heads, wo[...].reshape(D, D))
    low[...] = xall[p, core].reshape(ROWS, D)

    def blocks(step, start=0):
        def one(i, carried):
            return step(pl.ds(multiple(i, 128), 128), i, carried)

        return lax.fori_loop(0, ROWS // 128, one, start)

    def mean(value):
        return jnp.mean(value, axis=1, keepdims=True)

    def column(value):
        return jnp.sum(value, axis=0, keepdims=True)

    def norm(hidden):
        centred = hidden - mean(hidden)
        scale = lax.rsqrt(mean(centred * centred) + 1e-05)
        return centred * scale, scale

    def first_norm(rows, i, carried):
        value, scale = norm(low[rows, :].astype(f32) + work[rows, :] + output_add)
        normed[rows, :] = value
        scales[0, rows, :] = jnp.broadcast_to(scale, (128, 128))
        value = value * gain_one + shift_one
        first[rows, :] = value
        low[rows, :] = value.astype(bf16)
        return carried

    blocks(first_norm)
    plane_relay("outer")
    for step in steps_all:
        along["far"].landed(step)
        source = at.from_z(step)
        net.start(("farc", step), far_at(source, core), far_at(source, core), at.to_core)

    plane_in("inner")
    inner_weight = iw[...].reshape(D, FF)
    for q in range(4):
        cols = pl.ds(D * q, D)
        slope[:, cols] = dot(low[...], inner_weight[:, D * q : D * q + D])
        add = vec[q][1:2, :].astype(f32)

        def activate(rows, i, carried, cols=cols, add=add):
            u = slope[rows, cols] + add
            gate = 0.5 * (1.0 + lax.erf(u * 0.7071067811865476))
            act[rows, cols] = (u * gate).astype(bf16)
            slope[rows, cols] = gate + u * jnp.exp(-0.5 * u * u) * 0.3989422804014327
            return carried

        blocks(activate)
        if q == 1:
            plane_last("outer")
    plane_in("outer")
    for step in steps_all:
        net.landed(("farc", step), far_at(at.from_z(step), other), at.to_core)
    total = None
    for q in range(4):
        term = dot(act[:, D * q : D * q + D], ow[q].reshape(D, D))
        total = term if total is None else total + term
    work[...] = total

    nothing = jnp.zeros((1, D), f32)

    def second_norm(rows, i, carried):
        gains, shifts, biases = carried
        value, scale = norm(first[rows, :] + work[rows, :] + outer_add)
        slot = c * ROWS + i * 128 + lax.broadcasted_iota(jnp.int32, (128, D), 0)
        keep = slot < count
        lower[rows, :] = jnp.where(keep, value * gain_two + shift_two, 0.0).astype(bf16)
        upstream = jnp.where(keep, cot[rows, :].astype(f32), 0.0)
        product = upstream * value
        scaled = upstream * gain_two
        grad = scale * (scaled - mean(scaled) - value * mean(scaled * value))
        second[rows, :] = grad
        cot[rows, :] = grad.astype(bf16)
        return gains + column(product), shifts + column(upstream), biases + column(grad)

    gain_two_grad, shift_two_grad, outer_bias_grad = blocks(second_norm, (nothing,) * 3)
    local(lower, low_out)

    for copy in kept:
        copy.wait()
    for name in ("rx0", "ry1", "cx", "cy", "cd"):
        net.finish(name)
    def outer_row(t, chip, side):
        j = 2 * chip + side
        return xall.at[t, j // 4, j % 4]

    for q in range(4):
        term = dot_tn(act[:, D * q : D * q + D], cot[...]).astype(bf16)
        xall[q] = term.reshape(2, 4, 96, D)
        for r in range(4):
            net.start(("go", q, r), outer_row(q, chips[r], other), ro.at[r, q], at.to_core)

    upper, under = pl.ds(0, 48), pl.ds(48, 48)

    def outer_pair(chip, shard):
        j = 2 * chip + core
        return xall.at[pl.ds(shard, 2), j // 4, j % 4, under]

    def outer_add_core():
        for q in range(4):
            for r in range(4):
                net.landed(("go", q, r), ro.at[r, q], at.to_core)

        def one(t, carried):
            for r in range(4):
                ref = outer_row(t, chips[r], core)
                ref[...] = added(ref[...], ro[r, t])
            return carried

        lax.fori_loop(0, GROUP, one, 0)
        net.start("oxn", outer_pair(p_x, 0), ax.at[0], at.to_x)
        net.start("oyn", outer_pair(p_y, 2), ay.at[0], at.to_y)
        net.start("oxd", outer_pair(p_d, 0), ax.at[1], at.to_x)
        net.start("oyd", outer_pair(p_d, 2), ay.at[1], at.to_y)

        for r in range(2):
            for step in (2, 1, 3):
                device = at.to_z(step)
                net.start(
                    ("uz", r, step),
                    outer_row(device[1], chips[r], core).at[upper],
                    az.at[r, step - 1],
                    device,
                )

    def outer_add_shards():
        for r in range(2):
            total = outer_row(z, chips[r], core).at[upper][...].astype(f32)
            for step in steps_all:
                net.landed(("uz", r, step), az.at[r, step - 1], at.to_z(step))
                total = total + az[r, step - 1].astype(f32)
            summed[r] = total.astype(bf16)
        local(summed, summed_out)

    def outer_add_plane():
        net.landed("oxn", ax.at[0], at.to_x)
        net.landed("oyn", ay.at[0], at.to_y)
        net.landed("oxd", ax.at[1], at.to_x)
        net.landed("oyd", ay.at[1], at.to_y)
        for t in range(2):
            for shard, chip, ref in (
                (t, p, ax.at[0, t]),
                (t, p_y, ax.at[1, t]),
                (t + 2, p, ay.at[0, t]),
                (t + 2, p_x, ay.at[1, t]),
            ):
                row = outer_row(shard, chip, core).at[under]
                row[...] = added(row[...], ref[...])

    total = None
    for q in range(4):
        cols = pl.ds(D * q, D)
        work[...] = dot_nt(cot[...], ow[q].reshape(D, D))

        def slopes(rows, i, carried, cols=cols):
            grad = work[rows, :] * slope[rows, cols]
            act[rows, cols] = grad.astype(bf16)
            return carried + column(grad)

        small[q, 1:2, :] = blocks(slopes, nothing)
        grads = act[:, D * q : D * q + D]
        term = dot_nt(grads, inner_weight[:, D * q : D * q + D])
        total = term if total is None else total + term
        if q == 0:
            outer_add_core()
    work[...] = total

    def first_back(rows, i, carried):
        gains, shifts, biases = carried
        value = normed[rows, :]
        upstream = second[rows, :] + work[rows, :]
        scaled = upstream * gain_one
        grad = scales[0, rows, 0:1] * (scaled - mean(scaled) - value * mean(scaled * value))
        first[rows, :] = grad
        lower_grad[rows, :] = grad.astype(bf16)
        return gains + column(upstream * value), shifts + column(upstream), biases + column(grad)

    lower_grad = cot
    gain_one_grad, shift_one_grad, output_bias_grad = blocks(first_back, (nothing,) * 3)
    local(first, hg_out)
    mg[...] = dot_nt(wo[...].reshape(D, D), lower_grad[...]).astype(bf16).reshape(GROUP, 192, ROWS)
    for r in range(3):
        net.start(("mg", r), mg.at[chips[r]], mg_out.at[r], devices[r])
    local(mg.at[p], mg_out.at[3])
    for q in range(4):
        grads = act[:, D * q : D * q + D]
        gi[:, :, D * q : D * q + D] = dot_tn(low[...], grads).astype(bf16).reshape(GROUP, 192, D)
    local(gi, gi_out)
    gw[...] = dot(heads, lower_grad[...]).astype(bf16).reshape(GROUP, GROUP, 48, D)
    local(gw, gw_out)
    narrow = [
        output_bias_grad,
        gain_one_grad,
        shift_one_grad,
        outer_bias_grad,
        gain_two_grad,
        shift_two_grad,
    ]
    for t in range(GROUP):
        small[t, 0:1, :] = nothing
        for i, value in enumerate(narrow):
            small[t, 2 + i : 3 + i, :] = value
    local(small, small_out)
    outer_add_plane()
    outer_add_shards()
    for r in range(4):
        j = 2 * chips[r] + core
        local(xall.at[:, j // 4, j % 4], own_out.at[r])
    for r in range(3):
        net.landed(("mg", r), mg_out.at[r], devices[r])
    waited = len(opening) + len(owned)
    for copy in slots[waited:]:
        if not any(copy is other_copy for other_copy in kept):
            copy.wait()
    net.drain()


FORWARD_COPIES = 140


def forward_call(*operands):
    any_ = pl.BlockSpec(memory_space=pl.ANY)
    shape = jax.ShapeDtypeStruct
    vmem = pltpu.VMEM
    return pl.pallas_call(
        forward_kernel,
        name="forward_attention",
        out_shape=(
            shape((ROWS, D), bf16),
            shape((4, 192, ROWS), bf16),
            shape((GROUP, 192, FF), bf16),
            shape((GROUP, GROUP, 48, D), bf16),
            shape((4, GROUP, 96, D), bf16),
            shape((2, 48, D), bf16),
            shape((ROWS, D), f32),
            shape((GROUP, 8, D), f32),
            shape((4, 4, 96, D), bf16),
            shape((GROUP, 2, 96, WIDE), bf16),
            shape((LOCAL, 128, QUERIES), bf16),
            shape((LOCAL, SLOTS, 128), bf16),
            shape((LOCAL, SLOTS, 128), bf16),
            shape((LOCAL, 64, SLOTS), bf16),
            shape((LOCAL, 64, QUERIES), f32),
            shape((LOCAL, 8, QUERIES), f32),
        ),
        in_specs=[pl.BlockSpec(memory_space=pltpu.SMEM)] + [any_] * 7,
        out_specs=[any_] * 16,
        scratch_shapes=[
            vmem((GROUP, 2, 4, 96, D), bf16),
            vmem((GROUP, 2, 96, WIDE), bf16),
            vmem((GROUP, 16, D), bf16),
            vmem((LOCAL, 128, QUERIES), bf16),
            vmem((LOCAL, SLOTS, 128), bf16),
            vmem((LOCAL, SLOTS, 128), bf16),
            vmem((LOCAL, 64, SLOTS), bf16),
            vmem((LOCAL, 80, SLOTS), bf16),
            vmem((LOCAL, 64, QUERIES), f32),
            vmem((LOCAL, 8, QUERIES), f32),
            vmem((4, 192, ROWS), bf16),
            vmem((GROUP, 192, ROWS), bf16),
            vmem((80, TILE), f32),
            vmem((8, TILE), f32),
            vmem((GROUP, 192, FF), bf16),
            vmem((GROUP, 2, CTX, 48, D), bf16),
            vmem((GROUP, GROUP, 48, D), bf16),
            vmem((ROWS, D), bf16),
            vmem((ROWS, D), f32),
            vmem((ROWS, D), f32),
            vmem((ROWS, D), f32),
            vmem((ROWS, D), f32),
            vmem((ROWS, FF), f32),
            vmem((ROWS, FF), bf16),
            vmem((ROWS, D), bf16),
            vmem((ROWS, D), bf16),
            vmem((GROUP, 192, FF), bf16),
            vmem((GROUP, GROUP, 48, D), bf16),
            vmem((GROUP, 192, ROWS), bf16),
            vmem((GROUP, 8, D), f32),
            vmem((1, ROWS, 128), f32),
            vmem((4, GROUP, 96, D), bf16),
            vmem((2, 2, 48, D), bf16),
            vmem((2, 2, 48, D), bf16),
            vmem((2, 3, 48, D), bf16),
            vmem((2, 48, D), bf16),
            pltpu.SemaphoreType.DMA((FORWARD_COPIES,)),
            pltpu.SemaphoreType.DMA((FORWARD_COPIES,)),
            pltpu.SemaphoreType.DMA((48,)),
        ],
        compiler_params=pltpu.CompilerParams(
            collective_id=0, has_side_effects=True, vmem_limit_bytes=67043328
        ),
    )(*operands)


def split_weights(place_p, query_weight, key_weight, value_weight):
    def columns(weight):
        return lax.dynamic_slice_in_dim(weight, place_p * 192, 192, axis=1)

    rows = query_weight.shape[0]
    pair = jnp.concatenate(
        [columns(key_weight).reshape(rows, 3, 64), columns(value_weight).reshape(rows, 3, 64)],
        axis=2,
    ).reshape(rows, 384)
    fill = jnp.zeros((rows, 64), bf16)
    return jnp.concatenate([pair, columns(query_weight), fill], axis=1).reshape(2, 96, WIDE)


def pack_vectors(query_bias, value_bias, inner_bias, vectors):
    nothing = jnp.zeros((3, 64), bf16)
    first = jnp.concatenate(
        [
            jnp.concatenate([nothing, value_bias.reshape(3, 64)], axis=1).reshape(384),
            query_bias,
            jnp.zeros((192,), bf16),
        ]
    )
    rest = jnp.stack(vectors)[:, None, :]
    mine = lax.broadcasted_iota(jnp.int32, (1, GROUP, 1), 1) == lax.axis_index(FSDP)
    rest = jnp.where(mine, rest, 0).astype(bf16).reshape(len(vectors), D)
    return jnp.concatenate([first[None], inner_bias[None], rest, jnp.zeros((8, D), bf16)])


SPAN = 256


def backward_kernel(
    mg_in,
    ot_in,
    lse_in,
    qt_in,
    ka_in,
    va_in,
    kt_in,
    gi_in,
    gw_in,
    own_in,
    summed_in,
    xs_in,
    wqkv_in,
    hg_in,
    small_in,
    dx_out,
    gqkv_out,
    gi_out,
    go_out,
    gw_out,
    small_out,
    mg,
    ot,
    lse,
    qa,
    qz,
    ka,
    va,
    kt,
    da,
    dz,
    kv,
    rkv,
    dq,
    so,
    si,
    ri,
    aix,
    aiy,
    boy,
    box,
    az,
    su,
    ux,
    uy,
    vx,
    vy,
    done_o,
    biy,
    bix,
    zo,
    zi,
    xs,
    wqkv,
    dqkv,
    sdx,
    rx,
    ry,
    bx,
    by,
    hg,
    dw,
    dwl,
    rdw,
    rzw,
    small,
    rsz,
    rsc,
    rsp,
    ssum,
    sends,
    receives,
    locals_,
):
    at = Place()
    net = Net(sends, receives)
    c, z, core, p = at.c, at.z, at.core, at.p
    other = 1 - core
    chips = [at.p_d, at.p_x, at.p_y, p]
    devices = [at.to_d, at.to_x, at.to_y]
    slots = []

    def local(src, dst):
        copy = pltpu.make_async_copy(src, dst, locals_.at[len(slots)])
        slots.append(copy)
        copy.start()
        return copy

    greet(at)
    upper, under = pl.ds(0, 48), pl.ds(48, 48)
    fore, aft = pl.ds(0, 2), pl.ds(2, 2)
    front, back = pl.ds(0, 384), pl.ds(384, 384)
    net.start("oby", own_in.at[2, fore, under], boy, at.to_y)
    net.start("obx", own_in.at[1, aft, under], box, at.to_x)
    for r in range(2, 4):
        for step in (2, 1, 3):
            device = at.to_z(step)
            net.start(
                ("uz", r, step), own_in.at[r, device[1], upper], az.at[r - 2, step - 1], device
            )
    loads = [
        local(mg_in, mg),
        local(ot_in, ot),
        local(lse_in, lse),
        local(qt_in, qa),
        local(ka_in, ka),
        local(va_in, va),
        local(kt_in, kt),
    ]

    def i_at(chip, side):
        return gi_in.at[:, :, pl.ds(multiple(2 * chip + side, 384), 384)]

    def w_at(chip, side):
        return gw_in.at[:, chip, :, pl.ds(multiple(side, 384), 384)]

    halves = [local(own_in, so), local(summed_in, su.at[pl.ds(0, 2)])]
    for r in range(4):
        net.start(("gi", r), i_at(chips[r], other), ri.at[r, :, 0:192], at.to_core)
        net.start(("gw", r), w_at(chips[r], other), ri.at[r, :, 192:240], at.to_core)
        halves.append(local(i_at(chips[r], core), si.at[r, :, 0:192]))
        halves.append(local(w_at(chips[r], core), si.at[r, :, 192:240]))
    later = [local(wqkv_in, wqkv), local(hg_in, hg), local(small_in, small)]
    for r in range(4):
        later.append(local(xs_in.at[r], xs.at[r]))

    for copy in loads:
        copy.wait()
    row16 = lax.broadcasted_iota(jnp.int32, (16, QUERIES), 0)
    row128 = lax.broadcasted_iota(jnp.int32, (128, QUERIES), 0)
    for h in range(LOCAL):
        high, middle, rest = parts_of(-lse[h, 0:1, :])
        qz[h] = jnp.where(row128 < 64, qa[h].astype(f32), 0.0).astype(bf16)
        qa[h, 64:80, :] = jnp.where(
            row16 == 0,
            1.0,
            jnp.where(
                row16 == 1, high, jnp.where(row16 == 2, middle, jnp.where(row16 == 3, rest, 0.0))
            ),
        ).astype(bf16)
        kv[h] = jnp.zeros((SLOTS, 128), f32)
        dz[h, 0:64, :] = jnp.zeros((64, QUERIES), bf16)
        da[h, 80:128, :] = jnp.zeros((48, QUERIES), bf16)
    row16 = lax.broadcasted_iota(jnp.int32, (16, ROWS), 0)
    for r in range(4):
        cols = pl.ds(ROWS * r, ROWS)
        for h in range(LOCAL):
            grad = mg[r, 64 * h : 64 * h + 64, :]
            delta = jnp.sum(grad.astype(f32) * ot[h, :, cols], axis=0, keepdims=True)
            high, middle, rest = parts_of(-delta)
            da[h, 0:64, cols] = grad
            dz[h, 64:128, cols] = grad
            da[h, 64:80, cols] = jnp.where(
                row16 == 0,
                high,
                jnp.where(row16 == 1, middle, jnp.where(row16 == 2, rest, 0.0)),
            ).astype(bf16)

    left, right = pl.ds(0, 128), pl.ds(128, 112)

    def along_shards(step):
        def one(t, carried):
            step(t)
            return carried

        lax.fori_loop(0, GROUP, one, 0)

    upper, under = pl.ds(0, 48), pl.ds(48, 48)

    def outer_second():
        halves[0].wait()
        net.landed("oby", boy, at.to_y)
        net.landed("obx", box, at.to_x)
        for t in range(2):
            so[3, t, under] = added(so[3, t, under], boy[t])
            so[3, t + 2, under] = added(so[3, t + 2, under], box[t])
        for i in range(1, GROUP):
            net.launch(
                ("oz", i),
                lambda i=i: (so.at[3, at.to_z(i)[1], under], zo.at[i - 1], at.to_z(i)),
            )

    def outer_shards():
        halves[1].wait()
        for r in range(2, 4):
            total = so[r, z, upper].astype(f32)
            for i in range(1, GROUP):
                net.landed(("uz", r, i), az.at[r - 2, i - 1], at.to_z(i))
                total = total + az[r - 2, i - 1].astype(f32)
            su[r] = total.astype(bf16)
        net.launch("uxn", lambda: (su.at[1, :, front], ux.at[0], at.to_x))
        net.launch("uyn", lambda: (su.at[2, :, back], uy.at[0], at.to_y))
        net.launch("uxd", lambda: (su.at[0, :, front], ux.at[1], at.to_x))
        net.launch("uyd", lambda: (su.at[0, :, back], uy.at[1], at.to_y))

    def outer_third():
        net.landed("uxn", ux.at[0], at.to_x)
        net.landed("uyn", uy.at[0], at.to_y)
        net.landed("uxd", ux.at[1], at.to_x)
        net.landed("uyd", uy.at[1], at.to_y)
        su[2, :, front] = added(su[2, :, front], ux[1])
        su[1, :, back] = added(su[1, :, back], uy[1])
        net.launch("uby", lambda: (su.at[2, :, front], vy, at.to_y))
        net.launch("ubx", lambda: (su.at[1, :, back], vx, at.to_x))
        su[3, :, front] = added(su[3, :, front], ux[0])
        su[3, :, back] = added(su[3, :, back], uy[0])

    def outer_last():
        total = so[3, z, under].astype(f32)
        for i in range(1, GROUP):
            net.landed(("oz", i), zo.at[i - 1], at.to_z(i))
            total = total + zo[i - 1].astype(f32)
        done_o[48:96] = total.astype(bf16)
        net.landed("uby", vy, at.to_y)
        net.landed("ubx", vx, at.to_x)
        done_o[0:48, front] = added(su[3, :, front], vy[...])
        done_o[0:48, back] = added(su[3, :, back], vx[...])

    def inner_core():
        for copy in halves[2:]:
            copy.wait()
        for r in range(4):
            net.landed(("gi", r), ri.at[r, :, 0:192], at.to_core)
            net.landed(("gw", r), ri.at[r, :, 192:240], at.to_core)

        def step(t):
            for r in range(4):
                si[r, t] = added(si[r, t], ri[r, t])

        along_shards(step)
        net.launch("ixn", lambda: (si.at[1, :, left], aix.at[0], at.to_x))
        net.launch("iyn", lambda: (si.at[2, :, right], aiy.at[0], at.to_y))
        net.launch("ixd", lambda: (si.at[0, :, left], aix.at[1], at.to_x))
        net.launch("iyd", lambda: (si.at[0, :, right], aiy.at[1], at.to_y))

    def inner_first():
        net.landed("ixn", aix.at[0], at.to_x)
        net.landed("iyn", aiy.at[0], at.to_y)
        net.landed("ixd", aix.at[1], at.to_x)
        net.landed("iyd", aiy.at[1], at.to_y)

        def step(t):
            si[2, t, left] = added(si[2, t, left], aix[1, t])
            si[1, t, right] = added(si[1, t, right], aiy[1, t])
            si[3, t, left] = added(si[3, t, left], aix[0, t])
            si[3, t, right] = added(si[3, t, right], aiy[0, t])

        along_shards(step)
        net.launch("iby", lambda: (si.at[2, :, left], biy, at.to_y))
        net.launch("ibx", lambda: (si.at[1, :, right], bix, at.to_x))

    def inner_second():
        net.landed("iby", biy, at.to_y)
        net.landed("ibx", bix, at.to_x)

        def step(t):
            si[3, t, left] = added(si[3, t, left], biy[t])
            si[3, t, right] = added(si[3, t, right], bix[t])

        along_shards(step)
        for i in range(1, GROUP):
            net.launch(
                ("iz", i), lambda i=i: (si.at[3, at.to_z(i)[1]], zi.at[i - 1], at.to_z(i))
            )

    def inner_last():
        total = si[3, z].astype(f32)
        for i in range(1, GROUP):
            net.landed(("iz", i), zi.at[i - 1], at.to_z(i))
            total = total + zi[i - 1].astype(f32)
        si[3, z] = total.astype(bf16)

    def go_at(chip, side):
        return go_out.at[2 * chip + side]

    def gi_at(chip, side):
        return gi_out.at[:, pl.ds(multiple(2 * chip + side, 384), 384)]

    def gw_at(chip, side):
        return gw_out.at[chip, :, pl.ds(multiple(side, 384), 384)]

    place_of = {"o": go_at, "i": gi_at, "w": gw_at}
    via_x = {"o": False, "i": True, "w": False}
    mine = {
        "o": lambda: done_o,
        "i": lambda: si.at[3, z, 0:192],
        "w": lambda: si.at[3, z, 192:240],
    }

    def spread(name):
        place = place_of[name]
        for tag, device in (("x", at.to_x), ("y", at.to_y), ("c", at.to_core)):
            net.launch(
                ("f", name, tag), lambda device=device: (mine[name](), place(p, core), device)
            )

    def pass_on(name):
        place = place_of[name]

        def hand(tag, chip, device):
            net.launch(
                ("f", name, tag), lambda: (place(chip, core), place(chip, core), device)
            )

        net.landed(("f", name, "x"), place(at.p_x, core), at.to_x)
        net.landed(("f", name, "y"), place(at.p_y, core), at.to_y)
        if via_x[name]:
            hand("r", at.p_y, at.to_x)
        else:
            hand("r", at.p_x, at.to_y)
        hand("cx", at.p_x, at.to_core)
        hand("cy", at.p_y, at.to_core)

    def finish_spread(name):
        place = place_of[name]
        far = place(at.p_d, core)
        net.landed(("f", name, "r"), far, at.to_x if via_x[name] else at.to_y)
        net.start(("f", name, "cd"), far, far, at.to_core)

    def close_spread(name):
        place = place_of[name]
        for tag, chip in (("c", p), ("cx", at.p_x), ("cy", at.p_y), ("cd", at.p_d)):
            net.landed(("f", name, tag), place(chip, other), at.to_core)

    def swap_kv(h):
        for r in range(4):
            net.launch(
                ("kv", h, r),
                lambda r=r: (
                    kv.at[h, pl.ds(multiple(2 * chips[r] + other, ROWS), ROWS)],
                    rkv.at[h, r],
                    at.to_core,
                ),
            )

    def attend(h, tile):
        cols = pl.ds(multiple(tile, TILE), TILE)
        queries = qa[h, :, cols]
        upstream = da[h, :, cols]
        queries_only = qz[h, :, cols]
        upstream_only = dz[h, :, cols]
        dq[h, :, cols] = jnp.zeros((64, TILE), f32)

        def some(half, carried):
            for j in range(SLOTS // SPAN // 2):
                rows = pl.ds(multiple(half * (SLOTS // SPAN // 2) + j, SPAN), SPAN)
                probs = jnp.exp(dot(ka[h, rows, :], queries))
                grads = (probs * dot(va[h, rows, :], upstream)).astype(bf16)
                kv[h, rows, :] += dot_nt(grads, queries_only) + dot_nt(
                    probs.astype(bf16), upstream_only
                )
                dq[h, :, cols] += dot(kt[h, :, rows], grads)
            return carried

        lax.fori_loop(0, 2, some, 0)

    plan = {
        1: [inner_core, outer_second],
        2: [lambda: swap_kv(0)],
        3: [outer_shards],
        4: [lambda: swap_kv(1), inner_first, outer_third],
        5: [inner_second, outer_last, lambda: spread("o")],
    }

    def take(steps):
        for step in steps:
            step()

    def unit(u, carried):
        for when, steps in plan.items():
            pl.when(u == when)(functools.partial(take, steps))
        attend(u // 2, u % 2)
        return carried

    lax.fori_loop(0, 2 * LOCAL, unit, 0)
    swap_kv(2)
    pass_on("o")
    local(done_o, go_at(p, core))

    for copy in later:
        copy.wait()
    weights = wqkv[...].reshape(D, WIDE)
    for h in range(LOCAL):
        for r in range(4):
            net.landed(("kv", h, r), rkv.at[h, r], at.to_core)
    sums = jnp.zeros((1, WIDE), f32)
    top, low = pl.ds(0, 192), pl.ds(192, 192)
    for r in range(4):
        cols = pl.ds(ROWS * r, ROWS)
        rows = pl.ds(multiple(2 * chips[r] + core, ROWS), ROWS)
        for h in range(LOCAL):
            dqkv[r, :, 128 * h : 128 * h + 128] = (kv[h, rows, :] + rkv[h, r]).astype(bf16)
        turned = jnp.concatenate(
            [dq[h, :, cols] for h in range(LOCAL)] + [jnp.zeros((64, ROWS), f32)], axis=0
        )
        dqkv[r, :, 384:WIDE] = (turned.T * 0.125).astype(bf16)
        block = dqkv[r]
        sums = sums + jnp.sum(block.astype(f32), axis=0, keepdims=True)
        update = dot_nt(block, weights)
        if r < 3:
            sdx[r] = update.astype(bf16)
        else:
            hg[...] += update
        if r == 1:
            net.start("dxn", sdx.at[1, top], rx.at[0], at.to_x)
            net.start("dxd", sdx.at[0, top], rx.at[1], at.to_x)
        if r == 2:
            net.start("dyn", sdx.at[2, low], ry.at[0], at.to_y)
            net.start("dyd", sdx.at[0, low], ry.at[1], at.to_y)
    small[p, 0:1, 0:WIDE] += sums
    for step in range(1, GROUP):
        net.start(("sz", step), small.at[at.to_z(step)[1]], rsz.at[step - 1], at.to_z(step))

    total = None
    for r in range(4):
        term = lax.dot_general(
            xs[r].reshape(ROWS, D), dqkv[r], (((0,), (0,)), ((), ())), preferred_element_type=f32
        )
        total = term if total is None else total + term
    dw[...] = total.reshape(GROUP, 2, 96, WIDE)
    dwl[...] = dw[:, other].astype(bf16)
    net.start("dwc", dwl, rdw, at.to_core)

    for step in range(1, GROUP):
        net.landed(("sz", step), rsz.at[step - 1], at.to_z(step))
    small[z] = small[z] + rsz[0] + rsz[1] + rsz[2]
    net.start("sc", small.at[z], rsc, at.to_core)
    net.landed("dwc", rdw, at.to_core)
    for t in range(GROUP):
        rdw[t] = added(dw[t, core], rdw[t])
    for step in range(1, GROUP):
        net.start(("dwz", step), rdw.at[at.to_z(step)[1]], rzw.at[step - 1], at.to_z(step))
    net.landed("sc", rsc, at.to_core)
    rsc[...] = small[z] + rsc[...]
    for r in range(3):
        net.start(("sp", r), rsc, rsp.at[r], devices[r])

    inner_last()
    for name in ("i", "w"):
        spread(name)
        local(mine[name](), place_of[name](p, core))

    net.landed("dxn", rx.at[0], at.to_x)
    net.landed("dxd", rx.at[1], at.to_x)
    sdx[2, top] = added(sdx[2, top], rx[1])
    net.start("dby", sdx.at[2, top], by, at.to_y)
    net.landed("dyn", ry.at[0], at.to_y)
    net.landed("dyd", ry.at[1], at.to_y)
    sdx[1, low] = added(sdx[1, low], ry[1])
    net.start("dbx", sdx.at[1, low], bx, at.to_x)
    hg[top] += rx[0].astype(f32)
    hg[low] += ry[0].astype(f32)

    for step in range(1, GROUP):
        net.landed(("dwz", step), rzw.at[step - 1], at.to_z(step))
    finished = rdw[z].astype(f32)
    for step in range(GROUP - 1):
        finished = finished + rzw[step].astype(f32)
    rdw[z] = finished.astype(bf16)
    for r in range(3):
        net.start(("fq", r), rdw.at[z], gqkv_out.at[p, core], devices[r])
    net.start("fqc", rdw.at[z], gqkv_out.at[p, core], at.to_core)
    local(rdw.at[z], gqkv_out.at[p, core])

    for r in range(3):
        net.landed(("sp", r), rsp.at[r], devices[r])
    ssum[...] = rsc[...] + rsp[0] + rsp[1] + rsp[2]
    local(ssum, small_out)

    for name in ("i", "w"):
        pass_on(name)
    for r in range(3):
        ref = gqkv_out.at[chips[r], core]
        net.landed(("fq", r), ref, devices[r])
        net.start(("fqc", r), ref, ref, at.to_core)

    net.landed("dby", by, at.to_y)
    net.landed("dbx", bx, at.to_x)
    sdx[3, top] = (hg[top] + by[...].astype(f32)).astype(bf16)
    sdx[3, low] = (hg[low] + bx[...].astype(f32)).astype(bf16)
    local(sdx.at[3], dx_out)

    for name in ("o", "i", "w"):
        finish_spread(name)
    for name in ("o", "i", "w"):
        close_spread(name)
    net.landed("fqc", gqkv_out.at[p, other], at.to_core)
    for r in range(3):
        net.landed(("fqc", r), gqkv_out.at[chips[r], other], at.to_core)
    done = len(loads) + len(halves) + len(later)
    for copy in slots[done:]:
        copy.wait()
    net.drain()


BACKWARD_COPIES = 110


def backward_call(*operands):
    any_ = pl.BlockSpec(memory_space=pl.ANY)
    shape = jax.ShapeDtypeStruct
    vmem = pltpu.VMEM
    return pl.pallas_call(
        backward_kernel,
        name="backward_attention",
        out_shape=(
            shape((ROWS, D), bf16),
            shape((GROUP, 2, 96, WIDE), bf16),
            shape((192, FF), bf16),
            shape((CTX, 96, D), bf16),
            shape((GROUP, 48, D), bf16),
            shape((8, D), f32),
        ),
        in_specs=[any_] * 15,
        out_specs=[any_] * 6,
        scratch_shapes=[
            vmem((4, 192, ROWS), bf16),
            vmem((LOCAL, 64, QUERIES), f32),
            vmem((LOCAL, 8, QUERIES), f32),
            vmem((LOCAL, 128, QUERIES), bf16),
            vmem((LOCAL, 128, QUERIES), bf16),
            vmem((LOCAL, SLOTS, 128), bf16),
            vmem((LOCAL, SLOTS, 128), bf16),
            vmem((LOCAL, 64, SLOTS), bf16),
            vmem((LOCAL, 128, QUERIES), bf16),
            vmem((LOCAL, 128, QUERIES), bf16),
            vmem((LOCAL, SLOTS, 128), f32),
            vmem((LOCAL, 4, ROWS, 128), f32),
            vmem((LOCAL, 64, QUERIES), f32),
            vmem((4, GROUP, 96, D), bf16),
            vmem((4, GROUP, 240, 384), bf16),
            vmem((4, GROUP, 240, 384), bf16),
            vmem((2, GROUP, 128, 384), bf16),
            vmem((2, GROUP, 112, 384), bf16),
            vmem((2, 48, D), bf16),
            vmem((2, 48, D), bf16),
            vmem((2, 3, 48, D), bf16),
            vmem((4, 48, D), bf16),
            vmem((2, 48, 384), bf16),
            vmem((2, 48, 384), bf16),
            vmem((48, 384), bf16),
            vmem((48, 384), bf16),
            vmem((96, D), bf16),
            vmem((GROUP, 128, 384), bf16),
            vmem((GROUP, 112, 384), bf16),
            vmem((3, 48, D), bf16),
            vmem((3, 240, 384), bf16),
            vmem((4, 4, 96, D), bf16),
            vmem((GROUP, 2, 96, WIDE), bf16),
            vmem((4, ROWS, WIDE), bf16),
            vmem((4, ROWS, D), bf16),
            vmem((2, 192, D), bf16),
            vmem((2, 192, D), bf16),
            vmem((192, D), bf16),
            vmem((192, D), bf16),
            vmem((ROWS, D), f32),
            vmem((GROUP, 2, 96, WIDE), f32),
            vmem((GROUP, 96, WIDE), bf16),
            vmem((GROUP, 96, WIDE), bf16),
            vmem((3, 96, WIDE), bf16),
            vmem((GROUP, 8, D), f32),
            vmem((3, 8, D), f32),
            vmem((8, D), f32),
            vmem((3, 8, D), f32),
            vmem((8, D), f32),
            pltpu.SemaphoreType.DMA((BACKWARD_COPIES,)),
            pltpu.SemaphoreType.DMA((BACKWARD_COPIES,)),
            pltpu.SemaphoreType.DMA((48,)),
        ],
        compiler_params=pltpu.CompilerParams(
            collective_id=1, has_side_effects=True, vmem_limit_bytes=63 << 20
        ),
    )(*operands)


def finish_kernel(
    low_in, dx_in, gqkv_in, gi_in, go_in, gw_in,
    low_out, dx_out, q_out, k_out, v_out, gi_out, go_out, gw_out,
    low, dx, gqkv, gi, go, gw, q, k, v, wide_i, wide_o, wide_w, reads, writes,
):
    loads = [
        pltpu.make_async_copy(src, dst, reads.at[i])
        for i, (src, dst) in enumerate(
            ((gi_in, gi), (go_in, go), (gw_in, gw), (gqkv_in, gqkv), (low_in, low), (dx_in, dx))
        )
    ]
    for copy in loads:
        copy.start()
    stores = []

    def store(src, dst):
        copy = pltpu.make_async_copy(src, dst, writes.at[len(stores)])
        stores.append(copy)
        copy.start()

    for copy, narrow, wide, dst in (
        (loads[0], gi, wide_i, gi_out),
        (loads[1], go, wide_o, go_out),
        (loads[2], gw, wide_w, gw_out),
    ):
        copy.wait()
        wide[...] = narrow[...].astype(f32)
        store(wide, dst)
    loads[3].wait()
    lane = lax.broadcasted_iota(jnp.int32, (192, 128), 1)

    def piece(chip, tile, side, wanted):
        value = gqkv[chip, :, 128 * tile : 128 * tile + 128].astype(f32)
        return value if side == wanted else pltpu.roll(value, 64, 1)

    for tile in range(6):
        cols = pl.ds(128 * tile, 128)
        left, right = [divmod(g, LOCAL) for g in (2 * tile, 2 * tile + 1)]
        for ref, place in (
            (k, lambda h: (h, 0)),
            (v, lambda h: (h, 1)),
            (q, lambda h: (3 + h // 2, h % 2)),
        ):
            a = piece(left[0], *place(left[1]), 0)
            b = piece(right[0], *place(right[1]), 1)
            ref[:, cols] = jnp.where(lane < 64, a, b)
    for src, dst in ((q, q_out), (k, k_out), (v, v_out)):
        store(src, dst)
    loads[4].wait()
    store(low, low_out)
    loads[5].wait()
    store(dx, dx_out)
    for copy in stores:
        copy.wait()


def finish_call(*operands):
    any_ = pl.BlockSpec(memory_space=pl.ANY)
    vmem = pltpu.VMEM
    square, wide = (192, D), (192, FF)
    shapes = [((ROWS, D), bf16)] * 2 + [(square, f32)] * 3
    shapes += [(wide, f32), ((D, D), f32), (square, f32)]
    return pl.pallas_call(
        finish_kernel,
        name="finish",
        out_shape=[jax.ShapeDtypeStruct(*pair) for pair in shapes],
        in_specs=[any_] * 6,
        out_specs=[any_] * 8,
        scratch_shapes=[
            vmem((ROWS, D), bf16),
            vmem((ROWS, D), bf16),
            vmem((GROUP, 192, WIDE), bf16),
            vmem(wide, bf16),
            vmem((D, D), bf16),
            vmem(square, bf16),
            vmem(square, f32),
            vmem(square, f32),
            vmem(square, f32),
            vmem(wide, f32),
            vmem((D, D), f32),
            vmem(square, f32),
            pltpu.SemaphoreType.DMA((6,)),
            pltpu.SemaphoreType.DMA((8,)),
        ],
        compiler_params=pltpu.CompilerParams(vmem_limit_bytes=67043328),
    )(*operands)


def small_plane(
    states,
    lengths,
    query_weight,
    query_bias,
    key_weight,
    value_weight,
    value_bias,
    output_weight,
    output_bias,
    first_gain,
    first_shift,
    inner_weight,
    inner_bias,
    outer_weight,
    outer_bias,
    second_gain,
    second_shift,
    cotangent,
):
    cycle_place = lax.axis_index(RING)
    shard = lax.axis_index(FSDP)
    wqkv = split_weights(cycle_place // 2, query_weight, key_weight, value_weight)
    vectors = pack_vectors(
        query_bias,
        value_bias,
        inner_bias,
        [output_bias, first_gain, first_shift, outer_bias, second_gain, second_shift],
    )
    low, mg, gi, gw, own, summed, hg, small, xs, wall, qt, ka, va, kt, ot, lse = (
        forward_call(
            lengths,
            states.reshape(4, 96, D),
            wqkv,
            vectors,
            inner_weight,
            outer_weight.reshape(2, CTX, 48, D),
            output_weight.reshape(GROUP, 48, D),
            cotangent[0],
        )
    )
    dx, gqkv, gi, go, gw, sums = backward_call(
        mg, ot, lse, qt, ka, va, kt, gi, gw, own, summed, xs, wall, hg, small
    )
    low, dx, gq, gk, gv, gi, go, gw = finish_call(
        low,
        dx,
        gqkv.reshape(GROUP, 192, WIDE),
        gi,
        go.reshape(D, D),
        gw.reshape(192, D),
    )
    narrow = lax.dynamic_slice_in_dim(sums[2:8], shard * 192, 192, axis=1)
    value_bias_grad = sums[0, :384].reshape(LOCAL, 2, 64)[:, 1].reshape(192)
    return (
        low[None],
        dx[None],
        gq,
        sums[0, 384:576],
        gk,
        gv,
        value_bias_grad,
        gw,
        narrow[0],
        narrow[1],
        narrow[2],
        gi,
        sums[1],
        go,
        narrow[3],
        narrow[4],
        narrow[5],
    )


def keep_state(carried):
    return carried


def per_device(
    states,
    lengths,
    query_weight,
    query_bias,
    key_weight,
    value_weight,
    value_bias,
    output_weight,
    output_bias,
    first_gain,
    first_shift,
    inner_weight,
    inner_bias,
    outer_weight,
    outer_bias,
    second_gain,
    second_shift,
    cotangent,
):
    row_count = states.shape[1]
    cycle_size = lax.axis_size(RING)
    cycle_place = lax.axis_index(RING)
    sequence = lax.axis_index(FSDP)
    length = lengths[sequence]
    offsets = jnp.arange(row_count, dtype=jnp.int32)
    row_keep = cycle_place * row_count + offsets < length
    inputs = states[0]
    input_float = inputs.astype(jnp.float32)
    attention_set = (
        lax.all_gather(query_weight, FSDP, axis=0, tiled=True),
        lax.all_gather(key_weight, FSDP, axis=0, tiled=True),
        lax.all_gather(value_weight, FSDP, axis=0, tiled=True),
        lax.all_gather(output_weight, FSDP, axis=0, tiled=True),
        lax.all_gather(query_bias, FSDP, axis=0, tiled=True),
        lax.all_gather(value_bias, FSDP, axis=0, tiled=True),
        lax.all_gather(output_bias, FSDP, axis=0, tiled=True),
        lax.all_gather(first_gain, FSDP, axis=0, tiled=True),
        lax.all_gather(first_shift, FSDP, axis=0, tiled=True),
    )
    query_full = attention_set[0]
    key_full = attention_set[1]
    value_full = attention_set[2]
    output_full = attention_set[3]
    query_add = attention_set[4].astype(jnp.float32)
    value_add = attention_set[5].astype(jnp.float32)
    output_add = attention_set[6].astype(jnp.float32)
    gain_one = attention_set[7].astype(jnp.float32)
    shift_one = attention_set[8].astype(jnp.float32)
    queries = (
        (jnp.dot(inputs, query_full, preferred_element_type=jnp.float32) + query_add) * 0.125
    ).astype(jnp.bfloat16)
    key_rows = jnp.dot(inputs, key_full, preferred_element_type=jnp.float32).astype(jnp.bfloat16)
    values = (jnp.dot(inputs, value_full, preferred_element_type=jnp.float32) + value_add).astype(
        jnp.bfloat16
    )
    query_heads = queries.reshape(row_count, H, HD)

    def forward_block(key_block, value_block, key_start, running_state):

        def forward_compute(carried):
            running, exp_total, accum = carried
            key_keep = key_start + offsets < length
            scores = jnp.einsum(
                "qhd,khd->hqk",
                query_heads,
                key_block.reshape(row_count, H, HD),
                preferred_element_type=jnp.float32,
            )
            scores = jnp.where(key_keep[None, None, :], scores, -1e30)
            newest = jnp.maximum(running, jnp.max(scores, axis=2))
            factor = jnp.exp(running - newest)
            weights = jnp.exp(scores - newest[:, :, None])
            exp_total = exp_total * factor + jnp.sum(weights, axis=2)
            update = jnp.einsum(
                "hqk,khd->qhd",
                weights.astype(jnp.bfloat16),
                value_block.reshape(row_count, H, HD),
                preferred_element_type=jnp.float32,
            )
            accum = accum * factor.T[:, :, None] + update
            return (newest, exp_total, accum)

        return lax.cond(key_start < length, forward_compute, keep_state, running_state)

    start_state = (
        jnp.full((H, row_count), -1e30, jnp.float32),
        jnp.zeros((H, row_count), jnp.float32),
        jnp.zeros((row_count, H, HD), jnp.float32),
    )

    def cycle_turn(turn_index, carried):
        key_block, value_block, running_state = carried
        owner_index = (cycle_place - turn_index) % cycle_size
        running_state = forward_block(
            key_block, value_block, owner_index * row_count, running_state
        )
        key_block, value_block = passed_along((key_block, value_block), RING, 1)
        return (key_block, value_block, running_state)

    key_block, value_block, running_state = lax.fori_loop(
        0, cycle_size - 1, cycle_turn, (key_rows, values, start_state)
    )
    last_owner = (cycle_place + 1) % cycle_size
    running, exp_total, accum = forward_block(
        key_block, value_block, last_owner * row_count, running_state
    )
    log_total = running + jnp.log(exp_total)
    attention_value = (accum / exp_total.T[:, :, None]).reshape(row_count, D)
    mixed = attention_value.astype(jnp.bfloat16)
    attended = jnp.dot(mixed, output_full, preferred_element_type=jnp.float32) + output_add
    first_normed, first_scale = normalize(input_float + attended)
    first = first_normed * gain_one + shift_one
    first_low = first.astype(jnp.bfloat16)
    feed_set = (
        lax.all_gather(inner_weight, FSDP, axis=0, tiled=True),
        lax.all_gather(outer_weight, FSDP, axis=0, tiled=True),
        lax.all_gather(inner_bias, FSDP, axis=0, tiled=True),
        lax.all_gather(outer_bias, FSDP, axis=0, tiled=True),
        lax.all_gather(second_gain, FSDP, axis=0, tiled=True),
        lax.all_gather(second_shift, FSDP, axis=0, tiled=True),
    )
    inner_full = feed_set[0]
    outer_full = feed_set[1]
    inner_add = feed_set[2].astype(jnp.float32)
    outer_add = feed_set[3].astype(jnp.float32)
    gain_two = feed_set[4].astype(jnp.float32)
    shift_two = feed_set[5].astype(jnp.float32)
    inner = jnp.dot(first_low, inner_full, preferred_element_type=jnp.float32) + inner_add
    activated = jax.nn.gelu(inner, approximate=False).astype(jnp.bfloat16)
    outer = jnp.dot(activated, outer_full, preferred_element_type=jnp.float32) + outer_add
    second_normed, second_scale = normalize(first + outer)
    second = second_normed * gain_two + shift_two
    layer_output = jnp.where(row_keep[:, None], second, 0.0).astype(jnp.bfloat16)[None]
    query_full = attention_set[0]
    key_full = attention_set[1]
    value_full = attention_set[2]
    output_full = attention_set[3]
    gain_one = attention_set[7].astype(jnp.float32)
    inner_full = feed_set[0]
    outer_full = feed_set[1]
    gain_two = feed_set[4].astype(jnp.float32)
    upstream = jnp.where(row_keep[:, None], cotangent[0].astype(jnp.float32), 0.0)
    second_grad, second_gain_grad, second_shift_grad = norm_back(
        upstream, second_normed, second_scale, gain_two
    )
    outer_low = second_grad.astype(jnp.bfloat16)
    outer_bias_grad = jnp.sum(second_grad, axis=0)
    outer_weight_grad = jnp.dot(activated.T, outer_low, preferred_element_type=jnp.float32)
    inner_grad = jnp.dot(outer_low, outer_full.T, preferred_element_type=jnp.float32) * gelu_slope(
        inner
    )
    inner_low = inner_grad.astype(jnp.bfloat16)
    inner_bias_grad = jnp.sum(inner_grad, axis=0)
    inner_weight_grad = jnp.dot(first_low.T, inner_low, preferred_element_type=jnp.float32)
    first_grad = second_grad + jnp.dot(inner_low, inner_full.T, preferred_element_type=jnp.float32)
    hidden_grad, first_gain_grad, first_shift_grad = norm_back(
        first_grad, first_normed, first_scale, gain_one
    )
    attended_low = hidden_grad.astype(jnp.bfloat16)
    output_bias_grad = jnp.sum(hidden_grad, axis=0)
    output_weight_grad = jnp.dot(mixed.T, attended_low, preferred_element_type=jnp.float32)
    mixed_grad = jnp.dot(attended_low, output_full.T, preferred_element_type=jnp.float32).astype(
        jnp.bfloat16
    )
    delta = jnp.sum(
        (mixed_grad.astype(jnp.float32) * attention_value).reshape(row_count, H, HD), axis=2
    ).T

    def back_block(
        query_block,
        upstream_block,
        log_block,
        delta_block,
        key_block,
        value_block,
        key_start,
        grads,
    ):

        def back_compute(carried):
            query_grad, key_grad, value_grad = carried
            key_keep = key_start + offsets < length
            query_three = query_block.reshape(row_count, H, HD)
            upstream_three = upstream_block.reshape(row_count, H, HD)
            key_three = key_block.reshape(row_count, H, HD)
            value_three = value_block.reshape(row_count, H, HD)
            scores = jnp.einsum(
                "qhd,khd->hqk", query_three, key_three, preferred_element_type=jnp.float32
            )
            weights = jnp.where(
                key_keep[None, None, :], jnp.exp(scores - log_block[:, :, None]), 0.0
            )
            weight_grad = jnp.einsum(
                "qhd,khd->hqk", upstream_three, value_three, preferred_element_type=jnp.float32
            )
            score_grad = (weights * (weight_grad - delta_block[:, :, None])).astype(jnp.bfloat16)
            query_grad = query_grad + jnp.einsum(
                "hqk,khd->qhd", score_grad, key_three, preferred_element_type=jnp.float32
            ).reshape(row_count, D)
            key_grad = key_grad + jnp.einsum(
                "hqk,qhd->khd", score_grad, query_three, preferred_element_type=jnp.float32
            ).reshape(row_count, D)
            value_grad = value_grad + jnp.einsum(
                "hqk,qhd->khd",
                weights.astype(jnp.bfloat16),
                upstream_three,
                preferred_element_type=jnp.float32,
            ).reshape(row_count, D)
            return (query_grad, key_grad, value_grad)

        return lax.cond(key_start < length, back_compute, keep_state, grads)

    zero_grad = jnp.zeros((row_count, D), jnp.float32)

    def key_turn(turn_index, carried):
        key_block, value_block, query_grad, key_grad, value_grad = carried
        owner_index = (cycle_place - turn_index) % cycle_size
        query_grad, key_grad, value_grad = back_block(
            queries,
            mixed_grad,
            log_total,
            delta,
            key_block,
            value_block,
            owner_index * row_count,
            (query_grad, key_grad, value_grad),
        )
        key_block, value_block = passed_along((key_block, value_block), RING, 1)
        key_grad, value_grad = (
            passed_along(key_grad.astype(jnp.bfloat16), RING, 1).astype(key_grad.dtype),
            passed_along(value_grad.astype(jnp.bfloat16), RING, 1).astype(value_grad.dtype),
        )
        return (key_block, value_block, query_grad, key_grad, value_grad)

    key_block, value_block, query_grad, key_grad, value_grad = lax.fori_loop(
        0, cycle_size - 1, key_turn, (key_rows, values, zero_grad, zero_grad, zero_grad)
    )
    query_grad, key_grad, value_grad = back_block(
        queries,
        mixed_grad,
        log_total,
        delta,
        key_block,
        value_block,
        last_owner * row_count,
        (query_grad, key_grad, value_grad),
    )
    key_grad, value_grad = (
        passed_along(key_grad.astype(jnp.bfloat16), RING, 1).astype(key_grad.dtype),
        passed_along(value_grad.astype(jnp.bfloat16), RING, 1).astype(value_grad.dtype),
    )
    query_low = query_grad.astype(jnp.bfloat16) * 0.125
    key_low = key_grad.astype(jnp.bfloat16)
    value_low = value_grad.astype(jnp.bfloat16)
    query_weight_grad = jnp.dot(inputs.T, query_low, preferred_element_type=jnp.float32)
    query_bias_grad = jnp.sum(query_low.astype(jnp.float32), axis=0)
    key_weight_grad = jnp.dot(inputs.T, key_low, preferred_element_type=jnp.float32)
    value_weight_grad = jnp.dot(inputs.T, value_low, preferred_element_type=jnp.float32)
    value_bias_grad = jnp.sum(value_low.astype(jnp.float32), axis=0)
    input_grad = (
        hidden_grad
        + jnp.dot(query_low, query_full.T, preferred_element_type=jnp.float32)
        + jnp.dot(key_low, key_full.T, preferred_element_type=jnp.float32)
        + jnp.dot(value_low, value_full.T, preferred_element_type=jnp.float32)
    ).astype(jnp.bfloat16)[None]
    local_grads = (
        query_weight_grad,
        query_bias_grad,
        key_weight_grad,
        value_weight_grad,
        value_bias_grad,
        output_weight_grad,
        output_bias_grad,
        first_gain_grad,
        first_shift_grad,
        inner_weight_grad,
        inner_bias_grad,
        outer_weight_grad,
        outer_bias_grad,
        second_gain_grad,
        second_shift_grad,
    )
    shards = (
        lax.psum_scatter(
            local_grads[0].astype(jnp.bfloat16), FSDP, scatter_dimension=0, tiled=True
        ).astype(jnp.float32),
        lax.psum_scatter(
            local_grads[1].astype(jnp.bfloat16), FSDP, scatter_dimension=0, tiled=True
        ).astype(jnp.float32),
        lax.psum_scatter(
            local_grads[2].astype(jnp.bfloat16), FSDP, scatter_dimension=0, tiled=True
        ).astype(jnp.float32),
        lax.psum_scatter(
            local_grads[3].astype(jnp.bfloat16), FSDP, scatter_dimension=0, tiled=True
        ).astype(jnp.float32),
        lax.psum_scatter(
            local_grads[4].astype(jnp.bfloat16), FSDP, scatter_dimension=0, tiled=True
        ).astype(jnp.float32),
        lax.psum_scatter(
            local_grads[5].astype(jnp.bfloat16), FSDP, scatter_dimension=0, tiled=True
        ).astype(jnp.float32),
        lax.psum_scatter(
            local_grads[6].astype(jnp.bfloat16), FSDP, scatter_dimension=0, tiled=True
        ).astype(jnp.float32),
        lax.psum_scatter(
            local_grads[7].astype(jnp.bfloat16), FSDP, scatter_dimension=0, tiled=True
        ).astype(jnp.float32),
        lax.psum_scatter(
            local_grads[8].astype(jnp.bfloat16), FSDP, scatter_dimension=0, tiled=True
        ).astype(jnp.float32),
        lax.psum_scatter(
            local_grads[9].astype(jnp.bfloat16), FSDP, scatter_dimension=0, tiled=True
        ).astype(jnp.float32),
        lax.psum_scatter(
            local_grads[10].astype(jnp.bfloat16), FSDP, scatter_dimension=0, tiled=True
        ).astype(jnp.float32),
        lax.psum_scatter(
            local_grads[11].astype(jnp.bfloat16), FSDP, scatter_dimension=0, tiled=True
        ).astype(jnp.float32),
        lax.psum_scatter(
            local_grads[12].astype(jnp.bfloat16), FSDP, scatter_dimension=0, tiled=True
        ).astype(jnp.float32),
        lax.psum_scatter(
            local_grads[13].astype(jnp.bfloat16), FSDP, scatter_dimension=0, tiled=True
        ).astype(jnp.float32),
        lax.psum_scatter(
            local_grads[14].astype(jnp.bfloat16), FSDP, scatter_dimension=0, tiled=True
        ).astype(jnp.float32),
    )
    totals = (
        lax.psum(shards[0].astype(jnp.bfloat16), RING).astype(jnp.float32),
        lax.psum(shards[1].astype(jnp.bfloat16), RING).astype(jnp.float32),
        lax.psum(shards[2].astype(jnp.bfloat16), RING).astype(jnp.float32),
        lax.psum(shards[3].astype(jnp.bfloat16), RING).astype(jnp.float32),
        lax.psum(shards[4].astype(jnp.bfloat16), RING).astype(jnp.float32),
        lax.psum(shards[5].astype(jnp.bfloat16), RING).astype(jnp.float32),
        lax.psum(shards[6].astype(jnp.bfloat16), RING).astype(jnp.float32),
        lax.psum(shards[7].astype(jnp.bfloat16), RING).astype(jnp.float32),
        lax.psum(shards[8].astype(jnp.bfloat16), RING).astype(jnp.float32),
        lax.psum(shards[9].astype(jnp.bfloat16), RING).astype(jnp.float32),
        lax.psum(shards[10].astype(jnp.bfloat16), RING).astype(jnp.float32),
        lax.psum(shards[11].astype(jnp.bfloat16), RING).astype(jnp.float32),
        lax.psum(shards[12].astype(jnp.bfloat16), RING).astype(jnp.float32),
        lax.psum(shards[13].astype(jnp.bfloat16), RING).astype(jnp.float32),
        lax.psum(shards[14].astype(jnp.bfloat16), RING).astype(jnp.float32),
    )
    return (
        layer_output,
        input_grad,
        totals[0],
        totals[1],
        totals[2],
        totals[3],
        totals[4],
        totals[5],
        totals[6],
        totals[7],
        totals[8],
        totals[9],
        totals[10],
        totals[11],
        totals[12],
        totals[13],
        totals[14],
    )


def solution(mesh):
    small = mesh.shape[RING] == CTX and mesh.shape[FSDP] == GROUP
    return jax.shard_map(
        small_plane if small else per_device,
        mesh=mesh,
        in_specs=(
            P(FSDP, RING, None),
            P(),
            P(FSDP, None),
            P(FSDP),
            P(FSDP, None),
            P(FSDP, None),
            P(FSDP),
            P(FSDP, None),
            P(FSDP),
            P(FSDP),
            P(FSDP),
            P(FSDP, None),
            P(FSDP),
            P(FSDP, None),
            P(FSDP),
            P(FSDP),
            P(FSDP),
            P(FSDP, RING, None),
        ),
        out_specs=(
            P(FSDP, RING, None),
            P(FSDP, RING, None),
            P(FSDP, None),
            P(FSDP),
            P(FSDP, None),
            P(FSDP, None),
            P(FSDP),
            P(FSDP, None),
            P(FSDP),
            P(FSDP),
            P(FSDP),
            P(FSDP, None),
            P(FSDP),
            P(FSDP, None),
            P(FSDP),
            P(FSDP),
            P(FSDP),
        ),
        check_vma=False,
    )
```
